32 devices in a mesh: dp: 8 (over y, x, core), expert: 4 (over z).
Axes of the slice: x: 2, y: 2, z: 4, core: 2. Of those that a mesh axis runs over, the one named last changes fastest.
Arguments:
- hidden: bfloat16 [16384, 1024], P(('dp', 'expert')), may hold values from -6 to 6
- cotangent: bfloat16 [16384, 1024], P(('dp', 'expert')), may hold values from -6 to 6
- lengths: int32 [32], replicated, may hold values from 128 to 512, as said below
- adapter_ids: int32 [32], replicated, may hold values from 0 to 7
- routes: int32 [16384, 8], P('dp'), may hold values from 0 to 15, all different within a row; in each aligned block of 512 rows (0 to 511, 512 to 1023, ...) at most 384 rows name the same one
- attn_gain: bfloat16 [1024], replicated, may hold values from 0.25 to 1.75
- ffn_gain: bfloat16 [1024], replicated, may hold values from 0.25 to 1.75
- query_key_value_weight: bfloat16 [1024, 2048], P('dp'), may hold values from -0.1875 to 0.1875
- w_out: bfloat16 [1024, 1024], P('dp'), may hold values from -0.75 to 0.75
- w_router: bfloat16 [1024, 16], replicated, may hold values from -0.09375 to 0.09375
- w_gate_up: bfloat16 [16, 1024, 1024], P('expert'), may hold values from -0.1875 to 0.1875
- w_down: bfloat16 [16, 512, 1024], P('expert'), may hold values from -0.75 to 0.75
- attention_lowmap: bfloat16 [4, 8, 1024, 16], P(None, None, 'dp'), may hold values from -0.1875 to 0.1875
- attention_query_key_value_upmap: bfloat16 [8, 16, 2048], P(None, None, 'dp'), may hold values from -1.5 to 1.5
- attention_output_upmap: bfloat16 [8, 16, 1024], P(None, None, 'dp'), may hold values from -6 to 6
- expert_gate_up_lowmap: bfloat16 [16, 8, 1024, 32], P('expert'), may hold values from -0.1875 to 0.1875
- expert_gate_up_upmap: bfloat16 [16, 8, 2, 16, 512], P('expert'), may hold values from -1.5 to 1.5
- expert_down_lowmap: bfloat16 [16, 8, 512, 16], P('expert'), may hold values from -0.25 to 0.25
- expert_down_upmap: bfloat16 [16, 8, 16, 1024], P('expert'), may hold values from -4 to 4
Outputs:
- out: bfloat16 [16384, 1024], P(('dp', 'expert'))
- grad_hidden: bfloat16 [16384, 1024], P(('dp', 'expert'))
- grad_mixer_a: float32 [4, 8, 1024, 16], P(None, None, ('dp', 'expert'))
- grad_mixer_b_qkv: float32 [8, 16, 2048], P(None, None, ('dp', 'expert'))
- grad_mixer_b_out: float32 [8, 16, 1024], P(None, None, ('dp', 'expert'))
- grad_exp_a_in: float32 [16, 8, 1024, 32], P('expert', None, 'dp')
- grad_exp_b_in: float32 [16, 8, 2, 16, 512], P('expert', None, None, None, 'dp')
- grad_exp_a_down: float32 [16, 8, 512, 16], P('expert', None, 'dp')
- grad_exp_b_down: float32 [16, 8, 16, 1024], P('expert', None, None, 'dp')
The draws below stay inside these ranges and needn't reach their ends.
Inputs may be any that keep to these rules, and one draw needn't show every extreme that they name: `routes`: each row names 8 different experts. Among the 512 rows of one sequence no expert is named more than 384 times, and in every draw some sequence names some expert exactly 384 times. `lengths`: some sequence is 512 long in every draw.
All inputs are finite; a program needn't handle non-finite values.
Results may differ from the reference program's by a relative error of at most 0.022.
The reference program's roundings to bfloat16 on the way count: a program that leaves them out, or rounds other values in their place, can miss the bound.
Values may be sent and summed in bfloat16 or wider, within the bound.
No kernel may reach another device: no remote copies, remote signals or barrier semaphores. Data moves between devices by JAX's collectives and lax.ppermute only.
A program may use at most 320 MiB of HBM per device.

```python
import math
import jax
import jax.numpy as jnp
import numpy as np
from jax import lax

MODEL_WIDTH = 1024
HQ = 16
KVH = 8
HS = 64
H = 512
TOP = 8
R = 16
NA = 8
SEQUENCE_SLOTS = 512
EXPERTS = 16
SEQS = 32
TOKEN_SLOTS = 16384
CAP = 384
QD = 1024
QKV = 2048
N_DP = 8
N_EXPERT = 4


def draw_lengths(key, part):
    first_key, second_key = jax.random.split(key)
    drawn = jax.random.randint(first_key, (SEQS,), SEQUENCE_SLOTS // 4, SEQUENCE_SLOTS + 1, dtype=jnp.int32)
    longest = jax.random.randint(second_key, (), 0, SEQS, dtype=jnp.int32)
    return jnp.where(jnp.arange(SEQS, dtype=jnp.int32) == longest, SEQUENCE_SLOTS, drawn).astype(jnp.int32)


def place_ends(values, stream_key, smallest, largest):
    dims = values.shape
    index_at = [jax.random.randint(jax.random.fold_in(stream_key, axis), (), 0, dims[axis]) for axis in range(len(dims))]
    values = values.at[tuple(index_at)].set(smallest)
    longest = dims.index(max(dims))
    index_at[longest] = (index_at[longest] + 1) % dims[longest]
    return values.at[tuple(index_at)].set(largest)


def levels(rng, dims, cuts, least, top_value):
    level = 1.0
    for position, blocks in cuts:
        heights = jax.random.uniform(jax.random.fold_in(jax.random.fold_in(rng, 6), position), (blocks,), jnp.float32, least / len(cuts), top_value / len(cuts))
        level = level * jnp.repeat(jnp.exp(heights), dims[position] // blocks).reshape((-1,) + (1,) * (len(dims) - 1 - position))
    return level


def assign_block(rng, own, number, rows, count, top, limit, skew):
    ranking = jax.random.permutation(rng, count)
    packed, usual = portions_of(count, rows * top, limit, skew, True), portions_of(count, rows * top, limit, skew, False)
    places = jnp.arange(count)

    def named(sizes, offset_by):
        used = int((sizes > 0).sum())
        fixed = max(1, used // 4)
        moved = fixed + (places - fixed + offset_by * (used - fixed)) % max(1, count - fixed)
        return jnp.zeros((count,), jnp.int32).at[ranking[jnp.where(places < fixed, places, moved)]].set(jnp.asarray(sizes, jnp.int32))

    sizes = jnp.where(number % 4 == 0, named(packed, number // 4), named(usual, number - number // 4 - 1))
    mixed = jax.random.permutation(jax.random.fold_in(own, 3), count)
    source_of, receiver = mixed[0:count // 2 * 2:2], mixed[1:count // 2 * 2:2]
    margin = jnp.minimum(sizes[source_of] - 1, limit - sizes[receiver]) // 2
    margin = jnp.where((source_of == ranking[0]) | (receiver == ranking[0]) | (sizes[receiver] == 0), 0, jnp.maximum(margin, 0))
    moved = jax.random.randint(jax.random.fold_in(own, 4), (count // 2,), 0, 1 << 20) % (margin + 1)
    sizes = sizes.at[source_of].add(-moved).at[receiver].add(moved)
    labels = jnp.searchsorted(jnp.cumsum(sizes), jnp.arange(rows * top), side="right").astype(jnp.int32)
    table = labels.reshape(top, rows).T
    table = table[jax.random.permutation(jax.random.fold_in(own, 1), rows)]
    offset_by = jax.random.randint(jax.random.fold_in(own, 2), (rows, 1), 0, top)
    return jnp.take_along_axis(table, (jnp.arange(top)[None, :] + offset_by) % top, axis=1)


def portions_of(count, total, bound, slope, full):
    weights = [(1 << 20) // math.isqrt(rank ** slope) + 1 for rank in range(1, count + 1)]
    largest = bound if full else min(bound, max(-(-total // count), total * weights[0] // sum(weights)))
    least = 1 if total - largest >= count - 1 else 0
    holding, spare = [largest] + [least] * (count - 1), total - largest - least * (count - 1)
    while spare > 0:
        candidates = [i for i in range(1, count) if holding[i] < largest] or [i for i in range(1, count) if holding[i] < bound]
        whole, remaining = sum([weights[i] for i in candidates]), spare
        for i in candidates:
            more = min(bound - holding[i], max(1, remaining * weights[i] // whole), spare)
            holding[i] = holding[i] + more
            spare = spare - more
    return np.array(holding)


def noise(rng, shape, scale, limit, pieces=(), held_as=jnp.bfloat16):
    entries = scale * jax.random.normal(rng, shape, jnp.float32)
    if pieces:
        entries = entries * levels(rng, shape, pieces, -0.22, 0.18)
    return jnp.clip(entries, -limit, limit).astype(held_as)


def setup_inputs(seed: int = 0) -> dict:
    keys = jax.random.split(jax.random.key(seed), 20)
    hidden = noise(keys[0], (TOKEN_SLOTS, MODEL_WIDTH), 1.0, 6.0, ((0, 32),))
    cotangent = noise(keys[1], (TOKEN_SLOTS, MODEL_WIDTH), 1.0, 6.0, ((0, 32),))
    lengths = draw_lengths(jax.random.fold_in(keys[19], 71), 0)
    adapter_ids = place_ends(jax.random.randint(keys[3], (SEQS,), 0, NA), jax.random.fold_in(keys[3], 1), 0, NA - 1).astype(jnp.int32)
    routes_keys = jax.random.split(jax.random.fold_in(keys[4], 1), TOKEN_SLOTS // SEQUENCE_SLOTS)
    routes_turns = jax.random.permutation(jax.random.fold_in(keys[4], 3), TOKEN_SLOTS // SEQUENCE_SLOTS)
    routes = jax.vmap(lambda own, number: assign_block(jax.random.fold_in(keys[4], 2), own, number, SEQUENCE_SLOTS, EXPERTS, TOP, CAP, 1))(routes_keys, routes_turns).reshape((TOKEN_SLOTS, TOP))
    attn_gain = jnp.clip(1.0 + 0.15 * jax.random.normal(keys[5], (MODEL_WIDTH,), jnp.float32), 0.25, 1.75).astype(jnp.bfloat16)
    ffn_gain = jnp.clip(1.0 + 0.15 * jax.random.normal(keys[6], (MODEL_WIDTH,), jnp.float32), 0.25, 1.75).astype(jnp.bfloat16)
    query_key_value_weight = noise(keys[7], (MODEL_WIDTH, QKV), MODEL_WIDTH ** -0.5, 0.1875, ((0, 8),))
    w_out = noise(keys[8], (QD, MODEL_WIDTH), (QD // 16) ** -0.5, 0.75, ((0, 8),))
    w_router = noise(keys[9], (MODEL_WIDTH, EXPERTS), (0.5 / MODEL_WIDTH ** 0.5), 0.09375)
    w_gate_up = noise(keys[10], (EXPERTS, MODEL_WIDTH, 2 * H), MODEL_WIDTH ** -0.5, 0.1875, ((0, 4),))
    w_down = noise(keys[11], (EXPERTS, H, MODEL_WIDTH), (H // 8) ** -0.5, 0.75, ((0, 4),))
    attention_lowmap = noise(keys[12], (4, NA, MODEL_WIDTH, R), MODEL_WIDTH ** -0.5, 0.1875, ((2, 8),))
    attention_query_key_value_upmap = noise(keys[13], (NA, R, QKV), R ** -0.5, 1.5, ((2, 8),))
    attention_output_upmap = noise(keys[14], (NA, R, MODEL_WIDTH), (R // 16) ** -0.5, 6.0, ((2, 8),))
    expert_gate_up_lowmap = noise(keys[15], (EXPERTS, NA, MODEL_WIDTH, 2 * R), MODEL_WIDTH ** -0.5, 0.1875, ((0, 4),))
    expert_gate_up_upmap = noise(keys[16], (EXPERTS, NA, 2, R, H), R ** -0.5, 1.5, ((0, 4),))
    expert_down_lowmap = noise(keys[17], (EXPERTS, NA, H, R), H ** -0.5, 0.25, ((0, 4),))
    expert_down_upmap = noise(keys[18], (EXPERTS, NA, R, MODEL_WIDTH), (R // 8) ** -0.5, 4.0, ((0, 4),))
    return dict(hidden=hidden, cotangent=cotangent, lengths=lengths, adapter_ids=adapter_ids, routes=routes, attn_gain=attn_gain, ffn_gain=ffn_gain, query_key_value_weight=query_key_value_weight, w_out=w_out, w_router=w_router, w_gate_up=w_gate_up, w_down=w_down, attention_lowmap=attention_lowmap, attention_query_key_value_upmap=attention_query_key_value_upmap, attention_output_upmap=attention_output_upmap, expert_gate_up_lowmap=expert_gate_up_lowmap, expert_gate_up_upmap=expert_gate_up_upmap, expert_down_lowmap=expert_down_lowmap, expert_down_upmap=expert_down_upmap)


highest_precision = lax.Precision.HIGHEST
epsilon = 1e-06

@jax.custom_vjp
def low(v):
    return lax.optimization_barrier(v.astype(jnp.bfloat16)).astype(jnp.float32)

@jax.custom_vjp
def reduced_backward(v):
    return v

def low_keep(v):
    return (low(v), None)

def low_pass(kept, grad):
    return (grad,)

def back_keep(v):
    return (v, None)

def back_low(kept, grad):
    return (low(grad),)
low.defvjp(low_keep, low_pass)
reduced_backward.defvjp(back_keep, back_low)

def route_slots(routed_token_rows, experts, capacity):
    count_rows = routed_token_rows.shape[0] * routed_token_rows.shape[1]
    flat_routes = routed_token_rows.reshape(count_rows)
    member = (flat_routes[:, None] == jnp.arange(experts, dtype=jnp.int32)[None, :]).astype(jnp.int32)
    earlier = jnp.cumsum(member, 0, dtype=jnp.int32) - member
    route_slot = lax.optimization_barrier(jnp.sum(earlier * member, 1)).astype(jnp.int32)
    slot_table = jnp.full((experts, capacity), -1, jnp.int32)
    slot_table = slot_table.at[flat_routes, route_slot].set(jnp.arange(count_rows, dtype=jnp.int32))
    return (route_slot.reshape(routed_token_rows.shape), slot_table)

def norm_rows(value_rows, gain):
    scale = lax.rsqrt(lax.optimization_barrier(jnp.mean(value_rows * value_rows, -1, keepdims=True)) + epsilon)
    return value_rows * scale * gain

def rope_tables(rows_count, width):
    half_width = width // 2
    frequency = 10000.0 ** (-2.0 * jnp.arange(half_width, dtype=jnp.float32) / width)
    angles = jnp.arange(rows_count, dtype=jnp.float32)[:, None] * frequency[None, :]
    return (jnp.cos(angles)[:, None, :], jnp.sin(angles)[:, None, :])

def rotate(value_rows, cos_table, sin_table):
    half_width = value_rows.shape[-1] // 2
    first_half, second_half = (value_rows[..., :half_width], value_rows[..., half_width:])
    return jnp.concatenate([first_half * cos_table - second_half * sin_table, second_half * cos_table + first_half * sin_table], -1)

def residual_block_forward(value_rows, length_value, adapter_item, routed_token_rows, weight_collection, trainable_params):
    attn_gain, ffn_gain, query_key_value_weight, w_out, w_router, w_gate_up, w_down = weight_collection
    attention_lowmap, attention_query_key_value_upmap, attention_output_upmap, expert_gate_up_lowmap, expert_gate_up_upmap, expert_down_lowmap, expert_down_upmap = trainable_params
    query_total_width = HQ * HS
    key_value_width = KVH * HS
    chooser = (jnp.arange(NA, dtype=jnp.int32) == adapter_item).astype(jnp.float32)
    normed_hidden = low(norm_rows(value_rows, attn_gain))
    reduced_product = reduced_backward(low(jnp.einsum('td,jadr->tjar', normed_hidden, attention_lowmap[:3], precision=highest_precision))) * chooser[None, None, :, None]
    adapter_parts = jnp.concatenate([jnp.einsum('une,neq->uq', reduced_product[:, 0], attention_query_key_value_upmap[:, :, :query_total_width], precision=highest_precision), jnp.einsum('une,neq->uq', reduced_product[:, 1], attention_query_key_value_upmap[:, :, query_total_width:query_total_width + key_value_width], precision=highest_precision), jnp.einsum('une,neq->uq', reduced_product[:, 2], attention_query_key_value_upmap[:, :, query_total_width + key_value_width:], precision=highest_precision)], -1)
    projected_rows = reduced_backward(jnp.dot(normed_hidden, query_key_value_weight, precision=highest_precision) + adapter_parts)
    cos_table, sin_table = rope_tables(SEQUENCE_SLOTS, HS)
    queries = low(rotate(projected_rows[:, :query_total_width].reshape(SEQUENCE_SLOTS, HQ, HS), cos_table, sin_table)).reshape(SEQUENCE_SLOTS, KVH, HQ // KVH, HS)
    key_heads = low(rotate(projected_rows[:, query_total_width:query_total_width + key_value_width].reshape(SEQUENCE_SLOTS, KVH, HS), cos_table, sin_table))
    value_heads = low(projected_rows[:, query_total_width + key_value_width:].reshape(SEQUENCE_SLOTS, KVH, HS))
    scores = reduced_backward(0.125 * jnp.einsum('qhgd,shd->hgqs', queries, key_heads, precision=highest_precision))
    positions = jnp.arange(SEQUENCE_SLOTS, dtype=jnp.int32)
    allowed = (positions[None, :] <= positions[:, None]) & (positions[None, :] < length_value)
    scores = jnp.where(allowed, scores, -1e+30)
    shifted = jnp.exp(scores - lax.optimization_barrier(jnp.max(scores, -1, keepdims=True)))
    probabilities = low(shifted / lax.optimization_barrier(jnp.sum(shifted, -1, keepdims=True)))
    attended = reduced_backward(low(jnp.einsum('hgqs,shd->qhgd', probabilities, value_heads, precision=highest_precision))).reshape(SEQUENCE_SLOTS, query_total_width)
    low_out = reduced_backward(low(jnp.einsum('td,adr->tar', attended, attention_lowmap[3], precision=highest_precision))) * chooser[None, :, None]
    branch = reduced_backward(jnp.dot(attended, w_out, precision=highest_precision) + jnp.einsum('une,neq->uq', low_out, attention_output_upmap, precision=highest_precision))
    mid_stream = value_rows + branch
    normed_mid = low(norm_rows(mid_stream, ffn_gain))
    logits = jnp.dot(normed_mid, w_router, precision=highest_precision)
    chosen = jnp.take_along_axis(logits, routed_token_rows, 1)
    shifted_gate = jnp.exp(chosen - lax.optimization_barrier(jnp.max(chosen, -1, keepdims=True)))
    gate_weights = shifted_gate / lax.optimization_barrier(jnp.sum(shifted_gate, -1, keepdims=True))
    route_slot, slot_table = route_slots(routed_token_rows, EXPERTS, CAP)
    filled = slot_table >= 0
    source_rows = jnp.where(filled, slot_table // TOP, 0)
    occupied = filled.astype(jnp.float32)[..., None]
    expert_rows = reduced_backward(normed_mid[source_rows] * occupied)
    member = occupied * chooser
    low_in = reduced_backward(low(jnp.einsum('ecd,eadr->ecar', expert_rows, expert_gate_up_lowmap, precision=highest_precision))) * member[..., None]
    gate_up = jnp.einsum('ecd,edh->ech', expert_rows, w_gate_up, precision=highest_precision) + jnp.concatenate([jnp.einsum('ecar,earh->ech', low_in[..., :R], expert_gate_up_upmap[:, :, 0], precision=highest_precision), jnp.einsum('ecar,earh->ech', low_in[..., R:], expert_gate_up_upmap[:, :, 1], precision=highest_precision)], -1)
    gate_up = reduced_backward(gate_up)
    activated = low(jax.nn.silu(gate_up[..., :H]) * gate_up[..., H:])
    low_down = reduced_backward(low(jnp.einsum('ech,eahr->ecar', activated, expert_down_lowmap, precision=highest_precision))) * member[..., None]
    expert_out = reduced_backward(low(jnp.einsum('ech,ehd->ecd', activated, w_down, precision=highest_precision) + jnp.einsum('ecar,eard->ecd', low_down, expert_down_upmap, precision=highest_precision)))
    picked = expert_out.reshape(EXPERTS * CAP, MODEL_WIDTH)[routed_token_rows * CAP + route_slot]
    return mid_stream + lax.optimization_barrier(jnp.sum(gate_weights[..., None] * picked, 1))

def reference(hidden, cotangent, lengths, adapter_ids, routes, attn_gain, ffn_gain, query_key_value_weight, w_out, w_router, w_gate_up, w_down, attention_lowmap, attention_query_key_value_upmap, attention_output_upmap, expert_gate_up_lowmap, expert_gate_up_upmap, expert_down_lowmap, expert_down_upmap):
    block_list = N_DP * N_EXPERT
    weight_collection = tuple((single_item.astype(jnp.float32) for single_item in (attn_gain, ffn_gain, query_key_value_weight, w_out, w_router, w_gate_up, w_down)))
    trainable_params = tuple((single_item.astype(jnp.float32) for single_item in (attention_lowmap, attention_query_key_value_upmap, attention_output_upmap, expert_gate_up_lowmap, expert_gate_up_upmap, expert_down_lowmap, expert_down_upmap)))
    residual_stream = hidden.astype(jnp.float32).reshape(block_list, SEQUENCE_SLOTS, MODEL_WIDTH)
    route_blocks = routes.reshape(block_list, SEQUENCE_SLOTS, TOP)

    def forward_pass(input_items, trainable_collection):

        def one_block(piece_list):
            return jax.checkpoint(residual_block_forward)(piece_list[0], piece_list[1], piece_list[2], piece_list[3], weight_collection, trainable_collection)
        return lax.map(one_block, (input_items, lengths, adapter_ids, route_blocks))
    output_items, pullback_function = jax.vjp(forward_pass, residual_stream, trainable_params)
    stream_gradient, trainable_gradient = pullback_function(cotangent.astype(jnp.float32).reshape(block_list, SEQUENCE_SLOTS, MODEL_WIDTH))
    return (output_items.reshape(TOKEN_SLOTS, MODEL_WIDTH).astype(jnp.bfloat16), stream_gradient.reshape(TOKEN_SLOTS, MODEL_WIDTH).astype(jnp.bfloat16), trainable_gradient[0], trainable_gradient[1], trainable_gradient[2], trainable_gradient[3], trainable_gradient[4], trainable_gradient[5], trainable_gradient[6])
```

```python
import numpy as np
import jax
import jax.numpy as jnp
from jax import lax
from jax.experimental import pallas as pl
from jax.experimental.pallas import tpu as pltpu
from jax.sharding import PartitionSpec as P

MODEL_WIDTH = 1024
HQ = 16
KVH = 8
HS = 64
H = 512
TOP = 8
R = 16
NA = 8
QD = HQ * HS
KD = KVH * HS
QKV = QD + 2 * KD

epsilon = 1e-06
f32 = jnp.float32
bf16 = jnp.bfloat16


def nn(left, right):
    return lax.dot_general(left, right, (((1,), (0,)), ((), ())), preferred_element_type=f32)


def nt(left, right):
    return lax.dot_general(left, right, (((1,), (1,)), ((), ())), preferred_element_type=f32)


def tn(left, right):
    return lax.dot_general(left, right, (((0,), (0,)), ((), ())), preferred_element_type=f32)


def lanes_of(shape):
    return lax.broadcasted_iota(jnp.int32, shape, len(shape) - 1)


def row_scale(rows):
    return lax.rsqrt(jnp.mean(rows * rows, -1, keepdims=True) + epsilon)


def norm_back(rows, gain, grad):
    scale = row_scale(rows)
    scaled = grad * gain
    return scale * scaled - rows * (scale * scale * scale) * jnp.mean(
        rows * scaled, -1, keepdims=True
    )


def rope_swap(rows):
    width = rows.shape[-1]
    lane = lanes_of(rows.shape)
    return jnp.where(
        lane % HS < HS // 2,
        pltpu.roll(rows, width - HS // 2, 1),
        pltpu.roll(rows, HS // 2, 1),
    )


def both_halves(pair, half):
    rows = pair.astype(f32)
    lane = lanes_of(rows.shape)
    rolled = pltpu.roll(rows, HS, 1)
    keep = (lane < HS) == (half == 0)
    return jnp.where(keep, rows, rolled).astype(bf16)


def stacked_heads(pair):
    lane = lanes_of(pair.shape)
    zero = jnp.zeros_like(pair)
    return jnp.concatenate(
        [jnp.where(lane < HS, pair, zero), jnp.where(lane < HS, zero, pair)], 0
    )


def params_of(count):
    return pltpu.CompilerParams(
        dimension_semantics=("arbitrary",) * count, vmem_limit_bytes=56 * 1024 * 1024
    )


def project_kernel(hid, gain, weight, low_map, up_map, cos, sin, qkv, low, normed):
    step = pl.program_id(0)
    blocks = pl.num_programs(0)

    @pl.when(step == 0)
    def _():
        rows = hid[...].astype(f32)
        value = (rows * row_scale(rows) * gain[...].astype(f32)).astype(bf16)
        normed[...] = value
        low[...] = nt(value, low_map[...]).astype(bf16)

    value = nn(normed[...], weight[...]) + nn(low[...], up_map[...])

    @pl.when(step < blocks * 3 // 4)
    def _():
        for part in range(value.shape[1] // 128):
            piece = value[:, part * 128 : part * 128 + 128]
            turned = piece * cos[...] + rope_swap(piece) * sin[...]
            qkv[:, part * 128 : part * 128 + 128] = turned.astype(bf16)

    @pl.when(step >= blocks * 3 // 4)
    def _():
        qkv[...] = value.astype(bf16)


def project(hidden, gain, weight, low_map, up_map, cos, sin):
    rows = hidden.shape[0]
    block = 256
    ranks = low_map.shape[0]
    full = lambda shape: pl.BlockSpec(shape, lambda n: (0, 0))
    return pl.pallas_call(
        project_kernel,
        grid=(QKV // block,),
        in_specs=[
            full((rows, MODEL_WIDTH)),
            full((1, MODEL_WIDTH)),
            pl.BlockSpec((MODEL_WIDTH, block), lambda n: (0, n)),
            full((ranks, MODEL_WIDTH)),
            pl.BlockSpec((ranks, block), lambda n: (0, n)),
            full((rows, 128)),
            full((rows, 128)),
        ],
        out_specs=[
            pl.BlockSpec((rows, block), lambda n: (0, n)),
            full((rows, ranks)),
            full((rows, MODEL_WIDTH)),
        ],
        out_shape=[
            jax.ShapeDtypeStruct((rows, QKV), bf16),
            jax.ShapeDtypeStruct((rows, ranks), bf16),
            jax.ShapeDtypeStruct((rows, MODEL_WIDTH), bf16),
        ],
        compiler_params=params_of(1),
        name="project",
        cost_estimate=pl.CostEstimate(
            flops=2 * rows * QKV * MODEL_WIDTH, transcendentals=0, bytes_accessed=8 << 20
        ),
    )(hidden, gain, weight, low_map, up_map, cos, sin)


ROWB = 128


def masked_scores(length, queries, keys, start, count):
    scores = 0.125 * nt(queries, keys)
    row = lax.broadcasted_iota(jnp.int32, scores.shape, 0)
    col = lanes_of(scores.shape)
    allowed = (col <= start + row % ROWB) & (col < length)
    return scores, allowed


def attend_kernel(scalars, query, key, value, result, lse):
    half = pl.program_id(0) % 2
    length = scalars[0]
    keys = both_halves(key[...], half)
    values = both_halves(value[...], half)
    rows = query.shape[0]
    for start in range(0, rows, ROWB):
        count = start + ROWB
        stacked = stacked_heads(query[start:count, :])
        scores, allowed = masked_scores(length, stacked, keys[:count], start, count)
        scores = jnp.where(allowed, scores, -1e30)
        top = jnp.max(scores, -1, keepdims=True)
        shifted = jnp.exp(scores - top)
        total = jnp.sum(shifted, -1, keepdims=True)
        prob = (shifted * (1.0 / total)).astype(bf16)
        mixed = nn(prob, values[:count])
        lane = lanes_of((ROWB, 128))
        result[start:count, :] = jnp.where(lane < HS, mixed[:ROWB], mixed[ROWB:]).astype(bf16)
        logs = top + jnp.log(total)
        lse[0, start:count, :] = jnp.concatenate([logs[:ROWB], logs[ROWB:]], 1)


def attend(length, qkv):
    rows = qkv.shape[0]
    pairs = KVH
    return pl.pallas_call(
        attend_kernel,
        grid_spec=pltpu.PrefetchScalarGridSpec(
            num_scalar_prefetch=1,
            grid=(pairs,),
            in_specs=[
                pl.BlockSpec((rows, 128), lambda g, s: (0, g)),
                pl.BlockSpec((rows, 128), lambda g, s: (0, QD // 128 + g // 2)),
                pl.BlockSpec((rows, 128), lambda g, s: (0, (QD + KD) // 128 + g // 2)),
            ],
            out_specs=[
                pl.BlockSpec((rows, 128), lambda g, s: (0, g)),
                pl.BlockSpec((1, rows, 2), lambda g, s: (g, 0, 0)),
            ],
        ),
        out_shape=[
            jax.ShapeDtypeStruct((rows, QD), bf16),
            jax.ShapeDtypeStruct((pairs, rows, 2), f32),
        ],
        compiler_params=params_of(1),
        name="attend",
        cost_estimate=pl.CostEstimate(
            flops=8 * rows * rows * QD, transcendentals=rows * rows * HQ, bytes_accessed=4 << 20
        ),
    )(length, qkv, qkv, qkv)


def attend_back_kernel(
    scalars, query, key, value, grad, lse, cos, sin, grad_query, grad_key, grad_value, key_acc, value_acc
):
    half = pl.program_id(0) % 2
    length = scalars[0]
    keys = both_halves(key[...], half)
    values = both_halves(value[...], half)
    rows = query.shape[0]
    key_acc[...] = jnp.zeros_like(key_acc)
    value_acc[...] = jnp.zeros_like(value_acc)
    for start in range(0, rows, ROWB):
        count = start + ROWB
        stacked = stacked_heads(query[start:count, :])
        grads = stacked_heads(grad[start:count, :])
        scores, allowed = masked_scores(length, stacked, keys[:count], start, count)
        logs = lse[0, start:count, :]
        logs = jnp.concatenate([logs[:, 0:1], logs[:, 1:2]], 0)
        prob = jnp.where(allowed, jnp.exp(scores - logs), 0.0)
        grad_prob = nt(grads, values[:count])
        delta = jnp.sum(prob * grad_prob, -1, keepdims=True)
        grad_score = (prob * (grad_prob - delta)).astype(bf16)
        mixed = nn(grad_score, keys[:count])
        lane = lanes_of((ROWB, 128))
        turned = 0.125 * jnp.where(lane < HS, mixed[:ROWB], mixed[ROWB:])
        turned = turned * cos[start:count, :] - rope_swap(turned) * sin[start:count, :]
        grad_query[start:count, :] = turned.astype(bf16)
        key_acc[:count, :] += tn(grad_score, stacked)
        value_acc[:count, :] += tn(prob.astype(bf16), grads)
    total = key_acc[...]
    total = 0.125 * (total + pltpu.roll(total, HS, 1))
    total = (total * cos[...] - rope_swap(total) * sin[...]).astype(bf16)
    other = value_acc[...]
    other = (other + pltpu.roll(other, HS, 1)).astype(bf16)

    @pl.when(half == 0)
    def _():
        grad_key[...] = total
        grad_value[...] = other

    @pl.when(half == 1)
    def _():
        low_half = lanes_of(total.shape) < HS
        grad_key[...] = jnp.where(low_half, grad_key[...], total)
        grad_value[...] = jnp.where(low_half, grad_value[...], other)


def attend_back(length, qkv, grad, lse, cos, sin):
    rows = qkv.shape[0]
    pairs = KVH
    return pl.pallas_call(
        attend_back_kernel,
        grid_spec=pltpu.PrefetchScalarGridSpec(
            num_scalar_prefetch=1,
            grid=(pairs,),
            in_specs=[
                pl.BlockSpec((rows, 128), lambda g, s: (0, g)),
                pl.BlockSpec((rows, 128), lambda g, s: (0, QD // 128 + g // 2)),
                pl.BlockSpec((rows, 128), lambda g, s: (0, (QD + KD) // 128 + g // 2)),
                pl.BlockSpec((rows, 128), lambda g, s: (0, g)),
                pl.BlockSpec((1, rows, 2), lambda g, s: (g, 0, 0)),
                pl.BlockSpec((rows, 128), lambda g, s: (0, 0)),
                pl.BlockSpec((rows, 128), lambda g, s: (0, 0)),
            ],
            out_specs=[
                pl.BlockSpec((rows, 128), lambda g, s: (0, g)),
                pl.BlockSpec((rows, 128), lambda g, s: (0, g // 2)),
                pl.BlockSpec((rows, 128), lambda g, s: (0, g // 2)),
            ],
            scratch_shapes=[pltpu.VMEM((rows, 128), f32), pltpu.VMEM((rows, 128), f32)],
        ),
        out_shape=[
            jax.ShapeDtypeStruct((rows, QD), bf16),
            jax.ShapeDtypeStruct((rows, KD), bf16),
            jax.ShapeDtypeStruct((rows, KD), bf16),
        ],
        compiler_params=params_of(1),
        name="attend_back",
        cost_estimate=pl.CostEstimate(
            flops=20 * rows * rows * QD, transcendentals=rows * rows * HQ, bytes_accessed=8 << 20
        ),
    )(length, qkv, qkv, qkv, grad, lse, cos, sin)


def close_kernel(att, hid, gain, weight, low_map, up_map, mid, normed, low):
    value = att[...]
    low_value = nt(value, low_map[...]).astype(bf16)
    low[...] = low_value
    stream = hid[...].astype(f32) + (nn(value, weight[...]) + nn(low_value, up_map[...]))
    mid[...] = stream
    normed[...] = (stream * row_scale(stream) * gain[...].astype(f32)).astype(bf16)


def close_mixer(att, hidden, gain, weight, low_map, up_map):
    rows = hidden.shape[0]
    block = 256
    ranks = low_map.shape[0]
    full = lambda shape: pl.BlockSpec(shape, lambda n: (0, 0))
    part = lambda width: pl.BlockSpec((block, width), lambda n: (n, 0))
    return pl.pallas_call(
        close_kernel,
        grid=(rows // block,),
        in_specs=[
            part(QD),
            part(MODEL_WIDTH),
            full((1, MODEL_WIDTH)),
            full((QD, MODEL_WIDTH)),
            full((ranks, QD)),
            full((ranks, MODEL_WIDTH)),
        ],
        out_specs=[part(MODEL_WIDTH), part(MODEL_WIDTH), part(ranks)],
        out_shape=[
            jax.ShapeDtypeStruct((rows, MODEL_WIDTH), f32),
            jax.ShapeDtypeStruct((rows, MODEL_WIDTH), bf16),
            jax.ShapeDtypeStruct((rows, ranks), bf16),
        ],
        compiler_params=params_of(1),
        name="close_mixer",
        cost_estimate=pl.CostEstimate(
            flops=2 * rows * QD * MODEL_WIDTH, transcendentals=0, bytes_accessed=8 << 20
        ),
    )(att, hidden, gain, weight, low_map, up_map)


def expert_kernel(
    scalars,
    x,
    cot,
    routes,
    router,
    w_in,
    w_down,
    a_in,
    b_in,
    a_down,
    b_down,
    out,
    grad_normed,
    grad_gate,
    gates_out,
    grad_a_in,
    grad_b_in,
    grad_a_down,
    grad_b_down,
    gates,
    gate_sums,
    low_in,
    low_in_turned,
    b_in_all,
    back_low,
    gated_low,
    back_in,
    acts,
    grads,
    low_grads,
    out_acc,
    grad_acc,
):
    expert = pl.program_id(0)
    last = pl.num_programs(0) - 1
    rows = x.shape[0]
    block = 256
    local = a_in.shape[0]
    a_in_all = a_in[...].reshape(local * 2 * R, MODEL_WIDTH)
    a_down_all = a_down[...].reshape(local * R, H)
    b_down_all = b_down[...].reshape(local * R, MODEL_WIDTH)

    @pl.when(expert == 0)
    def _():
        logits = nt(x[...], router[...])
        lane = lanes_of(logits.shape)
        chosen = lane == routes[:, 0:1]
        for k in range(1, TOP):
            chosen = chosen | (lane == routes[:, k : k + 1])
        top = jnp.max(jnp.where(chosen, logits, -1e30), -1, keepdims=True)
        shifted = jnp.where(chosen, jnp.exp(jnp.where(chosen, logits - top, 0.0)), 0.0)
        weights = shifted / jnp.sum(shifted, -1, keepdims=True)
        gates[...] = weights
        gates_out[...] = weights.T[: gates_out.shape[0], :]
        low = nt(x[...], a_in_all)
        low_in[...] = low.astype(bf16)
        low_in_turned[...] = low.T.astype(bf16)
        back_low[...] = nt(cot[...], b_down_all)
        b_in_all[...] = jnp.zeros_like(b_in_all)
        for e in range(local):
            b_in_all[e * 2 * R : e * 2 * R + R, :H] = b_in[e, 0, 0]
            b_in_all[e * 2 * R + R : (e + 1) * 2 * R, H:] = b_in[e, 0, 1]
        gate_sums[...] = jnp.zeros_like(gate_sums)
        gated_low[...] = jnp.zeros_like(gated_low)
        back_in[...] = jnp.zeros_like(back_in)
        out_acc[...] = jnp.zeros_like(out_acc)
        grad_acc[...] = jnp.zeros_like(grad_acc)
        grad_a_down[...] = jnp.zeros_like(grad_a_down)

    def row_step(index, carry):
        at = pl.ds(pl.multiple_of(index * block, block), block)
        lane_in = lanes_of((block, local * 2 * R))
        lane_down = lanes_of((block, local * R))
        in_mine = (lane_in >= expert * 2 * R) & (lane_in < (expert + 1) * 2 * R)
        down_mine = (lane_down >= expert * R) & (lane_down < (expert + 1) * R)
        gate_all = gates[at, :]
        gate_lane = lanes_of(gate_all.shape) == expert
        weight = jnp.sum(jnp.where(gate_lane, gate_all, 0.0), -1, keepdims=True)
        mine = low_in[at, :]
        mine = jnp.where(in_mine, mine, jnp.zeros_like(mine))
        both = nn(x[at, :], w_in[0]) + nn(mine, b_in_all[...])
        gate = both[:, :H]
        upper = both[:, H:]
        sigmoid = jax.nn.sigmoid(gate)
        silu = gate * sigmoid
        act = (silu * upper).astype(bf16)
        acts[at, :] = act
        act_wide = act.astype(f32)
        low = jnp.where(down_mine, nt(act, a_down_all), 0.0).astype(bf16).astype(f32)
        plain = nt(cot[at, :], w_down[0])
        low_plain = back_low[at, :]
        dots = jnp.sum(act_wide * plain, -1, keepdims=True) + jnp.sum(
            low * low_plain, -1, keepdims=True
        )
        gate_sums[at, :] += jnp.where(gate_lane, dots, 0.0)
        low_grad = jnp.where(down_mine, weight * low_plain, 0.0).astype(bf16)
        low_grads[at, :] = low_grad
        grad_act = weight * plain + nn(low_grad, a_down_all)
        grad_first = grad_act * upper * sigmoid * (1.0 + gate * (1.0 - sigmoid))
        grad_second = grad_act * silu
        grad_both = jnp.concatenate(
            [grad_first.astype(bf16), grad_second.astype(bf16)], 1
        )
        grads[at, :] = grad_both
        gated_low[at, :] += (weight * low).astype(bf16)
        out_acc[at, :] += nn((weight * act_wide).astype(bf16), w_down[0])
        grad_acc[at, :] += nt(grad_both, w_in[0])
        low_back = jnp.where(in_mine, nt(grad_both, b_in_all[...]), 0.0)
        back_in[at, :] += low_back.astype(bf16)
        return carry

    lax.fori_loop(0, rows // block, row_step, 0)

    turned = low_in_turned[pl.ds(pl.multiple_of(expert * 2 * R, 2 * R), 2 * R), :]
    product = nn(turned, grads[...])
    grad_b_in[0, :R, :] = product[:R, :H].astype(bf16)
    grad_b_in[0, R:, :] = product[R:, H:].astype(bf16)
    grad_a_down[...] += tn(low_grads[...], acts[...]).astype(bf16)

    @pl.when(expert == last)
    def _():
        out[...] = (out_acc[...] + nn(gated_low[...], b_down_all)).astype(bf16)
        grad_normed[...] = (grad_acc[...] + nn(back_in[...], a_in_all)).astype(bf16)
        grad_a_in[...] = tn(back_in[...], x[...]).astype(bf16)
        grad_b_down[...] = tn(gated_low[...], cot[...]).astype(bf16)
        grad_gate[...] = gate_sums[...].T[: grad_gate.shape[0], :]


def run_experts(scalars, x, cot, routes, router, w_in, w_down, a_in, b_in, a_down, b_down, experts):
    rows = x.shape[0]
    local = w_in.shape[0]
    ranks_in = local * 2 * R
    ranks_down = local * R
    full = lambda shape: pl.BlockSpec(shape, lambda e, s: (0,) * len(shape))
    return pl.pallas_call(
        expert_kernel,
        grid_spec=pltpu.PrefetchScalarGridSpec(
            num_scalar_prefetch=1,
            grid=(local,),
            in_specs=[
                full((rows, MODEL_WIDTH)),
                full((rows, MODEL_WIDTH)),
                pl.BlockSpec((rows, TOP), lambda e, s: (s[0], 0)),
                full((128, MODEL_WIDTH)),
                pl.BlockSpec((1, MODEL_WIDTH, 2 * H), lambda e, s: (e, 0, 0)),
                pl.BlockSpec((1, H, MODEL_WIDTH), lambda e, s: (e, 0, 0)),
                pl.BlockSpec((local, 1, 2 * R, MODEL_WIDTH), lambda e, s: (0, s[1], 0, 0)),
                pl.BlockSpec((local, 1, 2, R, H), lambda e, s: (0, s[1], 0, 0, 0)),
                pl.BlockSpec((local, 1, R, H), lambda e, s: (0, s[1], 0, 0)),
                pl.BlockSpec((local, 1, R, MODEL_WIDTH), lambda e, s: (0, s[1], 0, 0)),
            ],
            out_specs=[
                full((rows, MODEL_WIDTH)),
                full((rows, MODEL_WIDTH)),
                full((8, rows)),
                full((experts, rows)),
                full((ranks_in, MODEL_WIDTH)),
                pl.BlockSpec((1, 2 * R, H), lambda e, s: (e, 0, 0)),
                full((ranks_down, H)),
                full((ranks_down, MODEL_WIDTH)),
            ],
            scratch_shapes=[
                pltpu.VMEM((rows, 128), f32),
                pltpu.VMEM((rows, 128), f32),
                pltpu.VMEM((rows, ranks_in), bf16),
                pltpu.VMEM((ranks_in, rows), bf16),
                pltpu.VMEM((ranks_in, 2 * H), bf16),
                pltpu.VMEM((rows, ranks_down), f32),
                pltpu.VMEM((rows, ranks_down), bf16),
                pltpu.VMEM((rows, ranks_in), bf16),
                pltpu.VMEM((rows, H), bf16),
                pltpu.VMEM((rows, 2 * H), bf16),
                pltpu.VMEM((rows, ranks_down), bf16),
                pltpu.VMEM((rows, MODEL_WIDTH), f32),
                pltpu.VMEM((rows, MODEL_WIDTH), f32),
            ],
        ),
        out_shape=[
            jax.ShapeDtypeStruct((rows, MODEL_WIDTH), bf16),
            jax.ShapeDtypeStruct((rows, MODEL_WIDTH), bf16),
            jax.ShapeDtypeStruct((8, rows), f32),
            jax.ShapeDtypeStruct((experts, rows), f32),
            jax.ShapeDtypeStruct((ranks_in, MODEL_WIDTH), bf16),
            jax.ShapeDtypeStruct((local, 2 * R, H), bf16),
            jax.ShapeDtypeStruct((ranks_down, H), bf16),
            jax.ShapeDtypeStruct((ranks_down, MODEL_WIDTH), bf16),
        ],
        compiler_params=params_of(1),
        name="experts",
        cost_estimate=pl.CostEstimate(
            flops=local * rows * 9 * (1 << 20),
            transcendentals=local * rows * H,
            bytes_accessed=20 << 20,
        ),
    )(scalars, x, cot, routes, router, w_in, w_down, a_in, b_in, a_down, b_down)


def open_back_kernel(
    count,
    cot,
    mid,
    gain,
    gate_grads,
    gates,
    router,
    weight,
    low_map,
    up_map,
    low,
    att,
    *rest,
):
    parts = rest[:count]
    grad_mid, grad_att, grad_up, grad_low = rest[count:]
    gate_value = gates[...]
    gate_grad = gate_grads[...]
    logit = gate_value * (gate_grad - jnp.sum(gate_value * gate_grad, 0, keepdims=True))
    first = logit.astype(bf16)
    left = logit - first.astype(f32)
    second = left.astype(bf16)
    third = (left - second.astype(f32)).astype(bf16)
    grad = tn(first, router[...]) + (tn(second, router[...]) + tn(third, router[...]))
    for piece in parts:
        grad = grad + piece[...].astype(f32)
    total = cot[...].astype(f32) + norm_back(mid[...], gain[...].astype(f32), grad)
    grad_mid[...] = total
    branch = total.astype(bf16)
    low_grad = nt(branch, up_map[...]).astype(bf16)
    grad_att[...] = (nt(branch, weight[...]) + nn(low_grad, low_map[...])).astype(bf16)
    up_part = tn(low[...], branch)
    low_part = tn(low_grad, att[...])

    @pl.when(pl.program_id(0) == 0)
    def _():
        grad_up[...] = up_part
        grad_low[...] = low_part

    @pl.when(pl.program_id(0) > 0)
    def _():
        grad_up[...] += up_part
        grad_low[...] += low_part


def open_back(cot, mid, gain, gate_grads, gates, router, weight, low_map, up_map, low, att, parts):
    rows = cot.shape[0]
    block = 256
    ranks = low_map.shape[0]
    experts = gates.shape[0]
    full = lambda shape: pl.BlockSpec(shape, lambda n: (0, 0))
    part = lambda width: pl.BlockSpec((block, width), lambda n: (n, 0))
    across = pl.BlockSpec((experts, block), lambda n: (0, n))
    count = len(parts)

    def body(*refs):
        open_back_kernel(count, *refs)

    return pl.pallas_call(
        body,
        grid=(rows // block,),
        in_specs=[
            part(MODEL_WIDTH),
            part(MODEL_WIDTH),
            full((1, MODEL_WIDTH)),
            across,
            across,
            full((experts, MODEL_WIDTH)),
            full((QD, MODEL_WIDTH)),
            full((ranks, QD)),
            full((ranks, MODEL_WIDTH)),
            part(ranks),
            part(QD),
        ]
        + [part(MODEL_WIDTH)] * count,
        out_specs=[
            part(MODEL_WIDTH),
            part(QD),
            full((ranks, MODEL_WIDTH)),
            full((ranks, QD)),
        ],
        out_shape=[
            jax.ShapeDtypeStruct((rows, MODEL_WIDTH), f32),
            jax.ShapeDtypeStruct((rows, QD), bf16),
            jax.ShapeDtypeStruct((ranks, MODEL_WIDTH), f32),
            jax.ShapeDtypeStruct((ranks, QD), f32),
        ],
        compiler_params=params_of(1),
        name="open_back",
        cost_estimate=pl.CostEstimate(
            flops=2 * rows * QD * MODEL_WIDTH, transcendentals=0, bytes_accessed=14 << 20
        ),
    )(cot, mid, gain, gate_grads, gates, router, weight, low_map, up_map, low, att, *parts)


def adapters_back_kernel(
    grad_query, grad_key, grad_value, low, normed, up_map, grad_up, grad_low, low_out
):
    pieces = (grad_query, grad_key, grad_value)
    bounds = (0, QD, QD + KD, QKV)
    back = None
    for at in range(3):
        block = pieces[at][...]
        product = tn(low[...], block)
        grad_up[:, bounds[at] : bounds[at + 1]] = product[at * R : (at + 1) * R]
        part = nt(block, up_map[:, bounds[at] : bounds[at + 1]])
        back = part if back is None else back + part
    value = back.astype(bf16)
    low_out[...] = value
    grad_low[...] = tn(value, normed[...])


def adapters_back(grad_query, grad_key, grad_value, low, normed, up_map):
    rows = normed.shape[0]
    ranks = up_map.shape[0]
    return pl.pallas_call(
        adapters_back_kernel,
        out_shape=[
            jax.ShapeDtypeStruct((R, QKV), f32),
            jax.ShapeDtypeStruct((ranks, MODEL_WIDTH), f32),
            jax.ShapeDtypeStruct((rows, ranks), bf16),
        ],
        compiler_params=pltpu.CompilerParams(vmem_limit_bytes=56 * 1024 * 1024),
        name="adapters_back",
        cost_estimate=pl.CostEstimate(
            flops=6 * rows * 256 * QKV, transcendentals=0, bytes_accessed=4 << 20
        ),
    )(grad_query, grad_key, grad_value, low, normed, up_map)


def input_back_kernel(grad_query, grad_key, grad_value, low, weight, low_map, hid, gain, mid, grad):
    total = nt(grad_query[...], weight[:, :QD])
    total = total + nt(grad_key[...], weight[:, QD : QD + KD])
    total = total + nt(grad_value[...], weight[:, QD + KD :])
    total = total + nn(low[...], low_map[...])
    rows = hid[...].astype(f32)
    grad[...] = (mid[...] + norm_back(rows, gain[...].astype(f32), total)).astype(bf16)


def input_back(grad_query, grad_key, grad_value, low, weight, low_map, hidden, gain, mid):
    rows = hidden.shape[0]
    block = 256
    ranks = low_map.shape[0]
    full = lambda shape: pl.BlockSpec(shape, lambda n: (0, 0))
    part = lambda width: pl.BlockSpec((block, width), lambda n: (n, 0))
    return pl.pallas_call(
        input_back_kernel,
        grid=(rows // block,),
        in_specs=[
            part(QD),
            part(KD),
            part(KD),
            part(ranks),
            full((MODEL_WIDTH, QKV)),
            full((ranks, MODEL_WIDTH)),
            part(MODEL_WIDTH),
            full((1, MODEL_WIDTH)),
            part(MODEL_WIDTH),
        ],
        out_specs=part(MODEL_WIDTH),
        out_shape=jax.ShapeDtypeStruct((rows, MODEL_WIDTH), bf16),
        compiler_params=params_of(1),
        name="input_back",
        cost_estimate=pl.CostEstimate(
            flops=2 * rows * QKV * MODEL_WIDTH, transcendentals=0, bytes_accessed=12 << 20
        ),
    )(grad_query, grad_key, grad_value, low, weight, low_map, hidden, gain, mid)


def sum_experts_kernel(ids, wide, narrow, a_in, b_in, a_down, b_down):
    local = a_in.shape[0]
    for ref in (a_in, b_in, a_down, b_down):
        ref[...] = jnp.zeros_like(ref)

    def step(index, carry):
        tag = ids[index]
        for e in range(local):
            a_in[e, tag] += wide[index, e * 2 * R : (e + 1) * 2 * R, :].astype(f32)
            at = local * 2 * R + e * R
            b_down[e, tag] += wide[index, at : at + R, :].astype(f32)
            b_in[e, tag] += narrow[index, e * 2 * R : (e + 1) * 2 * R, :].astype(f32)
            a_down[e, tag] += narrow[index, at : at + R, :].astype(f32)
        return carry

    lax.fori_loop(0, wide.shape[0], step, 0)


def sum_experts(ids, wide, narrow, local):
    lanes = wide.shape[2]
    small = narrow.shape[2]
    vmem = pl.BlockSpec(memory_space=pltpu.VMEM)
    return pl.pallas_call(
        sum_experts_kernel,
        in_specs=[pl.BlockSpec(memory_space=pltpu.SMEM), vmem, vmem],
        out_specs=[vmem, vmem, vmem, vmem],
        out_shape=[
            jax.ShapeDtypeStruct((local, NA, 2 * R, lanes), f32),
            jax.ShapeDtypeStruct((local, NA, 2 * R, small), f32),
            jax.ShapeDtypeStruct((local, NA, R, small), f32),
            jax.ShapeDtypeStruct((local, NA, R, lanes), f32),
        ],
        compiler_params=pltpu.CompilerParams(vmem_limit_bytes=56 * 1024 * 1024),
        name="sum_experts",
    )(ids, wide, narrow)


def sum_mixer_kernel(ids, pieces, grad_low, grad_up, grad_out, acc):
    width = grad_low.shape[-1]
    acc[...] = jnp.zeros_like(acc)

    def step(index, carry):
        acc[ids[index]] += pieces[index]
        return carry

    lax.fori_loop(0, pieces.shape[0], step, 0)
    total = acc[...]
    for at in range(4):
        grad_low[at] = total[:, :, at * width : (at + 1) * width]
    grad_up[...] = total[:, :, 4 * width : 6 * width]
    grad_out[...] = total[:, :, 6 * width : 7 * width]


def sum_mixer(ids, pieces):
    width = pieces.shape[2] // 8
    vmem = pl.BlockSpec(memory_space=pltpu.VMEM)
    return pl.pallas_call(
        sum_mixer_kernel,
        in_specs=[pl.BlockSpec(memory_space=pltpu.SMEM), vmem],
        out_specs=[vmem, vmem, vmem],
        out_shape=[
            jax.ShapeDtypeStruct((4, NA, R, width), f32),
            jax.ShapeDtypeStruct((NA, R, 2 * width), f32),
            jax.ShapeDtypeStruct((NA, R, width), f32),
        ],
        scratch_shapes=[pltpu.VMEM((NA, R, 8 * width), f32)],
        compiler_params=pltpu.CompilerParams(vmem_limit_bytes=56 * 1024 * 1024),
        name="sum_mixer",
    )(ids, pieces)


def rope_tables(rows):
    half = HS // 2
    frequency = (10000.0 ** (-2.0 * np.arange(half, dtype=np.float32) / HS)).astype(np.float32)
    angles = np.arange(rows, dtype=np.float32)[:, None] * frequency[None, :]
    cos = np.cos(angles.astype(np.float64)).astype(np.float32)
    sin = np.sin(angles.astype(np.float64)).astype(np.float32)
    return (
        jnp.asarray(np.concatenate([cos, cos, cos, cos], 1)),
        jnp.asarray(np.concatenate([-sin, sin, -sin, sin], 1)),
    )


def on_device(
    hidden,
    cotangent,
    lengths,
    adapter_ids,
    routes,
    attn_gain,
    ffn_gain,
    query_key_value_weight,
    w_out,
    w_router,
    w_gate_up,
    w_down,
    attention_lowmap,
    attention_query_key_value_upmap,
    attention_output_upmap,
    expert_gate_up_lowmap,
    expert_gate_up_upmap,
    expert_down_lowmap,
    expert_down_upmap,
):
    groups = lax.axis_size("expert")
    owners = lax.axis_size("dp")
    place = lax.axis_index("expert")
    row = lax.axis_index("dp")
    devices = groups * owners
    sequence = row * groups + place
    rows = hidden.shape[0]
    experts = w_router.shape[1]
    local = w_gate_up.shape[0]
    width = MODEL_WIDTH // owners
    attn_gain = attn_gain.reshape(1, MODEL_WIDTH)
    ffn_gain = ffn_gain.reshape(1, MODEL_WIDTH)
    length = lax.dynamic_slice(lengths, (sequence,), (1,))
    forward = [(at, (at + 1) % groups) for at in range(groups)]

    mine = lax.dynamic_slice(adapter_ids.reshape(owners, groups), (0, place), (owners, 1))[:, 0]
    low_turned = attention_lowmap.transpose(1, 0, 3, 2).reshape(NA, 4 * R, width)
    up_turned = (
        attention_query_key_value_upmap.reshape(NA, R, 2, width)
        .transpose(0, 2, 1, 3)
        .reshape(NA, 2 * R, width)
    )
    adapters = jnp.concatenate([low_turned, up_turned, attention_output_upmap], 1)[mine]
    adapters = lax.all_to_all(adapters, "dp", 0, 0, tiled=True)
    weight_in = lax.all_gather(query_key_value_weight, "dp", axis=0, tiled=True)
    weight_out = lax.all_gather(w_out, "dp", axis=0, tiled=True)

    low_map = adapters[:, : 4 * R].transpose(1, 0, 2).reshape(4 * R, MODEL_WIDTH)
    up = (
        adapters[:, 4 * R : 6 * R]
        .reshape(owners, 2, R, width)
        .transpose(2, 0, 1, 3)
        .reshape(R, QKV)
    )
    up_out = adapters[:, 6 * R :].transpose(1, 0, 2).reshape(R, MODEL_WIDTH)
    column = jnp.arange(QKV, dtype=jnp.int32)
    part = jnp.where(column < QD, 0, jnp.where(column < QD + KD, 1, 2))
    up_map = jnp.where(
        part[None, None, :] == jnp.arange(4, dtype=jnp.int32)[:, None, None], up[None], 0
    ).reshape(4 * R, QKV)
    up_out_map = jnp.concatenate([jnp.zeros((3 * R, MODEL_WIDTH), bf16), up_out], 0)

    cos, sin = rope_tables(rows)

    cots = [cotangent]
    for _ in range(groups - 1):
        cots.append(lax.ppermute(cots[-1], "expert", forward))

    qkv, low, normed_in = project(hidden, attn_gain, weight_in, low_map, up_map, cos, sin)
    attended, lse = attend(length, qkv)
    mid, normed_mid, low_out = close_mixer(
        attended, hidden, ffn_gain, weight_out, low_map, up_out_map
    )

    first = place * local
    routes_here = (routes - first + experts) % experts
    router = jnp.roll(w_router.T, -first, axis=0)
    router_wide = jnp.concatenate(
        [router, jnp.zeros((128 - experts, MODEL_WIDTH), router.dtype)], 0
    )
    a_in = expert_gate_up_lowmap.transpose(0, 1, 3, 2)
    a_down = expert_down_lowmap.transpose(0, 1, 3, 2)

    xs = [normed_mid]
    for _ in range(groups - 1):
        xs.append(lax.ppermute(xs[-1], "expert", forward))

    outs, grads, dots, wides, narrows, order = [], [], [], [], [], []
    gates = None
    for at in range(groups):
        source = (place - at + groups) % groups
        tag = adapter_ids[row * groups + source]
        order.append(source)
        scalars = jnp.stack([source, tag]).astype(jnp.int32)
        (
            out_part,
            grad_part,
            dot_part,
            gate_part,
            g_a_in,
            g_b_in,
            g_a_down,
            g_b_down,
        ) = run_experts(
            scalars,
            xs[at],
            cots[at],
            routes_here,
            router_wide,
            w_gate_up,
            w_down,
            a_in,
            expert_gate_up_upmap,
            a_down,
            expert_down_upmap,
            experts,
        )
        if at == 0:
            gates = gate_part
        else:
            back = [(i, (i - at) % groups) for i in range(groups)]
            grad_part = lax.ppermute(grad_part, "expert", back)
            dot_part = lax.ppermute(dot_part, "expert", back)
            out_part = lax.ppermute(out_part, "expert", back)
        outs.append(out_part)
        grads.append(grad_part)
        dots.append(dot_part[:local])
        wides.append(jnp.concatenate([g_a_in, g_b_down], 0))
        narrows.append(jnp.concatenate([g_b_in.reshape(local * 2 * R, H), g_a_down], 0))

    wide = jnp.stack(wides, 0)
    narrow = jnp.stack(narrows, 0)
    wide = wide.reshape(groups, wide.shape[1], owners, width).transpose(2, 0, 1, 3)
    narrow = narrow.reshape(groups, narrow.shape[1], owners, width // 2).transpose(2, 0, 1, 3)
    wide = lax.all_to_all(wide, "dp", 0, 0, tiled=True)
    narrow = lax.all_to_all(narrow, "dp", 0, 0, tiled=True)
    wide = wide.reshape(devices, wide.shape[2], width)
    narrow = narrow.reshape(devices, narrow.shape[2], width // 2)
    order_ids = adapter_ids.reshape(owners, groups)[:, jnp.stack(order)].reshape(devices)
    g_a_in, g_b_in, g_a_down, g_b_down = sum_experts(order_ids, wide, narrow, local)

    gate_grads = jnp.concatenate(dots, 0)
    grad_mid, grad_attended, grad_up_out, grad_low_out = open_back(
        cotangent,
        mid,
        ffn_gain,
        gate_grads,
        gates,
        router,
        weight_out,
        low_map,
        up_out_map,
        low_out,
        attended,
        grads,
    )
    grad_query, grad_key, grad_value = attend_back(length, qkv, grad_attended, lse, cos, sin)
    grad_up, grad_low, back_low = adapters_back(
        grad_query, grad_key, grad_value, low, normed_in, up_map
    )

    grad_low = grad_low + grad_low_out
    small = MODEL_WIDTH // devices
    packed = jnp.concatenate(
        [
            grad_low.reshape(4, R, devices, small).transpose(2, 1, 0, 3).reshape(devices, R, 4 * small),
            grad_up.reshape(R, devices, 2 * small).transpose(1, 0, 2),
            grad_up_out[3 * R :].reshape(R, devices, small).transpose(1, 0, 2),
            jnp.zeros((devices, R, small), f32),
        ],
        -1,
    )
    packed = lax.all_to_all(packed, ("dp", "expert"), 0, 0, tiled=True)
    m_a, m_b, m_o = sum_mixer(adapter_ids, packed)

    grad_hidden = input_back(
        grad_query, grad_key, grad_value, back_low, weight_in, low_map, hidden, attn_gain, grad_mid
    )
    total = mid
    for piece in outs:
        total = total + piece.astype(f32)
    out = total.astype(bf16)
    return (
        out,
        grad_hidden,
        m_a.transpose(0, 1, 3, 2),
        m_b,
        m_o,
        g_a_in.transpose(0, 1, 3, 2),
        g_b_in.reshape(local, NA, 2, R, width // 2),
        g_a_down.transpose(0, 1, 3, 2),
        g_b_down,
    )


def solution(mesh):
    in_specs = (
        P(("dp", "expert"), None),
        P(("dp", "expert"), None),
        P(),
        P(),
        P("dp", None),
        P(),
        P(),
        P("dp", None),
        P("dp", None),
        P(),
        P("expert", None, None),
        P("expert", None, None),
        P(None, None, "dp", None),
        P(None, None, "dp"),
        P(None, None, "dp"),
        P("expert", None, None, None),
        P("expert", None, None, None, None),
        P("expert", None, None, None),
        P("expert", None, None, None),
    )
    out_specs = (
        P(("dp", "expert"), None),
        P(("dp", "expert"), None),
        P(None, None, ("dp", "expert"), None),
        P(None, None, ("dp", "expert")),
        P(None, None, ("dp", "expert")),
        P("expert", None, "dp", None),
        P("expert", None, None, None, "dp"),
        P("expert", None, "dp", None),
        P("expert", None, None, "dp"),
    )
    return jax.shard_map(
        on_device, mesh=mesh, in_specs=in_specs, out_specs=out_specs, check_vma=False
    )
```

```python
import numpy as np
import jax
import jax.numpy as jnp
from jax import lax
from jax.experimental import pallas as pl
from jax.experimental.pallas import tpu as pltpu
from jax.sharding import PartitionSpec as P

MODEL_WIDTH = 1024
HQ = 16
KVH = 8
HS = 64
H = 512
TOP = 8
R = 16
NA = 8
QD = HQ * HS
KD = KVH * HS
QKV = QD + 2 * KD

epsilon = 1e-06
f32 = jnp.float32
bf16 = jnp.bfloat16


def nn(left, right):
    return lax.dot_general(left, right, (((1,), (0,)), ((), ())), preferred_element_type=f32)


def nt(left, right):
    return lax.dot_general(left, right, (((1,), (1,)), ((), ())), preferred_element_type=f32)


def tn(left, right):
    return lax.dot_general(left, right, (((0,), (0,)), ((), ())), preferred_element_type=f32)


def lanes_of(shape):
    return lax.broadcasted_iota(jnp.int32, shape, len(shape) - 1)


def row_scale(rows):
    return lax.rsqrt(jnp.mean(rows * rows, -1, keepdims=True) + epsilon)


def norm_back(rows, gain, grad):
    scale = row_scale(rows)
    scaled = grad * gain
    return scale * scaled - rows * (scale * scale * scale) * jnp.mean(
        rows * scaled, -1, keepdims=True
    )


def rope_swap(rows):
    width = rows.shape[-1]
    lane = lanes_of(rows.shape)
    return jnp.where(
        lane % HS < HS // 2,
        pltpu.roll(rows, width - HS // 2, 1),
        pltpu.roll(rows, HS // 2, 1),
    )


def both_halves(pair, half):
    rows = pair.astype(f32)
    lane = lanes_of(rows.shape)
    rolled = pltpu.roll(rows, HS, 1)
    keep = (lane < HS) == (half == 0)
    return jnp.where(keep, rows, rolled).astype(bf16)


def stacked_heads(pair):
    lane = lanes_of(pair.shape)
    zero = jnp.zeros_like(pair)
    return jnp.concatenate(
        [jnp.where(lane < HS, pair, zero), jnp.where(lane < HS, zero, pair)], 0
    )


def params_of(count):
    return pltpu.CompilerParams(
        dimension_semantics=("arbitrary",) * count, vmem_limit_bytes=56 * 1024 * 1024
    )


BLOCK = 128
BLOCKS = MODEL_WIDTH // BLOCK
HALF = MODEL_WIDTH // 2


def column(order, at):
    return pl.ds(pl.multiple_of(order[at] * BLOCK, BLOCK), BLOCK)


def project_kernel(
    order, hid, gain, weight_a, weight_b, low_map, up_map, cos, sin, qkv, low, normed, turned_rows
):
    step = pl.program_id(0)
    blocks = pl.num_programs(0)

    @pl.when(step == 0)
    def _():
        rows = hid[...].astype(f32)
        value = (rows * row_scale(rows) * gain[...].astype(f32)).astype(bf16)
        normed[...] = value
        low[...] = nt(value, low_map[...]).astype(bf16)
        for at in range(BLOCKS):
            turned_rows[:, at * BLOCK : (at + 1) * BLOCK] = normed[:, column(order, at)]

    value = (
        nn(turned_rows[:, :HALF], weight_a[...])
        + nn(turned_rows[:, HALF:], weight_b[...])
        + nn(low[...], up_map[...])
    )

    @pl.when(step < blocks * 3 // 4)
    def _():
        for part in range(value.shape[1] // 128):
            piece = value[:, part * 128 : part * 128 + 128]
            turned = piece * cos[...] + rope_swap(piece) * sin[...]
            qkv[:, part * 128 : part * 128 + 128] = turned.astype(bf16)

    @pl.when(step >= blocks * 3 // 4)
    def _():
        qkv[...] = value.astype(bf16)


def project(order, hidden, gain, weights, low_map, up_map, cos, sin):
    rows = hidden.shape[0]
    block = 256
    ranks = low_map.shape[0]
    full = lambda shape: pl.BlockSpec(shape, lambda n, s: (0, 0))
    return pl.pallas_call(
        project_kernel,
        grid_spec=pltpu.PrefetchScalarGridSpec(
            num_scalar_prefetch=1,
            grid=(QKV // block,),
            in_specs=[
                full((rows, MODEL_WIDTH)),
                full((1, MODEL_WIDTH)),
                pl.BlockSpec((HALF, block), lambda n, s: (0, n)),
                pl.BlockSpec((HALF, block), lambda n, s: (0, n)),
                full((ranks, MODEL_WIDTH)),
                pl.BlockSpec((ranks, block), lambda n, s: (0, n)),
                full((rows, 128)),
                full((rows, 128)),
            ],
            out_specs=[
                pl.BlockSpec((rows, block), lambda n, s: (0, n)),
                full((rows, ranks)),
                full((rows, MODEL_WIDTH)),
            ],
            scratch_shapes=[pltpu.VMEM((rows, MODEL_WIDTH), bf16)],
        ),
        out_shape=[
            jax.ShapeDtypeStruct((rows, QKV), bf16),
            jax.ShapeDtypeStruct((rows, ranks), bf16),
            jax.ShapeDtypeStruct((rows, MODEL_WIDTH), bf16),
        ],
        compiler_params=params_of(1),
        name="project",
        cost_estimate=pl.CostEstimate(
            flops=2 * rows * QKV * MODEL_WIDTH, transcendentals=0, bytes_accessed=8 << 20
        ),
    )(order, hidden, gain, *weights, low_map, up_map, cos, sin)


ROWB = 128


def masked_scores(length, queries, keys, start, count):
    scores = 0.125 * nt(queries, keys)
    row = lax.broadcasted_iota(jnp.int32, scores.shape, 0)
    col = lanes_of(scores.shape)
    allowed = (col <= start + row % ROWB) & (col < length)
    return scores, allowed


def attend_kernel(scalars, query, key, value, result, lse):
    half = pl.program_id(0) % 2
    length = scalars[0]
    keys = both_halves(key[...], half)
    values = both_halves(value[...], half)
    rows = query.shape[0]
    for start in range(0, rows, ROWB):
        count = start + ROWB
        stacked = stacked_heads(query[start:count, :])
        scores, allowed = masked_scores(length, stacked, keys[:count], start, count)
        scores = jnp.where(allowed, scores, -1e30)
        top = jnp.max(scores, -1, keepdims=True)
        shifted = jnp.exp(scores - top)
        total = jnp.sum(shifted, -1, keepdims=True)
        prob = (shifted * (1.0 / total)).astype(bf16)
        mixed = nn(prob, values[:count])
        lane = lanes_of((ROWB, 128))
        result[start:count, :] = jnp.where(lane < HS, mixed[:ROWB], mixed[ROWB:]).astype(bf16)
        logs = top + jnp.log(total)
        lse[0, start:count, :] = jnp.concatenate([logs[:ROWB], logs[ROWB:]], 1)


def attend(length, qkv):
    rows = qkv.shape[0]
    pairs = KVH
    return pl.pallas_call(
        attend_kernel,
        grid_spec=pltpu.PrefetchScalarGridSpec(
            num_scalar_prefetch=1,
            grid=(pairs,),
            in_specs=[
                pl.BlockSpec((rows, 128), lambda g, s: (0, g)),
                pl.BlockSpec((rows, 128), lambda g, s: (0, QD // 128 + g // 2)),
                pl.BlockSpec((rows, 128), lambda g, s: (0, (QD + KD) // 128 + g // 2)),
            ],
            out_specs=[
                pl.BlockSpec((rows, 128), lambda g, s: (0, g)),
                pl.BlockSpec((1, rows, 2), lambda g, s: (g, 0, 0)),
            ],
        ),
        out_shape=[
            jax.ShapeDtypeStruct((rows, QD), bf16),
            jax.ShapeDtypeStruct((pairs, rows, 2), f32),
        ],
        compiler_params=params_of(1),
        name="attend",
        cost_estimate=pl.CostEstimate(
            flops=8 * rows * rows * QD, transcendentals=rows * rows * HQ, bytes_accessed=4 << 20
        ),
    )(length, qkv, qkv, qkv)


def attend_back_kernel(
    scalars, query, key, value, grad, lse, cos, sin, grad_query, grad_key, grad_value, key_acc, value_acc
):
    half = pl.program_id(0) % 2
    length = scalars[0]
    keys = both_halves(key[...], half)
    values = both_halves(value[...], half)
    rows = query.shape[0]
    key_acc[...] = jnp.zeros_like(key_acc)
    value_acc[...] = jnp.zeros_like(value_acc)
    for start in range(0, rows, ROWB):
        count = start + ROWB
        stacked = stacked_heads(query[start:count, :])
        grads = stacked_heads(grad[start:count, :])
        scores, allowed = masked_scores(length, stacked, keys[:count], start, count)
        logs = lse[0, start:count, :]
        logs = jnp.concatenate([logs[:, 0:1], logs[:, 1:2]], 0)
        prob = jnp.where(allowed, jnp.exp(scores - logs), 0.0)
        grad_prob = nt(grads, values[:count])
        delta = jnp.sum(prob * grad_prob, -1, keepdims=True)
        grad_score = (prob * (grad_prob - delta)).astype(bf16)
        mixed = nn(grad_score, keys[:count])
        lane = lanes_of((ROWB, 128))
        turned = 0.125 * jnp.where(lane < HS, mixed[:ROWB], mixed[ROWB:])
        turned = turned * cos[start:count, :] - rope_swap(turned) * sin[start:count, :]
        grad_query[start:count, :] = turned.astype(bf16)
        key_acc[:count, :] += tn(grad_score, stacked)
        value_acc[:count, :] += tn(prob.astype(bf16), grads)
    total = key_acc[...]
    total = 0.125 * (total + pltpu.roll(total, HS, 1))
    total = (total * cos[...] - rope_swap(total) * sin[...]).astype(bf16)
    other = value_acc[...]
    other = (other + pltpu.roll(other, HS, 1)).astype(bf16)

    @pl.when(half == 0)
    def _():
        grad_key[...] = total
        grad_value[...] = other

    @pl.when(half == 1)
    def _():
        low_half = lanes_of(total.shape) < HS
        grad_key[...] = jnp.where(low_half, grad_key[...], total)
        grad_value[...] = jnp.where(low_half, grad_value[...], other)


def attend_back(length, qkv, grad, lse, cos, sin):
    rows = qkv.shape[0]
    pairs = KVH
    return pl.pallas_call(
        attend_back_kernel,
        grid_spec=pltpu.PrefetchScalarGridSpec(
            num_scalar_prefetch=1,
            grid=(pairs,),
            in_specs=[
                pl.BlockSpec((rows, 128), lambda g, s: (0, g)),
                pl.BlockSpec((rows, 128), lambda g, s: (0, QD // 128 + g // 2)),
                pl.BlockSpec((rows, 128), lambda g, s: (0, (QD + KD) // 128 + g // 2)),
                pl.BlockSpec((rows, 128), lambda g, s: (0, g)),
                pl.BlockSpec((1, rows, 2), lambda g, s: (g, 0, 0)),
                pl.BlockSpec((rows, 128), lambda g, s: (0, 0)),
                pl.BlockSpec((rows, 128), lambda g, s: (0, 0)),
            ],
            out_specs=[
                pl.BlockSpec((rows, 128), lambda g, s: (0, g)),
                pl.BlockSpec((rows, 128), lambda g, s: (0, g // 2)),
                pl.BlockSpec((rows, 128), lambda g, s: (0, g // 2)),
            ],
            scratch_shapes=[pltpu.VMEM((rows, 128), f32), pltpu.VMEM((rows, 128), f32)],
        ),
        out_shape=[
            jax.ShapeDtypeStruct((rows, QD), bf16),
            jax.ShapeDtypeStruct((rows, KD), bf16),
            jax.ShapeDtypeStruct((rows, KD), bf16),
        ],
        compiler_params=params_of(1),
        name="attend_back",
        cost_estimate=pl.CostEstimate(
            flops=20 * rows * rows * QD, transcendentals=rows * rows * HQ, bytes_accessed=8 << 20
        ),
    )(length, qkv, qkv, qkv, grad, lse, cos, sin)


def close_kernel(order, att, hid, gain, weight_a, weight_b, low_map, up_map, mid, normed, low):
    low_value = nt(att[...], low_map[...]).astype(bf16)
    low[...] = low_value
    turned = jnp.concatenate([att[:, column(order, at)] for at in range(BLOCKS)], 1)
    stream = hid[...].astype(f32) + (
        nn(turned[:, :HALF], weight_a[...])
        + nn(turned[:, HALF:], weight_b[...])
        + nn(low_value, up_map[...])
    )
    mid[...] = stream
    normed[...] = (stream * row_scale(stream) * gain[...].astype(f32)).astype(bf16)


def close_mixer(order, att, hidden, gain, weights, low_map, up_map):
    rows = hidden.shape[0]
    block = 256
    ranks = low_map.shape[0]
    full = lambda shape: pl.BlockSpec(shape, lambda n, s: (0, 0))
    part = lambda width: pl.BlockSpec((block, width), lambda n, s: (n, 0))
    return pl.pallas_call(
        close_kernel,
        grid_spec=pltpu.PrefetchScalarGridSpec(
            num_scalar_prefetch=1,
            grid=(rows // block,),
            in_specs=[
                part(QD),
                part(MODEL_WIDTH),
                full((1, MODEL_WIDTH)),
                full((HALF, MODEL_WIDTH)),
                full((HALF, MODEL_WIDTH)),
                full((ranks, QD)),
                full((ranks, MODEL_WIDTH)),
            ],
            out_specs=[part(MODEL_WIDTH), part(MODEL_WIDTH), part(ranks)],
        ),
        out_shape=[
            jax.ShapeDtypeStruct((rows, MODEL_WIDTH), f32),
            jax.ShapeDtypeStruct((rows, MODEL_WIDTH), bf16),
            jax.ShapeDtypeStruct((rows, ranks), bf16),
        ],
        compiler_params=params_of(1),
        name="close_mixer",
        cost_estimate=pl.CostEstimate(
            flops=2 * rows * QD * MODEL_WIDTH, transcendentals=0, bytes_accessed=8 << 20
        ),
    )(order, att, hidden, gain, *weights, low_map, up_map)


def side_by_side(left, right):
    values = []
    for at in range(BLOCKS):
        tile = slice(at // 2 * BLOCK, (at // 2 + 1) * BLOCK)
        low_half = lanes_of((R, BLOCK)) < BLOCK // 2
        if at % 2 == 0:
            value = jnp.where(low_half, left[:, tile], pltpu.roll(right[:, tile], BLOCK // 2, 1))
        else:
            value = jnp.where(low_half, pltpu.roll(left[:, tile], BLOCK // 2, 1), right[:, tile])
        values.append(value.astype(bf16))
    return values


def expert_kernel(
    scalars,
    x,
    cot,
    routes,
    router,
    w_in,
    w_down,
    a_in,
    b_in,
    a_down,
    b_down,
    *rest,
):
    (
        out,
        grad_normed,
        gates_out,
        packed,
        gates,
        gate_sums,
        low_in,
        low_in_turned,
        b_in_all,
        back_low,
        gated_low,
        back_in,
        acts,
        grads,
        low_grads,
        down_acc,
        out_acc,
        grad_acc,
    ) = rest[-18:]
    expert = pl.program_id(0)
    last = pl.num_programs(0) - 1
    rows = x.shape[0]
    block = 256
    local = a_in.shape[0]
    a_in_all = a_in[...].reshape(local * 2 * R, MODEL_WIDTH)
    a_down_all = a_down[...].reshape(local * R, H)
    b_down_all = b_down[...].reshape(local * R, MODEL_WIDTH)

    @pl.when(expert == 0)
    def _():
        logits = nt(x[...], router[...])
        lane = lanes_of(logits.shape)
        chosen = lane == routes[:, 0:1]
        for k in range(1, TOP):
            chosen = chosen | (lane == routes[:, k : k + 1])
        top = jnp.max(jnp.where(chosen, logits, -1e30), -1, keepdims=True)
        shifted = jnp.where(chosen, jnp.exp(jnp.where(chosen, logits - top, 0.0)), 0.0)
        weights = shifted / jnp.sum(shifted, -1, keepdims=True)
        gates[...] = weights
        gates_out[...] = weights.T[: gates_out.shape[0], :]
        low = nt(x[...], a_in_all)
        low_in[...] = low.astype(bf16)
        low_in_turned[...] = low.T.astype(bf16)
        back_low[...] = nt(cot[...], b_down_all)
        b_in_all[...] = jnp.zeros_like(b_in_all)
        for e in range(local):
            b_in_all[e * 2 * R : e * 2 * R + R, :H] = b_in[e, 0, 0]
            b_in_all[e * 2 * R + R : (e + 1) * 2 * R, H:] = b_in[e, 0, 1]
        gate_sums[...] = jnp.zeros_like(gate_sums)
        gated_low[...] = jnp.zeros_like(gated_low)
        back_in[...] = jnp.zeros_like(back_in)
        out_acc[...] = jnp.zeros_like(out_acc)
        grad_acc[...] = jnp.zeros_like(grad_acc)
        down_acc[...] = jnp.zeros_like(down_acc)

    def row_step(index, carry):
        at = pl.ds(pl.multiple_of(index * block, block), block)
        lane_in = lanes_of((block, local * 2 * R))
        lane_down = lanes_of((block, local * R))
        in_mine = (lane_in >= expert * 2 * R) & (lane_in < (expert + 1) * 2 * R)
        down_mine = (lane_down >= expert * R) & (lane_down < (expert + 1) * R)
        gate_all = gates[at, :]
        gate_lane = lanes_of(gate_all.shape) == expert
        weight = jnp.sum(jnp.where(gate_lane, gate_all, 0.0), -1, keepdims=True)
        mine = low_in[at, :]
        mine = jnp.where(in_mine, mine, jnp.zeros_like(mine))
        both = nn(x[at, :], w_in[0]) + nn(mine, b_in_all[...])
        gate = both[:, :H]
        upper = both[:, H:]
        sigmoid = jax.nn.sigmoid(gate)
        silu = gate * sigmoid
        act = (silu * upper).astype(bf16)
        acts[at, :] = act
        act_wide = act.astype(f32)
        low = jnp.where(down_mine, nt(act, a_down_all), 0.0).astype(bf16).astype(f32)
        plain = nt(cot[at, :], w_down[0])
        low_plain = back_low[at, :]
        dots = jnp.sum(act_wide * plain, -1, keepdims=True) + jnp.sum(
            low * low_plain, -1, keepdims=True
        )
        sum_lane = lanes_of(gate_all.shape) == expert + scalars[2]
        gate_sums[at, :] += jnp.where(sum_lane, dots, 0.0)
        low_grad = jnp.where(down_mine, weight * low_plain, 0.0).astype(bf16)
        low_grads[at, :] = low_grad
        grad_act = weight * plain + nn(low_grad, a_down_all)
        grad_first = grad_act * upper * sigmoid * (1.0 + gate * (1.0 - sigmoid))
        grad_second = grad_act * silu
        grad_both = jnp.concatenate(
            [grad_first.astype(bf16), grad_second.astype(bf16)], 1
        )
        grads[at, :] = grad_both
        gated_low[at, :] += (weight * low).astype(bf16)
        out_acc[at, :] += nn((weight * act_wide).astype(bf16), w_down[0])
        grad_acc[at, :] += nt(grad_both, w_in[0])
        low_back = jnp.where(in_mine, nt(grad_both, b_in_all[...]), 0.0)
        back_in[at, :] += low_back.astype(bf16)
        return carry

    lax.fori_loop(0, rows // block, row_step, 0)

    turned = low_in_turned[pl.ds(pl.multiple_of(expert * 2 * R, 2 * R), 2 * R), :]
    product = nn(turned, grads[...])
    first_b_in = local * 3 * R
    here = pl.ds(pl.multiple_of(first_b_in + expert * R, R), R)
    for at, value in enumerate(side_by_side(product[:R, :H], product[R:, H:])):
        packed[at, 0, here, :] = value
    down_acc[...] += tn(low_grads[...], acts[...])

    @pl.when(expert == last)
    def _():
        out[...] = (out_acc[...] + nn(gated_low[...], b_down_all)).astype(bf16)
        grad_normed[:rows, :] = (grad_acc[...] + nn(back_in[...], a_in_all)).astype(bf16)
        experts = gates_out.shape[0]
        sums = gate_sums[...].T[:experts, :]
        sums = jnp.concatenate([sums[: experts // 2], sums[experts // 2 :]], 1)
        high = sums.astype(bf16).astype(f32)
        grad_normed[rows:, :] = jnp.concatenate([high, sums - high], 0).astype(bf16)
        wide = tn(back_in[...], x[...]).astype(bf16)
        tall = tn(gated_low[...], cot[...]).astype(bf16)
        for at in range(BLOCKS):
            columns = slice(at * BLOCK, (at + 1) * BLOCK)
            packed[at, 0, : local * 2 * R, :] = wide[:, columns]
            packed[at, 0, local * 2 * R : first_b_in, :] = tall[:, columns]
        for pair in range(local // 2):
            lower = down_acc[pair * 2 * R : pair * 2 * R + R, :]
            upper = down_acc[pair * 2 * R + R : (pair + 1) * 2 * R, :]
            row = local * 4 * R + pair * R
            for at, value in enumerate(side_by_side(lower, upper)):
                packed[at, 0, row : row + R, :] = value


def run_experts(
    scalars, x, cot, routes, router, w_in, w_down, a_in, b_in, a_down, b_down, experts, slots, packed
):
    rows = x.shape[0]
    local = w_in.shape[0]
    ranks_in = local * 2 * R
    ranks_down = local * R
    height = local * 9 * R // 2
    kept = [] if packed is None else [packed]
    full = lambda shape: pl.BlockSpec(shape, lambda e, s: (0,) * len(shape))
    return pl.pallas_call(
        expert_kernel,
        grid_spec=pltpu.PrefetchScalarGridSpec(
            num_scalar_prefetch=1,
            grid=(local,),
            in_specs=[
                full((rows, MODEL_WIDTH)),
                pl.BlockSpec((rows, MODEL_WIDTH), lambda e, s: (s[4], 0)),
                pl.BlockSpec((rows, TOP), lambda e, s: (s[0], 0)),
                full((128, MODEL_WIDTH)),
                pl.BlockSpec((1, MODEL_WIDTH, 2 * H), lambda e, s: (e, 0, 0)),
                pl.BlockSpec((1, H, MODEL_WIDTH), lambda e, s: (e, 0, 0)),
                pl.BlockSpec((local, 1, 2 * R, MODEL_WIDTH), lambda e, s: (0, s[1], 0, 0)),
                pl.BlockSpec((local, 1, 2, R, H), lambda e, s: (0, s[1], 0, 0, 0)),
                pl.BlockSpec((local, 1, R, H), lambda e, s: (0, s[1], 0, 0)),
                pl.BlockSpec((local, 1, R, MODEL_WIDTH), lambda e, s: (0, s[1], 0, 0)),
            ]
            + [pl.BlockSpec(memory_space=pl.ANY)] * len(kept),
            out_specs=[
                full((rows, MODEL_WIDTH)),
                full((rows + experts, MODEL_WIDTH)),
                full((experts, rows)),
                pl.BlockSpec((BLOCKS, 1, height, BLOCK), lambda e, s: (0, s[3], 0, 0)),
            ],
            scratch_shapes=[
                pltpu.VMEM((rows, 128), f32),
                pltpu.VMEM((rows, 128), f32),
                pltpu.VMEM((rows, ranks_in), bf16),
                pltpu.VMEM((ranks_in, rows), bf16),
                pltpu.VMEM((ranks_in, 2 * H), bf16),
                pltpu.VMEM((rows, ranks_down), f32),
                pltpu.VMEM((rows, ranks_down), bf16),
                pltpu.VMEM((rows, ranks_in), bf16),
                pltpu.VMEM((rows, H), bf16),
                pltpu.VMEM((rows, 2 * H), bf16),
                pltpu.VMEM((rows, ranks_down), bf16),
                pltpu.VMEM((ranks_down, H), f32),
                pltpu.VMEM((rows, MODEL_WIDTH), f32),
                pltpu.VMEM((rows, MODEL_WIDTH), f32),
            ],
        ),
        out_shape=[
            jax.ShapeDtypeStruct((rows, MODEL_WIDTH), bf16),
            jax.ShapeDtypeStruct((rows + experts, MODEL_WIDTH), bf16),
            jax.ShapeDtypeStruct((experts, rows), f32),
            jax.ShapeDtypeStruct((BLOCKS, slots, height, BLOCK), bf16),
        ],
        input_output_aliases={11: 3} if kept else {},
        compiler_params=params_of(1),
        name="experts",
        cost_estimate=pl.CostEstimate(
            flops=local * rows * 9 * (1 << 20),
            transcendentals=local * rows * H,
            bytes_accessed=20 << 20,
        ),
    )(scalars, x, cot, routes, router, w_in, w_down, a_in, b_in, a_down, b_down, *kept)


def open_back_kernel(count, order, cot, mid, gain, gates, router, weight_a, weight_b, low_map, up_map, low, att, *rest):
    parts = rest[:count]
    sums = rest[count : 3 * count]
    grad_mid, grad_att, grad_up, grad_low, columns = rest[3 * count :]
    gate_value = gates[...]
    half = gate_value.shape[0] // 2
    sides = []
    for side in range(2):
        value = None
        for at in range(count):
            pair = sums[2 * at + side][...].astype(f32)
            pair = pair[:half] + pair[half:]
            value = pair if value is None else value + pair
        sides.append(value)
    gate_grad = jnp.concatenate(sides, 0)
    logit = gate_value * (gate_grad - jnp.sum(gate_value * gate_grad, 0, keepdims=True))
    first = logit.astype(bf16)
    left = logit - first.astype(f32)
    second = left.astype(bf16)
    third = (left - second.astype(f32)).astype(bf16)
    grad = tn(first, router[...]) + (tn(second, router[...]) + tn(third, router[...]))
    for piece in parts:
        grad = grad + piece[...].astype(f32)
    total = cot[...].astype(f32) + norm_back(mid[...], gain[...].astype(f32), grad)
    grad_mid[...] = total
    branch = total.astype(bf16)
    low_grad = nt(branch, up_map[...]).astype(bf16)
    columns[...] = nn(low_grad, low_map[...])
    for side, weight in enumerate((weight_a, weight_b)):
        value = nt(branch, weight[...])
        for at in range(BLOCKS // 2):
            columns[:, column(order, side * BLOCKS // 2 + at)] += value[:, at * BLOCK : (at + 1) * BLOCK]
    grad_att[...] = columns[...].astype(bf16)
    up_part = tn(low[...], branch)
    low_part = tn(low_grad, att[...])

    @pl.when(pl.program_id(0) == 0)
    def _():
        grad_up[...] = up_part
        grad_low[...] = low_part

    @pl.when(pl.program_id(0) > 0)
    def _():
        grad_up[...] += up_part
        grad_low[...] += low_part


def open_back(order, cot, mid, gain, gates, router, weights, low_map, up_map, low, att, parts):
    rows = cot.shape[0]
    block = 256
    ranks = low_map.shape[0]
    experts = gates.shape[0]
    full = lambda shape: pl.BlockSpec(shape, lambda n, s: (0, 0))
    part = lambda width: pl.BlockSpec((block, width), lambda n, s: (n, 0))
    count = len(parts)
    below = rows // experts
    sums = [
        pl.BlockSpec((experts, block), lambda n, s: (below, n)),
        pl.BlockSpec((experts, block), lambda n, s: (below, rows // block + n)),
    ]

    def body(*refs):
        open_back_kernel(count, *refs)

    return pl.pallas_call(
        body,
        grid_spec=pltpu.PrefetchScalarGridSpec(
            num_scalar_prefetch=1,
            grid=(rows // block,),
            in_specs=[
                part(MODEL_WIDTH),
                part(MODEL_WIDTH),
                full((1, MODEL_WIDTH)),
                pl.BlockSpec((experts, block), lambda n, s: (0, n)),
                full((experts, MODEL_WIDTH)),
                full((HALF, MODEL_WIDTH)),
                full((HALF, MODEL_WIDTH)),
                full((ranks, QD)),
                full((ranks, MODEL_WIDTH)),
                part(ranks),
                part(QD),
            ]
            + [part(MODEL_WIDTH)] * count
            + sums * count,
            out_specs=[
                part(MODEL_WIDTH),
                part(QD),
                full((ranks, MODEL_WIDTH)),
                full((ranks, QD)),
            ],
            scratch_shapes=[pltpu.VMEM((block, QD), f32)],
        ),
        out_shape=[
            jax.ShapeDtypeStruct((rows, MODEL_WIDTH), f32),
            jax.ShapeDtypeStruct((rows, QD), bf16),
            jax.ShapeDtypeStruct((ranks, MODEL_WIDTH), f32),
            jax.ShapeDtypeStruct((ranks, QD), f32),
        ],
        compiler_params=params_of(1),
        name="open_back",
        cost_estimate=pl.CostEstimate(
            flops=2 * rows * QD * MODEL_WIDTH, transcendentals=0, bytes_accessed=14 << 20
        ),
    )(
        order, cot, mid, gain, gates, router, *weights, low_map, up_map, low, att, *parts,
        *[piece for piece in parts for _ in range(2)],
    )


def adapters_back_kernel(
    grad_query, grad_key, grad_value, low, normed, up_map, grad_up, grad_low, low_out
):
    pieces = (grad_query, grad_key, grad_value)
    bounds = (0, QD, QD + KD, QKV)
    back = None
    for at in range(3):
        block = pieces[at][...]
        product = tn(low[...], block)
        grad_up[:, bounds[at] : bounds[at + 1]] = product[at * R : (at + 1) * R]
        part = nt(block, up_map[:, bounds[at] : bounds[at + 1]])
        back = part if back is None else back + part
    value = back.astype(bf16)
    low_out[...] = value
    grad_low[...] = tn(value, normed[...])


def adapters_back(grad_query, grad_key, grad_value, low, normed, up_map):
    rows = normed.shape[0]
    ranks = up_map.shape[0]
    return pl.pallas_call(
        adapters_back_kernel,
        out_shape=[
            jax.ShapeDtypeStruct((R, QKV), f32),
            jax.ShapeDtypeStruct((ranks, MODEL_WIDTH), f32),
            jax.ShapeDtypeStruct((rows, ranks), bf16),
        ],
        compiler_params=pltpu.CompilerParams(vmem_limit_bytes=56 * 1024 * 1024),
        name="adapters_back",
        cost_estimate=pl.CostEstimate(
            flops=6 * rows * 256 * QKV, transcendentals=0, bytes_accessed=4 << 20
        ),
    )(grad_query, grad_key, grad_value, low, normed, up_map)


def input_back_kernel(
    order, grad_query, grad_key, grad_value, low, weight_a, weight_b, low_map, hid, gain, mid, grad, columns
):
    columns[...] = nn(low[...], low_map[...])
    for side, weight in enumerate((weight_a, weight_b)):
        value = nt(grad_query[...], weight[:, :QD])
        value = value + nt(grad_key[...], weight[:, QD : QD + KD])
        value = value + nt(grad_value[...], weight[:, QD + KD :])
        for at in range(BLOCKS // 2):
            columns[:, column(order, side * BLOCKS // 2 + at)] += value[:, at * BLOCK : (at + 1) * BLOCK]
    rows = hid[...].astype(f32)
    grad[...] = (mid[...] + norm_back(rows, gain[...].astype(f32), columns[...])).astype(bf16)


def input_back(order, grad_query, grad_key, grad_value, low, weights, low_map, hidden, gain, mid):
    rows = hidden.shape[0]
    block = 256
    ranks = low_map.shape[0]
    full = lambda shape: pl.BlockSpec(shape, lambda n, s: (0, 0))
    part = lambda width: pl.BlockSpec((block, width), lambda n, s: (n, 0))
    return pl.pallas_call(
        input_back_kernel,
        grid_spec=pltpu.PrefetchScalarGridSpec(
            num_scalar_prefetch=1,
            grid=(rows // block,),
            in_specs=[
                part(QD),
                part(KD),
                part(KD),
                part(ranks),
                full((HALF, QKV)),
                full((HALF, QKV)),
                full((ranks, MODEL_WIDTH)),
                part(MODEL_WIDTH),
                full((1, MODEL_WIDTH)),
                part(MODEL_WIDTH),
            ],
            out_specs=part(MODEL_WIDTH),
            scratch_shapes=[pltpu.VMEM((block, MODEL_WIDTH), f32)],
        ),
        out_shape=jax.ShapeDtypeStruct((rows, MODEL_WIDTH), bf16),
        compiler_params=params_of(1),
        name="input_back",
        cost_estimate=pl.CostEstimate(
            flops=2 * rows * QKV * MODEL_WIDTH, transcendentals=0, bytes_accessed=12 << 20
        ),
    )(order, grad_query, grad_key, grad_value, low, *weights, low_map, hidden, gain, mid)


def sum_experts_kernel(ids, pieces, a_in, b_in, a_down, b_down, acc):
    local = a_in.shape[0]
    small = a_down.shape[-1]
    acc[...] = jnp.zeros_like(acc)

    def step(index, carry):
        acc[ids[index]] += pieces[index].astype(f32)
        return carry

    lax.fori_loop(0, pieces.shape[0], step, 0)
    for e in range(local):
        a_in[e] = acc[:, e * 2 * R : (e + 1) * 2 * R, :]
        at = local * 2 * R + e * R
        b_down[e] = acc[:, at : at + R, :]
        at = local * 3 * R + e * R
        both = acc[:, at : at + R, :]
        b_in[e, :, 0] = both[:, :, :small]
        b_in[e, :, 1] = both[:, :, small:]
        at = local * 4 * R + e // 2 * R
        a_down[e] = acc[:, at : at + R, e % 2 * small : (e % 2 + 1) * small]


def sum_experts(ids, pieces, local):
    height = pieces.shape[1]
    lanes = pieces.shape[2]
    small = lanes // 2
    vmem = pl.BlockSpec(memory_space=pltpu.VMEM)
    return pl.pallas_call(
        sum_experts_kernel,
        in_specs=[pl.BlockSpec(memory_space=pltpu.SMEM), vmem],
        out_specs=[vmem, vmem, vmem, vmem],
        out_shape=[
            jax.ShapeDtypeStruct((local, NA, 2 * R, lanes), f32),
            jax.ShapeDtypeStruct((local, NA, 2, R, small), f32),
            jax.ShapeDtypeStruct((local, NA, R, small), f32),
            jax.ShapeDtypeStruct((local, NA, R, lanes), f32),
        ],
        scratch_shapes=[pltpu.VMEM((NA, height, lanes), f32)],
        compiler_params=pltpu.CompilerParams(vmem_limit_bytes=56 * 1024 * 1024),
        name="sum_experts",
    )(ids, pieces)


def sum_mixer_kernel(ids, pieces, grad_low, grad_up, grad_out, acc):
    width = grad_low.shape[-1]
    acc[...] = jnp.zeros_like(acc)

    def step(index, carry):
        acc[ids[index]] += pieces[index]
        return carry

    lax.fori_loop(0, pieces.shape[0], step, 0)
    total = acc[...]
    for at in range(4):
        grad_low[at] = total[:, :, at * width : (at + 1) * width]
    grad_up[...] = total[:, :, 4 * width : 6 * width]
    grad_out[...] = total[:, :, 6 * width : 7 * width]


def sum_mixer(ids, pieces):
    width = pieces.shape[2] // 8
    vmem = pl.BlockSpec(memory_space=pltpu.VMEM)
    return pl.pallas_call(
        sum_mixer_kernel,
        in_specs=[pl.BlockSpec(memory_space=pltpu.SMEM), vmem],
        out_specs=[vmem, vmem, vmem],
        out_shape=[
            jax.ShapeDtypeStruct((4, NA, R, width), f32),
            jax.ShapeDtypeStruct((NA, R, 2 * width), f32),
            jax.ShapeDtypeStruct((NA, R, width), f32),
        ],
        scratch_shapes=[pltpu.VMEM((NA, R, 8 * width), f32)],
        compiler_params=pltpu.CompilerParams(vmem_limit_bytes=56 * 1024 * 1024),
        name="sum_mixer",
    )(ids, pieces)


def rope_tables(rows):
    half = HS // 2
    frequency = (10000.0 ** (-2.0 * np.arange(half, dtype=np.float32) / HS)).astype(np.float32)
    angles = np.arange(rows, dtype=np.float32)[:, None] * frequency[None, :]
    cos = np.cos(angles.astype(np.float64)).astype(np.float32)
    sin = np.sin(angles.astype(np.float64)).astype(np.float32)
    return (
        jnp.asarray(np.concatenate([cos, cos, cos, cos], 1)),
        jnp.asarray(np.concatenate([-sin, sin, -sin, sin], 1)),
    )


def swap(value, bit):
    return lax.ppermute(value, "dp", [(at, at ^ bit) for at in range(BLOCKS)])


def gather_rows(weight):
    if lax.axis_size("dp") != BLOCKS:
        whole = lax.all_gather(weight, "dp", axis=0, tiled=True)
        return whole[:HALF], whole[HALF:]
    middle = weight.shape[0] // 2
    one = swap(weight, 2)
    two = swap(weight, 4)
    both = [swap(two[:middle], 2), swap(one[middle:], 4)]
    near = jnp.concatenate([weight, one, two] + both, 0)
    return near, swap(near, 1)


def order_of(row):
    if lax.axis_size("dp") != BLOCKS:
        return jnp.arange(BLOCKS, dtype=jnp.int32)
    return row.astype(jnp.int32) ^ jnp.array([0, 2, 4, 6, 1, 3, 5, 7], jnp.int32)


def to_owners(packed, owners, local):
    split = owners // BLOCKS
    if split == 1:
        return packed
    slots = packed.shape[1]
    edge = local * 3 * R
    wide = packed[:, :, :edge].reshape(BLOCKS, slots, edge, split, BLOCK // split)
    wide = wide.transpose(0, 3, 1, 2, 4).reshape(owners, slots, edge, BLOCK // split)
    rest = packed.shape[2] - edge
    narrow = packed[:, :, edge:].reshape(BLOCKS, slots, rest, 2, split, BLOCK // 2 // split)
    narrow = narrow.transpose(0, 4, 1, 2, 3, 5).reshape(owners, slots, rest, BLOCK // split)
    return jnp.concatenate([wide, narrow], 2)


def joined(left, right):
    return (left.astype(f32) + right.astype(f32)).astype(bf16)


def on_device(
    hidden,
    cotangent,
    lengths,
    adapter_ids,
    routes,
    attn_gain,
    ffn_gain,
    query_key_value_weight,
    w_out,
    w_router,
    w_gate_up,
    w_down,
    attention_lowmap,
    attention_query_key_value_upmap,
    attention_output_upmap,
    expert_gate_up_lowmap,
    expert_gate_up_upmap,
    expert_down_lowmap,
    expert_down_upmap,
):
    groups = lax.axis_size("expert")
    owners = lax.axis_size("dp")
    place = lax.axis_index("expert")
    row = lax.axis_index("dp")
    devices = groups * owners
    sequence = row * groups + place
    rows = hidden.shape[0]
    experts = w_router.shape[1]
    local = w_gate_up.shape[0]
    width = MODEL_WIDTH // owners
    attn_gain = attn_gain.reshape(1, MODEL_WIDTH)
    ffn_gain = ffn_gain.reshape(1, MODEL_WIDTH)
    length = lax.dynamic_slice(lengths, (sequence,), (1,))
    forward = [(at, (at + 1) % groups) for at in range(groups)]

    mine = lax.dynamic_slice(adapter_ids.reshape(owners, groups), (0, place), (owners, 1))[:, 0]
    low_turned = attention_lowmap.transpose(1, 0, 3, 2).reshape(NA, 4 * R, width)
    up_turned = (
        attention_query_key_value_upmap.reshape(NA, R, 2, width)
        .transpose(0, 2, 1, 3)
        .reshape(NA, 2 * R, width)
    )
    adapters = jnp.concatenate([low_turned, up_turned, attention_output_upmap], 1)[mine]
    adapters = lax.all_to_all(adapters, "dp", 0, 0, tiled=True)
    order = order_of(row)
    weight_in = gather_rows(query_key_value_weight)
    late, weight_in = lax.optimization_barrier((w_out, weight_in))
    weight_out = gather_rows(late)

    low_map = adapters[:, : 4 * R].transpose(1, 0, 2).reshape(4 * R, MODEL_WIDTH)
    up = (
        adapters[:, 4 * R : 6 * R]
        .reshape(owners, 2, R, width)
        .transpose(2, 0, 1, 3)
        .reshape(R, QKV)
    )
    up_out = adapters[:, 6 * R :].transpose(1, 0, 2).reshape(R, MODEL_WIDTH)
    column = jnp.arange(QKV, dtype=jnp.int32)
    part = jnp.where(column < QD, 0, jnp.where(column < QD + KD, 1, 2))
    up_map = jnp.where(
        part[None, None, :] == jnp.arange(4, dtype=jnp.int32)[:, None, None], up[None], 0
    ).reshape(4 * R, QKV)
    up_out_map = jnp.concatenate([jnp.zeros((3 * R, MODEL_WIDTH), bf16), up_out], 0)

    cos, sin = rope_tables(rows)

    cots = lax.all_gather(cotangent, "expert", axis=0, tiled=True)

    qkv, low, normed_in = project(order, hidden, attn_gain, weight_in, low_map, up_map, cos, sin)
    attended, lse = attend(length, qkv)
    mid, normed_mid, low_out = close_mixer(
        order, attended, hidden, ffn_gain, weight_out, low_map, up_out_map
    )

    first = place * local
    routes_here = (routes - first + experts) % experts
    router = jnp.roll(w_router.T, -first, axis=0)
    router_wide = jnp.concatenate(
        [router, jnp.zeros((128 - experts, MODEL_WIDTH), router.dtype)], 0
    )
    a_in = expert_gate_up_lowmap.transpose(0, 1, 3, 2)
    a_down = expert_down_lowmap.transpose(0, 1, 3, 2)

    source = (place - jnp.arange(groups, dtype=jnp.int32) + groups) % groups
    tags = adapter_ids.reshape(owners, groups)[:, source]
    at = jnp.arange(groups, dtype=jnp.int32)
    table = jnp.stack(
        [source, lax.dynamic_slice(tags, (row, 0), (1, groups))[0], at * local, at, jnp.where(at == 0, 0, source)], 1
    )

    x = normed_mid
    packed = None
    for at in range(groups):
        out_part, grad_part, gate_part, packed = run_experts(
            table[at],
            x,
            cotangent if at == 0 else cots,
            routes_here,
            router_wide,
            w_gate_up,
            w_down,
            a_in,
            expert_gate_up_upmap,
            a_down,
            expert_down_upmap,
            experts,
            groups,
            packed,
        )
        if at < groups - 1:
            x = lax.ppermute(x, "expert", forward)
        if at == 0:
            gates, out_here, grad_here = gate_part, out_part, grad_part
            continue
        if at > 1:
            grad_part = joined(grad_part, grad_far)
            out_part = joined(out_part, out_far)
        grad_far = lax.ppermute(grad_part, "expert", forward)
        out_far = lax.ppermute(out_part, "expert", forward)

    pieces = lax.all_to_all(to_owners(packed, owners, local), "dp", 0, 0, tiled=True)
    pieces = pieces.reshape(devices, pieces.shape[2], width)
    g_a_in, g_b_in, g_a_down, g_b_down = sum_experts(tags.reshape(devices), pieces, local)

    grad_mid, grad_attended, grad_up_out, grad_low_out = open_back(
        order,
        cotangent,
        mid,
        ffn_gain,
        gates,
        router,
        weight_out,
        low_map,
        up_out_map,
        low_out,
        attended,
        [grad_here, grad_far],
    )
    grad_query, grad_key, grad_value = attend_back(length, qkv, grad_attended, lse, cos, sin)
    grad_up, grad_low, back_low = adapters_back(
        grad_query, grad_key, grad_value, low, normed_in, up_map
    )

    grad_low = grad_low + grad_low_out
    small = MODEL_WIDTH // devices
    packed = jnp.concatenate(
        [
            grad_low.reshape(4, R, devices, small).transpose(2, 1, 0, 3).reshape(devices, R, 4 * small),
            grad_up.reshape(R, devices, 2 * small).transpose(1, 0, 2),
            grad_up_out[3 * R :].reshape(R, devices, small).transpose(1, 0, 2),
            jnp.zeros((devices, R, small), f32),
        ],
        -1,
    )
    packed = lax.all_to_all(packed, ("dp", "expert"), 0, 0, tiled=True)
    m_a, m_b, m_o = sum_mixer(adapter_ids, packed)

    grad_hidden = input_back(
        order, grad_query, grad_key, grad_value, back_low, weight_in, low_map, hidden, attn_gain, grad_mid
    )
    out = (mid + out_here.astype(f32) + out_far.astype(f32)).astype(bf16)
    return (
        out,
        grad_hidden,
        m_a.transpose(0, 1, 3, 2),
        m_b,
        m_o,
        g_a_in.transpose(0, 1, 3, 2),
        g_b_in,
        g_a_down.transpose(0, 1, 3, 2),
        g_b_down,
    )


def solution(mesh):
    in_specs = (
        P(("dp", "expert"), None),
        P(("dp", "expert"), None),
        P(),
        P(),
        P("dp", None),
        P(),
        P(),
        P("dp", None),
        P("dp", None),
        P(),
        P("expert", None, None),
        P("expert", None, None),
        P(None, None, "dp", None),
        P(None, None, "dp"),
        P(None, None, "dp"),
        P("expert", None, None, None),
        P("expert", None, None, None, None),
        P("expert", None, None, None),
        P("expert", None, None, None),
    )
    out_specs = (
        P(("dp", "expert"), None),
        P(("dp", "expert"), None),
        P(None, None, ("dp", "expert"), None),
        P(None, None, ("dp", "expert")),
        P(None, None, ("dp", "expert")),
        P("expert", None, "dp", None),
        P("expert", None, None, None, "dp"),
        P("expert", None, "dp", None),
        P("expert", None, None, "dp"),
    )
    return jax.shard_map(
        on_device, mesh=mesh, in_specs=in_specs, out_specs=out_specs, check_vma=False
    )
```

```python
import numpy as np
import jax
import jax.numpy as jnp
from jax import lax
from jax.experimental import pallas as pl
from jax.experimental.pallas import tpu as pltpu
from jax.sharding import PartitionSpec as P

MODEL_WIDTH = 1024
HQ = 16
KVH = 8
HS = 64
H = 512
TOP = 8
R = 16
NA = 8
QD = HQ * HS
KD = KVH * HS
QKV = QD + 2 * KD

epsilon = 1e-06
f32 = jnp.float32
bf16 = jnp.bfloat16


def nn(left, right):
    return lax.dot_general(left, right, (((1,), (0,)), ((), ())), preferred_element_type=f32)


def nt(left, right):
    return lax.dot_general(left, right, (((1,), (1,)), ((), ())), preferred_element_type=f32)


def tn(left, right):
    return lax.dot_general(left, right, (((0,), (0,)), ((), ())), preferred_element_type=f32)


def lanes_of(shape):
    return lax.broadcasted_iota(jnp.int32, shape, len(shape) - 1)


def row_scale(rows):
    return lax.rsqrt(jnp.mean(rows * rows, -1, keepdims=True) + epsilon)


def norm_back(rows, gain, grad):
    scale = row_scale(rows)
    scaled = grad * gain
    return scale * scaled - rows * (scale * scale * scale) * jnp.mean(
        rows * scaled, -1, keepdims=True
    )


def rope_swap(rows):
    width = rows.shape[-1]
    lane = lanes_of(rows.shape)
    return jnp.where(
        lane % HS < HS // 2,
        pltpu.roll(rows, width - HS // 2, 1),
        pltpu.roll(rows, HS // 2, 1),
    )


def both_halves(pair, half):
    rows = pair.astype(f32)
    lane = lanes_of(rows.shape)
    rolled = pltpu.roll(rows, HS, 1)
    keep = (lane < HS) == (half == 0)
    return jnp.where(keep, rows, rolled).astype(bf16)


def stacked_heads(pair):
    lane = lanes_of(pair.shape)
    zero = jnp.zeros_like(pair)
    return jnp.concatenate(
        [jnp.where(lane < HS, pair, zero), jnp.where(lane < HS, zero, pair)], 0
    )


def params_of(count):
    return pltpu.CompilerParams(
        dimension_semantics=("arbitrary",) * count, vmem_limit_bytes=56 * 1024 * 1024
    )


BLOCK = 128
BLOCKS = MODEL_WIDTH // BLOCK
HALF = MODEL_WIDTH // 2


def column(order, at):
    return pl.ds(pl.multiple_of(order[at] * BLOCK, BLOCK), BLOCK)


def project_kernel(
    order, hid, gain, weight_a, weight_b, low_map, up_map, cos, sin, qkv, low, normed, turned_rows
):
    step = pl.program_id(0)
    blocks = pl.num_programs(0)

    @pl.when(step == 0)
    def _():
        rows = hid[...].astype(f32)
        value = (rows * row_scale(rows) * gain[...].astype(f32)).astype(bf16)
        normed[...] = value
        low[...] = nt(value, low_map[...]).astype(bf16)
        for at in range(BLOCKS):
            turned_rows[:, at * BLOCK : (at + 1) * BLOCK] = normed[:, column(order, at)]

    value = (
        nn(turned_rows[:, :HALF], weight_a[...])
        + nn(turned_rows[:, HALF:], weight_b[...])
        + nn(low[...], up_map[...])
    )

    @pl.when(step < blocks * 3 // 4)
    def _():
        for part in range(value.shape[1] // 128):
            piece = value[:, part * 128 : part * 128 + 128]
            turned = piece * cos[...] + rope_swap(piece) * sin[...]
            qkv[:, part * 128 : part * 128 + 128] = turned.astype(bf16)

    @pl.when(step >= blocks * 3 // 4)
    def _():
        qkv[...] = value.astype(bf16)


def project(order, hidden, gain, weights, low_map, up_map, cos, sin):
    rows = hidden.shape[0]
    block = 256
    ranks = low_map.shape[0]
    full = lambda shape: pl.BlockSpec(shape, lambda n, s: (0, 0))
    return pl.pallas_call(
        project_kernel,
        grid_spec=pltpu.PrefetchScalarGridSpec(
            num_scalar_prefetch=1,
            grid=(QKV // block,),
            in_specs=[
                full((rows, MODEL_WIDTH)),
                full((1, MODEL_WIDTH)),
                pl.BlockSpec((HALF, block), lambda n, s: (0, n)),
                pl.BlockSpec((HALF, block), lambda n, s: (0, n)),
                full((ranks, MODEL_WIDTH)),
                pl.BlockSpec((ranks, block), lambda n, s: (0, n)),
                full((rows, 128)),
                full((rows, 128)),
            ],
            out_specs=[
                pl.BlockSpec((rows, block), lambda n, s: (0, n)),
                full((rows, ranks)),
                full((rows, MODEL_WIDTH)),
            ],
            scratch_shapes=[pltpu.VMEM((rows, MODEL_WIDTH), bf16)],
        ),
        out_shape=[
            jax.ShapeDtypeStruct((rows, QKV), bf16),
            jax.ShapeDtypeStruct((rows, ranks), bf16),
            jax.ShapeDtypeStruct((rows, MODEL_WIDTH), bf16),
        ],
        compiler_params=params_of(1),
        name="project",
        cost_estimate=pl.CostEstimate(
            flops=2 * rows * QKV * MODEL_WIDTH, transcendentals=0, bytes_accessed=8 << 20
        ),
    )(order, hidden, gain, *weights, low_map, up_map, cos, sin)


ROWB = 128


def masked_scores(length, queries, keys, start, count):
    scores = 0.125 * nt(queries, keys)
    row = lax.broadcasted_iota(jnp.int32, scores.shape, 0)
    col = lanes_of(scores.shape)
    allowed = (col <= start + row % ROWB) & (col < length)
    return scores, allowed


def attend_kernel(scalars, query, key, value, result, lse):
    half = pl.program_id(0) % 2
    length = scalars[0]
    keys = both_halves(key[...], half)
    values = both_halves(value[...], half)
    rows = query.shape[0]
    for start in range(0, rows, ROWB):
        count = start + ROWB
        stacked = stacked_heads(query[start:count, :])
        scores, allowed = masked_scores(length, stacked, keys[:count], start, count)
        scores = jnp.where(allowed, scores, -1e30)
        top = jnp.max(scores, -1, keepdims=True)
        shifted = jnp.exp(scores - top)
        total = jnp.sum(shifted, -1, keepdims=True)
        prob = (shifted * (1.0 / total)).astype(bf16)
        mixed = nn(prob, values[:count])
        lane = lanes_of((ROWB, 128))
        result[start:count, :] = jnp.where(lane < HS, mixed[:ROWB], mixed[ROWB:]).astype(bf16)
        logs = top + jnp.log(total)
        lse[0, start:count, :] = jnp.concatenate([logs[:ROWB], logs[ROWB:]], 1)


def attend(length, qkv):
    rows = qkv.shape[0]
    pairs = KVH
    return pl.pallas_call(
        attend_kernel,
        grid_spec=pltpu.PrefetchScalarGridSpec(
            num_scalar_prefetch=1,
            grid=(pairs,),
            in_specs=[
                pl.BlockSpec((rows, 128), lambda g, s: (0, g)),
                pl.BlockSpec((rows, 128), lambda g, s: (0, QD // 128 + g // 2)),
                pl.BlockSpec((rows, 128), lambda g, s: (0, (QD + KD) // 128 + g // 2)),
            ],
            out_specs=[
                pl.BlockSpec((rows, 128), lambda g, s: (0, g)),
                pl.BlockSpec((1, rows, 2), lambda g, s: (g, 0, 0)),
            ],
        ),
        out_shape=[
            jax.ShapeDtypeStruct((rows, QD), bf16),
            jax.ShapeDtypeStruct((pairs, rows, 2), f32),
        ],
        compiler_params=params_of(1),
        name="attend",
        cost_estimate=pl.CostEstimate(
            flops=8 * rows * rows * QD, transcendentals=rows * rows * HQ, bytes_accessed=4 << 20
        ),
    )(length, qkv, qkv, qkv)


def attend_back_kernel(
    scalars, query, key, value, grad, lse, cos, sin, grad_query, grad_key, grad_value, key_acc, value_acc
):
    half = pl.program_id(0) % 2
    length = scalars[0]
    keys = both_halves(key[...], half)
    values = both_halves(value[...], half)
    rows = query.shape[0]
    key_acc[...] = jnp.zeros_like(key_acc)
    value_acc[...] = jnp.zeros_like(value_acc)
    for start in range(0, rows, ROWB):
        count = start + ROWB
        stacked = stacked_heads(query[start:count, :])
        grads = stacked_heads(grad[start:count, :])
        scores, allowed = masked_scores(length, stacked, keys[:count], start, count)
        logs = lse[0, start:count, :]
        logs = jnp.concatenate([logs[:, 0:1], logs[:, 1:2]], 0)
        prob = jnp.where(allowed, jnp.exp(scores - logs), 0.0)
        grad_prob = nt(grads, values[:count])
        delta = jnp.sum(prob * grad_prob, -1, keepdims=True)
        grad_score = (prob * (grad_prob - delta)).astype(bf16)
        mixed = nn(grad_score, keys[:count])
        lane = lanes_of((ROWB, 128))
        turned = 0.125 * jnp.where(lane < HS, mixed[:ROWB], mixed[ROWB:])
        turned = turned * cos[start:count, :] - rope_swap(turned) * sin[start:count, :]
        grad_query[start:count, :] = turned.astype(bf16)
        key_acc[:count, :] += tn(grad_score, stacked)
        value_acc[:count, :] += tn(prob.astype(bf16), grads)
    total = key_acc[...]
    total = 0.125 * (total + pltpu.roll(total, HS, 1))
    total = (total * cos[...] - rope_swap(total) * sin[...]).astype(bf16)
    other = value_acc[...]
    other = (other + pltpu.roll(other, HS, 1)).astype(bf16)

    @pl.when(half == 0)
    def _():
        grad_key[...] = total
        grad_value[...] = other

    @pl.when(half == 1)
    def _():
        low_half = lanes_of(total.shape) < HS
        grad_key[...] = jnp.where(low_half, grad_key[...], total)
        grad_value[...] = jnp.where(low_half, grad_value[...], other)


def attend_back(length, qkv, grad, lse, cos, sin):
    rows = qkv.shape[0]
    pairs = KVH
    return pl.pallas_call(
        attend_back_kernel,
        grid_spec=pltpu.PrefetchScalarGridSpec(
            num_scalar_prefetch=1,
            grid=(pairs,),
            in_specs=[
                pl.BlockSpec((rows, 128), lambda g, s: (0, g)),
                pl.BlockSpec((rows, 128), lambda g, s: (0, QD // 128 + g // 2)),
                pl.BlockSpec((rows, 128), lambda g, s: (0, (QD + KD) // 128 + g // 2)),
                pl.BlockSpec((rows, 128), lambda g, s: (0, g)),
                pl.BlockSpec((1, rows, 2), lambda g, s: (g, 0, 0)),
                pl.BlockSpec((rows, 128), lambda g, s: (0, 0)),
                pl.BlockSpec((rows, 128), lambda g, s: (0, 0)),
            ],
            out_specs=[
                pl.BlockSpec((rows, 128), lambda g, s: (0, g)),
                pl.BlockSpec((rows, 128), lambda g, s: (0, g // 2)),
                pl.BlockSpec((rows, 128), lambda g, s: (0, g // 2)),
            ],
            scratch_shapes=[pltpu.VMEM((rows, 128), f32), pltpu.VMEM((rows, 128), f32)],
        ),
        out_shape=[
            jax.ShapeDtypeStruct((rows, QD), bf16),
            jax.ShapeDtypeStruct((rows, KD), bf16),
            jax.ShapeDtypeStruct((rows, KD), bf16),
        ],
        compiler_params=params_of(1),
        name="attend_back",
        cost_estimate=pl.CostEstimate(
            flops=20 * rows * rows * QD, transcendentals=rows * rows * HQ, bytes_accessed=8 << 20
        ),
    )(length, qkv, qkv, qkv, grad, lse, cos, sin)


def close_kernel(order, att, hid, gain, weight_a, weight_b, low_map, up_map, mid, normed, low):
    low_value = nt(att[...], low_map[...]).astype(bf16)
    low[...] = low_value
    turned = jnp.concatenate([att[:, column(order, at)] for at in range(BLOCKS)], 1)
    stream = hid[...].astype(f32) + (
        nn(turned[:, :HALF], weight_a[...])
        + nn(turned[:, HALF:], weight_b[...])
        + nn(low_value, up_map[...])
    )
    mid[...] = stream
    normed[...] = (stream * row_scale(stream) * gain[...].astype(f32)).astype(bf16)


def close_mixer(order, att, hidden, gain, weights, low_map, up_map):
    rows = hidden.shape[0]
    block = 256
    ranks = low_map.shape[0]
    full = lambda shape: pl.BlockSpec(shape, lambda n, s: (0, 0))
    part = lambda width: pl.BlockSpec((block, width), lambda n, s: (n, 0))
    return pl.pallas_call(
        close_kernel,
        grid_spec=pltpu.PrefetchScalarGridSpec(
            num_scalar_prefetch=1,
            grid=(rows // block,),
            in_specs=[
                part(QD),
                part(MODEL_WIDTH),
                full((1, MODEL_WIDTH)),
                full((HALF, MODEL_WIDTH)),
                full((HALF, MODEL_WIDTH)),
                full((ranks, QD)),
                full((ranks, MODEL_WIDTH)),
            ],
            out_specs=[part(MODEL_WIDTH), part(MODEL_WIDTH), part(ranks)],
        ),
        out_shape=[
            jax.ShapeDtypeStruct((rows, MODEL_WIDTH), f32),
            jax.ShapeDtypeStruct((rows, MODEL_WIDTH), bf16),
            jax.ShapeDtypeStruct((rows, ranks), bf16),
        ],
        compiler_params=params_of(1),
        name="close_mixer",
        cost_estimate=pl.CostEstimate(
            flops=2 * rows * QD * MODEL_WIDTH, transcendentals=0, bytes_accessed=8 << 20
        ),
    )(order, att, hidden, gain, *weights, low_map, up_map)


def side_by_side(left, right):
    values = []
    for at in range(BLOCKS):
        tile = slice(at // 2 * BLOCK, (at // 2 + 1) * BLOCK)
        low_half = lanes_of((R, BLOCK)) < BLOCK // 2
        if at % 2 == 0:
            value = jnp.where(low_half, left[:, tile], pltpu.roll(right[:, tile], BLOCK // 2, 1))
        else:
            value = jnp.where(low_half, pltpu.roll(left[:, tile], BLOCK // 2, 1), right[:, tile])
        values.append(value.astype(bf16))
    return values


def expert_kernel(
    scalars,
    x,
    cot,
    routes,
    router,
    w_in,
    w_down,
    a_in,
    b_in,
    a_down,
    b_down,
    *rest,
):
    (
        sums_out,
        gates_out,
        packed,
        gates,
        gate_sums,
        low_in,
        low_in_turned,
        b_in_all,
        back_low,
        gated_low,
        back_in,
        acts,
        grads,
        low_grads,
        down_acc,
        out_acc,
        grad_acc,
    ) = rest[-17:]
    expert = pl.program_id(0)
    last = pl.num_programs(0) - 1
    rows = x.shape[0]
    block = rows
    local = a_in.shape[0]
    a_in_all = a_in[...].reshape(local * 2 * R, MODEL_WIDTH)
    a_down_all = a_down[...].reshape(local * R, H)
    b_down_all = b_down[...].reshape(local * R, MODEL_WIDTH)

    @pl.when(expert == 0)
    def _():
        logits = nt(x[...], router[...])
        lane = lanes_of(logits.shape)
        chosen = lane == routes[:, 0:1]
        for k in range(1, TOP):
            chosen = chosen | (lane == routes[:, k : k + 1])
        top = jnp.max(jnp.where(chosen, logits, -1e30), -1, keepdims=True)
        shifted = jnp.where(chosen, jnp.exp(jnp.where(chosen, logits - top, 0.0)), 0.0)
        weights = shifted / jnp.sum(shifted, -1, keepdims=True)
        gates[...] = weights
        gates_out[...] = weights.T[: gates_out.shape[0], :]
        low = nt(x[...], a_in_all)
        low_in[...] = low.astype(bf16)
        low_in_turned[...] = low.T.astype(bf16)
        back_low[...] = nt(cot[...], b_down_all)
        b_in_all[...] = jnp.zeros_like(b_in_all)
        for e in range(local):
            b_in_all[e * 2 * R : e * 2 * R + R, :H] = b_in[e, 0, 0]
            b_in_all[e * 2 * R + R : (e + 1) * 2 * R, H:] = b_in[e, 0, 1]
        gate_sums[...] = jnp.zeros_like(gate_sums)
        gated_low[...] = jnp.zeros_like(gated_low)
        back_in[...] = jnp.zeros_like(back_in)
        out_acc[...] = jnp.zeros_like(out_acc)
        grad_acc[...] = jnp.zeros_like(grad_acc)
        down_acc[...] = jnp.zeros_like(down_acc)

    def row_step(index, carry):
        at = pl.ds(pl.multiple_of(index * block, block), block)
        lane_in = lanes_of((block, local * 2 * R))
        lane_down = lanes_of((block, local * R))
        in_mine = (lane_in >= expert * 2 * R) & (lane_in < (expert + 1) * 2 * R)
        down_mine = (lane_down >= expert * R) & (lane_down < (expert + 1) * R)
        gate_all = gates[at, :]
        gate_lane = lanes_of(gate_all.shape) == expert
        weight = jnp.sum(jnp.where(gate_lane, gate_all, 0.0), -1, keepdims=True)
        mine = low_in[at, :]
        mine = jnp.where(in_mine, mine, jnp.zeros_like(mine))
        both = nn(x[at, :], w_in[0]) + nn(mine, b_in_all[...])
        gate = both[:, :H]
        upper = both[:, H:]
        sigmoid = jax.nn.sigmoid(gate)
        silu = gate * sigmoid
        act = (silu * upper).astype(bf16)
        acts[at, :] = act
        act_wide = act.astype(f32)
        low = jnp.where(down_mine, nt(act, a_down_all), 0.0).astype(bf16).astype(f32)
        plain = nt(cot[at, :], w_down[0])
        low_plain = back_low[at, :]
        dots = jnp.sum(act_wide * plain, -1, keepdims=True) + jnp.sum(
            low * low_plain, -1, keepdims=True
        )
        sum_lane = lanes_of(gate_all.shape) == expert + scalars[2]
        gate_sums[at, :] += jnp.where(sum_lane, dots, 0.0)
        low_grad = jnp.where(down_mine, weight * low_plain, 0.0).astype(bf16)
        low_grads[at, :] = low_grad
        grad_act = weight * plain + nn(low_grad, a_down_all)
        grad_first = grad_act * upper * sigmoid * (1.0 + gate * (1.0 - sigmoid))
        grad_second = grad_act * silu
        grad_both = jnp.concatenate(
            [grad_first.astype(bf16), grad_second.astype(bf16)], 1
        )
        grads[at, :] = grad_both
        gated_low[at, :] += (weight * low).astype(bf16)
        out_acc[at, :] += nn((weight * act_wide).astype(bf16), w_down[0])
        grad_acc[at, :] += nt(grad_both, w_in[0])
        low_back = jnp.where(in_mine, nt(grad_both, b_in_all[...]), 0.0)
        back_in[at, :] += low_back.astype(bf16)
        return carry

    lax.fori_loop(0, rows // block, row_step, 0)

    turned = low_in_turned[pl.ds(pl.multiple_of(expert * 2 * R, 2 * R), 2 * R), :]
    product = nn(turned, grads[...])
    first_b_in = local * 3 * R
    here = pl.ds(pl.multiple_of(first_b_in + expert * R, R), R)
    for at, value in enumerate(side_by_side(product[:R, :H], product[R:, H:])):
        packed[at, 0, here, :] = value
    down_acc[...] += tn(low_grads[...], acts[...])

    @pl.when(expert == last)
    def _():
        sums_out[:rows, :] = (grad_acc[...] + nn(back_in[...], a_in_all)).astype(bf16)
        experts = gates_out.shape[0]
        sums = gate_sums[...].T[:experts, :]
        sums = jnp.concatenate([sums[: experts // 2], sums[experts // 2 :]], 1)
        high = sums.astype(bf16).astype(f32)
        edge = rows + experts
        sums_out[rows:edge, :] = jnp.concatenate([high, sums - high], 0).astype(bf16)
        sums_out[edge:, :] = (out_acc[...] + nn(gated_low[...], b_down_all)).astype(bf16)
        wide = tn(back_in[...], x[...]).astype(bf16)
        tall = tn(gated_low[...], cot[...]).astype(bf16)
        for at in range(BLOCKS):
            columns = slice(at * BLOCK, (at + 1) * BLOCK)
            packed[at, 0, : local * 2 * R, :] = wide[:, columns]
            packed[at, 0, local * 2 * R : first_b_in, :] = tall[:, columns]
        for pair in range(local // 2):
            lower = down_acc[pair * 2 * R : pair * 2 * R + R, :]
            upper = down_acc[pair * 2 * R + R : (pair + 1) * 2 * R, :]
            row = local * 4 * R + pair * R
            for at, value in enumerate(side_by_side(lower, upper)):
                packed[at, 0, row : row + R, :] = value


def run_experts(
    scalars, x, cot, routes, router, w_in, w_down, a_in, b_in, a_down, b_down, experts, slots, packed
):
    rows = x.shape[0]
    local = w_in.shape[0]
    ranks_in = local * 2 * R
    ranks_down = local * R
    height = local * 9 * R // 2
    kept = [] if packed is None else [packed]
    full = lambda shape: pl.BlockSpec(shape, lambda e, s: (0,) * len(shape))
    return pl.pallas_call(
        expert_kernel,
        grid_spec=pltpu.PrefetchScalarGridSpec(
            num_scalar_prefetch=1,
            grid=(local,),
            in_specs=[
                full((rows, MODEL_WIDTH)),
                pl.BlockSpec((rows, MODEL_WIDTH), lambda e, s: (s[4], 0)),
                pl.BlockSpec((rows, TOP), lambda e, s: (s[0], 0)),
                full((128, MODEL_WIDTH)),
                pl.BlockSpec((1, MODEL_WIDTH, 2 * H), lambda e, s: (e, 0, 0)),
                pl.BlockSpec((1, H, MODEL_WIDTH), lambda e, s: (e, 0, 0)),
                pl.BlockSpec((local, 1, 2 * R, MODEL_WIDTH), lambda e, s: (0, s[1], 0, 0)),
                pl.BlockSpec((local, 1, 2, R, H), lambda e, s: (0, s[1], 0, 0, 0)),
                pl.BlockSpec((local, 1, R, H), lambda e, s: (0, s[1], 0, 0)),
                pl.BlockSpec((local, 1, R, MODEL_WIDTH), lambda e, s: (0, s[1], 0, 0)),
            ]
            + [pl.BlockSpec(memory_space=pl.ANY)] * len(kept),
            out_specs=[
                full((2 * rows + experts, MODEL_WIDTH)),
                full((experts, rows)),
                pl.BlockSpec((BLOCKS, 1, height, BLOCK), lambda e, s: (0, s[3], 0, 0)),
            ],
            scratch_shapes=[
                pltpu.VMEM((rows, 128), f32),
                pltpu.VMEM((rows, 128), f32),
                pltpu.VMEM((rows, ranks_in), bf16),
                pltpu.VMEM((ranks_in, rows), bf16),
                pltpu.VMEM((ranks_in, 2 * H), bf16),
                pltpu.VMEM((rows, ranks_down), f32),
                pltpu.VMEM((rows, ranks_down), bf16),
                pltpu.VMEM((rows, ranks_in), bf16),
                pltpu.VMEM((rows, H), bf16),
                pltpu.VMEM((rows, 2 * H), bf16),
                pltpu.VMEM((rows, ranks_down), bf16),
                pltpu.VMEM((ranks_down, H), f32),
                pltpu.VMEM((rows, MODEL_WIDTH), f32),
                pltpu.VMEM((rows, MODEL_WIDTH), f32),
            ],
        ),
        out_shape=[
            jax.ShapeDtypeStruct((2 * rows + experts, MODEL_WIDTH), bf16),
            jax.ShapeDtypeStruct((experts, rows), f32),
            jax.ShapeDtypeStruct((BLOCKS, slots, height, BLOCK), bf16),
        ],
        input_output_aliases={11: 2} if kept else {},
        compiler_params=params_of(1),
        name="experts",
        cost_estimate=pl.CostEstimate(
            flops=local * rows * 9 * (1 << 20),
            transcendentals=local * rows * H,
            bytes_accessed=20 << 20,
        ),
    )(scalars, x, cot, routes, router, w_in, w_down, a_in, b_in, a_down, b_down, *kept)


def open_back_kernel(count, order, cot, mid, gain, gates, router, weight_a, weight_b, low_map, up_map, low, att, *rest):
    parts = rest[:count]
    sums = rest[count : 3 * count]
    grad_mid, grad_att, grad_up, grad_low, columns = rest[3 * count :]
    gate_value = gates[...]
    half = gate_value.shape[0] // 2
    sides = []
    for side in range(2):
        value = None
        for at in range(count):
            pair = sums[2 * at + side][...].astype(f32)
            pair = pair[:half] + pair[half:]
            value = pair if value is None else value + pair
        sides.append(value)
    gate_grad = jnp.concatenate(sides, 0)
    logit = gate_value * (gate_grad - jnp.sum(gate_value * gate_grad, 0, keepdims=True))
    first = logit.astype(bf16)
    left = logit - first.astype(f32)
    second = left.astype(bf16)
    third = (left - second.astype(f32)).astype(bf16)
    grad = tn(first, router[...]) + (tn(second, router[...]) + tn(third, router[...]))
    for piece in parts:
        grad = grad + piece[...].astype(f32)
    total = cot[...].astype(f32) + norm_back(mid[...], gain[...].astype(f32), grad)
    grad_mid[...] = total
    branch = total.astype(bf16)
    low_grad = nt(branch, up_map[...]).astype(bf16)
    columns[...] = nn(low_grad, low_map[...])
    for side, weight in enumerate((weight_a, weight_b)):
        value = nt(branch, weight[...])
        for at in range(BLOCKS // 2):
            columns[:, column(order, side * BLOCKS // 2 + at)] += value[:, at * BLOCK : (at + 1) * BLOCK]
    grad_att[...] = columns[...].astype(bf16)
    up_part = tn(low[...], branch)
    low_part = tn(low_grad, att[...])

    @pl.when(pl.program_id(0) == 0)
    def _():
        grad_up[...] = up_part
        grad_low[...] = low_part

    @pl.when(pl.program_id(0) > 0)
    def _():
        grad_up[...] += up_part
        grad_low[...] += low_part


def open_back(order, cot, mid, gain, gates, router, weights, low_map, up_map, low, att, parts):
    rows = cot.shape[0]
    block = 256
    ranks = low_map.shape[0]
    experts = gates.shape[0]
    full = lambda shape: pl.BlockSpec(shape, lambda n, s: (0, 0))
    part = lambda width: pl.BlockSpec((block, width), lambda n, s: (n, 0))
    count = len(parts)
    below = rows // experts
    sums = [
        pl.BlockSpec((experts, block), lambda n, s: (below, n)),
        pl.BlockSpec((experts, block), lambda n, s: (below, rows // block + n)),
    ]

    def body(*refs):
        open_back_kernel(count, *refs)

    return pl.pallas_call(
        body,
        grid_spec=pltpu.PrefetchScalarGridSpec(
            num_scalar_prefetch=1,
            grid=(rows // block,),
            in_specs=[
                part(MODEL_WIDTH),
                part(MODEL_WIDTH),
                full((1, MODEL_WIDTH)),
                pl.BlockSpec((experts, block), lambda n, s: (0, n)),
                full((experts, MODEL_WIDTH)),
                full((HALF, MODEL_WIDTH)),
                full((HALF, MODEL_WIDTH)),
                full((ranks, QD)),
                full((ranks, MODEL_WIDTH)),
                part(ranks),
                part(QD),
            ]
            + [part(MODEL_WIDTH)] * count
            + sums * count,
            out_specs=[
                part(MODEL_WIDTH),
                part(QD),
                full((ranks, MODEL_WIDTH)),
                full((ranks, QD)),
            ],
            scratch_shapes=[pltpu.VMEM((block, QD), f32)],
        ),
        out_shape=[
            jax.ShapeDtypeStruct((rows, MODEL_WIDTH), f32),
            jax.ShapeDtypeStruct((rows, QD), bf16),
            jax.ShapeDtypeStruct((ranks, MODEL_WIDTH), f32),
            jax.ShapeDtypeStruct((ranks, QD), f32),
        ],
        compiler_params=params_of(1),
        name="open_back",
        cost_estimate=pl.CostEstimate(
            flops=2 * rows * QD * MODEL_WIDTH, transcendentals=0, bytes_accessed=14 << 20
        ),
    )(
        order, cot, mid, gain, gates, router, *weights, low_map, up_map, low, att, *parts,
        *[piece for piece in parts for _ in range(2)],
    )


def adapters_back_kernel(
    grad_query, grad_key, grad_value, low, normed, up_map, low_there, up_there, low_out, *results
):
    pieces = (grad_query, grad_key, grad_value)
    bounds = (0, QD, QD + KD, QKV)
    back = None
    ups = []
    for at in range(3):
        block = pieces[at][...]
        ups.append(tn(low[...], block)[at * R : (at + 1) * R])
        part = nt(block, up_map[:, bounds[at] : bounds[at + 1]])
        back = part if back is None else back + part
    value = back.astype(bf16)
    low_out[...] = value
    lows = tn(value, normed[...]) + low_there[...]
    if len(results) == 2:
        grad_up, grad_low = results
        grad_low[...] = lows
        for at in range(3):
            grad_up[:, bounds[at] : bounds[at + 1]] = ups[at]
        return
    (packed,) = results
    grad_up = jnp.concatenate(ups, 1)
    grad_out = up_there[3 * R :, :]
    small = BLOCK // 4
    lane = lanes_of((R, BLOCK))
    for owner in range(packed.shape[0]):
        tile = slice(owner // 4 * BLOCK, (owner // 4 + 1) * BLOCK)
        offset = owner % 4 * small
        first = jnp.zeros((R, BLOCK), f32)
        for at in range(4):
            piece = lows[at * R : (at + 1) * R, tile]
            shift = (at * small - offset) % BLOCK
            piece = pltpu.roll(piece, shift, 1) if shift else piece
            first = jnp.where((lane >= at * small) & (lane < (at + 1) * small), piece, first)
        piece = grad_up[:, owner // 2 * BLOCK : (owner // 2 + 1) * BLOCK]
        piece = pltpu.roll(piece, BLOCK // 2, 1) if owner % 2 else piece
        other = grad_out[:, tile]
        shift = (2 * small - offset) % BLOCK
        other = pltpu.roll(other, shift, 1) if shift else other
        packed[owner, :, :BLOCK] = first
        packed[owner, :, BLOCK:] = jnp.where(
            lane < 2 * small, piece, jnp.where(lane < 3 * small, other, 0.0)
        )


def adapters_back(grad_query, grad_key, grad_value, low, normed, up_map, low_there, up_there, devices):
    rows = normed.shape[0]
    ranks = up_map.shape[0]
    if devices * BLOCK // 4 == MODEL_WIDTH:
        results = [jax.ShapeDtypeStruct((devices, R, 2 * BLOCK), f32)]
    else:
        results = [
            jax.ShapeDtypeStruct((R, QKV), f32),
            jax.ShapeDtypeStruct((ranks, MODEL_WIDTH), f32),
        ]
    back_low, *results = pl.pallas_call(
        adapters_back_kernel,
        out_shape=[jax.ShapeDtypeStruct((rows, ranks), bf16)] + results,
        compiler_params=pltpu.CompilerParams(vmem_limit_bytes=56 * 1024 * 1024),
        name="adapters_back",
        cost_estimate=pl.CostEstimate(
            flops=6 * rows * 256 * QKV, transcendentals=0, bytes_accessed=4 << 20
        ),
    )(grad_query, grad_key, grad_value, low, normed, up_map, low_there, up_there)
    if len(results) == 1:
        return results[0], back_low
    grad_up, grad_low = results
    small = MODEL_WIDTH // devices
    packed = jnp.concatenate(
        [
            grad_low.reshape(4, R, devices, small).transpose(2, 1, 0, 3).reshape(devices, R, 4 * small),
            grad_up.reshape(R, devices, 2 * small).transpose(1, 0, 2),
            up_there[3 * R :].reshape(R, devices, small).transpose(1, 0, 2),
            jnp.zeros((devices, R, small), f32),
        ],
        -1,
    )
    return packed, back_low


def input_back_kernel(
    order, grad_query, grad_key, grad_value, low, weight_a, weight_b, low_map, hid, gain, mid, grad, columns
):
    columns[...] = nn(low[...], low_map[...])
    for side, weight in enumerate((weight_a, weight_b)):
        value = nt(grad_query[...], weight[:, :QD])
        value = value + nt(grad_key[...], weight[:, QD : QD + KD])
        value = value + nt(grad_value[...], weight[:, QD + KD :])
        for at in range(BLOCKS // 2):
            columns[:, column(order, side * BLOCKS // 2 + at)] += value[:, at * BLOCK : (at + 1) * BLOCK]
    rows = hid[...].astype(f32)
    grad[...] = (mid[...] + norm_back(rows, gain[...].astype(f32), columns[...])).astype(bf16)


def input_back(order, grad_query, grad_key, grad_value, low, weights, low_map, hidden, gain, mid):
    rows = hidden.shape[0]
    block = 256
    ranks = low_map.shape[0]
    full = lambda shape: pl.BlockSpec(shape, lambda n, s: (0, 0))
    part = lambda width: pl.BlockSpec((block, width), lambda n, s: (n, 0))
    return pl.pallas_call(
        input_back_kernel,
        grid_spec=pltpu.PrefetchScalarGridSpec(
            num_scalar_prefetch=1,
            grid=(rows // block,),
            in_specs=[
                part(QD),
                part(KD),
                part(KD),
                part(ranks),
                full((HALF, QKV)),
                full((HALF, QKV)),
                full((ranks, MODEL_WIDTH)),
                part(MODEL_WIDTH),
                full((1, MODEL_WIDTH)),
                part(MODEL_WIDTH),
            ],
            out_specs=part(MODEL_WIDTH),
            scratch_shapes=[pltpu.VMEM((block, MODEL_WIDTH), f32)],
        ),
        out_shape=jax.ShapeDtypeStruct((rows, MODEL_WIDTH), bf16),
        compiler_params=params_of(1),
        name="input_back",
        cost_estimate=pl.CostEstimate(
            flops=2 * rows * QKV * MODEL_WIDTH, transcendentals=0, bytes_accessed=12 << 20
        ),
    )(order, grad_query, grad_key, grad_value, low, *weights, low_map, hidden, gain, mid)


def sum_experts_kernel(ids, pieces, a_in, b_in, a_down, b_down, acc):
    local = a_in.shape[0]
    small = a_down.shape[-1]
    acc[...] = jnp.zeros_like(acc)

    def step(index, carry):
        acc[ids[index]] += pieces[index].astype(f32)
        return carry

    lax.fori_loop(0, pieces.shape[0], step, 0)
    for e in range(local):
        a_in[e] = acc[:, e * 2 * R : (e + 1) * 2 * R, :]
        at = local * 2 * R + e * R
        b_down[e] = acc[:, at : at + R, :]
        at = local * 3 * R + e * R
        both = acc[:, at : at + R, :]
        b_in[e, :, 0] = both[:, :, :small]
        b_in[e, :, 1] = both[:, :, small:]
        at = local * 4 * R + e // 2 * R
        a_down[e] = acc[:, at : at + R, e % 2 * small : (e % 2 + 1) * small]


def sum_experts(ids, pieces, local):
    height = pieces.shape[1]
    lanes = pieces.shape[2]
    small = lanes // 2
    vmem = pl.BlockSpec(memory_space=pltpu.VMEM)
    return pl.pallas_call(
        sum_experts_kernel,
        in_specs=[pl.BlockSpec(memory_space=pltpu.SMEM), vmem],
        out_specs=[vmem, vmem, vmem, vmem],
        out_shape=[
            jax.ShapeDtypeStruct((local, NA, 2 * R, lanes), f32),
            jax.ShapeDtypeStruct((local, NA, 2, R, small), f32),
            jax.ShapeDtypeStruct((local, NA, R, small), f32),
            jax.ShapeDtypeStruct((local, NA, R, lanes), f32),
        ],
        scratch_shapes=[pltpu.VMEM((NA, height, lanes), f32)],
        compiler_params=pltpu.CompilerParams(vmem_limit_bytes=56 * 1024 * 1024),
        name="sum_experts",
    )(ids, pieces)


def sum_mixer_kernel(ids, pieces, grad_low, grad_up, grad_out, acc):
    width = grad_low.shape[-1]
    acc[...] = jnp.zeros_like(acc)

    def step(index, carry):
        acc[ids[index]] += pieces[index]
        return carry

    lax.fori_loop(0, pieces.shape[0], step, 0)
    total = acc[...]
    for at in range(4):
        grad_low[at] = total[:, :, at * width : (at + 1) * width]
    grad_up[...] = total[:, :, 4 * width : 6 * width]
    grad_out[...] = total[:, :, 6 * width : 7 * width]


def sum_mixer(ids, pieces):
    width = pieces.shape[2] // 8
    vmem = pl.BlockSpec(memory_space=pltpu.VMEM)
    return pl.pallas_call(
        sum_mixer_kernel,
        in_specs=[pl.BlockSpec(memory_space=pltpu.SMEM), vmem],
        out_specs=[vmem, vmem, vmem],
        out_shape=[
            jax.ShapeDtypeStruct((4, NA, R, width), f32),
            jax.ShapeDtypeStruct((NA, R, 2 * width), f32),
            jax.ShapeDtypeStruct((NA, R, width), f32),
        ],
        scratch_shapes=[pltpu.VMEM((NA, R, 8 * width), f32)],
        compiler_params=pltpu.CompilerParams(vmem_limit_bytes=56 * 1024 * 1024),
        name="sum_mixer",
    )(ids, pieces)


def rope_tables(rows):
    half = HS // 2
    frequency = (10000.0 ** (-2.0 * np.arange(half, dtype=np.float32) / HS)).astype(np.float32)
    angles = np.arange(rows, dtype=np.float32)[:, None] * frequency[None, :]
    cos = np.cos(angles.astype(np.float64)).astype(np.float32)
    sin = np.sin(angles.astype(np.float64)).astype(np.float32)
    return (
        jnp.asarray(np.concatenate([cos, cos, cos, cos], 1)),
        jnp.asarray(np.concatenate([-sin, sin, -sin, sin], 1)),
    )


def swap(value, bit):
    return lax.ppermute(value, "dp", [(at, at ^ bit) for at in range(BLOCKS)])


def both_neighbours(weight):
    return swap(weight, 2), swap(weight, 4)


def across(pair):
    one, two = pair
    middle = one.shape[0] // 2
    return swap(two[:middle], 2), swap(one[middle:], 4)


def tied(value, *others):
    return lax.optimization_barrier((value, *others))[0]


def order_of(row):
    if lax.axis_size("dp") != BLOCKS:
        return jnp.arange(BLOCKS, dtype=jnp.int32)
    return row.astype(jnp.int32) ^ jnp.array([0, 2, 4, 6, 1, 3, 5, 7], jnp.int32)


def to_owners(packed, owners, local):
    split = owners // BLOCKS
    if split == 1:
        return packed
    slots = packed.shape[1]
    edge = local * 3 * R
    wide = packed[:, :, :edge].reshape(BLOCKS, slots, edge, split, BLOCK // split)
    wide = wide.transpose(0, 3, 1, 2, 4).reshape(owners, slots, edge, BLOCK // split)
    rest = packed.shape[2] - edge
    narrow = packed[:, :, edge:].reshape(BLOCKS, slots, rest, 2, split, BLOCK // 2 // split)
    narrow = narrow.transpose(0, 4, 1, 2, 3, 5).reshape(owners, slots, rest, BLOCK // split)
    return jnp.concatenate([wide, narrow], 2)


def joined(left, right):
    return (left.astype(f32) + right.astype(f32)).astype(bf16)


def on_device(
    hidden,
    cotangent,
    lengths,
    adapter_ids,
    routes,
    attn_gain,
    ffn_gain,
    query_key_value_weight,
    w_out,
    w_router,
    w_gate_up,
    w_down,
    attention_lowmap,
    attention_query_key_value_upmap,
    attention_output_upmap,
    expert_gate_up_lowmap,
    expert_gate_up_upmap,
    expert_down_lowmap,
    expert_down_upmap,
):
    groups = lax.axis_size("expert")
    owners = lax.axis_size("dp")
    place = lax.axis_index("expert")
    row = lax.axis_index("dp")
    devices = groups * owners
    sequence = row * groups + place
    rows = hidden.shape[0]
    experts = w_router.shape[1]
    local = w_gate_up.shape[0]
    width = MODEL_WIDTH // owners
    attn_gain = attn_gain.reshape(1, MODEL_WIDTH)
    ffn_gain = ffn_gain.reshape(1, MODEL_WIDTH)
    length = lax.dynamic_slice(lengths, (sequence,), (1,))
    forward = [(at, (at + 1) % groups) for at in range(groups)]
    backward = [(at, (at - 1) % groups) for at in range(groups)]

    mine = lax.dynamic_slice(adapter_ids.reshape(owners, groups), (0, place), (owners, 1))[:, 0]
    low_turned = attention_lowmap.transpose(1, 0, 3, 2).reshape(NA, 4 * R, width)
    up_turned = (
        attention_query_key_value_upmap.reshape(NA, R, 2, width)
        .transpose(0, 2, 1, 3)
        .reshape(NA, 2 * R, width)
    )
    adapters = jnp.concatenate([low_turned, up_turned, attention_output_upmap], 1)[mine]
    adapters = lax.all_to_all(adapters, "dp", 0, 0, tiled=True)
    order = order_of(row)
    short = owners == BLOCKS
    if short:
        pair_in = both_neighbours(query_key_value_weight)
        pair_out = both_neighbours(tied(w_out, *pair_in))
        near_in = jnp.concatenate([query_key_value_weight, *pair_in, *across(pair_in)], 0)
        weight_in = near_in, swap(near_in, 1)
        across_out = across(tied(pair_out, weight_in[1]))
    else:
        whole = lax.all_gather(query_key_value_weight, "dp", axis=0, tiled=True)
        weight_in = whole[:HALF], whole[HALF:]
        whole = lax.all_gather(w_out, "dp", axis=0, tiled=True)
        weight_out = whole[:HALF], whole[HALF:]

    low_map = adapters[:, : 4 * R].transpose(1, 0, 2).reshape(4 * R, MODEL_WIDTH)
    up = (
        adapters[:, 4 * R : 6 * R]
        .reshape(owners, 2, R, width)
        .transpose(2, 0, 1, 3)
        .reshape(R, QKV)
    )
    up_out = adapters[:, 6 * R :].transpose(1, 0, 2).reshape(R, MODEL_WIDTH)
    column = jnp.arange(QKV, dtype=jnp.int32)
    part = jnp.where(column < QD, 0, jnp.where(column < QD + KD, 1, 2))
    up_map = jnp.where(
        part[None, None, :] == jnp.arange(4, dtype=jnp.int32)[:, None, None], up[None], 0
    ).reshape(4 * R, QKV)
    up_out_map = jnp.concatenate([jnp.zeros((3 * R, MODEL_WIDTH), bf16), up_out], 0)

    cos, sin = rope_tables(rows)

    cots = lax.all_gather(cotangent, "expert", axis=0, tiled=True)

    qkv, low, normed_in = project(order, hidden, attn_gain, weight_in, low_map, up_map, cos, sin)
    if short:
        near_out = jnp.concatenate([w_out, *pair_out, *tied(across_out, low)], 0)
        weight_out = near_out, swap(near_out, 1)
    attended, lse = attend(length, qkv)
    mid, normed_mid, low_out = close_mixer(
        order, attended, hidden, ffn_gain, weight_out, low_map, up_out_map
    )

    first = place * local
    routes_here = (routes - first + experts) % experts
    router = jnp.roll(w_router.T, -first, axis=0)
    router_wide = jnp.concatenate(
        [router, jnp.zeros((128 - experts, MODEL_WIDTH), router.dtype)], 0
    )
    a_in = expert_gate_up_lowmap.transpose(0, 1, 3, 2)
    a_down = expert_down_lowmap.transpose(0, 1, 3, 2)

    offsets = [0, 1] + [groups - 1] * (groups > 2) + list(range(2, groups - 1))
    offset = jnp.array(offsets, jnp.int32)
    source = (place - offset + groups) % groups
    tags = adapter_ids.reshape(owners, groups)[:, source]
    slot = jnp.arange(groups, dtype=jnp.int32)
    table = jnp.stack(
        [
            source,
            lax.dynamic_slice(tags, (row, 0), (1, groups))[0],
            offset * local,
            slot,
            jnp.where(slot == 0, 0, source),
        ],
        1,
    )

    xs = {0: normed_mid, 1: lax.ppermute(normed_mid, "expert", forward)}
    if groups > 2:
        xs[groups - 1] = lax.ppermute(normed_mid, "expert", backward)
    packed = None
    ran = {}
    for at, offset in enumerate(offsets):
        ran[offset], gate_part, packed = run_experts(
            table[at],
            xs[offset],
            cotangent if at == 0 else cots,
            routes_here,
            router_wide,
            w_gate_up,
            w_down,
            a_in,
            expert_gate_up_upmap,
            a_down,
            expert_down_upmap,
            experts,
            groups,
            packed,
        )
        if offset == 0:
            gates = gate_part
            xs[1] = tied(xs[1], gates)
        if 2 <= offset + 2 < groups - 1:
            xs[offset + 2] = lax.ppermute(xs[offset + 1], "expert", forward)

    pieces = lax.all_to_all(to_owners(packed, owners, local), "dp", 0, 0, tiled=True)
    pieces = pieces.reshape(devices, pieces.shape[2], width)
    g_a_in, g_b_in, g_a_down, g_b_down = sum_experts(tags.reshape(devices), pieces, local)

    edge = rows + experts
    both_far = lax.ppermute(ran[1], "expert", forward)
    grad_far, out_far = both_far, both_far[edge:]
    for offset in range(2, groups):
        grad_part = joined(ran[offset][:edge], grad_far[:edge])
        if offset == groups - 1:
            grad_part = tied(grad_part, g_a_down)
        grad_far = lax.ppermute(grad_part, "expert", forward)
    for offset in range(2, groups):
        out_part = joined(ran[offset][edge:], out_far)
        out_far = lax.ppermute(tied(out_part, grad_far), "expert", forward)

    grad_mid, grad_attended, grad_up_out, grad_low_out = open_back(
        order,
        cotangent,
        mid,
        ffn_gain,
        gates,
        router,
        weight_out,
        low_map,
        up_out_map,
        low_out,
        attended,
        [ran[0], grad_far],
    )
    grad_query, grad_key, grad_value = attend_back(length, qkv, grad_attended, lse, cos, sin)
    packed, back_low = adapters_back(
        grad_query, grad_key, grad_value, low, normed_in, up_map, grad_low_out, grad_up_out, devices
    )
    packed = lax.all_to_all(packed, ("dp", "expert"), 0, 0, tiled=True)
    m_a, m_b, m_o = sum_mixer(adapter_ids, packed)

    grad_hidden = input_back(
        order, grad_query, grad_key, grad_value, back_low, weight_in, low_map, hidden, attn_gain, grad_mid
    )
    out = (mid + ran[0][edge:].astype(f32) + out_far.astype(f32)).astype(bf16)
    return (
        out,
        grad_hidden,
        m_a.transpose(0, 1, 3, 2),
        m_b,
        m_o,
        g_a_in.transpose(0, 1, 3, 2),
        g_b_in,
        g_a_down.transpose(0, 1, 3, 2),
        g_b_down,
    )


def solution(mesh):
    in_specs = (
        P(("dp", "expert"), None),
        P(("dp", "expert"), None),
        P(),
        P(),
        P("dp", None),
        P(),
        P(),
        P("dp", None),
        P("dp", None),
        P(),
        P("expert", None, None),
        P("expert", None, None),
        P(None, None, "dp", None),
        P(None, None, "dp"),
        P(None, None, "dp"),
        P("expert", None, None, None),
        P("expert", None, None, None, None),
        P("expert", None, None, None),
        P("expert", None, None, None),
    )
    out_specs = (
        P(("dp", "expert"), None),
        P(("dp", "expert"), None),
        P(None, None, ("dp", "expert"), None),
        P(None, None, ("dp", "expert")),
        P(None, None, ("dp", "expert")),
        P("expert", None, "dp", None),
        P("expert", None, None, None, "dp"),
        P("expert", None, "dp", None),
        P("expert", None, None, "dp"),
    )
    return jax.shard_map(
        on_device, mesh=mesh, in_specs=in_specs, out_specs=out_specs, check_vma=False
    )
```

```python
import numpy as np
import jax
import jax.numpy as jnp
from jax import lax
from jax.experimental import pallas as pl
from jax.experimental.pallas import tpu as pltpu
from jax.sharding import PartitionSpec as P

MODEL_WIDTH = 1024
HQ = 16
KVH = 8
HS = 64
H = 512
TOP = 8
R = 16
NA = 8
QD = HQ * HS
KD = KVH * HS
QKV = QD + 2 * KD

epsilon = 1e-06
f32 = jnp.float32
bf16 = jnp.bfloat16


def nn(left, right):
    return lax.dot_general(left, right, (((1,), (0,)), ((), ())), preferred_element_type=f32)


def nt(left, right):
    return lax.dot_general(left, right, (((1,), (1,)), ((), ())), preferred_element_type=f32)


def tn(left, right):
    return lax.dot_general(left, right, (((0,), (0,)), ((), ())), preferred_element_type=f32)


def lanes_of(shape):
    return lax.broadcasted_iota(jnp.int32, shape, len(shape) - 1)


def row_scale(rows):
    return lax.rsqrt(jnp.mean(rows * rows, -1, keepdims=True) + epsilon)


def norm_back(rows, gain, grad):
    scale = row_scale(rows)
    scaled = grad * gain
    return scale * scaled - rows * (scale * scale * scale) * jnp.mean(
        rows * scaled, -1, keepdims=True
    )


def rope_swap(rows):
    width = rows.shape[-1]
    lane = lanes_of(rows.shape)
    return jnp.where(
        lane % HS < HS // 2,
        pltpu.roll(rows, width - HS // 2, 1),
        pltpu.roll(rows, HS // 2, 1),
    )


def both_halves(pair, half):
    rows = pair.astype(f32)
    lane = lanes_of(rows.shape)
    rolled = pltpu.roll(rows, HS, 1)
    keep = (lane < HS) == (half == 0)
    return jnp.where(keep, rows, rolled).astype(bf16)


def stacked_heads(pair):
    lane = lanes_of(pair.shape)
    zero = jnp.zeros_like(pair)
    return jnp.concatenate(
        [jnp.where(lane < HS, pair, zero), jnp.where(lane < HS, zero, pair)], 0
    )


def params_of(count):
    return pltpu.CompilerParams(
        dimension_semantics=("arbitrary",) * count, vmem_limit_bytes=56 * 1024 * 1024
    )


BLOCK = 128
BLOCKS = MODEL_WIDTH // BLOCK
HALF = MODEL_WIDTH // 2


def column(order, at):
    return pl.ds(pl.multiple_of(order[at] * BLOCK, BLOCK), BLOCK)


def project_kernel(
    order, hid, gain, weight_a, weight_b, low_map, up_map, cos, sin, qkv, low, normed, turned_rows
):
    step = pl.program_id(0)
    blocks = pl.num_programs(0)

    @pl.when(step == 0)
    def _():
        rows = hid[...].astype(f32)
        value = (rows * row_scale(rows) * gain[...].astype(f32)).astype(bf16)
        normed[...] = value
        low[...] = nt(value, low_map[...]).astype(bf16)
        for at in range(BLOCKS):
            turned_rows[:, at * BLOCK : (at + 1) * BLOCK] = normed[:, column(order, at)]

    value = (
        nn(turned_rows[:, :HALF], weight_a[...])
        + nn(turned_rows[:, HALF:], weight_b[...])
        + nn(low[...], up_map[...])
    )

    @pl.when(step < blocks * 3 // 4)
    def _():
        for part in range(value.shape[1] // 128):
            piece = value[:, part * 128 : part * 128 + 128]
            turned = piece * cos[...] + rope_swap(piece) * sin[...]
            qkv[:, part * 128 : part * 128 + 128] = turned.astype(bf16)

    @pl.when(step >= blocks * 3 // 4)
    def _():
        qkv[...] = value.astype(bf16)


def project(order, hidden, gain, weights, low_map, up_map, cos, sin):
    rows = hidden.shape[0]
    block = 256
    ranks = low_map.shape[0]
    full = lambda shape: pl.BlockSpec(shape, lambda n, s: (0, 0))
    return pl.pallas_call(
        project_kernel,
        grid_spec=pltpu.PrefetchScalarGridSpec(
            num_scalar_prefetch=1,
            grid=(QKV // block,),
            in_specs=[
                full((rows, MODEL_WIDTH)),
                full((1, MODEL_WIDTH)),
                pl.BlockSpec((HALF, block), lambda n, s: (0, n)),
                pl.BlockSpec((HALF, block), lambda n, s: (0, n)),
                full((ranks, MODEL_WIDTH)),
                pl.BlockSpec((ranks, block), lambda n, s: (0, n)),
                full((rows, 128)),
                full((rows, 128)),
            ],
            out_specs=[
                pl.BlockSpec((rows, block), lambda n, s: (0, n)),
                full((rows, ranks)),
                full((rows, MODEL_WIDTH)),
            ],
            scratch_shapes=[pltpu.VMEM((rows, MODEL_WIDTH), bf16)],
        ),
        out_shape=[
            jax.ShapeDtypeStruct((rows, QKV), bf16),
            jax.ShapeDtypeStruct((rows, ranks), bf16),
            jax.ShapeDtypeStruct((rows, MODEL_WIDTH), bf16),
        ],
        compiler_params=params_of(1),
        name="project",
        cost_estimate=pl.CostEstimate(
            flops=2 * rows * QKV * MODEL_WIDTH, transcendentals=0, bytes_accessed=8 << 20
        ),
    )(order, hidden, gain, *weights, low_map, up_map, cos, sin)


ROWB = 128


def masked_scores(length, queries, keys, start, count):
    scores = 0.125 * nt(queries, keys)
    row = lax.broadcasted_iota(jnp.int32, scores.shape, 0)
    col = lanes_of(scores.shape)
    allowed = (col <= start + row % ROWB) & (col < length)
    return scores, allowed


def attend_kernel(scalars, query, key, value, result, lse):
    half = pl.program_id(0) % 2
    length = scalars[0]
    keys = both_halves(key[...], half)
    values = both_halves(value[...], half)
    rows = query.shape[0]
    for start in range(0, rows, ROWB):
        count = start + ROWB
        stacked = stacked_heads(query[start:count, :])
        scores, allowed = masked_scores(length, stacked, keys[:count], start, count)
        scores = jnp.where(allowed, scores, -1e30)
        top = jnp.max(scores, -1, keepdims=True)
        shifted = jnp.exp(scores - top)
        total = jnp.sum(shifted, -1, keepdims=True)
        prob = (shifted * (1.0 / total)).astype(bf16)
        mixed = nn(prob, values[:count])
        lane = lanes_of((ROWB, 128))
        result[start:count, :] = jnp.where(lane < HS, mixed[:ROWB], mixed[ROWB:]).astype(bf16)
        logs = top + jnp.log(total)
        lse[0, start:count, :] = jnp.concatenate([logs[:ROWB], logs[ROWB:]], 1)


def attend(length, qkv):
    rows = qkv.shape[0]
    pairs = KVH
    return pl.pallas_call(
        attend_kernel,
        grid_spec=pltpu.PrefetchScalarGridSpec(
            num_scalar_prefetch=1,
            grid=(pairs,),
            in_specs=[
                pl.BlockSpec((rows, 128), lambda g, s: (0, g)),
                pl.BlockSpec((rows, 128), lambda g, s: (0, QD // 128 + g // 2)),
                pl.BlockSpec((rows, 128), lambda g, s: (0, (QD + KD) // 128 + g // 2)),
            ],
            out_specs=[
                pl.BlockSpec((rows, 128), lambda g, s: (0, g)),
                pl.BlockSpec((1, rows, 2), lambda g, s: (g, 0, 0)),
            ],
        ),
        out_shape=[
            jax.ShapeDtypeStruct((rows, QD), bf16),
            jax.ShapeDtypeStruct((pairs, rows, 2), f32),
        ],
        compiler_params=params_of(1),
        name="attend",
        cost_estimate=pl.CostEstimate(
            flops=8 * rows * rows * QD, transcendentals=rows * rows * HQ, bytes_accessed=4 << 20
        ),
    )(length, qkv, qkv, qkv)


def attend_back_kernel(
    scalars, query, key, value, grad, lse, cos, sin, grad_query, grad_key, grad_value, key_acc, value_acc
):
    half = pl.program_id(0) % 2
    length = scalars[0]
    keys = both_halves(key[...], half)
    values = both_halves(value[...], half)
    rows = query.shape[0]
    key_acc[...] = jnp.zeros_like(key_acc)
    value_acc[...] = jnp.zeros_like(value_acc)
    for start in range(0, rows, ROWB):
        count = start + ROWB
        stacked = stacked_heads(query[start:count, :])
        grads = stacked_heads(grad[start:count, :])
        scores, allowed = masked_scores(length, stacked, keys[:count], start, count)
        logs = lse[0, start:count, :]
        logs = jnp.concatenate([logs[:, 0:1], logs[:, 1:2]], 0)
        prob = jnp.where(allowed, jnp.exp(scores - logs), 0.0)
        grad_prob = nt(grads, values[:count])
        delta = jnp.sum(prob * grad_prob, -1, keepdims=True)
        grad_score = (prob * (grad_prob - delta)).astype(bf16)
        mixed = nn(grad_score, keys[:count])
        lane = lanes_of((ROWB, 128))
        turned = 0.125 * jnp.where(lane < HS, mixed[:ROWB], mixed[ROWB:])
        turned = turned * cos[start:count, :] - rope_swap(turned) * sin[start:count, :]
        grad_query[start:count, :] = turned.astype(bf16)
        key_acc[:count, :] += tn(grad_score, stacked)
        value_acc[:count, :] += tn(prob.astype(bf16), grads)
    total = key_acc[...]
    total = 0.125 * (total + pltpu.roll(total, HS, 1))
    total = (total * cos[...] - rope_swap(total) * sin[...]).astype(bf16)
    other = value_acc[...]
    other = (other + pltpu.roll(other, HS, 1)).astype(bf16)

    @pl.when(half == 0)
    def _():
        grad_key[...] = total
        grad_value[...] = other

    @pl.when(half == 1)
    def _():
        low_half = lanes_of(total.shape) < HS
        grad_key[...] = jnp.where(low_half, grad_key[...], total)
        grad_value[...] = jnp.where(low_half, grad_value[...], other)


def attend_back(length, qkv, grad, lse, cos, sin):
    rows = qkv.shape[0]
    pairs = KVH
    return pl.pallas_call(
        attend_back_kernel,
        grid_spec=pltpu.PrefetchScalarGridSpec(
            num_scalar_prefetch=1,
            grid=(pairs,),
            in_specs=[
                pl.BlockSpec((rows, 128), lambda g, s: (0, g)),
                pl.BlockSpec((rows, 128), lambda g, s: (0, QD // 128 + g // 2)),
                pl.BlockSpec((rows, 128), lambda g, s: (0, (QD + KD) // 128 + g // 2)),
                pl.BlockSpec((rows, 128), lambda g, s: (0, g)),
                pl.BlockSpec((1, rows, 2), lambda g, s: (g, 0, 0)),
                pl.BlockSpec((rows, 128), lambda g, s: (0, 0)),
                pl.BlockSpec((rows, 128), lambda g, s: (0, 0)),
            ],
            out_specs=[
                pl.BlockSpec((rows, 128), lambda g, s: (0, g)),
                pl.BlockSpec((rows, 128), lambda g, s: (0, g // 2)),
                pl.BlockSpec((rows, 128), lambda g, s: (0, g // 2)),
            ],
            scratch_shapes=[pltpu.VMEM((rows, 128), f32), pltpu.VMEM((rows, 128), f32)],
        ),
        out_shape=[
            jax.ShapeDtypeStruct((rows, QD), bf16),
            jax.ShapeDtypeStruct((rows, KD), bf16),
            jax.ShapeDtypeStruct((rows, KD), bf16),
        ],
        compiler_params=params_of(1),
        name="attend_back",
        cost_estimate=pl.CostEstimate(
            flops=20 * rows * rows * QD, transcendentals=rows * rows * HQ, bytes_accessed=8 << 20
        ),
    )(length, qkv, qkv, qkv, grad, lse, cos, sin)


def close_kernel(order, att, hid, gain, weight_a, weight_b, low_map, up_map, mid, normed, low):
    low_value = nt(att[...], low_map[...]).astype(bf16)
    low[...] = low_value
    turned = jnp.concatenate([att[:, column(order, at)] for at in range(BLOCKS)], 1)
    stream = hid[...].astype(f32) + (
        nn(turned[:, :HALF], weight_a[...])
        + nn(turned[:, HALF:], weight_b[...])
        + nn(low_value, up_map[...])
    )
    mid[...] = stream
    normed[...] = (stream * row_scale(stream) * gain[...].astype(f32)).astype(bf16)


def close_mixer(order, att, hidden, gain, weights, low_map, up_map):
    rows = hidden.shape[0]
    block = 256
    ranks = low_map.shape[0]
    full = lambda shape: pl.BlockSpec(shape, lambda n, s: (0, 0))
    part = lambda width: pl.BlockSpec((block, width), lambda n, s: (n, 0))
    return pl.pallas_call(
        close_kernel,
        grid_spec=pltpu.PrefetchScalarGridSpec(
            num_scalar_prefetch=1,
            grid=(rows // block,),
            in_specs=[
                part(QD),
                part(MODEL_WIDTH),
                full((1, MODEL_WIDTH)),
                full((HALF, MODEL_WIDTH)),
                full((HALF, MODEL_WIDTH)),
                full((ranks, QD)),
                full((ranks, MODEL_WIDTH)),
            ],
            out_specs=[part(MODEL_WIDTH), part(MODEL_WIDTH), part(ranks)],
        ),
        out_shape=[
            jax.ShapeDtypeStruct((rows, MODEL_WIDTH), f32),
            jax.ShapeDtypeStruct((rows, MODEL_WIDTH), bf16),
            jax.ShapeDtypeStruct((rows, ranks), bf16),
        ],
        compiler_params=params_of(1),
        name="close_mixer",
        cost_estimate=pl.CostEstimate(
            flops=2 * rows * QD * MODEL_WIDTH, transcendentals=0, bytes_accessed=8 << 20
        ),
    )(order, att, hidden, gain, *weights, low_map, up_map)


def side_by_side(left, right):
    values = []
    for at in range(BLOCKS):
        tile = slice(at // 2 * BLOCK, (at // 2 + 1) * BLOCK)
        low_half = lanes_of((R, BLOCK)) < BLOCK // 2
        if at % 2 == 0:
            value = jnp.where(low_half, left[:, tile], pltpu.roll(right[:, tile], BLOCK // 2, 1))
        else:
            value = jnp.where(low_half, pltpu.roll(left[:, tile], BLOCK // 2, 1), right[:, tile])
        values.append(value.astype(bf16))
    return values


def expert_kernel(
    scalars,
    x,
    cot,
    routes,
    router,
    w_in,
    w_down,
    a_in,
    b_in,
    a_down,
    b_down,
    *rest,
):
    (
        sums_out,
        gates_out,
        packed,
        gates,
        gate_sums,
        low_in,
        low_in_turned,
        b_in_all,
        back_low,
        gated_low,
        back_in,
        acts,
        grads,
        low_grads,
        down_acc,
        out_acc,
        grad_acc,
    ) = rest[-17:]
    expert = pl.program_id(0)
    last = pl.num_programs(0) - 1
    rows = x.shape[0]
    block = rows
    local = a_in.shape[0]
    a_in_all = a_in[...].reshape(local * 2 * R, MODEL_WIDTH)
    a_down_all = a_down[...].reshape(local * R, H)
    b_down_all = b_down[...].reshape(local * R, MODEL_WIDTH)

    @pl.when(expert == 0)
    def _():
        logits = nt(x[...], router[...])
        lane = lanes_of(logits.shape)
        chosen = lane == routes[:, 0:1]
        for k in range(1, TOP):
            chosen = chosen | (lane == routes[:, k : k + 1])
        top = jnp.max(jnp.where(chosen, logits, -1e30), -1, keepdims=True)
        shifted = jnp.where(chosen, jnp.exp(jnp.where(chosen, logits - top, 0.0)), 0.0)
        weights = shifted / jnp.sum(shifted, -1, keepdims=True)
        gates[...] = weights
        gates_out[...] = weights.T[: gates_out.shape[0], :]
        low = nt(x[...], a_in_all)
        low_in[...] = low.astype(bf16)
        low_in_turned[...] = low.T.astype(bf16)
        back_low[...] = nt(cot[...], b_down_all)
        b_in_all[...] = jnp.zeros_like(b_in_all)
        for e in range(local):
            b_in_all[e * 2 * R : e * 2 * R + R, :H] = b_in[e, 0, 0]
            b_in_all[e * 2 * R + R : (e + 1) * 2 * R, H:] = b_in[e, 0, 1]
        gate_sums[...] = jnp.zeros_like(gate_sums)
        gated_low[...] = jnp.zeros_like(gated_low)
        back_in[...] = jnp.zeros_like(back_in)
        out_acc[...] = jnp.zeros_like(out_acc)
        grad_acc[...] = jnp.zeros_like(grad_acc)
        down_acc[...] = jnp.zeros_like(down_acc)

    def row_step(index, carry):
        at = pl.ds(pl.multiple_of(index * block, block), block)
        lane_in = lanes_of((block, local * 2 * R))
        lane_down = lanes_of((block, local * R))
        in_mine = (lane_in >= expert * 2 * R) & (lane_in < (expert + 1) * 2 * R)
        down_mine = (lane_down >= expert * R) & (lane_down < (expert + 1) * R)
        gate_all = gates[at, :]
        gate_lane = lanes_of(gate_all.shape) == expert
        weight = jnp.sum(jnp.where(gate_lane, gate_all, 0.0), -1, keepdims=True)
        mine = low_in[at, :]
        mine = jnp.where(in_mine, mine, jnp.zeros_like(mine))
        both = nn(x[at, :], w_in[0]) + nn(mine, b_in_all[...])
        gate = both[:, :H]
        upper = both[:, H:]
        sigmoid = jax.nn.sigmoid(gate)
        silu = gate * sigmoid
        act = (silu * upper).astype(bf16)
        acts[at, :] = act
        act_wide = act.astype(f32)
        low = jnp.where(down_mine, nt(act, a_down_all), 0.0).astype(bf16).astype(f32)
        plain = nt(cot[at, :], w_down[0])
        low_plain = back_low[at, :]
        dots = jnp.sum(act_wide * plain, -1, keepdims=True) + jnp.sum(
            low * low_plain, -1, keepdims=True
        )
        sum_lane = lanes_of(gate_all.shape) == expert + scalars[2]
        gate_sums[at, :] += jnp.where(sum_lane, dots, 0.0)
        low_grad = jnp.where(down_mine, weight * low_plain, 0.0).astype(bf16)
        low_grads[at, :] = low_grad
        grad_act = weight * plain + nn(low_grad, a_down_all)
        grad_first = grad_act * upper * sigmoid * (1.0 + gate * (1.0 - sigmoid))
        grad_second = grad_act * silu
        grad_both = jnp.concatenate(
            [grad_first.astype(bf16), grad_second.astype(bf16)], 1
        )
        grads[at, :] = grad_both
        gated_low[at, :] += (weight * low).astype(bf16)
        out_acc[at, :] += nn((weight * act_wide).astype(bf16), w_down[0])
        grad_acc[at, :] += nt(grad_both, w_in[0])
        low_back = jnp.where(in_mine, nt(grad_both, b_in_all[...]), 0.0)
        back_in[at, :] += low_back.astype(bf16)
        return carry

    lax.fori_loop(0, rows // block, row_step, 0)

    turned = low_in_turned[pl.ds(pl.multiple_of(expert * 2 * R, 2 * R), 2 * R), :]
    product = nn(turned, grads[...])
    first_b_in = local * 3 * R
    here = pl.ds(pl.multiple_of(first_b_in + expert * R, R), R)
    for at, value in enumerate(side_by_side(product[:R, :H], product[R:, H:])):
        packed[at, 0, here, :] = value
    down_acc[...] += tn(low_grads[...], acts[...])

    @pl.when(expert == last)
    def _():
        sums_out[:rows, :] = (grad_acc[...] + nn(back_in[...], a_in_all)).astype(bf16)
        experts = gates_out.shape[0]
        sums = gate_sums[...].T[:experts, :]
        sums = jnp.concatenate([sums[: experts // 2], sums[experts // 2 :]], 1)
        high = sums.astype(bf16).astype(f32)
        edge = rows + experts
        sums_out[rows:edge, :] = jnp.concatenate([high, sums - high], 0).astype(bf16)
        sums_out[edge:, :] = (out_acc[...] + nn(gated_low[...], b_down_all)).astype(bf16)
        wide = tn(back_in[...], x[...]).astype(bf16)
        tall = tn(gated_low[...], cot[...]).astype(bf16)
        for at in range(BLOCKS):
            columns = slice(at * BLOCK, (at + 1) * BLOCK)
            packed[at, 0, : local * 2 * R, :] = wide[:, columns]
            packed[at, 0, local * 2 * R : first_b_in, :] = tall[:, columns]
        for pair in range(local // 2):
            lower = down_acc[pair * 2 * R : pair * 2 * R + R, :]
            upper = down_acc[pair * 2 * R + R : (pair + 1) * 2 * R, :]
            row = local * 4 * R + pair * R
            for at, value in enumerate(side_by_side(lower, upper)):
                packed[at, 0, row : row + R, :] = value


def run_experts(
    scalars, x, cot, routes, router, w_in, w_down, a_in, b_in, a_down, b_down, experts, slots, packed
):
    rows = x.shape[0]
    local = w_in.shape[0]
    ranks_in = local * 2 * R
    ranks_down = local * R
    height = local * 9 * R // 2
    kept = [] if packed is None else [packed]
    full = lambda shape: pl.BlockSpec(shape, lambda e, s: (0,) * len(shape))
    return pl.pallas_call(
        expert_kernel,
        grid_spec=pltpu.PrefetchScalarGridSpec(
            num_scalar_prefetch=1,
            grid=(local,),
            in_specs=[
                full((rows, MODEL_WIDTH)),
                pl.BlockSpec((rows, MODEL_WIDTH), lambda e, s: (s[4], 0)),
                pl.BlockSpec((rows, TOP), lambda e, s: (s[0], 0)),
                full((128, MODEL_WIDTH)),
                pl.BlockSpec((1, MODEL_WIDTH, 2 * H), lambda e, s: (e, 0, 0)),
                pl.BlockSpec((1, H, MODEL_WIDTH), lambda e, s: (e, 0, 0)),
                pl.BlockSpec((local, 1, 2 * R, MODEL_WIDTH), lambda e, s: (0, s[1], 0, 0)),
                pl.BlockSpec((local, 1, 2, R, H), lambda e, s: (0, s[1], 0, 0, 0)),
                pl.BlockSpec((local, 1, R, H), lambda e, s: (0, s[1], 0, 0)),
                pl.BlockSpec((local, 1, R, MODEL_WIDTH), lambda e, s: (0, s[1], 0, 0)),
            ]
            + [pl.BlockSpec(memory_space=pl.ANY)] * len(kept),
            out_specs=[
                full((2 * rows + experts, MODEL_WIDTH)),
                full((experts, rows)),
                pl.BlockSpec((BLOCKS, 1, height, BLOCK), lambda e, s: (0, s[3], 0, 0)),
            ],
            scratch_shapes=[
                pltpu.VMEM((rows, 128), f32),
                pltpu.VMEM((rows, 128), f32),
                pltpu.VMEM((rows, ranks_in), bf16),
                pltpu.VMEM((ranks_in, rows), bf16),
                pltpu.VMEM((ranks_in, 2 * H), bf16),
                pltpu.VMEM((rows, ranks_down), f32),
                pltpu.VMEM((rows, ranks_down), bf16),
                pltpu.VMEM((rows, ranks_in), bf16),
                pltpu.VMEM((rows, H), bf16),
                pltpu.VMEM((rows, 2 * H), bf16),
                pltpu.VMEM((rows, ranks_down), bf16),
                pltpu.VMEM((ranks_down, H), f32),
                pltpu.VMEM((rows, MODEL_WIDTH), f32),
                pltpu.VMEM((rows, MODEL_WIDTH), f32),
            ],
        ),
        out_shape=[
            jax.ShapeDtypeStruct((2 * rows + experts, MODEL_WIDTH), bf16),
            jax.ShapeDtypeStruct((experts, rows), f32),
            jax.ShapeDtypeStruct((BLOCKS, slots, height, BLOCK), bf16),
        ],
        input_output_aliases={11: 2} if kept else {},
        compiler_params=params_of(1),
        name="experts",
        cost_estimate=pl.CostEstimate(
            flops=local * rows * 9 * (1 << 20),
            transcendentals=local * rows * H,
            bytes_accessed=20 << 20,
        ),
    )(scalars, x, cot, routes, router, w_in, w_down, a_in, b_in, a_down, b_down, *kept)


def open_back_kernel(count, order, cot, mid, gain, gates, router, weight_a, weight_b, low_map, up_map, low, att, *rest):
    parts = rest[:count]
    sums = rest[count : 3 * count]
    grad_mid, grad_att, grad_up, grad_low, columns = rest[3 * count :]
    gate_value = gates[...]
    half = gate_value.shape[0] // 2
    sides = []
    for side in range(2):
        value = None
        for at in range(count):
            pair = sums[2 * at + side][...].astype(f32)
            pair = pair[:half] + pair[half:]
            value = pair if value is None else value + pair
        sides.append(value)
    gate_grad = jnp.concatenate(sides, 0)
    logit = gate_value * (gate_grad - jnp.sum(gate_value * gate_grad, 0, keepdims=True))
    first = logit.astype(bf16)
    left = logit - first.astype(f32)
    second = left.astype(bf16)
    third = (left - second.astype(f32)).astype(bf16)
    grad = tn(first, router[...]) + (tn(second, router[...]) + tn(third, router[...]))
    for piece in parts:
        grad = grad + piece[...].astype(f32)
    total = cot[...].astype(f32) + norm_back(mid[...], gain[...].astype(f32), grad)
    grad_mid[...] = total
    branch = total.astype(bf16)
    low_grad = nt(branch, up_map[...]).astype(bf16)
    columns[...] = nn(low_grad, low_map[...])
    for side, weight in enumerate((weight_a, weight_b)):
        value = nt(branch, weight[...])
        for at in range(BLOCKS // 2):
            columns[:, column(order, side * BLOCKS // 2 + at)] += value[:, at * BLOCK : (at + 1) * BLOCK]
    grad_att[...] = columns[...].astype(bf16)
    up_part = tn(low[...], branch)
    low_part = tn(low_grad, att[...])

    @pl.when(pl.program_id(0) == 0)
    def _():
        grad_up[...] = up_part
        grad_low[...] = low_part

    @pl.when(pl.program_id(0) > 0)
    def _():
        grad_up[...] += up_part
        grad_low[...] += low_part


def open_back(order, cot, mid, gain, gates, router, weights, low_map, up_map, low, att, parts):
    rows = cot.shape[0]
    block = 256
    ranks = low_map.shape[0]
    experts = gates.shape[0]
    full = lambda shape: pl.BlockSpec(shape, lambda n, s: (0, 0))
    part = lambda width: pl.BlockSpec((block, width), lambda n, s: (n, 0))
    count = len(parts)
    below = rows // experts
    sums = [
        pl.BlockSpec((experts, block), lambda n, s: (below, n)),
        pl.BlockSpec((experts, block), lambda n, s: (below, rows // block + n)),
    ]

    def body(*refs):
        open_back_kernel(count, *refs)

    return pl.pallas_call(
        body,
        grid_spec=pltpu.PrefetchScalarGridSpec(
            num_scalar_prefetch=1,
            grid=(rows // block,),
            in_specs=[
                part(MODEL_WIDTH),
                part(MODEL_WIDTH),
                full((1, MODEL_WIDTH)),
                pl.BlockSpec((experts, block), lambda n, s: (0, n)),
                full((experts, MODEL_WIDTH)),
                full((HALF, MODEL_WIDTH)),
                full((HALF, MODEL_WIDTH)),
                full((ranks, QD)),
                full((ranks, MODEL_WIDTH)),
                part(ranks),
                part(QD),
            ]
            + [part(MODEL_WIDTH)] * count
            + sums * count,
            out_specs=[
                part(MODEL_WIDTH),
                part(QD),
                full((ranks, MODEL_WIDTH)),
                full((ranks, QD)),
            ],
            scratch_shapes=[pltpu.VMEM((block, QD), f32)],
        ),
        out_shape=[
            jax.ShapeDtypeStruct((rows, MODEL_WIDTH), f32),
            jax.ShapeDtypeStruct((rows, QD), bf16),
            jax.ShapeDtypeStruct((ranks, MODEL_WIDTH), f32),
            jax.ShapeDtypeStruct((ranks, QD), f32),
        ],
        compiler_params=params_of(1),
        name="open_back",
        cost_estimate=pl.CostEstimate(
            flops=2 * rows * QD * MODEL_WIDTH, transcendentals=0, bytes_accessed=14 << 20
        ),
    )(
        order, cot, mid, gain, gates, router, *weights, low_map, up_map, low, att, *parts,
        *[piece for piece in parts for _ in range(2)],
    )


def adapters_back_kernel(
    grad_query, grad_key, grad_value, low, normed, up_map, low_there, up_there, low_out, *results
):
    pieces = (grad_query, grad_key, grad_value)
    bounds = (0, QD, QD + KD, QKV)
    back = None
    ups = []
    for at in range(3):
        block = pieces[at][...]
        ups.append(tn(low[...], block)[at * R : (at + 1) * R])
        part = nt(block, up_map[:, bounds[at] : bounds[at + 1]])
        back = part if back is None else back + part
    value = back.astype(bf16)
    low_out[...] = value
    lows = tn(value, normed[...]) + low_there[...]
    if len(results) == 2:
        grad_up, grad_low = results
        grad_low[...] = lows
        for at in range(3):
            grad_up[:, bounds[at] : bounds[at + 1]] = ups[at]
        return
    (packed,) = results
    grad_up = jnp.concatenate(ups, 1)
    grad_out = up_there[3 * R :, :]
    small = BLOCK // 4
    lane = lanes_of((R, BLOCK))
    for owner in range(packed.shape[0]):
        tile = slice(owner // 4 * BLOCK, (owner // 4 + 1) * BLOCK)
        offset = owner % 4 * small
        first = jnp.zeros((R, BLOCK), f32)
        for at in range(4):
            piece = lows[at * R : (at + 1) * R, tile]
            shift = (at * small - offset) % BLOCK
            piece = pltpu.roll(piece, shift, 1) if shift else piece
            first = jnp.where((lane >= at * small) & (lane < (at + 1) * small), piece, first)
        piece = grad_up[:, owner // 2 * BLOCK : (owner // 2 + 1) * BLOCK]
        piece = pltpu.roll(piece, BLOCK // 2, 1) if owner % 2 else piece
        other = grad_out[:, tile]
        shift = (2 * small - offset) % BLOCK
        other = pltpu.roll(other, shift, 1) if shift else other
        packed[owner, :, :BLOCK] = first
        packed[owner, :, BLOCK:] = jnp.where(
            lane < 2 * small, piece, jnp.where(lane < 3 * small, other, 0.0)
        )


def adapters_back(grad_query, grad_key, grad_value, low, normed, up_map, low_there, up_there, devices):
    rows = normed.shape[0]
    ranks = up_map.shape[0]
    if devices * BLOCK // 4 == MODEL_WIDTH:
        results = [jax.ShapeDtypeStruct((devices, R, 2 * BLOCK), f32)]
    else:
        results = [
            jax.ShapeDtypeStruct((R, QKV), f32),
            jax.ShapeDtypeStruct((ranks, MODEL_WIDTH), f32),
        ]
    back_low, *results = pl.pallas_call(
        adapters_back_kernel,
        out_shape=[jax.ShapeDtypeStruct((rows, ranks), bf16)] + results,
        compiler_params=pltpu.CompilerParams(vmem_limit_bytes=56 * 1024 * 1024),
        name="adapters_back",
        cost_estimate=pl.CostEstimate(
            flops=6 * rows * 256 * QKV, transcendentals=0, bytes_accessed=4 << 20
        ),
    )(grad_query, grad_key, grad_value, low, normed, up_map, low_there, up_there)
    if len(results) == 1:
        return results[0], back_low
    grad_up, grad_low = results
    small = MODEL_WIDTH // devices
    packed = jnp.concatenate(
        [
            grad_low.reshape(4, R, devices, small).transpose(2, 1, 0, 3).reshape(devices, R, 4 * small),
            grad_up.reshape(R, devices, 2 * small).transpose(1, 0, 2),
            up_there[3 * R :].reshape(R, devices, small).transpose(1, 0, 2),
            jnp.zeros((devices, R, small), f32),
        ],
        -1,
    )
    return packed, back_low


def input_back_kernel(
    order, grad_query, grad_key, grad_value, low, weight_a, weight_b, low_map, hid, gain, mid, grad, columns
):
    columns[...] = nn(low[...], low_map[...])
    for side, weight in enumerate((weight_a, weight_b)):
        value = nt(grad_query[...], weight[:, :QD])
        value = value + nt(grad_key[...], weight[:, QD : QD + KD])
        value = value + nt(grad_value[...], weight[:, QD + KD :])
        for at in range(BLOCKS // 2):
            columns[:, column(order, side * BLOCKS // 2 + at)] += value[:, at * BLOCK : (at + 1) * BLOCK]
    rows = hid[...].astype(f32)
    grad[...] = (mid[...] + norm_back(rows, gain[...].astype(f32), columns[...])).astype(bf16)


def input_back(order, grad_query, grad_key, grad_value, low, weights, low_map, hidden, gain, mid):
    rows = hidden.shape[0]
    block = 256
    ranks = low_map.shape[0]
    full = lambda shape: pl.BlockSpec(shape, lambda n, s: (0, 0))
    part = lambda width: pl.BlockSpec((block, width), lambda n, s: (n, 0))
    return pl.pallas_call(
        input_back_kernel,
        grid_spec=pltpu.PrefetchScalarGridSpec(
            num_scalar_prefetch=1,
            grid=(rows // block,),
            in_specs=[
                part(QD),
                part(KD),
                part(KD),
                part(ranks),
                full((HALF, QKV)),
                full((HALF, QKV)),
                full((ranks, MODEL_WIDTH)),
                part(MODEL_WIDTH),
                full((1, MODEL_WIDTH)),
                part(MODEL_WIDTH),
            ],
            out_specs=part(MODEL_WIDTH),
            scratch_shapes=[pltpu.VMEM((block, MODEL_WIDTH), f32)],
        ),
        out_shape=jax.ShapeDtypeStruct((rows, MODEL_WIDTH), bf16),
        compiler_params=params_of(1),
        name="input_back",
        cost_estimate=pl.CostEstimate(
            flops=2 * rows * QKV * MODEL_WIDTH, transcendentals=0, bytes_accessed=12 << 20
        ),
    )(order, grad_query, grad_key, grad_value, low, *weights, low_map, hidden, gain, mid)


def sum_experts_kernel(ids, pieces, a_in, b_in, a_down, b_down, acc):
    local = a_in.shape[0]
    small = a_down.shape[-1]
    acc[...] = jnp.zeros_like(acc)

    def step(index, carry):
        acc[ids[index]] += pieces[index].astype(f32)
        return carry

    lax.fori_loop(0, pieces.shape[0], step, 0)
    for e in range(local):
        a_in[e] = acc[:, e * 2 * R : (e + 1) * 2 * R, :]
        at = local * 2 * R + e * R
        b_down[e] = acc[:, at : at + R, :]
        at = local * 3 * R + e * R
        both = acc[:, at : at + R, :]
        b_in[e, :, 0] = both[:, :, :small]
        b_in[e, :, 1] = both[:, :, small:]
        at = local * 4 * R + e // 2 * R
        a_down[e] = acc[:, at : at + R, e % 2 * small : (e % 2 + 1) * small]


def sum_experts(ids, pieces, local):
    height = pieces.shape[1]
    lanes = pieces.shape[2]
    small = lanes // 2
    vmem = pl.BlockSpec(memory_space=pltpu.VMEM)
    return pl.pallas_call(
        sum_experts_kernel,
        in_specs=[pl.BlockSpec(memory_space=pltpu.SMEM), vmem],
        out_specs=[vmem, vmem, vmem, vmem],
        out_shape=[
            jax.ShapeDtypeStruct((local, NA, 2 * R, lanes), f32),
            jax.ShapeDtypeStruct((local, NA, 2, R, small), f32),
            jax.ShapeDtypeStruct((local, NA, R, small), f32),
            jax.ShapeDtypeStruct((local, NA, R, lanes), f32),
        ],
        scratch_shapes=[pltpu.VMEM((NA, height, lanes), f32)],
        compiler_params=pltpu.CompilerParams(vmem_limit_bytes=56 * 1024 * 1024),
        name="sum_experts",
    )(ids, pieces)


def sum_mixer_kernel(ids, pieces, grad_low, grad_up, grad_out, acc):
    width = grad_low.shape[-1]
    acc[...] = jnp.zeros_like(acc)

    def step(index, carry):
        acc[ids[index]] += pieces[index]
        return carry

    lax.fori_loop(0, pieces.shape[0], step, 0)
    total = acc[...]
    for at in range(4):
        grad_low[at] = total[:, :, at * width : (at + 1) * width]
    grad_up[...] = total[:, :, 4 * width : 6 * width]
    grad_out[...] = total[:, :, 6 * width : 7 * width]


def sum_mixer(ids, pieces):
    width = pieces.shape[2] // 8
    vmem = pl.BlockSpec(memory_space=pltpu.VMEM)
    return pl.pallas_call(
        sum_mixer_kernel,
        in_specs=[pl.BlockSpec(memory_space=pltpu.SMEM), vmem],
        out_specs=[vmem, vmem, vmem],
        out_shape=[
            jax.ShapeDtypeStruct((4, NA, R, width), f32),
            jax.ShapeDtypeStruct((NA, R, 2 * width), f32),
            jax.ShapeDtypeStruct((NA, R, width), f32),
        ],
        scratch_shapes=[pltpu.VMEM((NA, R, 8 * width), f32)],
        compiler_params=pltpu.CompilerParams(vmem_limit_bytes=56 * 1024 * 1024),
        name="sum_mixer",
    )(ids, pieces)


def rope_tables(rows):
    half = HS // 2
    frequency = (10000.0 ** (-2.0 * np.arange(half, dtype=np.float32) / HS)).astype(np.float32)
    angles = np.arange(rows, dtype=np.float32)[:, None] * frequency[None, :]
    cos = np.cos(angles.astype(np.float64)).astype(np.float32)
    sin = np.sin(angles.astype(np.float64)).astype(np.float32)
    return (
        jnp.asarray(np.concatenate([cos, cos, cos, cos], 1)),
        jnp.asarray(np.concatenate([-sin, sin, -sin, sin], 1)),
    )


def swap(value, bit):
    return lax.ppermute(value, "dp", [(at, at ^ bit) for at in range(BLOCKS)])


def both_neighbours(weight):
    return swap(weight, 2), swap(weight, 4)


def across(pair):
    one, two = pair
    middle = one.shape[0] // 2
    return swap(two[:middle], 2), swap(one[middle:], 4)


def tied(*values):
    return lax.optimization_barrier(values)


def order_of(row):
    if lax.axis_size("dp") != BLOCKS:
        return jnp.arange(BLOCKS, dtype=jnp.int32)
    return row.astype(jnp.int32) ^ jnp.array([0, 2, 4, 6, 1, 3, 5, 7], jnp.int32)


def to_owners(packed, owners, local):
    split = owners // BLOCKS
    if split == 1:
        return packed
    slots = packed.shape[1]
    edge = local * 3 * R
    wide = packed[:, :, :edge].reshape(BLOCKS, slots, edge, split, BLOCK // split)
    wide = wide.transpose(0, 3, 1, 2, 4).reshape(owners, slots, edge, BLOCK // split)
    rest = packed.shape[2] - edge
    narrow = packed[:, :, edge:].reshape(BLOCKS, slots, rest, 2, split, BLOCK // 2 // split)
    narrow = narrow.transpose(0, 4, 1, 2, 3, 5).reshape(owners, slots, rest, BLOCK // split)
    return jnp.concatenate([wide, narrow], 2)


def joined(left, right):
    return (left.astype(f32) + right.astype(f32)).astype(bf16)


def on_device(
    hidden,
    cotangent,
    lengths,
    adapter_ids,
    routes,
    attn_gain,
    ffn_gain,
    query_key_value_weight,
    w_out,
    w_router,
    w_gate_up,
    w_down,
    attention_lowmap,
    attention_query_key_value_upmap,
    attention_output_upmap,
    expert_gate_up_lowmap,
    expert_gate_up_upmap,
    expert_down_lowmap,
    expert_down_upmap,
):
    groups = lax.axis_size("expert")
    owners = lax.axis_size("dp")
    place = lax.axis_index("expert")
    row = lax.axis_index("dp")
    devices = groups * owners
    sequence = row * groups + place
    rows = hidden.shape[0]
    experts = w_router.shape[1]
    local = w_gate_up.shape[0]
    width = MODEL_WIDTH // owners
    attn_gain = attn_gain.reshape(1, MODEL_WIDTH)
    ffn_gain = ffn_gain.reshape(1, MODEL_WIDTH)
    length = lax.dynamic_slice(lengths, (sequence,), (1,))
    forward = [(at, (at + 1) % groups) for at in range(groups)]
    backward = [(at, (at - 1) % groups) for at in range(groups)]

    mine = lax.dynamic_slice(adapter_ids.reshape(owners, groups), (0, place), (owners, 1))[:, 0]
    low_turned = attention_lowmap.transpose(1, 0, 3, 2).reshape(NA, 4 * R, width)
    up_turned = (
        attention_query_key_value_upmap.reshape(NA, R, 2, width)
        .transpose(0, 2, 1, 3)
        .reshape(NA, 2 * R, width)
    )
    adapters = jnp.concatenate([low_turned, up_turned, attention_output_upmap], 1)[mine]
    adapters = lax.all_to_all(adapters, "dp", 0, 0, tiled=True)
    order = order_of(row)
    short = owners == BLOCKS
    if short:
        pair_in = both_neighbours(query_key_value_weight)
        pair_out = both_neighbours(w_out)
        pair_in, pair_out = tied(pair_in, pair_out)
        across_in = across(pair_in)
        pair_out, across_in = tied(pair_out, across_in)
        near_in = jnp.concatenate([query_key_value_weight, *pair_in, *across_in], 0)
        weight_in = near_in, swap(near_in, 1)
        across_out = across(pair_out)
    else:
        whole = lax.all_gather(query_key_value_weight, "dp", axis=0, tiled=True)
        weight_in = whole[:HALF], whole[HALF:]
        whole = lax.all_gather(w_out, "dp", axis=0, tiled=True)
        weight_out = whole[:HALF], whole[HALF:]

    low_map = adapters[:, : 4 * R].transpose(1, 0, 2).reshape(4 * R, MODEL_WIDTH)
    up = (
        adapters[:, 4 * R : 6 * R]
        .reshape(owners, 2, R, width)
        .transpose(2, 0, 1, 3)
        .reshape(R, QKV)
    )
    up_out = adapters[:, 6 * R :].transpose(1, 0, 2).reshape(R, MODEL_WIDTH)
    column = jnp.arange(QKV, dtype=jnp.int32)
    part = jnp.where(column < QD, 0, jnp.where(column < QD + KD, 1, 2))
    up_map = jnp.where(
        part[None, None, :] == jnp.arange(4, dtype=jnp.int32)[:, None, None], up[None], 0
    ).reshape(4 * R, QKV)
    up_out_map = jnp.concatenate([jnp.zeros((3 * R, MODEL_WIDTH), bf16), up_out], 0)

    cos, sin = rope_tables(rows)

    cots = lax.all_gather(cotangent, "expert", axis=0, tiled=True)

    qkv, low, normed_in = project(order, hidden, attn_gain, weight_in, low_map, up_map, cos, sin)
    if short:
        across_out, low = tied(across_out, low)
        near_out = jnp.concatenate([w_out, *pair_out, *across_out], 0)
        weight_out = near_out, swap(near_out, 1)
    attended, lse = attend(length, qkv)
    mid, normed_mid, low_out = close_mixer(
        order, attended, hidden, ffn_gain, weight_out, low_map, up_out_map
    )

    first = place * local
    routes_here = (routes - first + experts) % experts
    router = jnp.roll(w_router.T, -first, axis=0)
    router_wide = jnp.concatenate(
        [router, jnp.zeros((128 - experts, MODEL_WIDTH), router.dtype)], 0
    )
    a_in = expert_gate_up_lowmap.transpose(0, 1, 3, 2)
    a_down = expert_down_lowmap.transpose(0, 1, 3, 2)

    offsets = [0, 1] + [groups - 1] * (groups > 2) + list(range(2, groups - 1))
    offset = jnp.array(offsets, jnp.int32)
    source = (place - offset + groups) % groups
    tags = adapter_ids.reshape(owners, groups)[:, source]
    slot = jnp.arange(groups, dtype=jnp.int32)
    table = jnp.stack(
        [
            source,
            lax.dynamic_slice(tags, (row, 0), (1, groups))[0],
            offset * local,
            slot,
            jnp.where(slot == 0, 0, source),
        ],
        1,
    )

    xs = {0: normed_mid, 1: lax.ppermute(normed_mid, "expert", forward)}
    packed = None
    ran = {}
    for at, offset in enumerate(offsets):
        ran[offset], gate_part, packed = run_experts(
            table[at],
            xs[offset],
            cotangent if at == 0 else cots,
            routes_here,
            router_wide,
            w_gate_up,
            w_down,
            a_in,
            expert_gate_up_upmap,
            a_down,
            expert_down_upmap,
            experts,
            groups,
            packed,
        )
        if at == 0:
            gates = gate_part
            if groups > 2:
                normed_mid, packed = tied(normed_mid, packed)
                xs[groups - 1] = lax.ppermute(normed_mid, "expert", backward)
        elif at < groups - 2:
            value, packed = tied(xs[at], packed)
            xs[at + 1] = lax.ppermute(value, "expert", forward)
        if at == 2:
            first_sums, packed = tied(ran[1], packed)

    pieces = lax.all_to_all(to_owners(packed, owners, local), "dp", 0, 0, tiled=True)
    pieces = pieces.reshape(devices, pieces.shape[2], width)
    g_a_in, g_b_in, g_a_down, g_b_down = sum_experts(tags.reshape(devices), pieces, local)

    edge = rows + experts
    both_far = lax.ppermute(first_sums if groups > 2 else ran[1], "expert", forward)
    grad_far, out_far = both_far, both_far[edge:]
    for offset in range(2, groups):
        grad_part = joined(ran[offset][:edge], grad_far[:edge])
        if offset == groups - 1:
            grad_part, g_a_down = tied(grad_part, g_a_down)
        grad_far = lax.ppermute(grad_part, "expert", forward)
    for offset in range(2, groups):
        out_part = joined(ran[offset][edge:], out_far)
        if offset == 2:
            out_part, grad_far = tied(out_part, grad_far)
        out_far = lax.ppermute(out_part, "expert", forward)

    grad_mid, grad_attended, grad_up_out, grad_low_out = open_back(
        order,
        cotangent,
        mid,
        ffn_gain,
        gates,
        router,
        weight_out,
        low_map,
        up_out_map,
        low_out,
        attended,
        [ran[0], grad_far],
    )
    grad_query, grad_key, grad_value = attend_back(length, qkv, grad_attended, lse, cos, sin)
    packed, back_low = adapters_back(
        grad_query, grad_key, grad_value, low, normed_in, up_map, grad_low_out, grad_up_out, devices
    )
    packed = lax.all_to_all(packed, ("dp", "expert"), 0, 0, tiled=True)
    m_a, m_b, m_o = sum_mixer(adapter_ids, packed)

    grad_hidden = input_back(
        order, grad_query, grad_key, grad_value, back_low, weight_in, low_map, hidden, attn_gain, grad_mid
    )
    out = (mid + ran[0][edge:].astype(f32) + out_far.astype(f32)).astype(bf16)
    return (
        out,
        grad_hidden,
        m_a.transpose(0, 1, 3, 2),
        m_b,
        m_o,
        g_a_in.transpose(0, 1, 3, 2),
        g_b_in,
        g_a_down.transpose(0, 1, 3, 2),
        g_b_down,
    )


def solution(mesh):
    in_specs = (
        P(("dp", "expert"), None),
        P(("dp", "expert"), None),
        P(),
        P(),
        P("dp", None),
        P(),
        P(),
        P("dp", None),
        P("dp", None),
        P(),
        P("expert", None, None),
        P("expert", None, None),
        P(None, None, "dp", None),
        P(None, None, "dp"),
        P(None, None, "dp"),
        P("expert", None, None, None),
        P("expert", None, None, None, None),
        P("expert", None, None, None),
        P("expert", None, None, None),
    )
    out_specs = (
        P(("dp", "expert"), None),
        P(("dp", "expert"), None),
        P(None, None, ("dp", "expert"), None),
        P(None, None, ("dp", "expert")),
        P(None, None, ("dp", "expert")),
        P("expert", None, "dp", None),
        P("expert", None, None, None, "dp"),
        P("expert", None, "dp", None),
        P("expert", None, None, "dp"),
    )
    return jax.shard_map(
        on_device, mesh=mesh, in_specs=in_specs, out_specs=out_specs, check_vma=False
    )
```

```python
import numpy as np
import jax
import jax.numpy as jnp
from jax import lax
from jax.experimental import pallas as pl
from jax.experimental.pallas import tpu as pltpu
from jax.sharding import PartitionSpec as P

MODEL_WIDTH = 1024
HQ = 16
KVH = 8
HS = 64
H = 512
TOP = 8
R = 16
NA = 8
QD = HQ * HS
KD = KVH * HS
QKV = QD + 2 * KD

epsilon = 1e-06
f32 = jnp.float32
bf16 = jnp.bfloat16


def nn(left, right):
    return lax.dot_general(left, right, (((1,), (0,)), ((), ())), preferred_element_type=f32)


def nt(left, right):
    return lax.dot_general(left, right, (((1,), (1,)), ((), ())), preferred_element_type=f32)


def tn(left, right):
    return lax.dot_general(left, right, (((0,), (0,)), ((), ())), preferred_element_type=f32)


def lanes_of(shape):
    return lax.broadcasted_iota(jnp.int32, shape, len(shape) - 1)


def row_scale(rows):
    return lax.rsqrt(jnp.mean(rows * rows, -1, keepdims=True) + epsilon)


def norm_back(rows, gain, grad):
    scale = row_scale(rows)
    scaled = grad * gain
    return scale * scaled - rows * (scale * scale * scale) * jnp.mean(
        rows * scaled, -1, keepdims=True
    )


def rope_swap(rows):
    width = rows.shape[-1]
    lane = lanes_of(rows.shape)
    return jnp.where(
        lane % HS < HS // 2,
        pltpu.roll(rows, width - HS // 2, 1),
        pltpu.roll(rows, HS // 2, 1),
    )


def both_halves(pair, half):
    rows = pair.astype(f32)
    lane = lanes_of(rows.shape)
    rolled = pltpu.roll(rows, HS, 1)
    keep = (lane < HS) == (half == 0)
    return jnp.where(keep, rows, rolled).astype(bf16)


def stacked_heads(pair):
    lane = lanes_of(pair.shape)
    zero = jnp.zeros_like(pair)
    return jnp.concatenate(
        [jnp.where(lane < HS, pair, zero), jnp.where(lane < HS, zero, pair)], 0
    )


def params_of(count):
    return pltpu.CompilerParams(
        dimension_semantics=("arbitrary",) * count, vmem_limit_bytes=56 * 1024 * 1024
    )


BLOCK = 128
BLOCKS = MODEL_WIDTH // BLOCK
HALF = MODEL_WIDTH // 2


def column(order, at):
    return pl.ds(pl.multiple_of(order[at] * BLOCK, BLOCK), BLOCK)


def halves(weights, width, index):
    there = 1 if weights[0] is weights[1] else 0
    return [
        pl.BlockSpec((HALF, width), lambda n, s: (0, index(n))),
        pl.BlockSpec((HALF, width), lambda n, s: (there, index(n))),
    ]


def project_kernel(
    order, hid, gain, weight_a, weight_b, low_map, up_map, cos, sin, qkv, low, normed, turned_rows
):
    step = pl.program_id(0)
    blocks = pl.num_programs(0)

    @pl.when(step == 0)
    def _():
        rows = hid[...].astype(f32)
        value = (rows * row_scale(rows) * gain[...].astype(f32)).astype(bf16)
        normed[...] = value
        low[...] = nt(value, low_map[...]).astype(bf16)
        for at in range(BLOCKS):
            turned_rows[:, at * BLOCK : (at + 1) * BLOCK] = normed[:, column(order, at)]

    value = (
        nn(turned_rows[:, :HALF], weight_a[...])
        + nn(turned_rows[:, HALF:], weight_b[...])
        + nn(low[...], up_map[...])
    )

    @pl.when(step < blocks * 3 // 4)
    def _():
        for part in range(value.shape[1] // 128):
            piece = value[:, part * 128 : part * 128 + 128]
            turned = piece * cos[...] + rope_swap(piece) * sin[...]
            qkv[:, part * 128 : part * 128 + 128] = turned.astype(bf16)

    @pl.when(step >= blocks * 3 // 4)
    def _():
        qkv[...] = value.astype(bf16)


def project(order, hidden, gain, weights, low_map, up_map, cos, sin):
    rows = hidden.shape[0]
    block = 256
    ranks = low_map.shape[0]
    full = lambda shape: pl.BlockSpec(shape, lambda n, s: (0, 0))
    return pl.pallas_call(
        project_kernel,
        grid_spec=pltpu.PrefetchScalarGridSpec(
            num_scalar_prefetch=1,
            grid=(QKV // block,),
            in_specs=[
                full((rows, MODEL_WIDTH)),
                full((1, MODEL_WIDTH)),
                *halves(weights, block, lambda n: n),
                full((ranks, MODEL_WIDTH)),
                pl.BlockSpec((ranks, block), lambda n, s: (0, n)),
                full((rows, 128)),
                full((rows, 128)),
            ],
            out_specs=[
                pl.BlockSpec((rows, block), lambda n, s: (0, n)),
                full((rows, ranks)),
                full((rows, MODEL_WIDTH)),
            ],
            scratch_shapes=[pltpu.VMEM((rows, MODEL_WIDTH), bf16)],
        ),
        out_shape=[
            jax.ShapeDtypeStruct((rows, QKV), bf16),
            jax.ShapeDtypeStruct((rows, ranks), bf16),
            jax.ShapeDtypeStruct((rows, MODEL_WIDTH), bf16),
        ],
        compiler_params=params_of(1),
        name="project",
        cost_estimate=pl.CostEstimate(
            flops=2 * rows * QKV * MODEL_WIDTH, transcendentals=0, bytes_accessed=8 << 20
        ),
    )(order, hidden, gain, *weights, low_map, up_map, cos, sin)


ROWB = 128


def length_row(length, count):
    col = lax.broadcasted_iota(jnp.int32, (1, count), 1)
    return jnp.where(col < length, 0.0, -1e30)


def causal_block():
    row = lax.broadcasted_iota(jnp.int32, (2 * ROWB, ROWB), 0) % ROWB
    return jnp.where(lanes_of((2 * ROWB, ROWB)) <= row, 0.0, -1e30)


def masked_scores(queries, keys, start, bias, causal):
    scores = nt((queries.astype(f32) * 0.125).astype(bf16), keys)
    count = start + ROWB
    near = scores[:, start:] + (bias[:, start:count] + causal)
    if start == 0:
        return near
    return jnp.concatenate([scores[:, :start] + bias[:, :start], near], 1)


def attend_kernel(scalars, query, key, value, result, lse):
    half = pl.program_id(0) % 2
    keys = both_halves(key[...], half)
    values = both_halves(value[...], half)
    rows = query.shape[0]
    bias = length_row(scalars[0], rows)
    causal = causal_block()
    for start in range(0, rows, ROWB):
        count = start + ROWB
        stacked = stacked_heads(query[start:count, :])
        scores = masked_scores(stacked, keys[:count], start, bias, causal)
        top = jnp.max(scores, -1, keepdims=True)
        shifted = jnp.exp(scores - top)
        total = jnp.sum(shifted, -1, keepdims=True)
        mixed = nn(shifted.astype(bf16), values[:count]) * (1.0 / total)
        lane = lanes_of((ROWB, 128))
        result[start:count, :] = jnp.where(lane < HS, mixed[:ROWB], mixed[ROWB:]).astype(bf16)
        logs = top + jnp.log(total)
        lse[0, start:count, :] = jnp.concatenate([logs[:ROWB], logs[ROWB:]], 1)


def attend(length, qkv):
    rows = qkv.shape[0]
    pairs = KVH
    return pl.pallas_call(
        attend_kernel,
        grid_spec=pltpu.PrefetchScalarGridSpec(
            num_scalar_prefetch=1,
            grid=(pairs,),
            in_specs=[
                pl.BlockSpec((rows, 128), lambda g, s: (0, g)),
                pl.BlockSpec((rows, 128), lambda g, s: (0, QD // 128 + g // 2)),
                pl.BlockSpec((rows, 128), lambda g, s: (0, (QD + KD) // 128 + g // 2)),
            ],
            out_specs=[
                pl.BlockSpec((rows, 128), lambda g, s: (0, g)),
                pl.BlockSpec((1, rows, 2), lambda g, s: (g, 0, 0)),
            ],
        ),
        out_shape=[
            jax.ShapeDtypeStruct((rows, QD), bf16),
            jax.ShapeDtypeStruct((pairs, rows, 2), f32),
        ],
        compiler_params=params_of(1),
        name="attend",
        cost_estimate=pl.CostEstimate(
            flops=8 * rows * rows * QD, transcendentals=rows * rows * HQ, bytes_accessed=4 << 20
        ),
    )(length, qkv, qkv, qkv)


def attend_back_kernel(
    scalars, query, key, value, grad, lse, cos, sin, grad_query, grad_key, grad_value, key_acc, value_acc
):
    half = pl.program_id(0) % 2
    bias = length_row(scalars[0], query.shape[0])
    causal = causal_block()
    keys = both_halves(key[...], half)
    values = both_halves(value[...], half)
    rows = query.shape[0]
    key_acc[...] = jnp.zeros_like(key_acc)
    value_acc[...] = jnp.zeros_like(value_acc)
    for start in range(0, rows, ROWB):
        count = start + ROWB
        stacked = stacked_heads(query[start:count, :])
        grads = stacked_heads(grad[start:count, :])
        scores = masked_scores(stacked, keys[:count], start, bias, causal)
        logs = lse[0, start:count, :]
        logs = jnp.concatenate([logs[:, 0:1], logs[:, 1:2]], 0)
        prob = jnp.exp(scores - logs)
        grad_prob = nt(grads, values[:count])
        delta = jnp.sum(prob * grad_prob, -1, keepdims=True)
        grad_score = (prob * (grad_prob - delta)).astype(bf16)
        mixed = nn(grad_score, keys[:count])
        lane = lanes_of((ROWB, 128))
        turned = 0.125 * jnp.where(lane < HS, mixed[:ROWB], mixed[ROWB:])
        turned = turned * cos[start:count, :] - rope_swap(turned) * sin[start:count, :]
        grad_query[start:count, :] = turned.astype(bf16)
        key_acc[:count, :] += tn(grad_score, stacked)
        value_acc[:count, :] += tn(prob.astype(bf16), grads)
    total = key_acc[...]
    total = 0.125 * (total + pltpu.roll(total, HS, 1))
    total = (total * cos[...] - rope_swap(total) * sin[...]).astype(bf16)
    other = value_acc[...]
    other = (other + pltpu.roll(other, HS, 1)).astype(bf16)

    @pl.when(half == 0)
    def _():
        grad_key[...] = total
        grad_value[...] = other

    @pl.when(half == 1)
    def _():
        low_half = lanes_of(total.shape) < HS
        grad_key[...] = jnp.where(low_half, grad_key[...], total)
        grad_value[...] = jnp.where(low_half, grad_value[...], other)


def attend_back(length, qkv, grad, lse, cos, sin):
    rows = qkv.shape[0]
    pairs = KVH
    return pl.pallas_call(
        attend_back_kernel,
        grid_spec=pltpu.PrefetchScalarGridSpec(
            num_scalar_prefetch=1,
            grid=(pairs,),
            in_specs=[
                pl.BlockSpec((rows, 128), lambda g, s: (0, g)),
                pl.BlockSpec((rows, 128), lambda g, s: (0, QD // 128 + g // 2)),
                pl.BlockSpec((rows, 128), lambda g, s: (0, (QD + KD) // 128 + g // 2)),
                pl.BlockSpec((rows, 128), lambda g, s: (0, g)),
                pl.BlockSpec((1, rows, 2), lambda g, s: (g, 0, 0)),
                pl.BlockSpec((rows, 128), lambda g, s: (0, 0)),
                pl.BlockSpec((rows, 128), lambda g, s: (0, 0)),
            ],
            out_specs=[
                pl.BlockSpec((rows, 128), lambda g, s: (0, g)),
                pl.BlockSpec((rows, 128), lambda g, s: (0, g // 2)),
                pl.BlockSpec((rows, 128), lambda g, s: (0, g // 2)),
            ],
            scratch_shapes=[pltpu.VMEM((rows, 128), f32), pltpu.VMEM((rows, 128), f32)],
        ),
        out_shape=[
            jax.ShapeDtypeStruct((rows, QD), bf16),
            jax.ShapeDtypeStruct((rows, KD), bf16),
            jax.ShapeDtypeStruct((rows, KD), bf16),
        ],
        compiler_params=params_of(1),
        name="attend_back",
        cost_estimate=pl.CostEstimate(
            flops=20 * rows * rows * QD, transcendentals=rows * rows * HQ, bytes_accessed=8 << 20
        ),
    )(length, qkv, qkv, qkv, grad, lse, cos, sin)


def close_kernel(order, att, hid, gain, weight_a, weight_b, low_map, up_map, mid, normed, low):
    low_value = nt(att[...], low_map[...]).astype(bf16)
    low[...] = low_value
    turned = jnp.concatenate([att[:, column(order, at)] for at in range(BLOCKS)], 1)
    stream = hid[...].astype(f32) + (
        nn(turned[:, :HALF], weight_a[...])
        + nn(turned[:, HALF:], weight_b[...])
        + nn(low_value, up_map[...])
    )
    mid[...] = stream
    normed[...] = (stream * row_scale(stream) * gain[...].astype(f32)).astype(bf16)


def close_mixer(order, att, hidden, gain, weights, low_map, up_map):
    rows = hidden.shape[0]
    block = 256
    ranks = low_map.shape[0]
    full = lambda shape: pl.BlockSpec(shape, lambda n, s: (0, 0))
    part = lambda width: pl.BlockSpec((block, width), lambda n, s: (n, 0))
    return pl.pallas_call(
        close_kernel,
        grid_spec=pltpu.PrefetchScalarGridSpec(
            num_scalar_prefetch=1,
            grid=(rows // block,),
            in_specs=[
                part(QD),
                part(MODEL_WIDTH),
                full((1, MODEL_WIDTH)),
                *halves(weights, MODEL_WIDTH, lambda n: 0),
                full((ranks, QD)),
                full((ranks, MODEL_WIDTH)),
            ],
            out_specs=[part(MODEL_WIDTH), part(MODEL_WIDTH), part(ranks)],
        ),
        out_shape=[
            jax.ShapeDtypeStruct((rows, MODEL_WIDTH), f32),
            jax.ShapeDtypeStruct((rows, MODEL_WIDTH), bf16),
            jax.ShapeDtypeStruct((rows, ranks), bf16),
        ],
        compiler_params=params_of(1),
        name="close_mixer",
        cost_estimate=pl.CostEstimate(
            flops=2 * rows * QD * MODEL_WIDTH, transcendentals=0, bytes_accessed=8 << 20
        ),
    )(order, att, hidden, gain, *weights, low_map, up_map)


def side_by_side(left, right):
    values = []
    for at in range(BLOCKS):
        tile = slice(at // 2 * BLOCK, (at // 2 + 1) * BLOCK)
        low_half = lanes_of((R, BLOCK)) < BLOCK // 2
        if at % 2 == 0:
            value = jnp.where(low_half, left[:, tile], pltpu.roll(right[:, tile], BLOCK // 2, 1))
        else:
            value = jnp.where(low_half, pltpu.roll(left[:, tile], BLOCK // 2, 1), right[:, tile])
        values.append(value.astype(bf16))
    return values


def expert_kernel(
    scalars,
    x,
    cot,
    routes,
    router,
    w_in,
    w_down,
    a_in,
    b_in,
    a_down,
    b_down,
    *rest,
):
    (
        out,
        grad_normed,
        gates_out,
        packed,
        gates,
        gate_sums,
        low_in,
        low_in_turned,
        b_in_all,
        back_low,
        gated_low,
        back_in,
        acts,
        grads,
        low_grads,
        down_acc,
        out_acc,
        grad_acc,
    ) = rest[-18:]
    expert = pl.program_id(0)
    last = pl.num_programs(0) - 1
    rows = x.shape[0]
    block = rows
    local = a_in.shape[0]
    a_in_all = a_in[...].reshape(local * 2 * R, MODEL_WIDTH)
    a_down_all = a_down[...].reshape(local * R, H)
    b_down_all = b_down[...].reshape(local * R, MODEL_WIDTH)

    @pl.when(expert == 0)
    def _():
        logits = nt(x[...], router[...])
        lane = lanes_of(logits.shape)
        chosen = lane == routes[:, 0:1]
        for k in range(1, TOP):
            chosen = chosen | (lane == routes[:, k : k + 1])
        top = jnp.max(jnp.where(chosen, logits, -1e30), -1, keepdims=True)
        shifted = jnp.where(chosen, jnp.exp(jnp.where(chosen, logits - top, 0.0)), 0.0)
        weights = shifted / jnp.sum(shifted, -1, keepdims=True)
        gates[...] = weights
        gates_out[...] = weights.T[: gates_out.shape[0], :]
        low = nt(x[...], a_in_all)
        low_in[...] = low.astype(bf16)
        low_in_turned[...] = low.T.astype(bf16)
        back_low[...] = nt(cot[...], b_down_all)
        b_in_all[...] = jnp.zeros_like(b_in_all)
        for e in range(local):
            b_in_all[e * 2 * R : e * 2 * R + R, :H] = b_in[e, 0, 0]
            b_in_all[e * 2 * R + R : (e + 1) * 2 * R, H:] = b_in[e, 0, 1]
        gate_sums[...] = jnp.zeros_like(gate_sums)
        gated_low[...] = jnp.zeros_like(gated_low)
        back_in[...] = jnp.zeros_like(back_in)
        out_acc[...] = jnp.zeros_like(out_acc)
        grad_acc[...] = jnp.zeros_like(grad_acc)
        down_acc[...] = jnp.zeros_like(down_acc)

    def row_step(index, carry):
        at = pl.ds(pl.multiple_of(index * block, block), block)
        lane_in = lanes_of((block, local * 2 * R))
        lane_down = lanes_of((block, local * R))
        in_mine = (lane_in >= expert * 2 * R) & (lane_in < (expert + 1) * 2 * R)
        down_mine = (lane_down >= expert * R) & (lane_down < (expert + 1) * R)
        gate_all = gates[at, :]
        gate_lane = lanes_of(gate_all.shape) == expert
        weight = jnp.sum(jnp.where(gate_lane, gate_all, 0.0), -1, keepdims=True)
        mine = low_in[at, :]
        mine = jnp.where(in_mine, mine, jnp.zeros_like(mine))
        both = nn(x[at, :], w_in[0]) + nn(mine, b_in_all[...])
        gate = both[:, :H]
        upper = both[:, H:]
        sigmoid = jax.nn.sigmoid(gate)
        silu = gate * sigmoid
        act = (silu * upper).astype(bf16)
        acts[at, :] = act
        act_wide = act.astype(f32)
        low = jnp.where(down_mine, nt(act, a_down_all), 0.0).astype(bf16).astype(f32)
        plain = nt(cot[at, :], w_down[0])
        low_plain = back_low[at, :]
        dots = jnp.sum(act_wide * plain, -1, keepdims=True) + jnp.sum(
            low * low_plain, -1, keepdims=True
        )
        sum_lane = lanes_of(gate_all.shape) == expert + scalars[2]
        gate_sums[at, :] += jnp.where(sum_lane, dots, 0.0)
        low_grad = jnp.where(down_mine, weight * low_plain, 0.0).astype(bf16)
        low_grads[at, :] = low_grad
        grad_act = weight * plain + nn(low_grad, a_down_all)
        grad_first = grad_act * upper * sigmoid * (1.0 + gate * (1.0 - sigmoid))
        grad_second = grad_act * silu
        grad_both = jnp.concatenate(
            [grad_first.astype(bf16), grad_second.astype(bf16)], 1
        )
        grads[at, :] = grad_both
        gated_low[at, :] += (weight * low).astype(bf16)
        out_acc[at, :] += nn((weight * act_wide).astype(bf16), w_down[0])
        grad_acc[at, :] += nt(grad_both, w_in[0])
        low_back = jnp.where(in_mine, nt(grad_both, b_in_all[...]), 0.0)
        back_in[at, :] += low_back.astype(bf16)
        return carry

    lax.fori_loop(0, rows // block, row_step, 0)

    turned = low_in_turned[pl.ds(pl.multiple_of(expert * 2 * R, 2 * R), 2 * R), :]
    product = nn(turned, grads[...])
    first_b_in = local * 3 * R
    here = pl.ds(pl.multiple_of(first_b_in + expert * R, R), R)
    for at, value in enumerate(side_by_side(product[:R, :H], product[R:, H:])):
        packed[at, 0, here, :] = value
    down_acc[...] += tn(low_grads[...], acts[...])

    @pl.when(expert == last)
    def _():
        out[...] = (out_acc[...] + nn(gated_low[...], b_down_all)).astype(bf16)
        grad_normed[:rows, :] = (grad_acc[...] + nn(back_in[...], a_in_all)).astype(bf16)
        experts = gates_out.shape[0]
        sums = gate_sums[...].T[:experts, :]
        sums = jnp.concatenate([sums[: experts // 2], sums[experts // 2 :]], 1)
        high = sums.astype(bf16).astype(f32)
        grad_normed[rows:, :] = jnp.concatenate([high, sums - high], 0).astype(bf16)
        wide = tn(back_in[...], x[...]).astype(bf16)
        tall = tn(gated_low[...], cot[...]).astype(bf16)
        for at in range(BLOCKS):
            columns = slice(at * BLOCK, (at + 1) * BLOCK)
            packed[at, 0, : local * 2 * R, :] = wide[:, columns]
            packed[at, 0, local * 2 * R : first_b_in, :] = tall[:, columns]
        for pair in range(local // 2):
            lower = down_acc[pair * 2 * R : pair * 2 * R + R, :]
            upper = down_acc[pair * 2 * R + R : (pair + 1) * 2 * R, :]
            row = local * 4 * R + pair * R
            for at, value in enumerate(side_by_side(lower, upper)):
                packed[at, 0, row : row + R, :] = value


def run_experts(
    scalars, x, cot, routes, router, w_in, w_down, a_in, b_in, a_down, b_down, experts, packed
):
    rows = x.shape[0]
    local = w_in.shape[0]
    ranks_in = local * 2 * R
    ranks_down = local * R
    height = packed.shape[2]
    full = lambda shape: pl.BlockSpec(shape, lambda e, s: (0,) * len(shape))
    return pl.pallas_call(
        expert_kernel,
        grid_spec=pltpu.PrefetchScalarGridSpec(
            num_scalar_prefetch=1,
            grid=(local,),
            in_specs=[
                full((rows, MODEL_WIDTH)),
                full((rows, MODEL_WIDTH)),
                pl.BlockSpec((rows, TOP), lambda e, s: (s[0], 0)),
                full((128, MODEL_WIDTH)),
                pl.BlockSpec((1, MODEL_WIDTH, 2 * H), lambda e, s: (e, 0, 0)),
                pl.BlockSpec((1, H, MODEL_WIDTH), lambda e, s: (e, 0, 0)),
                pl.BlockSpec((local, 1, 2 * R, MODEL_WIDTH), lambda e, s: (0, s[1], 0, 0)),
                pl.BlockSpec((local, 1, 2, R, H), lambda e, s: (0, s[1], 0, 0, 0)),
                pl.BlockSpec((local, 1, R, H), lambda e, s: (0, s[1], 0, 0)),
                pl.BlockSpec((local, 1, R, MODEL_WIDTH), lambda e, s: (0, s[1], 0, 0)),
            ]
            + [pl.BlockSpec(memory_space=pl.ANY)],
            out_specs=[
                full((rows, MODEL_WIDTH)),
                full((rows + experts, MODEL_WIDTH)),
                full((experts, rows)),
                pl.BlockSpec((BLOCKS, 1, height, BLOCK), lambda e, s: (0, s[3], 0, 0)),
            ],
            scratch_shapes=[
                pltpu.VMEM((rows, 128), f32),
                pltpu.VMEM((rows, 128), f32),
                pltpu.VMEM((rows, ranks_in), bf16),
                pltpu.VMEM((ranks_in, rows), bf16),
                pltpu.VMEM((ranks_in, 2 * H), bf16),
                pltpu.VMEM((rows, ranks_down), f32),
                pltpu.VMEM((rows, ranks_down), bf16),
                pltpu.VMEM((rows, ranks_in), bf16),
                pltpu.VMEM((rows, H), bf16),
                pltpu.VMEM((rows, 2 * H), bf16),
                pltpu.VMEM((rows, ranks_down), bf16),
                pltpu.VMEM((ranks_down, H), f32),
                pltpu.VMEM((rows, MODEL_WIDTH), f32),
                pltpu.VMEM((rows, MODEL_WIDTH), f32),
            ],
        ),
        out_shape=[
            jax.ShapeDtypeStruct((rows, MODEL_WIDTH), bf16),
            jax.ShapeDtypeStruct((rows + experts, MODEL_WIDTH), bf16),
            jax.ShapeDtypeStruct((experts, rows), f32),
            jax.ShapeDtypeStruct(packed.shape, bf16),
        ],
        input_output_aliases={11: 3},
        compiler_params=params_of(1),
        name="experts",
        cost_estimate=pl.CostEstimate(
            flops=local * rows * 9 * (1 << 20),
            transcendentals=local * rows * H,
            bytes_accessed=20 << 20,
        ),
    )(scalars, x, cot, routes, router, w_in, w_down, a_in, b_in, a_down, b_down, packed)


def room_for(shape):
    return pl.pallas_call(
        lambda ref: None,
        out_specs=pl.BlockSpec(memory_space=pl.ANY),
        out_shape=jax.ShapeDtypeStruct(shape, bf16),
        name="room",
    )()


def join_kernel(left, right, result):
    result[...] = (left[...].astype(f32) + right[...].astype(f32)).astype(bf16)


def joined(left, right):
    rows = left.shape[0]
    steps = max(count for count in range(1, 5) if rows % (16 * count) == 0)
    block = pl.BlockSpec((rows // steps, MODEL_WIDTH), lambda n: (n, 0))
    return pl.pallas_call(
        join_kernel,
        grid=(steps,),
        in_specs=[block, block],
        out_specs=block,
        out_shape=jax.ShapeDtypeStruct(left.shape, bf16),
        compiler_params=params_of(1),
        name="joined",
    )(left, right)


def finish_kernel(mid, here, far, result):
    result[...] = (mid[...] + here[...].astype(f32) + far[...].astype(f32)).astype(bf16)


def finish(mid, here, far):
    rows = mid.shape[0]
    block = pl.BlockSpec((rows // 4, MODEL_WIDTH), lambda n: (n, 0))
    return pl.pallas_call(
        finish_kernel,
        grid=(4,),
        in_specs=[block] * 3,
        out_specs=block,
        out_shape=jax.ShapeDtypeStruct(mid.shape, bf16),
        compiler_params=params_of(1),
        name="finish",
    )(mid, here, far)


def open_back_kernel(count, order, cot, mid, gain, gates, router, weight_a, weight_b, low_map, up_map, low, att, *rest):
    parts = rest[:count]
    sums = rest[count : 3 * count]
    grad_mid, grad_att, grad_up, grad_low, columns = rest[3 * count :]
    gate_value = gates[...]
    half = gate_value.shape[0] // 2
    sides = []
    for side in range(2):
        value = None
        for at in range(count):
            pair = sums[2 * at + side][...].astype(f32)
            pair = pair[:half] + pair[half:]
            value = pair if value is None else value + pair
        sides.append(value)
    gate_grad = jnp.concatenate(sides, 0)
    logit = gate_value * (gate_grad - jnp.sum(gate_value * gate_grad, 0, keepdims=True))
    first = logit.astype(bf16)
    left = logit - first.astype(f32)
    second = left.astype(bf16)
    third = (left - second.astype(f32)).astype(bf16)
    grad = tn(first, router[...]) + (tn(second, router[...]) + tn(third, router[...]))
    for piece in parts:
        grad = grad + piece[...].astype(f32)
    total = cot[...].astype(f32) + norm_back(mid[...], gain[...].astype(f32), grad)
    grad_mid[...] = total
    branch = total.astype(bf16)
    low_grad = nt(branch, up_map[...]).astype(bf16)
    columns[...] = nn(low_grad, low_map[...])
    for side, weight in enumerate((weight_a, weight_b)):
        value = nt(branch, weight[...])
        for at in range(BLOCKS // 2):
            columns[:, column(order, side * BLOCKS // 2 + at)] += value[:, at * BLOCK : (at + 1) * BLOCK]
    grad_att[...] = columns[...].astype(bf16)
    up_part = tn(low[...], branch)
    low_part = tn(low_grad, att[...])

    @pl.when(pl.program_id(0) == 0)
    def _():
        grad_up[...] = up_part
        grad_low[...] = low_part

    @pl.when(pl.program_id(0) > 0)
    def _():
        grad_up[...] += up_part
        grad_low[...] += low_part


def open_back(order, cot, mid, gain, gates, router, weights, low_map, up_map, low, att, parts):
    rows = cot.shape[0]
    block = 256
    ranks = low_map.shape[0]
    experts = gates.shape[0]
    full = lambda shape: pl.BlockSpec(shape, lambda n, s: (0, 0))
    part = lambda width: pl.BlockSpec((block, width), lambda n, s: (n, 0))
    count = len(parts)
    below = rows // experts
    sums = [
        pl.BlockSpec((experts, block), lambda n, s: (below, n)),
        pl.BlockSpec((experts, block), lambda n, s: (below, rows // block + n)),
    ]

    def body(*refs):
        open_back_kernel(count, *refs)

    return pl.pallas_call(
        body,
        grid_spec=pltpu.PrefetchScalarGridSpec(
            num_scalar_prefetch=1,
            grid=(rows // block,),
            in_specs=[
                part(MODEL_WIDTH),
                part(MODEL_WIDTH),
                full((1, MODEL_WIDTH)),
                pl.BlockSpec((experts, block), lambda n, s: (0, n)),
                full((experts, MODEL_WIDTH)),
                *halves(weights, MODEL_WIDTH, lambda n: 0),
                full((ranks, QD)),
                full((ranks, MODEL_WIDTH)),
                part(ranks),
                part(QD),
            ]
            + [part(MODEL_WIDTH)] * count
            + sums * count,
            out_specs=[
                part(MODEL_WIDTH),
                part(QD),
                full((ranks, MODEL_WIDTH)),
                full((ranks, QD)),
            ],
            scratch_shapes=[pltpu.VMEM((block, QD), f32)],
        ),
        out_shape=[
            jax.ShapeDtypeStruct((rows, MODEL_WIDTH), f32),
            jax.ShapeDtypeStruct((rows, QD), bf16),
            jax.ShapeDtypeStruct((ranks, MODEL_WIDTH), f32),
            jax.ShapeDtypeStruct((ranks, QD), f32),
        ],
        compiler_params=params_of(1),
        name="open_back",
        cost_estimate=pl.CostEstimate(
            flops=2 * rows * QD * MODEL_WIDTH, transcendentals=0, bytes_accessed=14 << 20
        ),
    )(
        order, cot, mid, gain, gates, router, *weights, low_map, up_map, low, att, *parts,
        *[piece for piece in parts for _ in range(2)],
    )


def adapters_back_kernel(
    grad_query, grad_key, grad_value, low, normed, up_map, low_there, up_there, low_out, *results
):
    pieces = (grad_query, grad_key, grad_value)
    bounds = (0, QD, QD + KD, QKV)
    back = None
    ups = []
    for at in range(3):
        block = pieces[at][...]
        ups.append(tn(low[...], block)[at * R : (at + 1) * R])
        part = nt(block, up_map[:, bounds[at] : bounds[at + 1]])
        back = part if back is None else back + part
    value = back.astype(bf16)
    low_out[...] = value
    lows = tn(value, normed[...]) + low_there[...]
    if len(results) == 2:
        grad_up, grad_low = results
        grad_low[...] = lows
        for at in range(3):
            grad_up[:, bounds[at] : bounds[at + 1]] = ups[at]
        return
    (packed,) = results
    grad_up = jnp.concatenate(ups, 1)
    grad_out = up_there[3 * R :, :]
    small = BLOCK // 4
    lane = lanes_of((R, BLOCK))
    for owner in range(packed.shape[0]):
        tile = slice(owner // 4 * BLOCK, (owner // 4 + 1) * BLOCK)
        offset = owner % 4 * small
        first = jnp.zeros((R, BLOCK), f32)
        for at in range(4):
            piece = lows[at * R : (at + 1) * R, tile]
            shift = (at * small - offset) % BLOCK
            piece = pltpu.roll(piece, shift, 1) if shift else piece
            first = jnp.where((lane >= at * small) & (lane < (at + 1) * small), piece, first)
        piece = grad_up[:, owner // 2 * BLOCK : (owner // 2 + 1) * BLOCK]
        piece = pltpu.roll(piece, BLOCK // 2, 1) if owner % 2 else piece
        other = grad_out[:, tile]
        shift = (2 * small - offset) % BLOCK
        other = pltpu.roll(other, shift, 1) if shift else other
        packed[owner, :, :BLOCK] = first
        packed[owner, :, BLOCK:] = jnp.where(
            lane < 2 * small, piece, jnp.where(lane < 3 * small, other, 0.0)
        )


def adapters_back(grad_query, grad_key, grad_value, low, normed, up_map, low_there, up_there, devices):
    rows = normed.shape[0]
    ranks = up_map.shape[0]
    if devices * BLOCK // 4 == MODEL_WIDTH:
        results = [jax.ShapeDtypeStruct((devices, R, 2 * BLOCK), f32)]
    else:
        results = [
            jax.ShapeDtypeStruct((R, QKV), f32),
            jax.ShapeDtypeStruct((ranks, MODEL_WIDTH), f32),
        ]
    back_low, *results = pl.pallas_call(
        adapters_back_kernel,
        out_shape=[jax.ShapeDtypeStruct((rows, ranks), bf16)] + results,
        compiler_params=pltpu.CompilerParams(vmem_limit_bytes=56 * 1024 * 1024),
        name="adapters_back",
        cost_estimate=pl.CostEstimate(
            flops=6 * rows * 256 * QKV, transcendentals=0, bytes_accessed=4 << 20
        ),
    )(grad_query, grad_key, grad_value, low, normed, up_map, low_there, up_there)
    if len(results) == 1:
        return results[0], back_low
    grad_up, grad_low = results
    small = MODEL_WIDTH // devices
    packed = jnp.concatenate(
        [
            grad_low.reshape(4, R, devices, small).transpose(2, 1, 0, 3).reshape(devices, R, 4 * small),
            grad_up.reshape(R, devices, 2 * small).transpose(1, 0, 2),
            up_there[3 * R :].reshape(R, devices, small).transpose(1, 0, 2),
            jnp.zeros((devices, R, small), f32),
        ],
        -1,
    )
    return packed, back_low


def input_back_kernel(
    order, grad_query, grad_key, grad_value, low, weight_a, weight_b, low_map, hid, gain, mid, grad, columns
):
    columns[...] = nn(low[...], low_map[...])
    for side, weight in enumerate((weight_a, weight_b)):
        value = nt(grad_query[...], weight[:, :QD])
        value = value + nt(grad_key[...], weight[:, QD : QD + KD])
        value = value + nt(grad_value[...], weight[:, QD + KD :])
        for at in range(BLOCKS // 2):
            columns[:, column(order, side * BLOCKS // 2 + at)] += value[:, at * BLOCK : (at + 1) * BLOCK]
    rows = hid[...].astype(f32)
    grad[...] = (mid[...] + norm_back(rows, gain[...].astype(f32), columns[...])).astype(bf16)


def input_back(order, grad_query, grad_key, grad_value, low, weights, low_map, hidden, gain, mid):
    rows = hidden.shape[0]
    block = 256
    ranks = low_map.shape[0]
    full = lambda shape: pl.BlockSpec(shape, lambda n, s: (0, 0))
    part = lambda width: pl.BlockSpec((block, width), lambda n, s: (n, 0))
    return pl.pallas_call(
        input_back_kernel,
        grid_spec=pltpu.PrefetchScalarGridSpec(
            num_scalar_prefetch=1,
            grid=(rows // block,),
            in_specs=[
                part(QD),
                part(KD),
                part(KD),
                part(ranks),
                *halves(weights, QKV, lambda n: 0),
                full((ranks, MODEL_WIDTH)),
                part(MODEL_WIDTH),
                full((1, MODEL_WIDTH)),
                part(MODEL_WIDTH),
            ],
            out_specs=part(MODEL_WIDTH),
            scratch_shapes=[pltpu.VMEM((block, MODEL_WIDTH), f32)],
        ),
        out_shape=jax.ShapeDtypeStruct((rows, MODEL_WIDTH), bf16),
        compiler_params=params_of(1),
        name="input_back",
        cost_estimate=pl.CostEstimate(
            flops=2 * rows * QKV * MODEL_WIDTH, transcendentals=0, bytes_accessed=12 << 20
        ),
    )(order, grad_query, grad_key, grad_value, low, *weights, low_map, hidden, gain, mid)


def sum_experts_kernel(ids, pieces, a_in, b_in, a_down, b_down, acc):
    local = a_in.shape[0]
    small = a_down.shape[-1]
    acc[...] = jnp.zeros_like(acc)

    def step(index, carry):
        acc[ids[index]] += pieces[index].astype(f32)
        return carry

    lax.fori_loop(0, pieces.shape[0], step, 0)
    for e in range(local):
        a_in[e] = acc[:, e * 2 * R : (e + 1) * 2 * R, :]
        at = local * 2 * R + e * R
        b_down[e] = acc[:, at : at + R, :]
        at = local * 3 * R + e * R
        both = acc[:, at : at + R, :]
        b_in[e, :, 0] = both[:, :, :small]
        b_in[e, :, 1] = both[:, :, small:]
        at = local * 4 * R + e // 2 * R
        a_down[e] = acc[:, at : at + R, e % 2 * small : (e % 2 + 1) * small]


def sum_experts(ids, pieces, local):
    height = pieces.shape[1]
    lanes = pieces.shape[2]
    small = lanes // 2
    vmem = pl.BlockSpec(memory_space=pltpu.VMEM)
    return pl.pallas_call(
        sum_experts_kernel,
        in_specs=[pl.BlockSpec(memory_space=pltpu.SMEM), vmem],
        out_specs=[vmem, vmem, vmem, vmem],
        out_shape=[
            jax.ShapeDtypeStruct((local, NA, 2 * R, lanes), f32),
            jax.ShapeDtypeStruct((local, NA, 2, R, small), f32),
            jax.ShapeDtypeStruct((local, NA, R, small), f32),
            jax.ShapeDtypeStruct((local, NA, R, lanes), f32),
        ],
        scratch_shapes=[pltpu.VMEM((NA, height, lanes), f32)],
        compiler_params=pltpu.CompilerParams(vmem_limit_bytes=56 * 1024 * 1024),
        name="sum_experts",
    )(ids, pieces)


def sum_mixer_kernel(ids, pieces, grad_low, grad_up, grad_out, acc):
    width = grad_low.shape[-1]
    acc[...] = jnp.zeros_like(acc)

    def step(index, carry):
        acc[ids[index]] += pieces[index]
        return carry

    lax.fori_loop(0, pieces.shape[0], step, 0)
    total = acc[...]
    for at in range(4):
        grad_low[at] = total[:, :, at * width : (at + 1) * width]
    grad_up[...] = total[:, :, 4 * width : 6 * width]
    grad_out[...] = total[:, :, 6 * width : 7 * width]


def sum_mixer(ids, pieces):
    width = pieces.shape[2] // 8
    vmem = pl.BlockSpec(memory_space=pltpu.VMEM)
    return pl.pallas_call(
        sum_mixer_kernel,
        in_specs=[pl.BlockSpec(memory_space=pltpu.SMEM), vmem],
        out_specs=[vmem, vmem, vmem],
        out_shape=[
            jax.ShapeDtypeStruct((4, NA, R, width), f32),
            jax.ShapeDtypeStruct((NA, R, 2 * width), f32),
            jax.ShapeDtypeStruct((NA, R, width), f32),
        ],
        scratch_shapes=[pltpu.VMEM((NA, R, 8 * width), f32)],
        compiler_params=pltpu.CompilerParams(vmem_limit_bytes=56 * 1024 * 1024),
        name="sum_mixer",
    )(ids, pieces)


def rope_tables(rows):
    half = HS // 2
    frequency = (10000.0 ** (-2.0 * np.arange(half, dtype=np.float32) / HS)).astype(np.float32)
    angles = np.arange(rows, dtype=np.float32)[:, None] * frequency[None, :]
    cos = np.cos(angles.astype(np.float64)).astype(np.float32)
    sin = np.sin(angles.astype(np.float64)).astype(np.float32)
    return (
        jnp.asarray(np.concatenate([cos, cos, cos, cos], 1)),
        jnp.asarray(np.concatenate([-sin, sin, -sin, sin], 1)),
    )


def swap(value, bit):
    return lax.ppermute(value, "dp", [(at, at ^ bit) for at in range(BLOCKS)])


def both_neighbours(weight):
    return swap(weight, 2), swap(weight, 4)


def across(pair):
    one, two = pair
    middle = one.shape[0] // 2
    return swap(two[:middle], 2), swap(one[middle:], 4)


def tied(*values):
    return lax.optimization_barrier(values)


def order_of(row):
    if lax.axis_size("dp") != BLOCKS:
        return jnp.arange(BLOCKS, dtype=jnp.int32)
    return row.astype(jnp.int32) ^ jnp.array([0, 2, 4, 6, 1, 3, 5, 7], jnp.int32)


def to_owners(packed, owners, local):
    split = owners // BLOCKS
    if split == 1:
        return packed
    slots = packed.shape[1]
    edge = local * 3 * R
    wide = packed[:, :, :edge].reshape(BLOCKS, slots, edge, split, BLOCK // split)
    wide = wide.transpose(0, 3, 1, 2, 4).reshape(owners, slots, edge, BLOCK // split)
    rest = packed.shape[2] - edge
    narrow = packed[:, :, edge:].reshape(BLOCKS, slots, rest, 2, split, BLOCK // 2 // split)
    narrow = narrow.transpose(0, 4, 1, 2, 3, 5).reshape(owners, slots, rest, BLOCK // split)
    return jnp.concatenate([wide, narrow], 2)


def on_device(
    hidden,
    cotangent,
    lengths,
    adapter_ids,
    routes,
    attn_gain,
    ffn_gain,
    query_key_value_weight,
    w_out,
    w_router,
    w_gate_up,
    w_down,
    attention_lowmap,
    attention_query_key_value_upmap,
    attention_output_upmap,
    expert_gate_up_lowmap,
    expert_gate_up_upmap,
    expert_down_lowmap,
    expert_down_upmap,
):
    groups = lax.axis_size("expert")
    owners = lax.axis_size("dp")
    place = lax.axis_index("expert")
    row = lax.axis_index("dp")
    devices = groups * owners
    sequence = row * groups + place
    rows = hidden.shape[0]
    experts = w_router.shape[1]
    local = w_gate_up.shape[0]
    width = MODEL_WIDTH // owners
    attn_gain = attn_gain.reshape(1, MODEL_WIDTH)
    ffn_gain = ffn_gain.reshape(1, MODEL_WIDTH)
    length = lax.dynamic_slice(lengths, (sequence,), (1,))
    forward = [(at, (at + 1) % groups) for at in range(groups)]
    backward = [(at, (at - 1) % groups) for at in range(groups)]

    mine = lax.dynamic_slice(adapter_ids.reshape(owners, groups), (0, place), (owners, 1))[:, 0]
    low_turned = attention_lowmap.transpose(1, 0, 3, 2).reshape(NA, 4 * R, width)
    up_turned = (
        attention_query_key_value_upmap.reshape(NA, R, 2, width)
        .transpose(0, 2, 1, 3)
        .reshape(NA, 2 * R, width)
    )
    adapters = jnp.concatenate([low_turned, up_turned, attention_output_upmap], 1)[mine]
    adapters = lax.all_to_all(adapters, "dp", 0, 0, tiled=True)
    order = order_of(row)
    plain = jnp.arange(BLOCKS, dtype=jnp.int32)
    cots = {0: cotangent, 1: lax.ppermute(cotangent, "expert", forward)}
    if owners == BLOCKS:
        pair_in = both_neighbours(query_key_value_weight)
        across_in = across(pair_in)
        w_out, across_in = tied(w_out, across_in)
        near_in = jnp.concatenate([query_key_value_weight, *pair_in, *across_in], 0)
        if groups > 2:
            near_in, cotangent, cots[1] = tied(near_in, cotangent, cots[1])
        weight_in = near_in, swap(near_in, 1)
    else:
        whole = lax.all_gather(query_key_value_weight, "dp", axis=0, tiled=True)
        weight_in = whole, whole
    if groups > 2:
        cots[groups - 1] = lax.ppermute(cotangent, "expert", backward)
    weight_out = lax.all_gather(w_out, "dp", axis=0, tiled=True)
    weight_out = weight_out, weight_out

    low_map = adapters[:, : 4 * R].transpose(1, 0, 2).reshape(4 * R, MODEL_WIDTH)
    up = (
        adapters[:, 4 * R : 6 * R]
        .reshape(owners, 2, R, width)
        .transpose(2, 0, 1, 3)
        .reshape(R, QKV)
    )
    up_out = adapters[:, 6 * R :].transpose(1, 0, 2).reshape(R, MODEL_WIDTH)
    column = jnp.arange(QKV, dtype=jnp.int32)
    part = jnp.where(column < QD, 0, jnp.where(column < QD + KD, 1, 2))
    up_map = jnp.where(
        part[None, None, :] == jnp.arange(4, dtype=jnp.int32)[:, None, None], up[None], 0
    ).reshape(4 * R, QKV)
    up_out_map = jnp.concatenate([jnp.zeros((3 * R, MODEL_WIDTH), bf16), up_out], 0)

    cos, sin = rope_tables(rows)

    qkv, low, normed_in = project(order, hidden, attn_gain, weight_in, low_map, up_map, cos, sin)
    if groups > 3:
        cots[1], low = tied(cots[1], low)
    for at in range(2, groups - 1):
        cots[at] = lax.ppermute(cots[at - 1], "expert", forward)
    attended, lse = attend(length, qkv)
    mid, normed_mid, low_out = close_mixer(
        plain, attended, hidden, ffn_gain, weight_out, low_map, up_out_map
    )

    first = place * local
    routes_here = (routes - first + experts) % experts
    router = jnp.roll(w_router.T, -first, axis=0)
    router_wide = jnp.concatenate(
        [router, jnp.zeros((128 - experts, MODEL_WIDTH), router.dtype)], 0
    )
    a_in = expert_gate_up_lowmap.transpose(0, 1, 3, 2)
    a_down = expert_down_lowmap.transpose(0, 1, 3, 2)

    offsets = [0, 1] + [groups - 1] * (groups > 2) + list(range(2, groups - 1))
    offset = jnp.array(offsets, jnp.int32)
    source = (place - offset + groups) % groups
    tags = adapter_ids.reshape(owners, groups)[:, source]
    slot = jnp.arange(groups, dtype=jnp.int32)
    table = jnp.stack(
        [
            source,
            lax.dynamic_slice(tags, (row, 0), (1, groups))[0],
            offset * local,
            slot,
        ],
        1,
    )

    xs = {0: normed_mid, 1: lax.ppermute(normed_mid, "expert", forward)}
    packed = room_for((BLOCKS, groups, local * 9 * R // 2, BLOCK))
    ran = {}
    for at, offset in enumerate(offsets):
        *ran[offset], gate_part, packed = run_experts(
            table[at],
            xs[offset],
            cots[offset],
            routes_here,
            router_wide,
            w_gate_up,
            w_down,
            a_in,
            expert_gate_up_upmap,
            a_down,
            expert_down_upmap,
            experts,
            packed,
        )
        if at == 0:
            gates = gate_part
            if groups > 2:
                normed_mid, packed = tied(normed_mid, packed)
                xs[groups - 1] = lax.ppermute(normed_mid, "expert", backward)
        elif at < groups - 2:
            value, packed = tied(xs[at], packed)
            xs[at + 1] = lax.ppermute(value, "expert", forward)
        if at == 2:
            ran[1][1], packed = tied(ran[1][1], packed)

    pieces = lax.all_to_all(to_owners(packed, owners, local), "dp", 0, 0, tiled=True)
    pieces = pieces.reshape(devices, pieces.shape[2], width)
    g_a_in, g_b_in, g_a_down, g_b_down = sum_experts(tags.reshape(devices), pieces, local)

    grad_far = lax.ppermute(ran[1][1], "expert", forward)
    for offset in range(2, groups):
        grad_part = joined(ran[offset][1], grad_far)
        if offset == groups - 1:
            grad_part, g_a_down = tied(grad_part, g_a_down)
        grad_far = lax.ppermute(grad_part, "expert", forward)
    out_part, grad_far = tied(ran[1][0], grad_far)
    out_far = lax.ppermute(out_part, "expert", forward)
    grad_mid, grad_attended, grad_up_out, grad_low_out = open_back(
        plain,
        cotangent,
        mid,
        ffn_gain,
        gates,
        router,
        weight_out,
        low_map,
        up_out_map,
        low_out,
        attended,
        [ran[0][1], grad_far],
    )
    grad_query, grad_key, grad_value = attend_back(length, qkv, grad_attended, lse, cos, sin)
    if groups > 2:
        out_far, grad_query = tied(out_far, grad_query)
        out_far = lax.ppermute(joined(ran[2][0], out_far), "expert", forward)
    packed, back_low = adapters_back(
        grad_query, grad_key, grad_value, low, normed_in, up_map, grad_low_out, grad_up_out, devices
    )
    packed = lax.all_to_all(packed, ("dp", "expert"), 0, 0, tiled=True)

    grad_hidden = input_back(
        order, grad_query, grad_key, grad_value, back_low, weight_in, low_map, hidden, attn_gain, grad_mid
    )
    if groups > 3:
        out_far, grad_hidden, packed = tied(out_far, grad_hidden, packed)
    for offset in range(3, groups):
        out_far = lax.ppermute(joined(ran[offset][0], out_far), "expert", forward)
    m_a, m_b, m_o = sum_mixer(adapter_ids, packed)
    out = finish(mid, ran[0][0], out_far)
    return (
        out,
        grad_hidden,
        m_a.transpose(0, 1, 3, 2),
        m_b,
        m_o,
        g_a_in.transpose(0, 1, 3, 2),
        g_b_in,
        g_a_down.transpose(0, 1, 3, 2),
        g_b_down,
    )


def solution(mesh):
    in_specs = (
        P(("dp", "expert"), None),
        P(("dp", "expert"), None),
        P(),
        P(),
        P("dp", None),
        P(),
        P(),
        P("dp", None),
        P("dp", None),
        P(),
        P("expert", None, None),
        P("expert", None, None),
        P(None, None, "dp", None),
        P(None, None, "dp"),
        P(None, None, "dp"),
        P("expert", None, None, None),
        P("expert", None, None, None, None),
        P("expert", None, None, None),
        P("expert", None, None, None),
    )
    out_specs = (
        P(("dp", "expert"), None),
        P(("dp", "expert"), None),
        P(None, None, ("dp", "expert"), None),
        P(None, None, ("dp", "expert")),
        P(None, None, ("dp", "expert")),
        P("expert", None, "dp", None),
        P("expert", None, None, None, "dp"),
        P("expert", None, "dp", None),
        P("expert", None, None, "dp"),
    )
    return jax.shard_map(
        on_device, mesh=mesh, in_specs=in_specs, out_specs=out_specs, check_vma=False
    )
```

```python
import numpy as np
import jax
import jax.numpy as jnp
from jax import lax
from jax.experimental import pallas as pl
from jax.experimental.pallas import tpu as pltpu
from jax.sharding import PartitionSpec as P

MODEL_WIDTH = 1024
HQ = 16
KVH = 8
HS = 64
H = 512
TOP = 8
R = 16
NA = 8
QD = HQ * HS
KD = KVH * HS
QKV = QD + 2 * KD

epsilon = 1e-06
f32 = jnp.float32
bf16 = jnp.bfloat16


def nn(left, right):
    return lax.dot_general(left, right, (((1,), (0,)), ((), ())), preferred_element_type=f32)


def nt(left, right):
    return lax.dot_general(left, right, (((1,), (1,)), ((), ())), preferred_element_type=f32)


def tn(left, right):
    return lax.dot_general(left, right, (((0,), (0,)), ((), ())), preferred_element_type=f32)


def lanes_of(shape):
    return lax.broadcasted_iota(jnp.int32, shape, len(shape) - 1)


def row_scale(rows):
    return lax.rsqrt(jnp.mean(rows * rows, -1, keepdims=True) + epsilon)


def norm_back(rows, gain, grad):
    scale = row_scale(rows)
    scaled = grad * gain
    return scale * scaled - rows * (scale * scale * scale) * jnp.mean(
        rows * scaled, -1, keepdims=True
    )


def rope_swap(rows):
    width = rows.shape[-1]
    lane = lanes_of(rows.shape)
    return jnp.where(
        lane % HS < HS // 2,
        pltpu.roll(rows, width - HS // 2, 1),
        pltpu.roll(rows, HS // 2, 1),
    )


def both_halves(pair, half):
    rows = pair.astype(f32)
    lane = lanes_of(rows.shape)
    rolled = pltpu.roll(rows, HS, 1)
    keep = (lane < HS) == (half == 0)
    return jnp.where(keep, rows, rolled).astype(bf16)


def stacked_heads(pair):
    lane = lanes_of(pair.shape)
    zero = jnp.zeros_like(pair)
    return jnp.concatenate(
        [jnp.where(lane < HS, pair, zero), jnp.where(lane < HS, zero, pair)], 0
    )


def params_of(count):
    return pltpu.CompilerParams(
        dimension_semantics=("arbitrary",) * count, vmem_limit_bytes=56 * 1024 * 1024
    )


BLOCK = 128
BLOCKS = MODEL_WIDTH // BLOCK
HALF = MODEL_WIDTH // 2


def column(order, at):
    return pl.ds(pl.multiple_of(order[at] * BLOCK, BLOCK), BLOCK)


def halves(weights, width, index):
    there = 1 if weights[0] is weights[1] else 0
    return [
        pl.BlockSpec((HALF, width), lambda n, s: (0, index(n))),
        pl.BlockSpec((HALF, width), lambda n, s: (there, index(n))),
    ]


def project_kernel(
    order, hid, gain, weight_a, weight_b, low_map, up_map, cos, sin, qkv, low, normed, turned_rows
):
    step = pl.program_id(0)
    blocks = pl.num_programs(0)

    @pl.when(step == 0)
    def _():
        rows = hid[...].astype(f32)
        value = (rows * row_scale(rows) * gain[...].astype(f32)).astype(bf16)
        normed[...] = value
        low[...] = nt(value, low_map[...]).astype(bf16)
        for at in range(BLOCKS):
            turned_rows[:, at * BLOCK : (at + 1) * BLOCK] = normed[:, column(order, at)]

    value = (
        nn(turned_rows[:, :HALF], weight_a[...])
        + nn(turned_rows[:, HALF:], weight_b[...])
        + nn(low[...], up_map[...])
    )

    @pl.when(step < blocks * 3 // 4)
    def _():
        for part in range(value.shape[1] // 128):
            piece = value[:, part * 128 : part * 128 + 128]
            turned = piece * cos[...] + rope_swap(piece) * sin[...]
            qkv[:, part * 128 : part * 128 + 128] = turned.astype(bf16)

    @pl.when(step >= blocks * 3 // 4)
    def _():
        qkv[...] = value.astype(bf16)


def project(order, hidden, gain, weights, low_map, up_map, cos, sin):
    rows = hidden.shape[0]
    block = 512
    ranks = low_map.shape[0]
    full = lambda shape: pl.BlockSpec(shape, lambda n, s: (0, 0))
    return pl.pallas_call(
        project_kernel,
        grid_spec=pltpu.PrefetchScalarGridSpec(
            num_scalar_prefetch=1,
            grid=(QKV // block,),
            in_specs=[
                full((rows, MODEL_WIDTH)),
                full((1, MODEL_WIDTH)),
                *halves(weights, block, lambda n: n),
                full((ranks, MODEL_WIDTH)),
                pl.BlockSpec((ranks, block), lambda n, s: (0, n)),
                full((rows, 128)),
                full((rows, 128)),
            ],
            out_specs=[
                pl.BlockSpec((rows, block), lambda n, s: (0, n)),
                full((rows, ranks)),
                full((rows, MODEL_WIDTH)),
            ],
            scratch_shapes=[pltpu.VMEM((rows, MODEL_WIDTH), bf16)],
        ),
        out_shape=[
            jax.ShapeDtypeStruct((rows, QKV), bf16),
            jax.ShapeDtypeStruct((rows, ranks), bf16),
            jax.ShapeDtypeStruct((rows, MODEL_WIDTH), bf16),
        ],
        compiler_params=params_of(1),
        name="project",
        cost_estimate=pl.CostEstimate(
            flops=2 * rows * QKV * MODEL_WIDTH, transcendentals=0, bytes_accessed=8 << 20
        ),
    )(order, hidden, gain, *weights, low_map, up_map, cos, sin)


ROWB = 128


def length_column(length, count):
    key = lax.broadcasted_iota(jnp.int32, (count, 1), 0)
    return jnp.where(key < length, 0.0, -1e30)


def causal_block():
    key = lax.broadcasted_iota(jnp.int32, (ROWB, 2 * ROWB), 0)
    return jnp.where(key <= lanes_of((ROWB, 2 * ROWB)) % ROWB, 0.0, -1e30)


def masked_scores(queries, keys, start, bias, causal):
    count = start + ROWB
    scores = nt(keys[:count], (queries.astype(f32) * 0.125).astype(bf16))
    near = scores[start:] + (bias[start:count] + causal)
    if start == 0:
        return near
    return jnp.concatenate([scores[:start] + bias[:start], near], 0)


def attend_kernel(scalars, query, key, value, result, lse):
    half = pl.program_id(0) % 2
    keys = both_halves(key[...], half)
    values = both_halves(value[...], half)
    rows = query.shape[0]
    bias = length_column(scalars[0], rows)
    causal = causal_block()
    for start in range(0, rows, ROWB):
        count = start + ROWB
        stacked = stacked_heads(query[start:count, :])
        scores = masked_scores(stacked, keys, start, bias, causal)
        top = jnp.max(scores, 0, keepdims=True)
        shifted = jnp.exp(scores - top)
        total = jnp.sum(shifted, 0, keepdims=True)
        prob = (shifted * (1.0 / total)).astype(bf16)
        mixed = tn(prob, values[:count])
        lane = lanes_of((ROWB, 128))
        result[start:count, :] = jnp.where(lane < HS, mixed[:ROWB], mixed[ROWB:]).astype(bf16)
        logs = top + jnp.log(total)
        lse[0, 0:1, start:count] = logs[:, :ROWB]
        lse[0, 1:2, start:count] = logs[:, ROWB:]


def attend(length, qkv):
    rows = qkv.shape[0]
    pairs = KVH
    return pl.pallas_call(
        attend_kernel,
        grid_spec=pltpu.PrefetchScalarGridSpec(
            num_scalar_prefetch=1,
            grid=(pairs,),
            in_specs=[
                pl.BlockSpec((rows, 128), lambda g, s: (0, g)),
                pl.BlockSpec((rows, 128), lambda g, s: (0, QD // 128 + g // 2)),
                pl.BlockSpec((rows, 128), lambda g, s: (0, (QD + KD) // 128 + g // 2)),
            ],
            out_specs=[
                pl.BlockSpec((rows, 128), lambda g, s: (0, g)),
                pl.BlockSpec((1, 2, rows), lambda g, s: (g, 0, 0)),
            ],
        ),
        out_shape=[
            jax.ShapeDtypeStruct((rows, QD), bf16),
            jax.ShapeDtypeStruct((pairs, 2, rows), f32),
        ],
        compiler_params=params_of(1),
        name="attend",
        cost_estimate=pl.CostEstimate(
            flops=8 * rows * rows * QD, transcendentals=rows * rows * HQ, bytes_accessed=4 << 20
        ),
    )(length, qkv, qkv, qkv)


def attend_back_kernel(
    scalars, query, key, value, grad, lse, cos, sin, grad_query, grad_key, grad_value, key_acc, value_acc
):
    half = pl.program_id(0) % 2
    keys = both_halves(key[...], half)
    values = both_halves(value[...], half)
    rows = query.shape[0]
    bias = length_column(scalars[0], rows)
    causal = causal_block()
    for start in reversed(range(0, rows, ROWB)):
        count = start + ROWB
        stacked = stacked_heads(query[start:count, :])
        grads = stacked_heads(grad[start:count, :])
        scores = masked_scores(stacked, keys, start, bias, causal)
        logs = jnp.concatenate([lse[0, 0:1, start:count], lse[0, 1:2, start:count]], 1)
        prob = jnp.exp(scores - logs)
        grad_prob = nt(values[:count], grads)
        delta = jnp.sum(prob * grad_prob, 0, keepdims=True)
        grad_score = (prob * (grad_prob - delta)).astype(bf16)
        mixed = tn(grad_score, keys[:count])
        lane = lanes_of((ROWB, 128))
        turned = 0.125 * jnp.where(lane < HS, mixed[:ROWB], mixed[ROWB:])
        turned = turned * cos[start:count, :] - rope_swap(turned) * sin[start:count, :]
        grad_query[start:count, :] = turned.astype(bf16)
        key_part = nn(grad_score, stacked)
        value_part = nn(prob.astype(bf16), grads)
        if count == rows:
            key_acc[...] = key_part
            value_acc[...] = value_part
        else:
            key_acc[:count, :] += key_part
            value_acc[:count, :] += value_part
    total = key_acc[...]
    total = 0.125 * (total + pltpu.roll(total, HS, 1))
    total = (total * cos[...] - rope_swap(total) * sin[...]).astype(bf16)
    other = value_acc[...]
    other = (other + pltpu.roll(other, HS, 1)).astype(bf16)

    @pl.when(half == 0)
    def _():
        grad_key[...] = total
        grad_value[...] = other

    @pl.when(half == 1)
    def _():
        low_half = lanes_of(total.shape) < HS
        grad_key[...] = jnp.where(low_half, grad_key[...], total)
        grad_value[...] = jnp.where(low_half, grad_value[...], other)


def attend_back(length, qkv, grad, lse, cos, sin):
    rows = qkv.shape[0]
    pairs = KVH
    return pl.pallas_call(
        attend_back_kernel,
        grid_spec=pltpu.PrefetchScalarGridSpec(
            num_scalar_prefetch=1,
            grid=(pairs,),
            in_specs=[
                pl.BlockSpec((rows, 128), lambda g, s: (0, g)),
                pl.BlockSpec((rows, 128), lambda g, s: (0, QD // 128 + g // 2)),
                pl.BlockSpec((rows, 128), lambda g, s: (0, (QD + KD) // 128 + g // 2)),
                pl.BlockSpec((rows, 128), lambda g, s: (0, g)),
                pl.BlockSpec((1, 2, rows), lambda g, s: (g, 0, 0)),
                pl.BlockSpec((rows, 128), lambda g, s: (0, 0)),
                pl.BlockSpec((rows, 128), lambda g, s: (0, 0)),
            ],
            out_specs=[
                pl.BlockSpec((rows, 128), lambda g, s: (0, g)),
                pl.BlockSpec((rows, 128), lambda g, s: (0, g // 2)),
                pl.BlockSpec((rows, 128), lambda g, s: (0, g // 2)),
            ],
            scratch_shapes=[pltpu.VMEM((rows, 128), f32), pltpu.VMEM((rows, 128), f32)],
        ),
        out_shape=[
            jax.ShapeDtypeStruct((rows, QD), bf16),
            jax.ShapeDtypeStruct((rows, KD), bf16),
            jax.ShapeDtypeStruct((rows, KD), bf16),
        ],
        compiler_params=params_of(1),
        name="attend_back",
        cost_estimate=pl.CostEstimate(
            flops=20 * rows * rows * QD, transcendentals=rows * rows * HQ, bytes_accessed=8 << 20
        ),
    )(length, qkv, qkv, qkv, grad, lse, cos, sin)


def close_kernel(order, att, hid, gain, weight_a, weight_b, low_map, up_map, mid, normed, low):
    low_value = nt(att[...], low_map[...]).astype(bf16)
    low[...] = low_value
    turned = jnp.concatenate([att[:, column(order, at)] for at in range(BLOCKS)], 1)
    stream = hid[...].astype(f32) + (
        nn(turned[:, :HALF], weight_a[...])
        + nn(turned[:, HALF:], weight_b[...])
        + nn(low_value, up_map[...])
    )
    mid[...] = stream
    normed[...] = (stream * row_scale(stream) * gain[...].astype(f32)).astype(bf16)


def close_mixer(order, att, hidden, gain, weights, low_map, up_map):
    rows = hidden.shape[0]
    block = 256
    ranks = low_map.shape[0]
    full = lambda shape: pl.BlockSpec(shape, lambda n, s: (0, 0))
    part = lambda width: pl.BlockSpec((block, width), lambda n, s: (n, 0))
    return pl.pallas_call(
        close_kernel,
        grid_spec=pltpu.PrefetchScalarGridSpec(
            num_scalar_prefetch=1,
            grid=(rows // block,),
            in_specs=[
                part(QD),
                part(MODEL_WIDTH),
                full((1, MODEL_WIDTH)),
                *halves(weights, MODEL_WIDTH, lambda n: QKV // MODEL_WIDTH),
                full((ranks, QD)),
                full((ranks, MODEL_WIDTH)),
            ],
            out_specs=[part(MODEL_WIDTH), part(MODEL_WIDTH), part(ranks)],
        ),
        out_shape=[
            jax.ShapeDtypeStruct((rows, MODEL_WIDTH), f32),
            jax.ShapeDtypeStruct((rows, MODEL_WIDTH), bf16),
            jax.ShapeDtypeStruct((rows, ranks), bf16),
        ],
        compiler_params=params_of(1),
        name="close_mixer",
        cost_estimate=pl.CostEstimate(
            flops=2 * rows * QD * MODEL_WIDTH, transcendentals=0, bytes_accessed=8 << 20
        ),
    )(order, att, hidden, gain, *weights, low_map, up_map)


def side_by_side(left, right):
    values = []
    for at in range(BLOCKS):
        tile = slice(at // 2 * BLOCK, (at // 2 + 1) * BLOCK)
        low_half = lanes_of((R, BLOCK)) < BLOCK // 2
        if at % 2 == 0:
            value = jnp.where(low_half, left[:, tile], pltpu.roll(right[:, tile], BLOCK // 2, 1))
        else:
            value = jnp.where(low_half, pltpu.roll(left[:, tile], BLOCK // 2, 1), right[:, tile])
        values.append(value.astype(bf16))
    return values


def expert_kernel(
    scalars,
    x,
    cot,
    routes,
    router,
    w_in,
    w_down,
    a_in,
    b_in,
    a_down,
    b_down,
    *rest,
):
    (
        sums_out,
        gates_out,
        packed,
        gates,
        gate_sums,
        low_in,
        low_in_turned,
        b_in_all,
        back_low,
        gated_low,
        back_in,
        acts,
        grads,
        low_grads,
        down_acc,
        out_acc,
        grad_acc,
    ) = rest[-17:]
    expert = pl.program_id(0)
    last = pl.num_programs(0) - 1
    rows = x.shape[0]
    block = rows
    local = a_in.shape[0]
    a_in_all = a_in[...].reshape(local * 2 * R, MODEL_WIDTH)
    a_down_all = a_down[...].reshape(local * R, H)
    b_down_all = b_down[...].reshape(local * R, MODEL_WIDTH)

    @pl.when(expert == 0)
    def _():
        logits = nt(x[...], router[...])
        lane = lanes_of(logits.shape)
        chosen = lane == routes[:, 0:1]
        for k in range(1, TOP):
            chosen = chosen | (lane == routes[:, k : k + 1])
        top = jnp.max(jnp.where(chosen, logits, -1e30), -1, keepdims=True)
        shifted = jnp.where(chosen, jnp.exp(jnp.where(chosen, logits - top, 0.0)), 0.0)
        weights = shifted / jnp.sum(shifted, -1, keepdims=True)
        gates[...] = weights
        gates_out[...] = weights.T[: gates_out.shape[0], :]
        low = nt(x[...], a_in_all)
        low_in[...] = low.astype(bf16)
        low_in_turned[...] = low.T.astype(bf16)
        back_low[...] = nt(cot[...], b_down_all)
        b_in_all[...] = jnp.zeros_like(b_in_all)
        for e in range(local):
            b_in_all[e * 2 * R : e * 2 * R + R, :H] = b_in[e, 0, 0]
            b_in_all[e * 2 * R + R : (e + 1) * 2 * R, H:] = b_in[e, 0, 1]
        gate_sums[...] = jnp.zeros_like(gate_sums)
        gated_low[...] = jnp.zeros_like(gated_low)
        back_in[...] = jnp.zeros_like(back_in)
        out_acc[...] = jnp.zeros_like(out_acc)
        grad_acc[...] = jnp.zeros_like(grad_acc)
        down_acc[...] = jnp.zeros_like(down_acc)

    def row_step(index, carry):
        at = pl.ds(pl.multiple_of(index * block, block), block)
        lane_in = lanes_of((block, local * 2 * R))
        lane_down = lanes_of((block, local * R))
        in_mine = (lane_in >= expert * 2 * R) & (lane_in < (expert + 1) * 2 * R)
        down_mine = (lane_down >= expert * R) & (lane_down < (expert + 1) * R)
        gate_all = gates[at, :]
        gate_lane = lanes_of(gate_all.shape) == expert
        weight = jnp.sum(jnp.where(gate_lane, gate_all, 0.0), -1, keepdims=True)
        mine = low_in[at, :]
        mine = jnp.where(in_mine, mine, jnp.zeros_like(mine))
        both = nn(x[at, :], w_in[0]) + nn(mine, b_in_all[...])
        gate = both[:, :H]
        upper = both[:, H:]
        sigmoid = jax.nn.sigmoid(gate)
        silu = gate * sigmoid
        act = (silu * upper).astype(bf16)
        acts[at, :] = act
        act_wide = act.astype(f32)
        low = jnp.where(down_mine, nt(act, a_down_all), 0.0).astype(bf16).astype(f32)
        plain = nt(cot[at, :], w_down[0])
        low_plain = back_low[at, :]
        dots = jnp.sum(act_wide * plain, -1, keepdims=True) + jnp.sum(
            low * low_plain, -1, keepdims=True
        )
        sum_lane = lanes_of(gate_all.shape) == expert + scalars[2]
        gate_sums[at, :] += jnp.where(sum_lane, dots, 0.0)
        low_grad = jnp.where(down_mine, weight * low_plain, 0.0).astype(bf16)
        low_grads[at, :] = low_grad
        grad_act = weight * plain + nn(low_grad, a_down_all)
        grad_first = grad_act * upper * sigmoid * (1.0 + gate * (1.0 - sigmoid))
        grad_second = grad_act * silu
        grad_both = jnp.concatenate(
            [grad_first.astype(bf16), grad_second.astype(bf16)], 1
        )
        grads[at, :] = grad_both
        gated_low[at, :] += (weight * low).astype(bf16)
        out_acc[at, :] += nn((weight * act_wide).astype(bf16), w_down[0])
        grad_acc[at, :] += nt(grad_both, w_in[0])
        low_back = jnp.where(in_mine, nt(grad_both, b_in_all[...]), 0.0)
        back_in[at, :] += low_back.astype(bf16)
        return carry

    lax.fori_loop(0, rows // block, row_step, 0)

    turned = low_in_turned[pl.ds(pl.multiple_of(expert * 2 * R, 2 * R), 2 * R), :]
    product = nn(turned, grads[...])
    first_b_in = local * 3 * R
    here = pl.ds(pl.multiple_of(first_b_in + expert * R, R), R)
    for at, value in enumerate(side_by_side(product[:R, :H], product[R:, H:])):
        packed[at, 0, here, :] = value
    down_acc[...] += tn(low_grads[...], acts[...])

    @pl.when(expert == last)
    def _():
        sums_out[:rows, :] = (grad_acc[...] + nn(back_in[...], a_in_all)).astype(bf16)
        experts = gates_out.shape[0]
        sums = gate_sums[...].T[:experts, :]
        sums = jnp.concatenate([sums[: experts // 2], sums[experts // 2 :]], 1)
        high = sums.astype(bf16).astype(f32)
        edge = rows + experts
        sums_out[rows:edge, :] = jnp.concatenate([high, sums - high], 0).astype(bf16)
        sums_out[edge:, :] = (out_acc[...] + nn(gated_low[...], b_down_all)).astype(bf16)
        wide = tn(back_in[...], x[...]).astype(bf16)
        tall = tn(gated_low[...], cot[...]).astype(bf16)
        for at in range(BLOCKS):
            columns = slice(at * BLOCK, (at + 1) * BLOCK)
            packed[at, 0, : local * 2 * R, :] = wide[:, columns]
            packed[at, 0, local * 2 * R : first_b_in, :] = tall[:, columns]
        for pair in range(local // 2):
            lower = down_acc[pair * 2 * R : pair * 2 * R + R, :]
            upper = down_acc[pair * 2 * R + R : (pair + 1) * 2 * R, :]
            row = local * 4 * R + pair * R
            for at, value in enumerate(side_by_side(lower, upper)):
                packed[at, 0, row : row + R, :] = value


def run_experts(
    scalars, x, cot, routes, router, w_in, w_down, a_in, b_in, a_down, b_down, experts, slots, packed
):
    rows = x.shape[0]
    local = w_in.shape[0]
    ranks_in = local * 2 * R
    ranks_down = local * R
    height = local * 9 * R // 2
    kept = [] if packed is None else [packed]
    full = lambda shape: pl.BlockSpec(shape, lambda e, s: (0,) * len(shape))
    return pl.pallas_call(
        expert_kernel,
        grid_spec=pltpu.PrefetchScalarGridSpec(
            num_scalar_prefetch=1,
            grid=(local,),
            in_specs=[
                full((rows, MODEL_WIDTH)),
                pl.BlockSpec((rows, MODEL_WIDTH), lambda e, s: (s[4], 0)),
                pl.BlockSpec((rows, TOP), lambda e, s: (s[0], 0)),
                full((128, MODEL_WIDTH)),
                pl.BlockSpec((1, MODEL_WIDTH, 2 * H), lambda e, s: (e, 0, 0)),
                pl.BlockSpec((1, H, MODEL_WIDTH), lambda e, s: (e, 0, 0)),
                pl.BlockSpec((local, 1, 2 * R, MODEL_WIDTH), lambda e, s: (0, s[1], 0, 0)),
                pl.BlockSpec((local, 1, 2, R, H), lambda e, s: (0, s[1], 0, 0, 0)),
                pl.BlockSpec((local, 1, R, H), lambda e, s: (0, s[1], 0, 0)),
                pl.BlockSpec((local, 1, R, MODEL_WIDTH), lambda e, s: (0, s[1], 0, 0)),
            ]
            + [pl.BlockSpec(memory_space=pl.ANY)] * len(kept),
            out_specs=[
                full((2 * rows + experts, MODEL_WIDTH)),
                full((experts, rows)),
                pl.BlockSpec((BLOCKS, 1, height, BLOCK), lambda e, s: (0, s[3], 0, 0)),
            ],
            scratch_shapes=[
                pltpu.VMEM((rows, 128), f32),
                pltpu.VMEM((rows, 128), f32),
                pltpu.VMEM((rows, ranks_in), bf16),
                pltpu.VMEM((ranks_in, rows), bf16),
                pltpu.VMEM((ranks_in, 2 * H), bf16),
                pltpu.VMEM((rows, ranks_down), f32),
                pltpu.VMEM((rows, ranks_down), bf16),
                pltpu.VMEM((rows, ranks_in), bf16),
                pltpu.VMEM((rows, H), bf16),
                pltpu.VMEM((rows, 2 * H), bf16),
                pltpu.VMEM((rows, ranks_down), bf16),
                pltpu.VMEM((ranks_down, H), f32),
                pltpu.VMEM((rows, MODEL_WIDTH), f32),
                pltpu.VMEM((rows, MODEL_WIDTH), f32),
            ],
        ),
        out_shape=[
            jax.ShapeDtypeStruct((2 * rows + experts, MODEL_WIDTH), bf16),
            jax.ShapeDtypeStruct((experts, rows), f32),
            jax.ShapeDtypeStruct((BLOCKS, slots, height, BLOCK), bf16),
        ],
        input_output_aliases={11: 2} if kept else {},
        compiler_params=params_of(1),
        name="experts",
        cost_estimate=pl.CostEstimate(
            flops=local * rows * 9 * (1 << 20),
            transcendentals=local * rows * H,
            bytes_accessed=20 << 20,
        ),
    )(scalars, x, cot, routes, router, w_in, w_down, a_in, b_in, a_down, b_down, *kept)


def open_back_kernel(count, order, cot, mid, gain, gates, router, weight_a, weight_b, low_map, up_map, low, att, *rest):
    parts = rest[:count]
    sums = rest[count : 3 * count]
    grad_mid, grad_att, grad_up, grad_low, columns = rest[3 * count :]
    gate_value = gates[...]
    half = gate_value.shape[0] // 2
    sides = []
    for side in range(2):
        value = None
        for at in range(count):
            pair = sums[2 * at + side][...].astype(f32)
            pair = pair[:half] + pair[half:]
            value = pair if value is None else value + pair
        sides.append(value)
    gate_grad = jnp.concatenate(sides, 0)
    logit = gate_value * (gate_grad - jnp.sum(gate_value * gate_grad, 0, keepdims=True))
    first = logit.astype(bf16)
    left = logit - first.astype(f32)
    second = left.astype(bf16)
    third = (left - second.astype(f32)).astype(bf16)
    grad = tn(first, router[...]) + (tn(second, router[...]) + tn(third, router[...]))
    for piece in parts:
        grad = grad + piece[...].astype(f32)
    total = cot[...].astype(f32) + norm_back(mid[...], gain[...].astype(f32), grad)
    grad_mid[...] = total
    branch = total.astype(bf16)
    low_grad = nt(branch, up_map[...]).astype(bf16)
    columns[...] = nn(low_grad, low_map[...])
    for side, weight in enumerate((weight_a, weight_b)):
        value = nt(branch, weight[...])
        for at in range(BLOCKS // 2):
            columns[:, column(order, side * BLOCKS // 2 + at)] += value[:, at * BLOCK : (at + 1) * BLOCK]
    grad_att[...] = columns[...].astype(bf16)
    up_part = tn(low[...], branch)
    low_part = tn(low_grad, att[...])

    @pl.when(pl.program_id(0) == 0)
    def _():
        grad_up[...] = up_part
        grad_low[...] = low_part

    @pl.when(pl.program_id(0) > 0)
    def _():
        grad_up[...] += up_part
        grad_low[...] += low_part


def open_back(order, cot, mid, gain, gates, router, weights, low_map, up_map, low, att, parts):
    rows = cot.shape[0]
    block = 256
    ranks = low_map.shape[0]
    experts = gates.shape[0]
    full = lambda shape: pl.BlockSpec(shape, lambda n, s: (0, 0))
    part = lambda width: pl.BlockSpec((block, width), lambda n, s: (n, 0))
    count = len(parts)
    below = rows // experts
    sums = [
        pl.BlockSpec((experts, block), lambda n, s: (below, n)),
        pl.BlockSpec((experts, block), lambda n, s: (below, rows // block + n)),
    ]

    def body(*refs):
        open_back_kernel(count, *refs)

    return pl.pallas_call(
        body,
        grid_spec=pltpu.PrefetchScalarGridSpec(
            num_scalar_prefetch=1,
            grid=(rows // block,),
            in_specs=[
                part(MODEL_WIDTH),
                part(MODEL_WIDTH),
                full((1, MODEL_WIDTH)),
                pl.BlockSpec((experts, block), lambda n, s: (0, n)),
                full((experts, MODEL_WIDTH)),
                *halves(weights, MODEL_WIDTH, lambda n: QKV // MODEL_WIDTH),
                full((ranks, QD)),
                full((ranks, MODEL_WIDTH)),
                part(ranks),
                part(QD),
            ]
            + [part(MODEL_WIDTH)] * count
            + sums * count,
            out_specs=[
                part(MODEL_WIDTH),
                part(QD),
                full((ranks, MODEL_WIDTH)),
                full((ranks, QD)),
            ],
            scratch_shapes=[pltpu.VMEM((block, QD), f32)],
        ),
        out_shape=[
            jax.ShapeDtypeStruct((rows, MODEL_WIDTH), f32),
            jax.ShapeDtypeStruct((rows, QD), bf16),
            jax.ShapeDtypeStruct((ranks, MODEL_WIDTH), f32),
            jax.ShapeDtypeStruct((ranks, QD), f32),
        ],
        compiler_params=params_of(1),
        name="open_back",
        cost_estimate=pl.CostEstimate(
            flops=2 * rows * QD * MODEL_WIDTH, transcendentals=0, bytes_accessed=14 << 20
        ),
    )(
        order, cot, mid, gain, gates, router, *weights, low_map, up_map, low, att, *parts,
        *[piece for piece in parts for _ in range(2)],
    )


def adapters_back_kernel(
    grad_query, grad_key, grad_value, low, normed, up_map, low_there, up_there, low_out, *results
):
    pieces = (grad_query, grad_key, grad_value)
    bounds = (0, QD, QD + KD, QKV)
    back = None
    ups = []
    for at in range(3):
        block = pieces[at][...]
        ups.append(tn(low[...], block)[at * R : (at + 1) * R])
        part = nt(block, up_map[:, bounds[at] : bounds[at + 1]])
        back = part if back is None else back + part
    value = back.astype(bf16)
    low_out[...] = value
    lows = tn(value, normed[...]) + low_there[...]
    if len(results) == 2:
        grad_up, grad_low = results
        grad_low[...] = lows
        for at in range(3):
            grad_up[:, bounds[at] : bounds[at + 1]] = ups[at]
        return
    (packed,) = results
    grad_up = jnp.concatenate(ups, 1)
    grad_out = up_there[3 * R :, :]
    small = BLOCK // 4
    lane = lanes_of((R, BLOCK))
    for owner in range(packed.shape[0]):
        tile = slice(owner // 4 * BLOCK, (owner // 4 + 1) * BLOCK)
        offset = owner % 4 * small
        first = jnp.zeros((R, BLOCK), f32)
        for at in range(4):
            piece = lows[at * R : (at + 1) * R, tile]
            shift = (at * small - offset) % BLOCK
            piece = pltpu.roll(piece, shift, 1) if shift else piece
            first = jnp.where((lane >= at * small) & (lane < (at + 1) * small), piece, first)
        piece = grad_up[:, owner // 2 * BLOCK : (owner // 2 + 1) * BLOCK]
        piece = pltpu.roll(piece, BLOCK // 2, 1) if owner % 2 else piece
        other = grad_out[:, tile]
        shift = (2 * small - offset) % BLOCK
        other = pltpu.roll(other, shift, 1) if shift else other
        packed[owner, :, :BLOCK] = first.astype(bf16)
        packed[owner, :, BLOCK:] = jnp.where(
            lane < 2 * small, piece, jnp.where(lane < 3 * small, other, 0.0)
        ).astype(bf16)


def adapters_back(grad_query, grad_key, grad_value, low, normed, up_map, low_there, up_there, devices):
    rows = normed.shape[0]
    ranks = up_map.shape[0]
    if devices * BLOCK // 4 == MODEL_WIDTH:
        results = [jax.ShapeDtypeStruct((devices, R, 2 * BLOCK), bf16)]
    else:
        results = [
            jax.ShapeDtypeStruct((R, QKV), f32),
            jax.ShapeDtypeStruct((ranks, MODEL_WIDTH), f32),
        ]
    back_low, *results = pl.pallas_call(
        adapters_back_kernel,
        out_shape=[jax.ShapeDtypeStruct((rows, ranks), bf16)] + results,
        compiler_params=pltpu.CompilerParams(vmem_limit_bytes=56 * 1024 * 1024),
        name="adapters_back",
        cost_estimate=pl.CostEstimate(
            flops=6 * rows * 256 * QKV, transcendentals=0, bytes_accessed=4 << 20
        ),
    )(grad_query, grad_key, grad_value, low, normed, up_map, low_there, up_there)
    if len(results) == 1:
        return results[0], back_low
    grad_up, grad_low = results
    small = MODEL_WIDTH // devices
    packed = jnp.concatenate(
        [
            grad_low.reshape(4, R, devices, small).transpose(2, 1, 0, 3).reshape(devices, R, 4 * small),
            grad_up.reshape(R, devices, 2 * small).transpose(1, 0, 2),
            up_there[3 * R :].reshape(R, devices, small).transpose(1, 0, 2),
            jnp.zeros((devices, R, small), f32),
        ],
        -1,
    )
    return packed.astype(bf16), back_low


def input_back_kernel(
    order, grad_query, grad_key, grad_value, low, weight_a, weight_b, low_map, hid, gain, mid, grad, columns
):
    columns[...] = nn(low[...], low_map[...])
    for side, weight in enumerate((weight_a, weight_b)):
        value = nt(grad_query[...], weight[:, :QD])
        value = value + nt(grad_key[...], weight[:, QD : QD + KD])
        value = value + nt(grad_value[...], weight[:, QD + KD :])
        for at in range(BLOCKS // 2):
            columns[:, column(order, side * BLOCKS // 2 + at)] += value[:, at * BLOCK : (at + 1) * BLOCK]
    rows = hid[...].astype(f32)
    grad[...] = (mid[...] + norm_back(rows, gain[...].astype(f32), columns[...])).astype(bf16)


def input_back(order, grad_query, grad_key, grad_value, low, weights, low_map, hidden, gain, mid):
    rows = hidden.shape[0]
    block = 256
    ranks = low_map.shape[0]
    full = lambda shape: pl.BlockSpec(shape, lambda n, s: (0, 0))
    part = lambda width: pl.BlockSpec((block, width), lambda n, s: (n, 0))
    return pl.pallas_call(
        input_back_kernel,
        grid_spec=pltpu.PrefetchScalarGridSpec(
            num_scalar_prefetch=1,
            grid=(rows // block,),
            in_specs=[
                part(QD),
                part(KD),
                part(KD),
                part(ranks),
                *halves(weights, QKV, lambda n: 0),
                full((ranks, MODEL_WIDTH)),
                part(MODEL_WIDTH),
                full((1, MODEL_WIDTH)),
                part(MODEL_WIDTH),
            ],
            out_specs=part(MODEL_WIDTH),
            scratch_shapes=[pltpu.VMEM((block, MODEL_WIDTH), f32)],
        ),
        out_shape=jax.ShapeDtypeStruct((rows, MODEL_WIDTH), bf16),
        compiler_params=params_of(1),
        name="input_back",
        cost_estimate=pl.CostEstimate(
            flops=2 * rows * QKV * MODEL_WIDTH, transcendentals=0, bytes_accessed=12 << 20
        ),
    )(order, grad_query, grad_key, grad_value, low, *weights, low_map, hidden, gain, mid)


def sum_experts_kernel(ids, pieces, a_in, b_in, a_down, b_down, acc):
    local = a_in.shape[0]
    small = a_down.shape[-1]
    acc[...] = jnp.zeros_like(acc)

    def step(index, carry):
        acc[ids[index]] += pieces[index].astype(f32)
        return carry

    lax.fori_loop(0, pieces.shape[0], step, 0)
    for e in range(local):
        a_in[e] = acc[:, e * 2 * R : (e + 1) * 2 * R, :]
        at = local * 2 * R + e * R
        b_down[e] = acc[:, at : at + R, :]
        at = local * 3 * R + e * R
        both = acc[:, at : at + R, :]
        b_in[e, :, 0] = both[:, :, :small]
        b_in[e, :, 1] = both[:, :, small:]
        at = local * 4 * R + e // 2 * R
        a_down[e] = acc[:, at : at + R, e % 2 * small : (e % 2 + 1) * small]


def sum_experts(ids, pieces, local):
    height = pieces.shape[1]
    lanes = pieces.shape[2]
    small = lanes // 2
    vmem = pl.BlockSpec(memory_space=pltpu.VMEM)
    return pl.pallas_call(
        sum_experts_kernel,
        in_specs=[pl.BlockSpec(memory_space=pltpu.SMEM), vmem],
        out_specs=[vmem, vmem, vmem, vmem],
        out_shape=[
            jax.ShapeDtypeStruct((local, NA, 2 * R, lanes), f32),
            jax.ShapeDtypeStruct((local, NA, 2, R, small), f32),
            jax.ShapeDtypeStruct((local, NA, R, small), f32),
            jax.ShapeDtypeStruct((local, NA, R, lanes), f32),
        ],
        scratch_shapes=[pltpu.VMEM((NA, height, lanes), f32)],
        compiler_params=pltpu.CompilerParams(vmem_limit_bytes=56 * 1024 * 1024),
        name="sum_experts",
    )(ids, pieces)


def sum_mixer_kernel(ids, pieces, grad_low, grad_up, grad_out, acc):
    width = grad_low.shape[-1]
    acc[...] = jnp.zeros_like(acc)

    def step(index, carry):
        acc[ids[index]] += pieces[index].astype(f32)
        return carry

    lax.fori_loop(0, pieces.shape[0], step, 0)
    total = acc[...]
    for at in range(4):
        grad_low[at] = total[:, :, at * width : (at + 1) * width]
    grad_up[...] = total[:, :, 4 * width : 6 * width]
    grad_out[...] = total[:, :, 6 * width : 7 * width]


def sum_mixer(ids, pieces):
    width = pieces.shape[2] // 8
    vmem = pl.BlockSpec(memory_space=pltpu.VMEM)
    return pl.pallas_call(
        sum_mixer_kernel,
        in_specs=[pl.BlockSpec(memory_space=pltpu.SMEM), vmem],
        out_specs=[vmem, vmem, vmem],
        out_shape=[
            jax.ShapeDtypeStruct((4, NA, R, width), f32),
            jax.ShapeDtypeStruct((NA, R, 2 * width), f32),
            jax.ShapeDtypeStruct((NA, R, width), f32),
        ],
        scratch_shapes=[pltpu.VMEM((NA, R, 8 * width), f32)],
        compiler_params=pltpu.CompilerParams(vmem_limit_bytes=56 * 1024 * 1024),
        name="sum_mixer",
    )(ids, pieces)


def rope_tables(rows):
    half = HS // 2
    frequency = (10000.0 ** (-2.0 * np.arange(half, dtype=np.float32) / HS)).astype(np.float32)
    angles = np.arange(rows, dtype=np.float32)[:, None] * frequency[None, :]
    cos = np.cos(angles.astype(np.float64)).astype(np.float32)
    sin = np.sin(angles.astype(np.float64)).astype(np.float32)
    return (
        jnp.asarray(np.concatenate([cos, cos, cos, cos], 1)),
        jnp.asarray(np.concatenate([-sin, sin, -sin, sin], 1)),
    )


def swap(value, bit):
    return lax.ppermute(value, "dp", [(at, at ^ bit) for at in range(BLOCKS)])


def both_neighbours(weight):
    return swap(weight, 2), swap(weight, 4)


def across(pair):
    one, two = pair
    middle = one.shape[0] // 2
    return swap(two[:middle], 2), swap(one[middle:], 4)


def tied(*values):
    return lax.optimization_barrier(values)


def order_of(row):
    if lax.axis_size("dp") != BLOCKS:
        return jnp.arange(BLOCKS, dtype=jnp.int32)
    return row.astype(jnp.int32) ^ jnp.array([0, 2, 4, 6, 1, 3, 5, 7], jnp.int32)


def to_owners(packed, owners, local):
    split = owners // BLOCKS
    if split == 1:
        return packed
    slots = packed.shape[1]
    edge = local * 3 * R
    wide = packed[:, :, :edge].reshape(BLOCKS, slots, edge, split, BLOCK // split)
    wide = wide.transpose(0, 3, 1, 2, 4).reshape(owners, slots, edge, BLOCK // split)
    rest = packed.shape[2] - edge
    narrow = packed[:, :, edge:].reshape(BLOCKS, slots, rest, 2, split, BLOCK // 2 // split)
    narrow = narrow.transpose(0, 4, 1, 2, 3, 5).reshape(owners, slots, rest, BLOCK // split)
    return jnp.concatenate([wide, narrow], 2)


def joined(left, right):
    return (left.astype(f32) + right.astype(f32)).astype(bf16)


def on_device(
    hidden,
    cotangent,
    lengths,
    adapter_ids,
    routes,
    attn_gain,
    ffn_gain,
    query_key_value_weight,
    w_out,
    w_router,
    w_gate_up,
    w_down,
    attention_lowmap,
    attention_query_key_value_upmap,
    attention_output_upmap,
    expert_gate_up_lowmap,
    expert_gate_up_upmap,
    expert_down_lowmap,
    expert_down_upmap,
):
    groups = lax.axis_size("expert")
    owners = lax.axis_size("dp")
    place = lax.axis_index("expert")
    row = lax.axis_index("dp")
    devices = groups * owners
    sequence = row * groups + place
    rows = hidden.shape[0]
    experts = w_router.shape[1]
    local = w_gate_up.shape[0]
    width = MODEL_WIDTH // owners
    attn_gain = attn_gain.reshape(1, MODEL_WIDTH)
    ffn_gain = ffn_gain.reshape(1, MODEL_WIDTH)
    length = lax.dynamic_slice(lengths, (sequence,), (1,))
    forward = [(at, (at + 1) % groups) for at in range(groups)]
    backward = [(at, (at - 1) % groups) for at in range(groups)]

    mine = lax.dynamic_slice(adapter_ids.reshape(owners, groups), (0, place), (owners, 1))[:, 0]
    low_turned = attention_lowmap.transpose(1, 0, 3, 2).reshape(NA, 4 * R, width)
    up_turned = (
        attention_query_key_value_upmap.reshape(NA, R, 2, width)
        .transpose(0, 2, 1, 3)
        .reshape(NA, 2 * R, width)
    )
    adapters = jnp.concatenate([low_turned, up_turned, attention_output_upmap], 1)[mine]
    adapters = lax.all_to_all(adapters, "dp", 0, 0, tiled=True)
    order = order_of(row)
    both = jnp.concatenate([query_key_value_weight, w_out], 1)
    if owners == BLOCKS:
        pair = both_neighbours(both)
        near = jnp.concatenate([both, *pair, *across(pair)], 0)
        near, adapters = tied(near, adapters)
        weights = near, swap(near, 1)
    else:
        whole = lax.all_gather(both, "dp", axis=0, tiled=True)
        weights = whole, whole

    low_map = adapters[:, : 4 * R].transpose(1, 0, 2).reshape(4 * R, MODEL_WIDTH)
    up = (
        adapters[:, 4 * R : 6 * R]
        .reshape(owners, 2, R, width)
        .transpose(2, 0, 1, 3)
        .reshape(R, QKV)
    )
    up_out = adapters[:, 6 * R :].transpose(1, 0, 2).reshape(R, MODEL_WIDTH)
    column = jnp.arange(QKV, dtype=jnp.int32)
    part = jnp.where(column < QD, 0, jnp.where(column < QD + KD, 1, 2))
    up_map = jnp.where(
        part[None, None, :] == jnp.arange(4, dtype=jnp.int32)[:, None, None], up[None], 0
    ).reshape(4 * R, QKV)
    up_out_map = jnp.concatenate([jnp.zeros((3 * R, MODEL_WIDTH), bf16), up_out], 0)

    cos, sin = rope_tables(rows)

    cots = lax.all_gather(cotangent, "expert", axis=0, tiled=True)

    qkv, low, normed_in = project(order, hidden, attn_gain, weights, low_map, up_map, cos, sin)
    attended, lse = attend(length, qkv)
    mid, normed_mid, low_out = close_mixer(
        order, attended, hidden, ffn_gain, weights, low_map, up_out_map
    )

    first = place * local
    routes_here = (routes - first + experts) % experts
    router = jnp.roll(w_router.T, -first, axis=0)
    router_wide = jnp.concatenate(
        [router, jnp.zeros((128 - experts, MODEL_WIDTH), router.dtype)], 0
    )
    a_in = expert_gate_up_lowmap.transpose(0, 1, 3, 2)
    a_down = expert_down_lowmap.transpose(0, 1, 3, 2)

    offsets = [0, 1] + [groups - 1] * (groups > 2) + list(range(2, groups - 1))
    offset = jnp.array(offsets, jnp.int32)
    source = (place - offset + groups) % groups
    tags = adapter_ids.reshape(owners, groups)[:, source]
    slot = jnp.arange(groups, dtype=jnp.int32)
    table = jnp.stack(
        [
            source,
            lax.dynamic_slice(tags, (row, 0), (1, groups))[0],
            offset * local,
            slot,
            jnp.where(slot == 0, 0, source),
        ],
        1,
    )

    xs = {0: normed_mid, 1: lax.ppermute(normed_mid, "expert", forward)}
    packed = None
    ran = {}
    for at, offset in enumerate(offsets):
        ran[offset], gate_part, packed = run_experts(
            table[at],
            xs[offset],
            cotangent if at == 0 else cots,
            routes_here,
            router_wide,
            w_gate_up,
            w_down,
            a_in,
            expert_gate_up_upmap,
            a_down,
            expert_down_upmap,
            experts,
            groups,
            packed,
        )
        if at == 0:
            gates = gate_part
            if groups > 2:
                normed_mid, packed = tied(normed_mid, packed)
                xs[groups - 1] = lax.ppermute(normed_mid, "expert", backward)
        elif at < groups - 2:
            value, packed = tied(xs[at], packed)
            xs[at + 1] = lax.ppermute(value, "expert", forward)
        if at == 2:
            first_sums, packed = tied(ran[1], packed)

    pieces = lax.all_to_all(to_owners(packed, owners, local), "dp", 0, 0, tiled=True)
    pieces = pieces.reshape(devices, pieces.shape[2], width)
    g_a_in, g_b_in, g_a_down, g_b_down = sum_experts(tags.reshape(devices), pieces, local)

    edge = rows + experts
    both_far = lax.ppermute(first_sums if groups > 2 else ran[1], "expert", forward)
    grad_far, out_far = both_far, both_far[edge:]
    for offset in range(2, groups):
        grad_part = joined(ran[offset][:edge], grad_far[:edge])
        if offset == groups - 1:
            grad_part, g_a_down = tied(grad_part, g_a_down)
        grad_far = lax.ppermute(grad_part, "expert", forward)
    if groups > 2:
        out_part = joined(ran[2][edge:], out_far)
        out_part, grad_far = tied(out_part, grad_far)
        out_far = lax.ppermute(out_part, "expert", forward)

    grad_mid, grad_attended, grad_up_out, grad_low_out = open_back(
        order,
        cotangent,
        mid,
        ffn_gain,
        gates,
        router,
        weights,
        low_map,
        up_out_map,
        low_out,
        attended,
        [ran[0], grad_far],
    )
    grad_query, grad_key, grad_value = attend_back(length, qkv, grad_attended, lse, cos, sin)
    out_far, grad_query = tied(out_far, grad_query)
    for offset in range(3, groups):
        out_far = lax.ppermute(joined(ran[offset][edge:], out_far), "expert", forward)
    packed, back_low = adapters_back(
        grad_query, grad_key, grad_value, low, normed_in, up_map, grad_low_out, grad_up_out, devices
    )
    packed = lax.all_to_all(packed, ("dp", "expert"), 0, 0, tiled=True)
    m_a, m_b, m_o = sum_mixer(adapter_ids, packed)

    grad_hidden = input_back(
        order, grad_query, grad_key, grad_value, back_low, weights, low_map, hidden, attn_gain, grad_mid
    )
    out = (mid + ran[0][edge:].astype(f32) + out_far.astype(f32)).astype(bf16)
    return (
        out,
        grad_hidden,
        m_a.transpose(0, 1, 3, 2),
        m_b,
        m_o,
        g_a_in.transpose(0, 1, 3, 2),
        g_b_in,
        g_a_down.transpose(0, 1, 3, 2),
        g_b_down,
    )


def solution(mesh):
    in_specs = (
        P(("dp", "expert"), None),
        P(("dp", "expert"), None),
        P(),
        P(),
        P("dp", None),
        P(),
        P(),
        P("dp", None),
        P("dp", None),
        P(),
        P("expert", None, None),
        P("expert", None, None),
        P(None, None, "dp", None),
        P(None, None, "dp"),
        P(None, None, "dp"),
        P("expert", None, None, None),
        P("expert", None, None, None, None),
        P("expert", None, None, None),
        P("expert", None, None, None),
    )
    out_specs = (
        P(("dp", "expert"), None),
        P(("dp", "expert"), None),
        P(None, None, ("dp", "expert"), None),
        P(None, None, ("dp", "expert")),
        P(None, None, ("dp", "expert")),
        P("expert", None, "dp", None),
        P("expert", None, None, None, "dp"),
        P("expert", None, "dp", None),
        P("expert", None, None, "dp"),
    )
    return jax.shard_map(
        on_device, mesh=mesh, in_specs=in_specs, out_specs=out_specs, check_vma=False
    )
```

```python
import numpy as np
import jax
import jax.numpy as jnp
from jax import lax
from jax.experimental import pallas as pl
from jax.experimental.pallas import tpu as pltpu
from jax.sharding import PartitionSpec as P

MODEL_WIDTH = 1024
HQ = 16
KVH = 8
HS = 64
H = 512
TOP = 8
R = 16
NA = 8
QD = HQ * HS
KD = KVH * HS
QKV = QD + 2 * KD

epsilon = 1e-06
f32 = jnp.float32
bf16 = jnp.bfloat16


def nn(left, right):
    return lax.dot_general(left, right, (((1,), (0,)), ((), ())), preferred_element_type=f32)


def nt(left, right):
    return lax.dot_general(left, right, (((1,), (1,)), ((), ())), preferred_element_type=f32)


def tn(left, right):
    return lax.dot_general(left, right, (((0,), (0,)), ((), ())), preferred_element_type=f32)


def lanes_of(shape):
    return lax.broadcasted_iota(jnp.int32, shape, len(shape) - 1)


def row_scale(rows):
    return lax.rsqrt(jnp.mean(rows * rows, -1, keepdims=True) + epsilon)


def norm_back(rows, gain, grad):
    scale = row_scale(rows)
    scaled = grad * gain
    return scale * scaled - rows * (scale * scale * scale) * jnp.mean(
        rows * scaled, -1, keepdims=True
    )


def rope_swap(rows):
    width = rows.shape[-1]
    lane = lanes_of(rows.shape)
    return jnp.where(
        lane % HS < HS // 2,
        pltpu.roll(rows, width - HS // 2, 1),
        pltpu.roll(rows, HS // 2, 1),
    )


def both_halves(pair, half):
    rows = pair.astype(f32)
    lane = lanes_of(rows.shape)
    rolled = pltpu.roll(rows, HS, 1)
    keep = (lane < HS) == (half == 0)
    return jnp.where(keep, rows, rolled).astype(bf16)


def stacked_heads(pair):
    lane = lanes_of(pair.shape)
    zero = jnp.zeros_like(pair)
    return jnp.concatenate(
        [jnp.where(lane < HS, pair, zero), jnp.where(lane < HS, zero, pair)], 0
    )


def params_of(count):
    return pltpu.CompilerParams(
        dimension_semantics=("arbitrary",) * count, vmem_limit_bytes=56 * 1024 * 1024
    )


BLOCK = 128
BLOCKS = MODEL_WIDTH // BLOCK
HALF = MODEL_WIDTH // 2


def column(order, at):
    return pl.ds(pl.multiple_of(order[at] * BLOCK, BLOCK), BLOCK)


def halves(weights, width, index):
    there = 1 if weights[0] is weights[1] else 0
    return [
        pl.BlockSpec((HALF, width), lambda n, s: (0, index(n))),
        pl.BlockSpec((HALF, width), lambda n, s: (there, index(n))),
    ]


def project_kernel(
    order, hid, gain, weight_a, weight_b, low_map, up_map, cos, sin, qkv, low, normed, turned_rows
):
    step = pl.program_id(0)
    blocks = pl.num_programs(0)

    @pl.when(step == 0)
    def _():
        rows = hid[...].astype(f32)
        value = (rows * row_scale(rows) * gain[...].astype(f32)).astype(bf16)
        normed[...] = value
        low[...] = nt(value, low_map[...]).astype(bf16)
        for at in range(BLOCKS):
            turned_rows[:, at * BLOCK : (at + 1) * BLOCK] = normed[:, column(order, at)]

    value = (
        nn(turned_rows[:, :HALF], weight_a[...])
        + nn(turned_rows[:, HALF:], weight_b[...])
        + nn(low[...], up_map[...])
    )

    @pl.when(step < blocks * 3 // 4)
    def _():
        for part in range(value.shape[1] // 128):
            piece = value[:, part * 128 : part * 128 + 128]
            turned = piece * cos[...] + rope_swap(piece) * sin[...]
            qkv[:, part * 128 : part * 128 + 128] = turned.astype(bf16)

    @pl.when(step >= blocks * 3 // 4)
    def _():
        qkv[...] = value.astype(bf16)


def project(order, hidden, gain, weights, low_map, up_map, cos, sin):
    rows = hidden.shape[0]
    block = 512
    ranks = low_map.shape[0]
    full = lambda shape: pl.BlockSpec(shape, lambda n, s: (0, 0))
    return pl.pallas_call(
        project_kernel,
        grid_spec=pltpu.PrefetchScalarGridSpec(
            num_scalar_prefetch=1,
            grid=(QKV // block,),
            in_specs=[
                full((rows, MODEL_WIDTH)),
                full((1, MODEL_WIDTH)),
                *halves(weights, block, lambda n: n),
                full((ranks, MODEL_WIDTH)),
                pl.BlockSpec((ranks, block), lambda n, s: (0, n)),
                full((rows, 128)),
                full((rows, 128)),
            ],
            out_specs=[
                pl.BlockSpec((rows, block), lambda n, s: (0, n)),
                full((rows, ranks)),
                full((rows, MODEL_WIDTH)),
            ],
            scratch_shapes=[pltpu.VMEM((rows, MODEL_WIDTH), bf16)],
        ),
        out_shape=[
            jax.ShapeDtypeStruct((rows, QKV), bf16),
            jax.ShapeDtypeStruct((rows, ranks), bf16),
            jax.ShapeDtypeStruct((rows, MODEL_WIDTH), bf16),
        ],
        compiler_params=params_of(1),
        name="project",
        cost_estimate=pl.CostEstimate(
            flops=2 * rows * QKV * MODEL_WIDTH, transcendentals=0, bytes_accessed=8 << 20
        ),
    )(order, hidden, gain, *weights, low_map, up_map, cos, sin)


ROWB = 128


def length_column(length, count):
    key = lax.broadcasted_iota(jnp.int32, (count, 1), 0)
    return jnp.where(key < length, 0.0, -1e30)


def causal_block():
    key = lax.broadcasted_iota(jnp.int32, (ROWB, 2 * ROWB), 0)
    return jnp.where(key <= lanes_of((ROWB, 2 * ROWB)) % ROWB, 0.0, -1e30)


def masked_scores(queries, keys, start, bias, causal):
    count = start + ROWB
    scores = nt(keys[:count], (queries.astype(f32) * 0.125).astype(bf16))
    near = scores[start:] + (bias[start:count] + causal)
    if start == 0:
        return near
    return jnp.concatenate([scores[:start] + bias[:start], near], 0)


def attend_kernel(scalars, query, key, value, result, lse):
    half = pl.program_id(0) % 2
    keys = both_halves(key[...], half)
    values = both_halves(value[...], half)
    rows = query.shape[0]
    bias = length_column(scalars[0], rows)
    causal = causal_block()
    for start in range(0, rows, ROWB):
        count = start + ROWB
        stacked = stacked_heads(query[start:count, :])
        scores = masked_scores(stacked, keys, start, bias, causal)
        top = jnp.max(scores, 0, keepdims=True)
        shifted = jnp.exp(scores - top)
        total = jnp.sum(shifted, 0, keepdims=True)
        prob = (shifted * (1.0 / total)).astype(bf16)
        mixed = tn(prob, values[:count])
        lane = lanes_of((ROWB, 128))
        result[start:count, :] = jnp.where(lane < HS, mixed[:ROWB], mixed[ROWB:]).astype(bf16)
        logs = top + jnp.log(total)
        lse[0, 0:1, start:count] = logs[:, :ROWB]
        lse[0, 1:2, start:count] = logs[:, ROWB:]


def attend(length, qkv):
    rows = qkv.shape[0]
    pairs = KVH
    return pl.pallas_call(
        attend_kernel,
        grid_spec=pltpu.PrefetchScalarGridSpec(
            num_scalar_prefetch=1,
            grid=(pairs,),
            in_specs=[
                pl.BlockSpec((rows, 128), lambda g, s: (0, g)),
                pl.BlockSpec((rows, 128), lambda g, s: (0, QD // 128 + g // 2)),
                pl.BlockSpec((rows, 128), lambda g, s: (0, (QD + KD) // 128 + g // 2)),
            ],
            out_specs=[
                pl.BlockSpec((rows, 128), lambda g, s: (0, g)),
                pl.BlockSpec((1, 2, rows), lambda g, s: (g, 0, 0)),
            ],
        ),
        out_shape=[
            jax.ShapeDtypeStruct((rows, QD), bf16),
            jax.ShapeDtypeStruct((pairs, 2, rows), f32),
        ],
        compiler_params=params_of(1),
        name="attend",
        cost_estimate=pl.CostEstimate(
            flops=8 * rows * rows * QD, transcendentals=rows * rows * HQ, bytes_accessed=4 << 20
        ),
    )(length, qkv, qkv, qkv)


def attend_back_kernel(
    scalars, query, key, value, grad, lse, cos, sin, grad_query, grad_key, grad_value, key_acc, value_acc
):
    half = pl.program_id(0) % 2
    keys = both_halves(key[...], half)
    values = both_halves(value[...], half)
    rows = query.shape[0]
    bias = length_column(scalars[0], rows)
    causal = causal_block()
    for start in reversed(range(0, rows, ROWB)):
        count = start + ROWB
        stacked = stacked_heads(query[start:count, :])
        grads = stacked_heads(grad[start:count, :])
        scores = masked_scores(stacked, keys, start, bias, causal)
        logs = jnp.concatenate([lse[0, 0:1, start:count], lse[0, 1:2, start:count]], 1)
        prob = jnp.exp(scores - logs)
        grad_prob = nt(values[:count], grads)
        delta = jnp.sum(prob * grad_prob, 0, keepdims=True)
        grad_score = (prob * (grad_prob - delta)).astype(bf16)
        mixed = tn(grad_score, keys[:count])
        lane = lanes_of((ROWB, 128))
        turned = 0.125 * jnp.where(lane < HS, mixed[:ROWB], mixed[ROWB:])
        turned = turned * cos[start:count, :] - rope_swap(turned) * sin[start:count, :]
        grad_query[start:count, :] = turned.astype(bf16)
        key_part = nn(grad_score, stacked)
        value_part = nn(prob.astype(bf16), grads)
        if count == rows:
            key_acc[...] = key_part
            value_acc[...] = value_part
        else:
            key_acc[:count, :] += key_part
            value_acc[:count, :] += value_part
    total = key_acc[...]
    total = 0.125 * (total + pltpu.roll(total, HS, 1))
    total = (total * cos[...] - rope_swap(total) * sin[...]).astype(bf16)
    other = value_acc[...]
    other = (other + pltpu.roll(other, HS, 1)).astype(bf16)

    @pl.when(half == 0)
    def _():
        grad_key[...] = total
        grad_value[...] = other

    @pl.when(half == 1)
    def _():
        low_half = lanes_of(total.shape) < HS
        grad_key[...] = jnp.where(low_half, grad_key[...], total)
        grad_value[...] = jnp.where(low_half, grad_value[...], other)


def attend_back(length, qkv, grad, lse, cos, sin):
    rows = qkv.shape[0]
    pairs = KVH
    return pl.pallas_call(
        attend_back_kernel,
        grid_spec=pltpu.PrefetchScalarGridSpec(
            num_scalar_prefetch=1,
            grid=(pairs,),
            in_specs=[
                pl.BlockSpec((rows, 128), lambda g, s: (0, g)),
                pl.BlockSpec((rows, 128), lambda g, s: (0, QD // 128 + g // 2)),
                pl.BlockSpec((rows, 128), lambda g, s: (0, (QD + KD) // 128 + g // 2)),
                pl.BlockSpec((rows, 128), lambda g, s: (0, g)),
                pl.BlockSpec((1, 2, rows), lambda g, s: (g, 0, 0)),
                pl.BlockSpec((rows, 128), lambda g, s: (0, 0)),
                pl.BlockSpec((rows, 128), lambda g, s: (0, 0)),
            ],
            out_specs=[
                pl.BlockSpec((rows, 128), lambda g, s: (0, g)),
                pl.BlockSpec((rows, 128), lambda g, s: (0, g // 2)),
                pl.BlockSpec((rows, 128), lambda g, s: (0, g // 2)),
            ],
            scratch_shapes=[pltpu.VMEM((rows, 128), f32), pltpu.VMEM((rows, 128), f32)],
        ),
        out_shape=[
            jax.ShapeDtypeStruct((rows, QD), bf16),
            jax.ShapeDtypeStruct((rows, KD), bf16),
            jax.ShapeDtypeStruct((rows, KD), bf16),
        ],
        compiler_params=params_of(1),
        name="attend_back",
        cost_estimate=pl.CostEstimate(
            flops=20 * rows * rows * QD, transcendentals=rows * rows * HQ, bytes_accessed=8 << 20
        ),
    )(length, qkv, qkv, qkv, grad, lse, cos, sin)


def close_kernel(order, att, hid, gain, weight_a, weight_b, low_map, up_map, mid, normed, low):
    low_value = nt(att[...], low_map[...]).astype(bf16)
    low[...] = low_value
    turned = jnp.concatenate([att[:, column(order, at)] for at in range(BLOCKS)], 1)
    stream = hid[...].astype(f32) + (
        nn(turned[:, :HALF], weight_a[...])
        + nn(turned[:, HALF:], weight_b[...])
        + nn(low_value, up_map[...])
    )
    mid[...] = stream
    normed[...] = (stream * row_scale(stream) * gain[...].astype(f32)).astype(bf16)


def close_mixer(order, att, hidden, gain, weights, low_map, up_map):
    rows = hidden.shape[0]
    block = 256
    ranks = low_map.shape[0]
    full = lambda shape: pl.BlockSpec(shape, lambda n, s: (0, 0))
    part = lambda width: pl.BlockSpec((block, width), lambda n, s: (n, 0))
    return pl.pallas_call(
        close_kernel,
        grid_spec=pltpu.PrefetchScalarGridSpec(
            num_scalar_prefetch=1,
            grid=(rows // block,),
            in_specs=[
                part(QD),
                part(MODEL_WIDTH),
                full((1, MODEL_WIDTH)),
                *halves(weights, MODEL_WIDTH, lambda n: QKV // MODEL_WIDTH),
                full((ranks, QD)),
                full((ranks, MODEL_WIDTH)),
            ],
            out_specs=[part(MODEL_WIDTH), part(MODEL_WIDTH), part(ranks)],
        ),
        out_shape=[
            jax.ShapeDtypeStruct((rows, MODEL_WIDTH), f32),
            jax.ShapeDtypeStruct((rows, MODEL_WIDTH), bf16),
            jax.ShapeDtypeStruct((rows, ranks), bf16),
        ],
        compiler_params=params_of(1),
        name="close_mixer",
        cost_estimate=pl.CostEstimate(
            flops=2 * rows * QD * MODEL_WIDTH, transcendentals=0, bytes_accessed=8 << 20
        ),
    )(order, att, hidden, gain, *weights, low_map, up_map)


def side_by_side(left, right):
    values = []
    for at in range(BLOCKS):
        tile = slice(at // 2 * BLOCK, (at // 2 + 1) * BLOCK)
        low_half = lanes_of((R, BLOCK)) < BLOCK // 2
        if at % 2 == 0:
            value = jnp.where(low_half, left[:, tile], pltpu.roll(right[:, tile], BLOCK // 2, 1))
        else:
            value = jnp.where(low_half, pltpu.roll(left[:, tile], BLOCK // 2, 1), right[:, tile])
        values.append(value.astype(bf16))
    return values


def expert_kernel(
    scalars,
    x,
    cot,
    routes,
    router,
    w_in,
    w_down,
    a_in,
    b_in,
    a_down,
    b_down,
    *rest,
):
    (
        out,
        grad_normed,
        gates_out,
        packed,
        gates,
        gate_sums,
        low_in,
        low_in_turned,
        b_in_all,
        back_low,
        gated_low,
        back_in,
        acts,
        grads,
        low_grads,
        down_acc,
        out_acc,
        grad_acc,
    ) = rest[-18:]
    expert = pl.program_id(0)
    last = pl.num_programs(0) - 1
    rows = x.shape[0]
    block = rows
    local = a_in.shape[0]
    a_in_all = a_in[...].reshape(local * 2 * R, MODEL_WIDTH)
    a_down_all = a_down[...].reshape(local * R, H)
    b_down_all = b_down[...].reshape(local * R, MODEL_WIDTH)

    @pl.when(expert == 0)
    def _():
        logits = nt(x[...], router[...])
        experts = gates_out.shape[0]
        lane = lanes_of(logits.shape)
        name = lane + scalars[4]
        name = jnp.where(name >= experts, name - experts, name)
        name = jnp.where(lane < experts, name, -1)
        chosen = name == routes[:, 0:1]
        for k in range(1, TOP):
            chosen = chosen | (name == routes[:, k : k + 1])
        top = jnp.max(jnp.where(chosen, logits, -1e30), -1, keepdims=True)
        shifted = jnp.where(chosen, jnp.exp(jnp.where(chosen, logits - top, 0.0)), 0.0)
        weights = shifted / jnp.sum(shifted, -1, keepdims=True)
        gates[...] = weights
        gates_out[...] = weights.T[: gates_out.shape[0], :]
        low = nt(x[...], a_in_all)
        low_in[...] = low.astype(bf16)
        low_in_turned[...] = low.T.astype(bf16)
        back_low[...] = nt(cot[...], b_down_all)
        b_in_all[...] = jnp.zeros_like(b_in_all)
        for e in range(local):
            b_in_all[e * 2 * R : e * 2 * R + R, :H] = b_in[e, 0, 0]
            b_in_all[e * 2 * R + R : (e + 1) * 2 * R, H:] = b_in[e, 0, 1]
        gate_sums[...] = jnp.zeros_like(gate_sums)
        gated_low[...] = jnp.zeros_like(gated_low)
        back_in[...] = jnp.zeros_like(back_in)
        out_acc[...] = jnp.zeros_like(out_acc)
        grad_acc[...] = jnp.zeros_like(grad_acc)
        down_acc[...] = jnp.zeros_like(down_acc)

    def row_step(index, carry):
        at = pl.ds(pl.multiple_of(index * block, block), block)
        lane_in = lanes_of((block, local * 2 * R))
        lane_down = lanes_of((block, local * R))
        in_mine = (lane_in >= expert * 2 * R) & (lane_in < (expert + 1) * 2 * R)
        down_mine = (lane_down >= expert * R) & (lane_down < (expert + 1) * R)
        gate_all = gates[at, :]
        gate_lane = lanes_of(gate_all.shape) == expert
        weight = jnp.sum(jnp.where(gate_lane, gate_all, 0.0), -1, keepdims=True)
        mine = low_in[at, :]
        mine = jnp.where(in_mine, mine, jnp.zeros_like(mine))
        both = nn(x[at, :], w_in[0]) + nn(mine, b_in_all[...])
        gate = both[:, :H]
        upper = both[:, H:]
        sigmoid = jax.nn.sigmoid(gate)
        silu = gate * sigmoid
        act = (silu * upper).astype(bf16)
        acts[at, :] = act
        act_wide = act.astype(f32)
        low = jnp.where(down_mine, nt(act, a_down_all), 0.0).astype(bf16).astype(f32)
        plain = nt(cot[at, :], w_down[0])
        low_plain = back_low[at, :]
        dots = jnp.sum(act_wide * plain, -1, keepdims=True) + jnp.sum(
            low * low_plain, -1, keepdims=True
        )
        sum_lane = lanes_of(gate_all.shape) == expert + scalars[2]
        gate_sums[at, :] += jnp.where(sum_lane, dots, 0.0)
        low_grad = jnp.where(down_mine, weight * low_plain, 0.0).astype(bf16)
        low_grads[at, :] = low_grad
        grad_act = weight * plain + nn(low_grad, a_down_all)
        grad_first = grad_act * upper * sigmoid * (1.0 + gate * (1.0 - sigmoid))
        grad_second = grad_act * silu
        grad_both = jnp.concatenate(
            [grad_first.astype(bf16), grad_second.astype(bf16)], 1
        )
        grads[at, :] = grad_both
        gated_low[at, :] += (weight * low).astype(bf16)
        out_acc[at, :] += nn((weight * act_wide).astype(bf16), w_down[0])
        grad_acc[at, :] += nt(grad_both, w_in[0])
        low_back = jnp.where(in_mine, nt(grad_both, b_in_all[...]), 0.0)
        back_in[at, :] += low_back.astype(bf16)
        return carry

    lax.fori_loop(0, rows // block, row_step, 0)

    turned = low_in_turned[pl.ds(pl.multiple_of(expert * 2 * R, 2 * R), 2 * R), :]
    product = nn(turned, grads[...])
    first_b_in = local * 3 * R
    here = pl.ds(pl.multiple_of(first_b_in + expert * R, R), R)
    for at, value in enumerate(side_by_side(product[:R, :H], product[R:, H:])):
        packed[at, 0, here, :] = value
    down_acc[...] += tn(low_grads[...], acts[...])

    @pl.when(expert == last)
    def _():
        out[...] = (out_acc[...] + nn(gated_low[...], b_down_all)).astype(bf16)
        grad_normed[:rows, :] = (grad_acc[...] + nn(back_in[...], a_in_all)).astype(bf16)
        experts = gates_out.shape[0]
        sums = gate_sums[...].T[:experts, :]
        sums = jnp.concatenate([sums[: experts // 2], sums[experts // 2 :]], 1)
        high = sums.astype(bf16).astype(f32)
        grad_normed[rows:, :] = jnp.concatenate([high, sums - high], 0).astype(bf16)
        wide = tn(back_in[...], x[...]).astype(bf16)
        tall = tn(gated_low[...], cot[...]).astype(bf16)
        for at in range(BLOCKS):
            columns = slice(at * BLOCK, (at + 1) * BLOCK)
            packed[at, 0, : local * 2 * R, :] = wide[:, columns]
            packed[at, 0, local * 2 * R : first_b_in, :] = tall[:, columns]
        for pair in range(local // 2):
            lower = down_acc[pair * 2 * R : pair * 2 * R + R, :]
            upper = down_acc[pair * 2 * R + R : (pair + 1) * 2 * R, :]
            row = local * 4 * R + pair * R
            for at, value in enumerate(side_by_side(lower, upper)):
                packed[at, 0, row : row + R, :] = value


def run_experts(
    scalars, x, cot, routes, router, w_in, w_down, a_in, b_in, a_down, b_down, experts, packed
):
    rows = x.shape[0]
    local = w_in.shape[0]
    ranks_in = local * 2 * R
    ranks_down = local * R
    height = packed.shape[2]
    full = lambda shape: pl.BlockSpec(shape, lambda e, s: (0,) * len(shape))
    return pl.pallas_call(
        expert_kernel,
        grid_spec=pltpu.PrefetchScalarGridSpec(
            num_scalar_prefetch=1,
            grid=(local,),
            in_specs=[
                full((rows, MODEL_WIDTH)),
                pl.BlockSpec((rows, MODEL_WIDTH), lambda e, s: (s[5], 0)),
                pl.BlockSpec((rows, TOP), lambda e, s: (s[0], 0)),
                full((128, MODEL_WIDTH)),
                pl.BlockSpec((1, MODEL_WIDTH, 2 * H), lambda e, s: (e, 0, 0)),
                pl.BlockSpec((1, H, MODEL_WIDTH), lambda e, s: (e, 0, 0)),
                pl.BlockSpec((local, 1, 2 * R, MODEL_WIDTH), lambda e, s: (0, s[1], 0, 0)),
                pl.BlockSpec((local, 1, 2, R, H), lambda e, s: (0, s[1], 0, 0, 0)),
                pl.BlockSpec((local, 1, R, H), lambda e, s: (0, s[1], 0, 0)),
                pl.BlockSpec((local, 1, R, MODEL_WIDTH), lambda e, s: (0, s[1], 0, 0)),
            ]
            + [pl.BlockSpec(memory_space=pl.ANY)],
            out_specs=[
                full((rows, MODEL_WIDTH)),
                full((rows + experts, MODEL_WIDTH)),
                full((experts, rows)),
                pl.BlockSpec((BLOCKS, 1, height, BLOCK), lambda e, s: (0, s[3], 0, 0)),
            ],
            scratch_shapes=[
                pltpu.VMEM((rows, 128), f32),
                pltpu.VMEM((rows, 128), f32),
                pltpu.VMEM((rows, ranks_in), bf16),
                pltpu.VMEM((ranks_in, rows), bf16),
                pltpu.VMEM((ranks_in, 2 * H), bf16),
                pltpu.VMEM((rows, ranks_down), f32),
                pltpu.VMEM((rows, ranks_down), bf16),
                pltpu.VMEM((rows, ranks_in), bf16),
                pltpu.VMEM((rows, H), bf16),
                pltpu.VMEM((rows, 2 * H), bf16),
                pltpu.VMEM((rows, ranks_down), bf16),
                pltpu.VMEM((ranks_down, H), f32),
                pltpu.VMEM((rows, MODEL_WIDTH), f32),
                pltpu.VMEM((rows, MODEL_WIDTH), f32),
            ],
        ),
        out_shape=[
            jax.ShapeDtypeStruct((rows, MODEL_WIDTH), bf16),
            jax.ShapeDtypeStruct((rows + experts, MODEL_WIDTH), bf16),
            jax.ShapeDtypeStruct((experts, rows), f32),
            jax.ShapeDtypeStruct(packed.shape, bf16),
        ],
        input_output_aliases={11: 3},
        compiler_params=params_of(1),
        name="experts",
        cost_estimate=pl.CostEstimate(
            flops=local * rows * 9 * (1 << 20),
            transcendentals=local * rows * H,
            bytes_accessed=20 << 20,
        ),
    )(scalars, x, cot, routes, router, w_in, w_down, a_in, b_in, a_down, b_down, packed)


def room_for(shape):
    return pl.pallas_call(
        lambda ref: None,
        out_specs=pl.BlockSpec(memory_space=pl.ANY),
        out_shape=jax.ShapeDtypeStruct(shape, bf16),
        name="room",
    )()


def pack_kernel(left, right, both, done):
    middle = left.shape[1]
    one = pltpu.make_async_copy(left, both.at[:, :middle], done.at[0])
    two = pltpu.make_async_copy(right, both.at[:, middle:], done.at[1])
    one.start()
    two.start()
    one.wait()
    two.wait()


def pack(left, right):
    anywhere = pl.BlockSpec(memory_space=pl.ANY)
    return pl.pallas_call(
        pack_kernel,
        in_specs=[anywhere, anywhere],
        out_specs=anywhere,
        out_shape=jax.ShapeDtypeStruct((left.shape[0], left.shape[1] + right.shape[1]), left.dtype),
        scratch_shapes=[pltpu.SemaphoreType.DMA((2,))],
        name="pack",
    )(left, right)


def open_back_kernel(count, order, cot, mid, gain, gates, router, weight_a, weight_b, low_map, up_map, low, att, *rest):
    parts = rest[:count]
    sums = rest[count : 3 * count]
    grad_mid, grad_att, grad_up, grad_low, columns = rest[3 * count :]
    gate_value = gates[...]
    half = gate_value.shape[0] // 2
    sides = []
    for side in range(2):
        value = None
        for at in range(count):
            pair = sums[2 * at + side][...].astype(f32)
            pair = pair[:half] + pair[half:]
            value = pair if value is None else value + pair
        sides.append(value)
    gate_grad = jnp.concatenate(sides, 0)
    logit = gate_value * (gate_grad - jnp.sum(gate_value * gate_grad, 0, keepdims=True))
    first = logit.astype(bf16)
    left = logit - first.astype(f32)
    second = left.astype(bf16)
    third = (left - second.astype(f32)).astype(bf16)
    grad = tn(first, router[...]) + (tn(second, router[...]) + tn(third, router[...]))
    for piece in parts:
        grad = grad + piece[...].astype(f32)
    total = cot[...].astype(f32) + norm_back(mid[...], gain[...].astype(f32), grad)
    grad_mid[...] = total
    branch = total.astype(bf16)
    low_grad = nt(branch, up_map[...]).astype(bf16)
    columns[...] = nn(low_grad, low_map[...])
    for side, weight in enumerate((weight_a, weight_b)):
        value = nt(branch, weight[...])
        for at in range(BLOCKS // 2):
            columns[:, column(order, side * BLOCKS // 2 + at)] += value[:, at * BLOCK : (at + 1) * BLOCK]
    grad_att[...] = columns[...].astype(bf16)
    up_part = tn(low[...], branch)
    low_part = tn(low_grad, att[...])

    @pl.when(pl.program_id(0) == 0)
    def _():
        grad_up[...] = up_part
        grad_low[...] = low_part

    @pl.when(pl.program_id(0) > 0)
    def _():
        grad_up[...] += up_part
        grad_low[...] += low_part


def open_back(order, cot, mid, gain, gates, router, weights, low_map, up_map, low, att, parts):
    rows = cot.shape[0]
    block = 256
    ranks = low_map.shape[0]
    experts = gates.shape[0]
    full = lambda shape: pl.BlockSpec(shape, lambda n, s: (0, 0))
    part = lambda width: pl.BlockSpec((block, width), lambda n, s: (n, 0))
    count = len(parts)
    below = rows // experts
    sums = [
        pl.BlockSpec((experts, block), lambda n, s: (below, n)),
        pl.BlockSpec((experts, block), lambda n, s: (below, rows // block + n)),
    ]

    def body(*refs):
        open_back_kernel(count, *refs)

    return pl.pallas_call(
        body,
        grid_spec=pltpu.PrefetchScalarGridSpec(
            num_scalar_prefetch=1,
            grid=(rows // block,),
            in_specs=[
                part(MODEL_WIDTH),
                part(MODEL_WIDTH),
                full((1, MODEL_WIDTH)),
                pl.BlockSpec((experts, block), lambda n, s: (0, n)),
                full((experts, MODEL_WIDTH)),
                *halves(weights, MODEL_WIDTH, lambda n: QKV // MODEL_WIDTH),
                full((ranks, QD)),
                full((ranks, MODEL_WIDTH)),
                part(ranks),
                part(QD),
            ]
            + [part(MODEL_WIDTH)] * count
            + sums * count,
            out_specs=[
                part(MODEL_WIDTH),
                part(QD),
                full((ranks, MODEL_WIDTH)),
                full((ranks, QD)),
            ],
            scratch_shapes=[pltpu.VMEM((block, QD), f32)],
        ),
        out_shape=[
            jax.ShapeDtypeStruct((rows, MODEL_WIDTH), f32),
            jax.ShapeDtypeStruct((rows, QD), bf16),
            jax.ShapeDtypeStruct((ranks, MODEL_WIDTH), f32),
            jax.ShapeDtypeStruct((ranks, QD), f32),
        ],
        compiler_params=params_of(1),
        name="open_back",
        cost_estimate=pl.CostEstimate(
            flops=2 * rows * QD * MODEL_WIDTH, transcendentals=0, bytes_accessed=14 << 20
        ),
    )(
        order, cot, mid, gain, gates, router, *weights, low_map, up_map, low, att, *parts,
        *[piece for piece in parts for _ in range(2)],
    )


def adapters_back_kernel(
    grad_query, grad_key, grad_value, low, normed, up_map, low_there, up_there, low_out, *results
):
    pieces = (grad_query, grad_key, grad_value)
    bounds = (0, QD, QD + KD, QKV)
    back = None
    ups = []
    for at in range(3):
        block = pieces[at][...]
        ups.append(tn(low[...], block)[at * R : (at + 1) * R])
        part = nt(block, up_map[:, bounds[at] : bounds[at + 1]])
        back = part if back is None else back + part
    value = back.astype(bf16)
    low_out[...] = value
    lows = tn(value, normed[...]) + low_there[...]
    if len(results) == 2:
        grad_up, grad_low = results
        grad_low[...] = lows
        for at in range(3):
            grad_up[:, bounds[at] : bounds[at + 1]] = ups[at]
        return
    (packed,) = results
    grad_up = jnp.concatenate(ups, 1)
    grad_out = up_there[3 * R :, :]
    small = BLOCK // 4
    lane = lanes_of((R, BLOCK))
    for owner in range(packed.shape[0]):
        tile = slice(owner // 4 * BLOCK, (owner // 4 + 1) * BLOCK)
        offset = owner % 4 * small
        first = jnp.zeros((R, BLOCK), f32)
        for at in range(4):
            piece = lows[at * R : (at + 1) * R, tile]
            shift = (at * small - offset) % BLOCK
            piece = pltpu.roll(piece, shift, 1) if shift else piece
            first = jnp.where((lane >= at * small) & (lane < (at + 1) * small), piece, first)
        piece = grad_up[:, owner // 2 * BLOCK : (owner // 2 + 1) * BLOCK]
        piece = pltpu.roll(piece, BLOCK // 2, 1) if owner % 2 else piece
        other = grad_out[:, tile]
        shift = (2 * small - offset) % BLOCK
        other = pltpu.roll(other, shift, 1) if shift else other
        packed[owner, :, :BLOCK] = first.astype(bf16)
        packed[owner, :, BLOCK:] = jnp.where(
            lane < 2 * small, piece, jnp.where(lane < 3 * small, other, 0.0)
        ).astype(bf16)


def adapters_back(grad_query, grad_key, grad_value, low, normed, up_map, low_there, up_there, devices):
    rows = normed.shape[0]
    ranks = up_map.shape[0]
    if devices * BLOCK // 4 == MODEL_WIDTH:
        results = [jax.ShapeDtypeStruct((devices, R, 2 * BLOCK), bf16)]
    else:
        results = [
            jax.ShapeDtypeStruct((R, QKV), f32),
            jax.ShapeDtypeStruct((ranks, MODEL_WIDTH), f32),
        ]
    back_low, *results = pl.pallas_call(
        adapters_back_kernel,
        out_shape=[jax.ShapeDtypeStruct((rows, ranks), bf16)] + results,
        compiler_params=pltpu.CompilerParams(vmem_limit_bytes=56 * 1024 * 1024),
        name="adapters_back",
        cost_estimate=pl.CostEstimate(
            flops=6 * rows * 256 * QKV, transcendentals=0, bytes_accessed=4 << 20
        ),
    )(grad_query, grad_key, grad_value, low, normed, up_map, low_there, up_there)
    if len(results) == 1:
        return results[0], back_low
    grad_up, grad_low = results
    small = MODEL_WIDTH // devices
    packed = jnp.concatenate(
        [
            grad_low.reshape(4, R, devices, small).transpose(2, 1, 0, 3).reshape(devices, R, 4 * small),
            grad_up.reshape(R, devices, 2 * small).transpose(1, 0, 2),
            up_there[3 * R :].reshape(R, devices, small).transpose(1, 0, 2),
            jnp.zeros((devices, R, small), f32),
        ],
        -1,
    )
    return packed.astype(bf16), back_low


def input_back_kernel(
    order, grad_query, grad_key, grad_value, low, weight_a, weight_b, low_map, hid, gain, mid, grad, columns
):
    columns[...] = nn(low[...], low_map[...])
    for side, weight in enumerate((weight_a, weight_b)):
        value = nt(grad_query[...], weight[:, :QD])
        value = value + nt(grad_key[...], weight[:, QD : QD + KD])
        value = value + nt(grad_value[...], weight[:, QD + KD :])
        for at in range(BLOCKS // 2):
            columns[:, column(order, side * BLOCKS // 2 + at)] += value[:, at * BLOCK : (at + 1) * BLOCK]
    rows = hid[...].astype(f32)
    grad[...] = (mid[...] + norm_back(rows, gain[...].astype(f32), columns[...])).astype(bf16)


def input_back(order, grad_query, grad_key, grad_value, low, weights, low_map, hidden, gain, mid):
    rows = hidden.shape[0]
    block = 256
    ranks = low_map.shape[0]
    full = lambda shape: pl.BlockSpec(shape, lambda n, s: (0, 0))
    part = lambda width: pl.BlockSpec((block, width), lambda n, s: (n, 0))
    return pl.pallas_call(
        input_back_kernel,
        grid_spec=pltpu.PrefetchScalarGridSpec(
            num_scalar_prefetch=1,
            grid=(rows // block,),
            in_specs=[
                part(QD),
                part(KD),
                part(KD),
                part(ranks),
                *halves(weights, QKV, lambda n: 0),
                full((ranks, MODEL_WIDTH)),
                part(MODEL_WIDTH),
                full((1, MODEL_WIDTH)),
                part(MODEL_WIDTH),
            ],
            out_specs=part(MODEL_WIDTH),
            scratch_shapes=[pltpu.VMEM((block, MODEL_WIDTH), f32)],
        ),
        out_shape=jax.ShapeDtypeStruct((rows, MODEL_WIDTH), bf16),
        compiler_params=params_of(1),
        name="input_back",
        cost_estimate=pl.CostEstimate(
            flops=2 * rows * QKV * MODEL_WIDTH, transcendentals=0, bytes_accessed=12 << 20
        ),
    )(order, grad_query, grad_key, grad_value, low, *weights, low_map, hidden, gain, mid)


def sum_experts_kernel(ids, pieces, a_in, b_in, a_down, b_down, acc):
    local = a_in.shape[0]
    small = a_down.shape[-1]
    acc[...] = jnp.zeros_like(acc)

    def step(index, carry):
        acc[ids[index]] += pieces[index].astype(f32)
        return carry

    lax.fori_loop(0, pieces.shape[0], step, 0)
    for e in range(local):
        a_in[e] = acc[:, e * 2 * R : (e + 1) * 2 * R, :]
        at = local * 2 * R + e * R
        b_down[e] = acc[:, at : at + R, :]
        at = local * 3 * R + e * R
        both = acc[:, at : at + R, :]
        b_in[e, :, 0] = both[:, :, :small]
        b_in[e, :, 1] = both[:, :, small:]
        at = local * 4 * R + e // 2 * R
        a_down[e] = acc[:, at : at + R, e % 2 * small : (e % 2 + 1) * small]


def sum_experts(ids, pieces, local):
    height = pieces.shape[1]
    lanes = pieces.shape[2]
    small = lanes // 2
    vmem = pl.BlockSpec(memory_space=pltpu.VMEM)
    return pl.pallas_call(
        sum_experts_kernel,
        in_specs=[pl.BlockSpec(memory_space=pltpu.SMEM), vmem],
        out_specs=[vmem, vmem, vmem, vmem],
        out_shape=[
            jax.ShapeDtypeStruct((local, NA, 2 * R, lanes), f32),
            jax.ShapeDtypeStruct((local, NA, 2, R, small), f32),
            jax.ShapeDtypeStruct((local, NA, R, small), f32),
            jax.ShapeDtypeStruct((local, NA, R, lanes), f32),
        ],
        scratch_shapes=[pltpu.VMEM((NA, height, lanes), f32)],
        compiler_params=pltpu.CompilerParams(vmem_limit_bytes=56 * 1024 * 1024),
        name="sum_experts",
    )(ids, pieces)


def sum_mixer_kernel(ids, pieces, grad_low, grad_up, grad_out, acc):
    width = grad_low.shape[-1]
    acc[...] = jnp.zeros_like(acc)

    def step(index, carry):
        acc[ids[index]] += pieces[index].astype(f32)
        return carry

    lax.fori_loop(0, pieces.shape[0], step, 0)
    total = acc[...]
    for at in range(4):
        grad_low[at] = total[:, :, at * width : (at + 1) * width]
    grad_up[...] = total[:, :, 4 * width : 6 * width]
    grad_out[...] = total[:, :, 6 * width : 7 * width]


def sum_mixer(ids, pieces):
    width = pieces.shape[2] // 8
    vmem = pl.BlockSpec(memory_space=pltpu.VMEM)
    return pl.pallas_call(
        sum_mixer_kernel,
        in_specs=[pl.BlockSpec(memory_space=pltpu.SMEM), vmem],
        out_specs=[vmem, vmem, vmem],
        out_shape=[
            jax.ShapeDtypeStruct((4, NA, R, width), f32),
            jax.ShapeDtypeStruct((NA, R, 2 * width), f32),
            jax.ShapeDtypeStruct((NA, R, width), f32),
        ],
        scratch_shapes=[pltpu.VMEM((NA, R, 8 * width), f32)],
        compiler_params=pltpu.CompilerParams(vmem_limit_bytes=56 * 1024 * 1024),
        name="sum_mixer",
    )(ids, pieces)


def rope_tables(rows):
    half = HS // 2
    frequency = (10000.0 ** (-2.0 * np.arange(half, dtype=np.float32) / HS)).astype(np.float32)
    angles = np.arange(rows, dtype=np.float32)[:, None] * frequency[None, :]
    cos = np.cos(angles.astype(np.float64)).astype(np.float32)
    sin = np.sin(angles.astype(np.float64)).astype(np.float32)
    return (
        jnp.asarray(np.concatenate([cos, cos, cos, cos], 1)),
        jnp.asarray(np.concatenate([-sin, sin, -sin, sin], 1)),
    )


def swap(value, bit):
    return lax.ppermute(value, "dp", [(at, at ^ bit) for at in range(BLOCKS)])


def both_neighbours(weight):
    return swap(weight, 2), swap(weight, 4)


def across(pair):
    one, two = pair
    middle = one.shape[0] // 2
    return swap(two[:middle], 2), swap(one[middle:], 4)


def tied(*values):
    return lax.optimization_barrier(values)


def order_of(row):
    if lax.axis_size("dp") != BLOCKS:
        return jnp.arange(BLOCKS, dtype=jnp.int32)
    return row.astype(jnp.int32) ^ jnp.array([0, 2, 4, 6, 1, 3, 5, 7], jnp.int32)


def to_owners(packed, owners, local):
    split = owners // BLOCKS
    if split == 1:
        return packed
    slots = packed.shape[1]
    edge = local * 3 * R
    wide = packed[:, :, :edge].reshape(BLOCKS, slots, edge, split, BLOCK // split)
    wide = wide.transpose(0, 3, 1, 2, 4).reshape(owners, slots, edge, BLOCK // split)
    rest = packed.shape[2] - edge
    narrow = packed[:, :, edge:].reshape(BLOCKS, slots, rest, 2, split, BLOCK // 2 // split)
    narrow = narrow.transpose(0, 4, 1, 2, 3, 5).reshape(owners, slots, rest, BLOCK // split)
    return jnp.concatenate([wide, narrow], 2)


def joined(left, right):
    return (left.astype(f32) + right.astype(f32)).astype(bf16)


def on_device(
    hidden,
    cotangent,
    lengths,
    adapter_ids,
    routes,
    attn_gain,
    ffn_gain,
    query_key_value_weight,
    w_out,
    w_router,
    w_gate_up,
    w_down,
    attention_lowmap,
    attention_query_key_value_upmap,
    attention_output_upmap,
    expert_gate_up_lowmap,
    expert_gate_up_upmap,
    expert_down_lowmap,
    expert_down_upmap,
):
    groups = lax.axis_size("expert")
    owners = lax.axis_size("dp")
    place = lax.axis_index("expert")
    row = lax.axis_index("dp")
    devices = groups * owners
    sequence = row * groups + place
    rows = hidden.shape[0]
    experts = w_router.shape[1]
    local = w_gate_up.shape[0]
    width = MODEL_WIDTH // owners
    attn_gain = attn_gain.reshape(1, MODEL_WIDTH)
    ffn_gain = ffn_gain.reshape(1, MODEL_WIDTH)
    length = lax.dynamic_slice(lengths, (sequence,), (1,))
    forward = [(at, (at + 1) % groups) for at in range(groups)]
    backward = [(at, (at - 1) % groups) for at in range(groups)]

    mine = lax.dynamic_slice(adapter_ids.reshape(owners, groups), (0, place), (owners, 1))[:, 0]
    low_turned = attention_lowmap.transpose(1, 0, 3, 2).reshape(NA, 4 * R, width)
    up_turned = (
        attention_query_key_value_upmap.reshape(NA, R, 2, width)
        .transpose(0, 2, 1, 3)
        .reshape(NA, 2 * R, width)
    )
    adapters = jnp.concatenate([low_turned, up_turned, attention_output_upmap], 1)[mine]
    adapters = lax.all_to_all(adapters, "dp", 0, 0, tiled=True)
    order = order_of(row)
    low_map = adapters[:, : 4 * R].transpose(1, 0, 2).reshape(4 * R, MODEL_WIDTH)
    up = (
        adapters[:, 4 * R : 6 * R]
        .reshape(owners, 2, R, width)
        .transpose(2, 0, 1, 3)
        .reshape(R, QKV)
    )
    up_out = adapters[:, 6 * R :].transpose(1, 0, 2).reshape(R, MODEL_WIDTH)
    column = jnp.arange(QKV, dtype=jnp.int32)
    part = jnp.where(column < QD, 0, jnp.where(column < QD + KD, 1, 2))
    up_map = jnp.where(
        part[None, None, :] == jnp.arange(4, dtype=jnp.int32)[:, None, None], up[None], 0
    ).reshape(4 * R, QKV)
    up_out_map = jnp.concatenate([jnp.zeros((3 * R, MODEL_WIDTH), bf16), up_out], 0)

    first = place * local
    router = jnp.roll(w_router.T, -first, axis=0)
    router_wide = jnp.concatenate(
        [router, jnp.zeros((128 - experts, MODEL_WIDTH), router.dtype)], 0
    )

    offsets = [0, 1] + [groups - 1] * (groups > 2) + list(range(2, groups - 1))
    offset = jnp.array(offsets, jnp.int32)
    source = (place - offset + groups) % groups
    tags = adapter_ids.reshape(owners, groups)[:, source]
    slot = jnp.arange(groups, dtype=jnp.int32)
    table = jnp.stack(
        [
            source,
            lax.dynamic_slice(tags, (row, 0), (1, groups))[0],
            offset * local,
            slot,
            jnp.full((groups,), first, jnp.int32),
            jnp.where(slot == 0, 0, source),
        ],
        1,
    )

    both = pack(query_key_value_weight, w_out)
    if owners == BLOCKS:
        pair = both_neighbours(both)
        pair, order, router, router_wide, table, tags, attn_gain, ffn_gain, length = tied(
            pair, order, router, router_wide, table, tags, attn_gain, ffn_gain, length
        )
        near = jnp.concatenate([both, *pair, *across(pair)], 0)
        near, low_map, up_map, up_out_map = tied(near, low_map, up_map, up_out_map)
        weights = near, swap(near, 1)
    else:
        whole = lax.all_gather(both, "dp", axis=0, tiled=True)
        weights = whole, whole

    cos, sin = rope_tables(rows)

    cots = lax.all_gather(cotangent, "expert", axis=0, tiled=True)

    qkv, low, normed_in = project(order, hidden, attn_gain, weights, low_map, up_map, cos, sin)
    attended, lse = attend(length, qkv)
    mid, normed_mid, low_out = close_mixer(
        order, attended, hidden, ffn_gain, weights, low_map, up_out_map
    )

    a_in = expert_gate_up_lowmap.transpose(0, 1, 3, 2)
    a_down = expert_down_lowmap.transpose(0, 1, 3, 2)

    xs = {0: normed_mid, 1: lax.ppermute(normed_mid, "expert", forward)}
    packed = room_for((BLOCKS, groups, local * 9 * R // 2, BLOCK))
    ran = {}
    for at, offset in enumerate(offsets):
        *ran[offset], gate_part, packed = run_experts(
            table[at],
            xs[offset],
            cotangent if at == 0 else cots,
            routes,
            router_wide,
            w_gate_up,
            w_down,
            a_in,
            expert_gate_up_upmap,
            a_down,
            expert_down_upmap,
            experts,
            packed,
        )
        if at == 0:
            gates = gate_part
            if groups > 2:
                normed_mid, packed = tied(normed_mid, packed)
                xs[groups - 1] = lax.ppermute(normed_mid, "expert", backward)
        elif at < groups - 2:
            value, packed = tied(xs[at], packed)
            xs[at + 1] = lax.ppermute(value, "expert", forward)
        if at == 2:
            ran[1][1], ran[1][0], packed = tied(ran[1][1], ran[1][0], packed)

    grad_far = lax.ppermute(ran[1][1], "expert", forward)
    out_far = lax.ppermute(ran[1][0], "expert", forward)
    for offset in range(2, groups):
        grad_part = joined(ran[offset][1], grad_far)
        if offset == 2:
            packed, out_far = tied(packed, out_far)
        if offset == groups - 1:
            pieces = lax.all_to_all(to_owners(packed, owners, local), "dp", 0, 0, tiled=True)
            pieces = pieces.reshape(devices, pieces.shape[2], width)
            g_a_in, g_b_in, g_a_down, g_b_down = sum_experts(tags.reshape(devices), pieces, local)
            grad_part, g_a_down = tied(grad_part, g_a_down)
        grad_far = lax.ppermute(grad_part, "expert", forward)
    if groups > 2:
        out_part = joined(ran[2][0], out_far)
        out_part, grad_far = tied(out_part, grad_far)
        out_far = lax.ppermute(out_part, "expert", forward)

    grad_mid, grad_attended, grad_up_out, grad_low_out = open_back(
        order,
        cotangent,
        mid,
        ffn_gain,
        gates,
        router,
        weights,
        low_map,
        up_out_map,
        low_out,
        attended,
        [ran[0][1], grad_far],
    )
    grad_query, grad_key, grad_value = attend_back(length, qkv, grad_attended, lse, cos, sin)
    out_far, grad_query = tied(out_far, grad_query)
    for offset in range(3, groups):
        out_far = lax.ppermute(joined(ran[offset][0], out_far), "expert", forward)
    packed, back_low = adapters_back(
        grad_query, grad_key, grad_value, low, normed_in, up_map, grad_low_out, grad_up_out, devices
    )
    packed = lax.all_to_all(packed, ("dp", "expert"), 0, 0, tiled=True)
    m_a, m_b, m_o = sum_mixer(adapter_ids, packed)

    grad_hidden = input_back(
        order, grad_query, grad_key, grad_value, back_low, weights, low_map, hidden, attn_gain, grad_mid
    )
    out = (mid + ran[0][0].astype(f32) + out_far.astype(f32)).astype(bf16)
    return (
        out,
        grad_hidden,
        m_a.transpose(0, 1, 3, 2),
        m_b,
        m_o,
        g_a_in.transpose(0, 1, 3, 2),
        g_b_in,
        g_a_down.transpose(0, 1, 3, 2),
        g_b_down,
    )


def solution(mesh):
    in_specs = (
        P(("dp", "expert"), None),
        P(("dp", "expert"), None),
        P(),
        P(),
        P("dp", None),
        P(),
        P(),
        P("dp", None),
        P("dp", None),
        P(),
        P("expert", None, None),
        P("expert", None, None),
        P(None, None, "dp", None),
        P(None, None, "dp"),
        P(None, None, "dp"),
        P("expert", None, None, None),
        P("expert", None, None, None, None),
        P("expert", None, None, None),
        P("expert", None, None, None),
    )
    out_specs = (
        P(("dp", "expert"), None),
        P(("dp", "expert"), None),
        P(None, None, ("dp", "expert"), None),
        P(None, None, ("dp", "expert")),
        P(None, None, ("dp", "expert")),
        P("expert", None, "dp", None),
        P("expert", None, None, None, "dp"),
        P("expert", None, "dp", None),
        P("expert", None, None, "dp"),
    )
    return jax.shard_map(
        on_device, mesh=mesh, in_specs=in_specs, out_specs=out_specs, check_vma=False
    )
```

```python
import numpy as np
import jax
import jax.numpy as jnp
from jax import lax
from jax.experimental import pallas as pl
from jax.experimental.pallas import tpu as pltpu
from jax.sharding import PartitionSpec as P

MODEL_WIDTH = 1024
HQ = 16
KVH = 8
HS = 64
H = 512
TOP = 8
R = 16
NA = 8
QD = HQ * HS
KD = KVH * HS
QKV = QD + 2 * KD

epsilon = 1e-06
f32 = jnp.float32
bf16 = jnp.bfloat16


def nn(left, right):
    return lax.dot_general(left, right, (((1,), (0,)), ((), ())), preferred_element_type=f32)


def nt(left, right):
    return lax.dot_general(left, right, (((1,), (1,)), ((), ())), preferred_element_type=f32)


def tn(left, right):
    return lax.dot_general(left, right, (((0,), (0,)), ((), ())), preferred_element_type=f32)


def lanes_of(shape):
    return lax.broadcasted_iota(jnp.int32, shape, len(shape) - 1)


def row_scale(rows):
    return lax.rsqrt(jnp.mean(rows * rows, -1, keepdims=True) + epsilon)


def norm_back(rows, gain, grad):
    scale = row_scale(rows)
    scaled = grad * gain
    return scale * scaled - rows * (scale * scale * scale) * jnp.mean(
        rows * scaled, -1, keepdims=True
    )


def rope_swap(rows):
    width = rows.shape[-1]
    lane = lanes_of(rows.shape)
    return jnp.where(
        lane % HS < HS // 2,
        pltpu.roll(rows, width - HS // 2, 1),
        pltpu.roll(rows, HS // 2, 1),
    )


def both_halves(pair, half):
    rows = pair.astype(f32)
    lane = lanes_of(rows.shape)
    rolled = pltpu.roll(rows, HS, 1)
    keep = (lane < HS) == (half == 0)
    return jnp.where(keep, rows, rolled).astype(bf16)


def stacked_heads(pair):
    lane = lanes_of(pair.shape)
    zero = jnp.zeros_like(pair)
    return jnp.concatenate(
        [jnp.where(lane < HS, pair, zero), jnp.where(lane < HS, zero, pair)], 0
    )


def params_of(count):
    return pltpu.CompilerParams(
        dimension_semantics=("arbitrary",) * count, vmem_limit_bytes=56 * 1024 * 1024
    )


BLOCK = 128
BLOCKS = MODEL_WIDTH // BLOCK
HALF = MODEL_WIDTH // 2


def column(order, at):
    return pl.ds(pl.multiple_of(order[at] * BLOCK, BLOCK), BLOCK)


def halves(weights, width, index):
    there = 1 if weights[0] is weights[1] else 0
    return [
        pl.BlockSpec((HALF, width), lambda n, s: (0, index(n))),
        pl.BlockSpec((HALF, width), lambda n, s: (there, index(n))),
    ]


def project_kernel(
    order, hid, gain, weight_a, weight_b, low_map, up_map, cos, sin, qkv, low, normed, turned_rows
):
    step = pl.program_id(0)
    blocks = pl.num_programs(0)

    @pl.when(step == 0)
    def _():
        rows = hid[...].astype(f32)
        value = (rows * row_scale(rows) * gain[...].astype(f32)).astype(bf16)
        normed[...] = value
        low[...] = nt(value, low_map[...]).astype(bf16)
        for at in range(BLOCKS):
            turned_rows[:, at * BLOCK : (at + 1) * BLOCK] = normed[:, column(order, at)]

    value = (
        nn(turned_rows[:, :HALF], weight_a[...])
        + nn(turned_rows[:, HALF:], weight_b[...])
        + nn(low[...], up_map[...])
    )

    @pl.when(step < blocks * 3 // 4)
    def _():
        for part in range(value.shape[1] // 128):
            piece = value[:, part * 128 : part * 128 + 128]
            turned = piece * cos[...] + rope_swap(piece) * sin[...]
            qkv[:, part * 128 : part * 128 + 128] = turned.astype(bf16)

    @pl.when(step >= blocks * 3 // 4)
    def _():
        qkv[...] = value.astype(bf16)


def project(order, hidden, gain, weights, low_map, up_map, cos, sin):
    rows = hidden.shape[0]
    block = 512
    ranks = low_map.shape[0]
    full = lambda shape: pl.BlockSpec(shape, lambda n, s: (0, 0))
    return pl.pallas_call(
        project_kernel,
        grid_spec=pltpu.PrefetchScalarGridSpec(
            num_scalar_prefetch=1,
            grid=(QKV // block,),
            in_specs=[
                full((rows, MODEL_WIDTH)),
                full((1, MODEL_WIDTH)),
                *halves(weights, block, lambda n: n),
                full((ranks, MODEL_WIDTH)),
                pl.BlockSpec((ranks, block), lambda n, s: (0, n)),
                full((rows, 128)),
                full((rows, 128)),
            ],
            out_specs=[
                pl.BlockSpec((rows, block), lambda n, s: (0, n)),
                full((rows, ranks)),
                full((rows, MODEL_WIDTH)),
            ],
            scratch_shapes=[pltpu.VMEM((rows, MODEL_WIDTH), bf16)],
        ),
        out_shape=[
            jax.ShapeDtypeStruct((rows, QKV), bf16),
            jax.ShapeDtypeStruct((rows, ranks), bf16),
            jax.ShapeDtypeStruct((rows, MODEL_WIDTH), bf16),
        ],
        compiler_params=params_of(1),
        name="project",
        cost_estimate=pl.CostEstimate(
            flops=2 * rows * QKV * MODEL_WIDTH, transcendentals=0, bytes_accessed=8 << 20
        ),
    )(order, hidden, gain, *weights, low_map, up_map, cos, sin)


ROWB = 128


def length_column(length, count):
    key = lax.broadcasted_iota(jnp.int32, (count, 1), 0)
    return jnp.where(key < length, 0.0, -1e30)


def causal_block():
    key = lax.broadcasted_iota(jnp.int32, (ROWB, 2 * ROWB), 0)
    return jnp.where(key <= lanes_of((ROWB, 2 * ROWB)) % ROWB, 0.0, -1e30)


def masked_scores(queries, keys, start, bias, causal):
    count = start + ROWB
    scores = nt(keys[:count], (queries.astype(f32) * 0.125).astype(bf16))
    near = scores[start:] + (bias[start:count] + causal)
    if start == 0:
        return near
    return jnp.concatenate([scores[:start] + bias[:start], near], 0)


def attend_kernel(scalars, query, key, value, result, lse):
    half = pl.program_id(0) % 2
    keys = both_halves(key[...], half)
    values = both_halves(value[...], half)
    rows = query.shape[0]
    bias = length_column(scalars[0], rows)
    causal = causal_block()
    for start in range(0, rows, ROWB):
        count = start + ROWB
        stacked = stacked_heads(query[start:count, :])
        scores = masked_scores(stacked, keys, start, bias, causal)
        top = jnp.max(scores, 0, keepdims=True)
        shifted = jnp.exp(scores - top)
        total = jnp.sum(shifted, 0, keepdims=True)
        prob = (shifted * (1.0 / total)).astype(bf16)
        mixed = tn(prob, values[:count])
        lane = lanes_of((ROWB, 128))
        result[start:count, :] = jnp.where(lane < HS, mixed[:ROWB], mixed[ROWB:]).astype(bf16)
        logs = top + jnp.log(total)
        lse[0, 0:1, start:count] = logs[:, :ROWB]
        lse[0, 1:2, start:count] = logs[:, ROWB:]


def attend(length, qkv):
    rows = qkv.shape[0]
    pairs = KVH
    return pl.pallas_call(
        attend_kernel,
        grid_spec=pltpu.PrefetchScalarGridSpec(
            num_scalar_prefetch=1,
            grid=(pairs,),
            in_specs=[
                pl.BlockSpec((rows, 128), lambda g, s: (0, g)),
                pl.BlockSpec((rows, 128), lambda g, s: (0, QD // 128 + g // 2)),
                pl.BlockSpec((rows, 128), lambda g, s: (0, (QD + KD) // 128 + g // 2)),
            ],
            out_specs=[
                pl.BlockSpec((rows, 128), lambda g, s: (0, g)),
                pl.BlockSpec((1, 2, rows), lambda g, s: (g, 0, 0)),
            ],
        ),
        out_shape=[
            jax.ShapeDtypeStruct((rows, QD), bf16),
            jax.ShapeDtypeStruct((pairs, 2, rows), f32),
        ],
        compiler_params=params_of(1),
        name="attend",
        cost_estimate=pl.CostEstimate(
            flops=8 * rows * rows * QD, transcendentals=rows * rows * HQ, bytes_accessed=4 << 20
        ),
    )(length, qkv, qkv, qkv)


def attend_back_kernel(
    scalars, query, key, value, grad, lse, cos, sin, grad_query, grad_key, grad_value, key_acc, value_acc
):
    half = pl.program_id(0) % 2
    keys = both_halves(key[...], half)
    values = both_halves(value[...], half)
    rows = query.shape[0]
    bias = length_column(scalars[0], rows)
    causal = causal_block()
    for start in reversed(range(0, rows, ROWB)):
        count = start + ROWB
        stacked = stacked_heads(query[start:count, :])
        grads = stacked_heads(grad[start:count, :])
        scores = masked_scores(stacked, keys, start, bias, causal)
        logs = jnp.concatenate([lse[0, 0:1, start:count], lse[0, 1:2, start:count]], 1)
        prob = jnp.exp(scores - logs)
        grad_prob = nt(values[:count], grads)
        delta = jnp.sum(prob * grad_prob, 0, keepdims=True)
        grad_score = (prob * (grad_prob - delta)).astype(bf16)
        mixed = tn(grad_score, keys[:count])
        lane = lanes_of((ROWB, 128))
        turned = 0.125 * jnp.where(lane < HS, mixed[:ROWB], mixed[ROWB:])
        turned = turned * cos[start:count, :] - rope_swap(turned) * sin[start:count, :]
        grad_query[start:count, :] = turned.astype(bf16)
        key_part = nn(grad_score, stacked)
        value_part = nn(prob.astype(bf16), grads)
        if count == rows:
            key_acc[...] = key_part
            value_acc[...] = value_part
        else:
            key_acc[:count, :] += key_part
            value_acc[:count, :] += value_part
    total = key_acc[...]
    total = 0.125 * (total + pltpu.roll(total, HS, 1))
    total = (total * cos[...] - rope_swap(total) * sin[...]).astype(bf16)
    other = value_acc[...]
    other = (other + pltpu.roll(other, HS, 1)).astype(bf16)

    @pl.when(half == 0)
    def _():
        grad_key[...] = total
        grad_value[...] = other

    @pl.when(half == 1)
    def _():
        low_half = lanes_of(total.shape) < HS
        grad_key[...] = jnp.where(low_half, grad_key[...], total)
        grad_value[...] = jnp.where(low_half, grad_value[...], other)


def attend_back(length, qkv, grad, lse, cos, sin):
    rows = qkv.shape[0]
    pairs = KVH
    return pl.pallas_call(
        attend_back_kernel,
        grid_spec=pltpu.PrefetchScalarGridSpec(
            num_scalar_prefetch=1,
            grid=(pairs,),
            in_specs=[
                pl.BlockSpec((rows, 128), lambda g, s: (0, g)),
                pl.BlockSpec((rows, 128), lambda g, s: (0, QD // 128 + g // 2)),
                pl.BlockSpec((rows, 128), lambda g, s: (0, (QD + KD) // 128 + g // 2)),
                pl.BlockSpec((rows, 128), lambda g, s: (0, g)),
                pl.BlockSpec((1, 2, rows), lambda g, s: (g, 0, 0)),
                pl.BlockSpec((rows, 128), lambda g, s: (0, 0)),
                pl.BlockSpec((rows, 128), lambda g, s: (0, 0)),
            ],
            out_specs=[
                pl.BlockSpec((rows, 128), lambda g, s: (0, g)),
                pl.BlockSpec((rows, 128), lambda g, s: (0, g // 2)),
                pl.BlockSpec((rows, 128), lambda g, s: (0, g // 2)),
            ],
            scratch_shapes=[pltpu.VMEM((rows, 128), f32), pltpu.VMEM((rows, 128), f32)],
        ),
        out_shape=[
            jax.ShapeDtypeStruct((rows, QD), bf16),
            jax.ShapeDtypeStruct((rows, KD), bf16),
            jax.ShapeDtypeStruct((rows, KD), bf16),
        ],
        compiler_params=params_of(1),
        name="attend_back",
        cost_estimate=pl.CostEstimate(
            flops=20 * rows * rows * QD, transcendentals=rows * rows * HQ, bytes_accessed=8 << 20
        ),
    )(length, qkv, qkv, qkv, grad, lse, cos, sin)


def close_kernel(order, att, hid, gain, weight_a, weight_b, low_map, up_map, mid, normed, low):
    low_value = nt(att[...], low_map[...]).astype(bf16)
    low[...] = low_value
    turned = jnp.concatenate([att[:, column(order, at)] for at in range(BLOCKS)], 1)
    stream = hid[...].astype(f32) + (
        nn(turned[:, :HALF], weight_a[...])
        + nn(turned[:, HALF:], weight_b[...])
        + nn(low_value, up_map[...])
    )
    mid[...] = stream
    normed[...] = (stream * row_scale(stream) * gain[...].astype(f32)).astype(bf16)


def close_mixer(order, att, hidden, gain, weights, low_map, up_map):
    rows = hidden.shape[0]
    block = 256
    ranks = low_map.shape[0]
    full = lambda shape: pl.BlockSpec(shape, lambda n, s: (0, 0))
    part = lambda width: pl.BlockSpec((block, width), lambda n, s: (n, 0))
    return pl.pallas_call(
        close_kernel,
        grid_spec=pltpu.PrefetchScalarGridSpec(
            num_scalar_prefetch=1,
            grid=(rows // block,),
            in_specs=[
                part(QD),
                part(MODEL_WIDTH),
                full((1, MODEL_WIDTH)),
                *halves(weights, MODEL_WIDTH, lambda n: QKV // MODEL_WIDTH),
                full((ranks, QD)),
                full((ranks, MODEL_WIDTH)),
            ],
            out_specs=[part(MODEL_WIDTH), part(MODEL_WIDTH), part(ranks)],
        ),
        out_shape=[
            jax.ShapeDtypeStruct((rows, MODEL_WIDTH), f32),
            jax.ShapeDtypeStruct((rows, MODEL_WIDTH), bf16),
            jax.ShapeDtypeStruct((rows, ranks), bf16),
        ],
        compiler_params=params_of(1),
        name="close_mixer",
        cost_estimate=pl.CostEstimate(
            flops=2 * rows * QD * MODEL_WIDTH, transcendentals=0, bytes_accessed=8 << 20
        ),
    )(order, att, hidden, gain, *weights, low_map, up_map)


def side_by_side(left, right):
    values = []
    for at in range(BLOCKS):
        tile = slice(at // 2 * BLOCK, (at // 2 + 1) * BLOCK)
        low_half = lanes_of((R, BLOCK)) < BLOCK // 2
        if at % 2 == 0:
            value = jnp.where(low_half, left[:, tile], pltpu.roll(right[:, tile], BLOCK // 2, 1))
        else:
            value = jnp.where(low_half, pltpu.roll(left[:, tile], BLOCK // 2, 1), right[:, tile])
        values.append(value.astype(bf16))
    return values


def expert_kernel(
    scalars,
    x,
    cot,
    routes,
    router,
    w_in,
    w_down,
    a_in,
    b_in,
    a_down,
    b_down,
    *rest,
):
    (
        sums_out,
        gates_out,
        packed,
        gates,
        gate_sums,
        low_in,
        low_in_turned,
        b_in_all,
        back_low,
        gated_low,
        back_in,
        acts,
        grads,
        low_grads,
        down_acc,
        out_acc,
        grad_acc,
    ) = rest[-17:]
    expert = pl.program_id(0)
    last = pl.num_programs(0) - 1
    rows = x.shape[0]
    block = rows
    local = a_in.shape[0]
    a_in_all = a_in[...].reshape(local * 2 * R, MODEL_WIDTH)
    a_down_all = a_down[...].reshape(local * R, H)
    b_down_all = b_down[...].reshape(local * R, MODEL_WIDTH)

    @pl.when(expert == 0)
    def _():
        logits = nt(x[...], router[...])
        experts = gates_out.shape[0]
        lane = lanes_of(logits.shape)
        name = lane + scalars[4]
        name = jnp.where(name >= experts, name - experts, name)
        name = jnp.where(lane < experts, name, -1)
        chosen = name == routes[:, 0:1]
        for k in range(1, TOP):
            chosen = chosen | (name == routes[:, k : k + 1])
        top = jnp.max(jnp.where(chosen, logits, -1e30), -1, keepdims=True)
        shifted = jnp.where(chosen, jnp.exp(jnp.where(chosen, logits - top, 0.0)), 0.0)
        weights = shifted / jnp.sum(shifted, -1, keepdims=True)
        gates[...] = weights
        gates_out[...] = weights.T[: gates_out.shape[0], :]
        low = nt(x[...], a_in_all)
        low_in[...] = low.astype(bf16)
        low_in_turned[...] = low.T.astype(bf16)
        back_low[...] = nt(cot[...], b_down_all)
        b_in_all[...] = jnp.zeros_like(b_in_all)
        for e in range(local):
            b_in_all[e * 2 * R : e * 2 * R + R, :H] = b_in[e, 0, 0]
            b_in_all[e * 2 * R + R : (e + 1) * 2 * R, H:] = b_in[e, 0, 1]
        gate_sums[...] = jnp.zeros_like(gate_sums)
        gated_low[...] = jnp.zeros_like(gated_low)
        back_in[...] = jnp.zeros_like(back_in)
        out_acc[...] = jnp.zeros_like(out_acc)
        grad_acc[...] = jnp.zeros_like(grad_acc)
        down_acc[...] = jnp.zeros_like(down_acc)

    def row_step(index, carry):
        at = pl.ds(pl.multiple_of(index * block, block), block)
        lane_in = lanes_of((block, local * 2 * R))
        lane_down = lanes_of((block, local * R))
        in_mine = (lane_in >= expert * 2 * R) & (lane_in < (expert + 1) * 2 * R)
        down_mine = (lane_down >= expert * R) & (lane_down < (expert + 1) * R)
        gate_all = gates[at, :]
        gate_lane = lanes_of(gate_all.shape) == expert
        weight = jnp.sum(jnp.where(gate_lane, gate_all, 0.0), -1, keepdims=True)
        mine = low_in[at, :]
        mine = jnp.where(in_mine, mine, jnp.zeros_like(mine))
        both = nn(x[at, :], w_in[0]) + nn(mine, b_in_all[...])
        gate = both[:, :H]
        upper = both[:, H:]
        sigmoid = jax.nn.sigmoid(gate)
        silu = gate * sigmoid
        act = (silu * upper).astype(bf16)
        acts[at, :] = act
        act_wide = act.astype(f32)
        low = jnp.where(down_mine, nt(act, a_down_all), 0.0).astype(bf16).astype(f32)
        plain = nt(cot[at, :], w_down[0])
        low_plain = back_low[at, :]
        dots = jnp.sum(act_wide * plain, -1, keepdims=True) + jnp.sum(
            low * low_plain, -1, keepdims=True
        )
        sum_lane = lanes_of(gate_all.shape) == expert + scalars[2]
        gate_sums[at, :] += jnp.where(sum_lane, dots, 0.0)
        low_grad = jnp.where(down_mine, weight * low_plain, 0.0).astype(bf16)
        low_grads[at, :] = low_grad
        grad_act = weight * plain + nn(low_grad, a_down_all)
        grad_first = grad_act * upper * sigmoid * (1.0 + gate * (1.0 - sigmoid))
        grad_second = grad_act * silu
        grad_both = jnp.concatenate(
            [grad_first.astype(bf16), grad_second.astype(bf16)], 1
        )
        grads[at, :] = grad_both
        gated_low[at, :] += (weight * low).astype(bf16)
        out_acc[at, :] += nn((weight * act_wide).astype(bf16), w_down[0])
        grad_acc[at, :] += nt(grad_both, w_in[0])
        low_back = jnp.where(in_mine, nt(grad_both, b_in_all[...]), 0.0)
        back_in[at, :] += low_back.astype(bf16)
        return carry

    lax.fori_loop(0, rows // block, row_step, 0)

    turned = low_in_turned[pl.ds(pl.multiple_of(expert * 2 * R, 2 * R), 2 * R), :]
    product = nn(turned, grads[...])
    first_b_in = local * 3 * R
    here = pl.ds(pl.multiple_of(first_b_in + expert * R, R), R)
    for at, value in enumerate(side_by_side(product[:R, :H], product[R:, H:])):
        packed[at, 0, here, :] = value
    down_acc[...] += tn(low_grads[...], acts[...])

    @pl.when(expert == last)
    def _():
        sums_out[:rows, :] = (grad_acc[...] + nn(back_in[...], a_in_all)).astype(bf16)
        experts = gates_out.shape[0]
        sums = gate_sums[...].T[:experts, :]
        sums = jnp.concatenate([sums[: experts // 2], sums[experts // 2 :]], 1)
        high = sums.astype(bf16).astype(f32)
        edge = rows + experts
        sums_out[rows:edge, :] = jnp.concatenate([high, sums - high], 0).astype(bf16)
        sums_out[edge:, :] = (out_acc[...] + nn(gated_low[...], b_down_all)).astype(bf16)
        wide = tn(back_in[...], x[...]).astype(bf16)
        tall = tn(gated_low[...], cot[...]).astype(bf16)
        for at in range(BLOCKS):
            columns = slice(at * BLOCK, (at + 1) * BLOCK)
            packed[at, 0, : local * 2 * R, :] = wide[:, columns]
            packed[at, 0, local * 2 * R : first_b_in, :] = tall[:, columns]
        for pair in range(local // 2):
            lower = down_acc[pair * 2 * R : pair * 2 * R + R, :]
            upper = down_acc[pair * 2 * R + R : (pair + 1) * 2 * R, :]
            row = local * 4 * R + pair * R
            for at, value in enumerate(side_by_side(lower, upper)):
                packed[at, 0, row : row + R, :] = value


def run_experts(
    scalars, x, cot, routes, router, w_in, w_down, a_in, b_in, a_down, b_down, experts, slots, packed
):
    rows = x.shape[0]
    local = w_in.shape[0]
    ranks_in = local * 2 * R
    ranks_down = local * R
    height = local * 9 * R // 2
    kept = [] if packed is None else [packed]
    full = lambda shape: pl.BlockSpec(shape, lambda e, s: (0,) * len(shape))
    return pl.pallas_call(
        expert_kernel,
        grid_spec=pltpu.PrefetchScalarGridSpec(
            num_scalar_prefetch=1,
            grid=(local,),
            in_specs=[
                full((rows, MODEL_WIDTH)),
                pl.BlockSpec((rows, MODEL_WIDTH), lambda e, s: (s[5], 0)),
                pl.BlockSpec((rows, TOP), lambda e, s: (s[0], 0)),
                full((128, MODEL_WIDTH)),
                pl.BlockSpec((1, MODEL_WIDTH, 2 * H), lambda e, s: (e, 0, 0)),
                pl.BlockSpec((1, H, MODEL_WIDTH), lambda e, s: (e, 0, 0)),
                pl.BlockSpec((local, 1, 2 * R, MODEL_WIDTH), lambda e, s: (0, s[1], 0, 0)),
                pl.BlockSpec((local, 1, 2, R, H), lambda e, s: (0, s[1], 0, 0, 0)),
                pl.BlockSpec((local, 1, R, H), lambda e, s: (0, s[1], 0, 0)),
                pl.BlockSpec((local, 1, R, MODEL_WIDTH), lambda e, s: (0, s[1], 0, 0)),
            ]
            + [pl.BlockSpec(memory_space=pl.ANY)] * len(kept),
            out_specs=[
                full((2 * rows + experts, MODEL_WIDTH)),
                full((experts, rows)),
                pl.BlockSpec((BLOCKS, 1, height, BLOCK), lambda e, s: (0, s[3], 0, 0)),
            ],
            scratch_shapes=[
                pltpu.VMEM((rows, 128), f32),
                pltpu.VMEM((rows, 128), f32),
                pltpu.VMEM((rows, ranks_in), bf16),
                pltpu.VMEM((ranks_in, rows), bf16),
                pltpu.VMEM((ranks_in, 2 * H), bf16),
                pltpu.VMEM((rows, ranks_down), f32),
                pltpu.VMEM((rows, ranks_down), bf16),
                pltpu.VMEM((rows, ranks_in), bf16),
                pltpu.VMEM((rows, H), bf16),
                pltpu.VMEM((rows, 2 * H), bf16),
                pltpu.VMEM((rows, ranks_down), bf16),
                pltpu.VMEM((ranks_down, H), f32),
                pltpu.VMEM((rows, MODEL_WIDTH), f32),
                pltpu.VMEM((rows, MODEL_WIDTH), f32),
            ],
        ),
        out_shape=[
            jax.ShapeDtypeStruct((2 * rows + experts, MODEL_WIDTH), bf16),
            jax.ShapeDtypeStruct((experts, rows), f32),
            jax.ShapeDtypeStruct((BLOCKS, slots, height, BLOCK), bf16),
        ],
        input_output_aliases={11: 2} if kept else {},
        compiler_params=params_of(1),
        name="experts",
        cost_estimate=pl.CostEstimate(
            flops=local * rows * 9 * (1 << 20),
            transcendentals=local * rows * H,
            bytes_accessed=20 << 20,
        ),
    )(scalars, x, cot, routes, router, w_in, w_down, a_in, b_in, a_down, b_down, *kept)


def pack_kernel(left, right, both):
    both[:, : left.shape[1]] = left[...]
    both[:, left.shape[1] :] = right[...]


def pack(left, right):
    return pl.pallas_call(
        pack_kernel,
        out_shape=jax.ShapeDtypeStruct((left.shape[0], left.shape[1] + right.shape[1]), left.dtype),
        name="pack",
    )(left, right)


def open_back_kernel(count, order, cot, mid, gain, gates, router, weight_a, weight_b, low_map, up_map, low, att, *rest):
    parts = rest[:count]
    sums = rest[count : 3 * count]
    grad_mid, grad_att, grad_up, grad_low, columns = rest[3 * count :]
    gate_value = gates[...]
    half = gate_value.shape[0] // 2
    sides = []
    for side in range(2):
        value = None
        for at in range(count):
            pair = sums[2 * at + side][...].astype(f32)
            pair = pair[:half] + pair[half:]
            value = pair if value is None else value + pair
        sides.append(value)
    gate_grad = jnp.concatenate(sides, 0)
    logit = gate_value * (gate_grad - jnp.sum(gate_value * gate_grad, 0, keepdims=True))
    first = logit.astype(bf16)
    left = logit - first.astype(f32)
    second = left.astype(bf16)
    third = (left - second.astype(f32)).astype(bf16)
    grad = tn(first, router[...]) + (tn(second, router[...]) + tn(third, router[...]))
    for piece in parts:
        grad = grad + piece[...].astype(f32)
    total = cot[...].astype(f32) + norm_back(mid[...], gain[...].astype(f32), grad)
    grad_mid[...] = total
    branch = total.astype(bf16)
    low_grad = nt(branch, up_map[...]).astype(bf16)
    columns[...] = nn(low_grad, low_map[...])
    for side, weight in enumerate((weight_a, weight_b)):
        value = nt(branch, weight[...])
        for at in range(BLOCKS // 2):
            columns[:, column(order, side * BLOCKS // 2 + at)] += value[:, at * BLOCK : (at + 1) * BLOCK]
    grad_att[...] = columns[...].astype(bf16)
    up_part = tn(low[...], branch)
    low_part = tn(low_grad, att[...])

    @pl.when(pl.program_id(0) == 0)
    def _():
        grad_up[...] = up_part
        grad_low[...] = low_part

    @pl.when(pl.program_id(0) > 0)
    def _():
        grad_up[...] += up_part
        grad_low[...] += low_part


def open_back(order, cot, mid, gain, gates, router, weights, low_map, up_map, low, att, parts):
    rows = cot.shape[0]
    block = 256
    ranks = low_map.shape[0]
    experts = gates.shape[0]
    full = lambda shape: pl.BlockSpec(shape, lambda n, s: (0, 0))
    part = lambda width: pl.BlockSpec((block, width), lambda n, s: (n, 0))
    count = len(parts)
    below = rows // experts
    sums = [
        pl.BlockSpec((experts, block), lambda n, s: (below, n)),
        pl.BlockSpec((experts, block), lambda n, s: (below, rows // block + n)),
    ]

    def body(*refs):
        open_back_kernel(count, *refs)

    return pl.pallas_call(
        body,
        grid_spec=pltpu.PrefetchScalarGridSpec(
            num_scalar_prefetch=1,
            grid=(rows // block,),
            in_specs=[
                part(MODEL_WIDTH),
                part(MODEL_WIDTH),
                full((1, MODEL_WIDTH)),
                pl.BlockSpec((experts, block), lambda n, s: (0, n)),
                full((experts, MODEL_WIDTH)),
                *halves(weights, MODEL_WIDTH, lambda n: QKV // MODEL_WIDTH),
                full((ranks, QD)),
                full((ranks, MODEL_WIDTH)),
                part(ranks),
                part(QD),
            ]
            + [part(MODEL_WIDTH)] * count
            + sums * count,
            out_specs=[
                part(MODEL_WIDTH),
                part(QD),
                full((ranks, MODEL_WIDTH)),
                full((ranks, QD)),
            ],
            scratch_shapes=[pltpu.VMEM((block, QD), f32)],
        ),
        out_shape=[
            jax.ShapeDtypeStruct((rows, MODEL_WIDTH), f32),
            jax.ShapeDtypeStruct((rows, QD), bf16),
            jax.ShapeDtypeStruct((ranks, MODEL_WIDTH), f32),
            jax.ShapeDtypeStruct((ranks, QD), f32),
        ],
        compiler_params=params_of(1),
        name="open_back",
        cost_estimate=pl.CostEstimate(
            flops=2 * rows * QD * MODEL_WIDTH, transcendentals=0, bytes_accessed=14 << 20
        ),
    )(
        order, cot, mid, gain, gates, router, *weights, low_map, up_map, low, att, *parts,
        *[piece for piece in parts for _ in range(2)],
    )


def adapters_back_kernel(
    grad_query, grad_key, grad_value, low, normed, up_map, low_there, up_there, low_out, *results
):
    pieces = (grad_query, grad_key, grad_value)
    bounds = (0, QD, QD + KD, QKV)
    back = None
    ups = []
    for at in range(3):
        block = pieces[at][...]
        ups.append(tn(low[...], block)[at * R : (at + 1) * R])
        part = nt(block, up_map[:, bounds[at] : bounds[at + 1]])
        back = part if back is None else back + part
    value = back.astype(bf16)
    low_out[...] = value
    lows = tn(value, normed[...]) + low_there[...]
    if len(results) == 2:
        grad_up, grad_low = results
        grad_low[...] = lows
        for at in range(3):
            grad_up[:, bounds[at] : bounds[at + 1]] = ups[at]
        return
    (packed,) = results
    grad_up = jnp.concatenate(ups, 1)
    grad_out = up_there[3 * R :, :]
    small = BLOCK // 4
    lane = lanes_of((R, BLOCK))
    for owner in range(packed.shape[0]):
        tile = slice(owner // 4 * BLOCK, (owner // 4 + 1) * BLOCK)
        offset = owner % 4 * small
        first = jnp.zeros((R, BLOCK), f32)
        for at in range(4):
            piece = lows[at * R : (at + 1) * R, tile]
            shift = (at * small - offset) % BLOCK
            piece = pltpu.roll(piece, shift, 1) if shift else piece
            first = jnp.where((lane >= at * small) & (lane < (at + 1) * small), piece, first)
        piece = grad_up[:, owner // 2 * BLOCK : (owner // 2 + 1) * BLOCK]
        piece = pltpu.roll(piece, BLOCK // 2, 1) if owner % 2 else piece
        other = grad_out[:, tile]
        shift = (2 * small - offset) % BLOCK
        other = pltpu.roll(other, shift, 1) if shift else other
        packed[owner, :, :BLOCK] = first.astype(bf16)
        packed[owner, :, BLOCK:] = jnp.where(
            lane < 2 * small, piece, jnp.where(lane < 3 * small, other, 0.0)
        ).astype(bf16)


def adapters_back(grad_query, grad_key, grad_value, low, normed, up_map, low_there, up_there, devices):
    rows = normed.shape[0]
    ranks = up_map.shape[0]
    if devices * BLOCK // 4 == MODEL_WIDTH:
        results = [jax.ShapeDtypeStruct((devices, R, 2 * BLOCK), bf16)]
    else:
        results = [
            jax.ShapeDtypeStruct((R, QKV), f32),
            jax.ShapeDtypeStruct((ranks, MODEL_WIDTH), f32),
        ]
    back_low, *results = pl.pallas_call(
        adapters_back_kernel,
        out_shape=[jax.ShapeDtypeStruct((rows, ranks), bf16)] + results,
        compiler_params=pltpu.CompilerParams(vmem_limit_bytes=56 * 1024 * 1024),
        name="adapters_back",
        cost_estimate=pl.CostEstimate(
            flops=6 * rows * 256 * QKV, transcendentals=0, bytes_accessed=4 << 20
        ),
    )(grad_query, grad_key, grad_value, low, normed, up_map, low_there, up_there)
    if len(results) == 1:
        return results[0], back_low
    grad_up, grad_low = results
    small = MODEL_WIDTH // devices
    packed = jnp.concatenate(
        [
            grad_low.reshape(4, R, devices, small).transpose(2, 1, 0, 3).reshape(devices, R, 4 * small),
            grad_up.reshape(R, devices, 2 * small).transpose(1, 0, 2),
            up_there[3 * R :].reshape(R, devices, small).transpose(1, 0, 2),
            jnp.zeros((devices, R, small), f32),
        ],
        -1,
    )
    return packed.astype(bf16), back_low


def input_back_kernel(
    order, grad_query, grad_key, grad_value, low, weight_a, weight_b, low_map, hid, gain, mid, grad, columns
):
    columns[...] = nn(low[...], low_map[...])
    for side, weight in enumerate((weight_a, weight_b)):
        value = nt(grad_query[...], weight[:, :QD])
        value = value + nt(grad_key[...], weight[:, QD : QD + KD])
        value = value + nt(grad_value[...], weight[:, QD + KD :])
        for at in range(BLOCKS // 2):
            columns[:, column(order, side * BLOCKS // 2 + at)] += value[:, at * BLOCK : (at + 1) * BLOCK]
    rows = hid[...].astype(f32)
    grad[...] = (mid[...] + norm_back(rows, gain[...].astype(f32), columns[...])).astype(bf16)


def input_back(order, grad_query, grad_key, grad_value, low, weights, low_map, hidden, gain, mid):
    rows = hidden.shape[0]
    block = 256
    ranks = low_map.shape[0]
    full = lambda shape: pl.BlockSpec(shape, lambda n, s: (0, 0))
    part = lambda width: pl.BlockSpec((block, width), lambda n, s: (n, 0))
    return pl.pallas_call(
        input_back_kernel,
        grid_spec=pltpu.PrefetchScalarGridSpec(
            num_scalar_prefetch=1,
            grid=(rows // block,),
            in_specs=[
                part(QD),
                part(KD),
                part(KD),
                part(ranks),
                *halves(weights, QKV, lambda n: 0),
                full((ranks, MODEL_WIDTH)),
                part(MODEL_WIDTH),
                full((1, MODEL_WIDTH)),
                part(MODEL_WIDTH),
            ],
            out_specs=part(MODEL_WIDTH),
            scratch_shapes=[pltpu.VMEM((block, MODEL_WIDTH), f32)],
        ),
        out_shape=jax.ShapeDtypeStruct((rows, MODEL_WIDTH), bf16),
        compiler_params=params_of(1),
        name="input_back",
        cost_estimate=pl.CostEstimate(
            flops=2 * rows * QKV * MODEL_WIDTH, transcendentals=0, bytes_accessed=12 << 20
        ),
    )(order, grad_query, grad_key, grad_value, low, *weights, low_map, hidden, gain, mid)


def sum_experts_kernel(ids, pieces, a_in, b_in, a_down, b_down, acc):
    local = a_in.shape[0]
    small = a_down.shape[-1]
    acc[...] = jnp.zeros_like(acc)

    def step(index, carry):
        acc[ids[index]] += pieces[index].astype(f32)
        return carry

    lax.fori_loop(0, pieces.shape[0], step, 0)
    for e in range(local):
        a_in[e] = acc[:, e * 2 * R : (e + 1) * 2 * R, :]
        at = local * 2 * R + e * R
        b_down[e] = acc[:, at : at + R, :]
        at = local * 3 * R + e * R
        both = acc[:, at : at + R, :]
        b_in[e, :, 0] = both[:, :, :small]
        b_in[e, :, 1] = both[:, :, small:]
        at = local * 4 * R + e // 2 * R
        a_down[e] = acc[:, at : at + R, e % 2 * small : (e % 2 + 1) * small]


def sum_experts(ids, pieces, local):
    height = pieces.shape[1]
    lanes = pieces.shape[2]
    small = lanes // 2
    vmem = pl.BlockSpec(memory_space=pltpu.VMEM)
    return pl.pallas_call(
        sum_experts_kernel,
        in_specs=[pl.BlockSpec(memory_space=pltpu.SMEM), vmem],
        out_specs=[vmem, vmem, vmem, vmem],
        out_shape=[
            jax.ShapeDtypeStruct((local, NA, 2 * R, lanes), f32),
            jax.ShapeDtypeStruct((local, NA, 2, R, small), f32),
            jax.ShapeDtypeStruct((local, NA, R, small), f32),
            jax.ShapeDtypeStruct((local, NA, R, lanes), f32),
        ],
        scratch_shapes=[pltpu.VMEM((NA, height, lanes), f32)],
        compiler_params=pltpu.CompilerParams(vmem_limit_bytes=56 * 1024 * 1024),
        name="sum_experts",
    )(ids, pieces)


def sum_mixer_kernel(ids, pieces, grad_low, grad_up, grad_out, acc):
    width = grad_low.shape[-1]
    acc[...] = jnp.zeros_like(acc)

    def step(index, carry):
        acc[ids[index]] += pieces[index].astype(f32)
        return carry

    lax.fori_loop(0, pieces.shape[0], step, 0)
    total = acc[...]
    for at in range(4):
        grad_low[at] = total[:, :, at * width : (at + 1) * width]
    grad_up[...] = total[:, :, 4 * width : 6 * width]
    grad_out[...] = total[:, :, 6 * width : 7 * width]


def sum_mixer(ids, pieces):
    width = pieces.shape[2] // 8
    vmem = pl.BlockSpec(memory_space=pltpu.VMEM)
    return pl.pallas_call(
        sum_mixer_kernel,
        in_specs=[pl.BlockSpec(memory_space=pltpu.SMEM), vmem],
        out_specs=[vmem, vmem, vmem],
        out_shape=[
            jax.ShapeDtypeStruct((4, NA, R, width), f32),
            jax.ShapeDtypeStruct((NA, R, 2 * width), f32),
            jax.ShapeDtypeStruct((NA, R, width), f32),
        ],
        scratch_shapes=[pltpu.VMEM((NA, R, 8 * width), f32)],
        compiler_params=pltpu.CompilerParams(vmem_limit_bytes=56 * 1024 * 1024),
        name="sum_mixer",
    )(ids, pieces)


def rope_tables(rows):
    half = HS // 2
    frequency = (10000.0 ** (-2.0 * np.arange(half, dtype=np.float32) / HS)).astype(np.float32)
    angles = np.arange(rows, dtype=np.float32)[:, None] * frequency[None, :]
    cos = np.cos(angles.astype(np.float64)).astype(np.float32)
    sin = np.sin(angles.astype(np.float64)).astype(np.float32)
    return (
        jnp.asarray(np.concatenate([cos, cos, cos, cos], 1)),
        jnp.asarray(np.concatenate([-sin, sin, -sin, sin], 1)),
    )


def swap(value, bit):
    return lax.ppermute(value, "dp", [(at, at ^ bit) for at in range(BLOCKS)])


def both_neighbours(weight):
    return swap(weight, 2), swap(weight, 4)


def across(pair):
    one, two = pair
    middle = one.shape[0] // 2
    return swap(two[:middle], 2), swap(one[middle:], 4)


def tied(*values):
    return lax.optimization_barrier(values)


def order_of(row):
    if lax.axis_size("dp") != BLOCKS:
        return jnp.arange(BLOCKS, dtype=jnp.int32)
    return row.astype(jnp.int32) ^ jnp.array([0, 2, 4, 6, 1, 3, 5, 7], jnp.int32)


def to_owners(packed, owners, local):
    split = owners // BLOCKS
    if split == 1:
        return packed
    slots = packed.shape[1]
    edge = local * 3 * R
    wide = packed[:, :, :edge].reshape(BLOCKS, slots, edge, split, BLOCK // split)
    wide = wide.transpose(0, 3, 1, 2, 4).reshape(owners, slots, edge, BLOCK // split)
    rest = packed.shape[2] - edge
    narrow = packed[:, :, edge:].reshape(BLOCKS, slots, rest, 2, split, BLOCK // 2 // split)
    narrow = narrow.transpose(0, 4, 1, 2, 3, 5).reshape(owners, slots, rest, BLOCK // split)
    return jnp.concatenate([wide, narrow], 2)


def joined(left, right):
    return (left.astype(f32) + right.astype(f32)).astype(bf16)


def on_device(
    hidden,
    cotangent,
    lengths,
    adapter_ids,
    routes,
    attn_gain,
    ffn_gain,
    query_key_value_weight,
    w_out,
    w_router,
    w_gate_up,
    w_down,
    attention_lowmap,
    attention_query_key_value_upmap,
    attention_output_upmap,
    expert_gate_up_lowmap,
    expert_gate_up_upmap,
    expert_down_lowmap,
    expert_down_upmap,
):
    groups = lax.axis_size("expert")
    owners = lax.axis_size("dp")
    place = lax.axis_index("expert")
    row = lax.axis_index("dp")
    devices = groups * owners
    sequence = row * groups + place
    rows = hidden.shape[0]
    experts = w_router.shape[1]
    local = w_gate_up.shape[0]
    width = MODEL_WIDTH // owners
    attn_gain = attn_gain.reshape(1, MODEL_WIDTH)
    ffn_gain = ffn_gain.reshape(1, MODEL_WIDTH)
    length = lax.dynamic_slice(lengths, (sequence,), (1,))
    forward = [(at, (at + 1) % groups) for at in range(groups)]
    backward = [(at, (at - 1) % groups) for at in range(groups)]

    mine = lax.dynamic_slice(adapter_ids.reshape(owners, groups), (0, place), (owners, 1))[:, 0]
    low_turned = attention_lowmap.transpose(1, 0, 3, 2).reshape(NA, 4 * R, width)
    up_turned = (
        attention_query_key_value_upmap.reshape(NA, R, 2, width)
        .transpose(0, 2, 1, 3)
        .reshape(NA, 2 * R, width)
    )
    adapters = jnp.concatenate([low_turned, up_turned, attention_output_upmap], 1)[mine]
    adapters = lax.all_to_all(adapters, "dp", 0, 0, tiled=True)
    order = order_of(row)
    first = place * local
    router = jnp.roll(w_router.T, -first, axis=0)
    router_wide = jnp.concatenate(
        [router, jnp.zeros((128 - experts, MODEL_WIDTH), router.dtype)], 0
    )

    offsets = [0, 1] + [groups - 1] * (groups > 2) + list(range(2, groups - 1))
    offset = jnp.array(offsets, jnp.int32)
    source = (place - offset + groups) % groups
    tags = adapter_ids.reshape(owners, groups)[:, source]
    slot = jnp.arange(groups, dtype=jnp.int32)
    table = jnp.stack(
        [
            source,
            lax.dynamic_slice(tags, (row, 0), (1, groups))[0],
            offset * local,
            slot,
            jnp.full((groups,), first, jnp.int32),
            jnp.where(slot == 0, 0, source),
        ],
        1,
    )

    both = pack(query_key_value_weight, w_out)
    if owners == BLOCKS:
        pair = both_neighbours(both)
        pair, order, router, router_wide, table, tags, attn_gain, ffn_gain, length = tied(
            pair, order, router, router_wide, table, tags, attn_gain, ffn_gain, length
        )
        near = jnp.concatenate([both, *pair, *across(pair)], 0)
        near, adapters = tied(near, adapters)
        weights = near, swap(near, 1)
    else:
        whole = lax.all_gather(both, "dp", axis=0, tiled=True)
        weights = whole, whole

    low_map = adapters[:, : 4 * R].transpose(1, 0, 2).reshape(4 * R, MODEL_WIDTH)
    up = (
        adapters[:, 4 * R : 6 * R]
        .reshape(owners, 2, R, width)
        .transpose(2, 0, 1, 3)
        .reshape(R, QKV)
    )
    up_out = adapters[:, 6 * R :].transpose(1, 0, 2).reshape(R, MODEL_WIDTH)
    column = jnp.arange(QKV, dtype=jnp.int32)
    part = jnp.where(column < QD, 0, jnp.where(column < QD + KD, 1, 2))
    up_map = jnp.where(
        part[None, None, :] == jnp.arange(4, dtype=jnp.int32)[:, None, None], up[None], 0
    ).reshape(4 * R, QKV)
    up_out_map = jnp.concatenate([jnp.zeros((3 * R, MODEL_WIDTH), bf16), up_out], 0)

    cos, sin = rope_tables(rows)

    cots = lax.all_gather(cotangent, "expert", axis=0, tiled=True)

    qkv, low, normed_in = project(order, hidden, attn_gain, weights, low_map, up_map, cos, sin)
    attended, lse = attend(length, qkv)
    mid, normed_mid, low_out = close_mixer(
        order, attended, hidden, ffn_gain, weights, low_map, up_out_map
    )

    a_in = expert_gate_up_lowmap.transpose(0, 1, 3, 2)
    a_down = expert_down_lowmap.transpose(0, 1, 3, 2)

    xs = {0: normed_mid, 1: lax.ppermute(normed_mid, "expert", forward)}
    packed = None
    ran = {}
    for at, offset in enumerate(offsets):
        ran[offset], gate_part, packed = run_experts(
            table[at],
            xs[offset],
            cotangent if at == 0 else cots,
            routes,
            router_wide,
            w_gate_up,
            w_down,
            a_in,
            expert_gate_up_upmap,
            a_down,
            expert_down_upmap,
            experts,
            groups,
            packed,
        )
        if at == 0:
            gates = gate_part
            if groups > 2:
                normed_mid, packed = tied(normed_mid, packed)
                xs[groups - 1] = lax.ppermute(normed_mid, "expert", backward)
        elif at < groups - 2:
            value, packed = tied(xs[at], packed)
            xs[at + 1] = lax.ppermute(value, "expert", forward)
        if at == 2:
            first_sums, packed = tied(ran[1], packed)

    pieces = lax.all_to_all(to_owners(packed, owners, local), "dp", 0, 0, tiled=True)
    pieces = pieces.reshape(devices, pieces.shape[2], width)
    g_a_in, g_b_in, g_a_down, g_b_down = sum_experts(tags.reshape(devices), pieces, local)

    edge = rows + experts
    both_far = lax.ppermute(first_sums if groups > 2 else ran[1], "expert", forward)
    grad_far, out_far = both_far, both_far[edge:]
    for offset in range(2, groups):
        grad_part = joined(ran[offset][:edge], grad_far[:edge])
        if offset == groups - 1:
            grad_part, g_a_down = tied(grad_part, g_a_down)
        grad_far = lax.ppermute(grad_part, "expert", forward)
    if groups > 2:
        out_part = joined(ran[2][edge:], out_far)
        out_part, grad_far = tied(out_part, grad_far)
        out_far = lax.ppermute(out_part, "expert", forward)

    grad_mid, grad_attended, grad_up_out, grad_low_out = open_back(
        order,
        cotangent,
        mid,
        ffn_gain,
        gates,
        router,
        weights,
        low_map,
        up_out_map,
        low_out,
        attended,
        [ran[0], grad_far],
    )
    grad_query, grad_key, grad_value = attend_back(length, qkv, grad_attended, lse, cos, sin)
    out_far, grad_query = tied(out_far, grad_query)
    for offset in range(3, groups):
        out_far = lax.ppermute(joined(ran[offset][edge:], out_far), "expert", forward)
    packed, back_low = adapters_back(
        grad_query, grad_key, grad_value, low, normed_in, up_map, grad_low_out, grad_up_out, devices
    )
    packed = lax.all_to_all(packed, ("dp", "expert"), 0, 0, tiled=True)
    m_a, m_b, m_o = sum_mixer(adapter_ids, packed)

    grad_hidden = input_back(
        order, grad_query, grad_key, grad_value, back_low, weights, low_map, hidden, attn_gain, grad_mid
    )
    out = (mid + ran[0][edge:].astype(f32) + out_far.astype(f32)).astype(bf16)
    return (
        out,
        grad_hidden,
        m_a.transpose(0, 1, 3, 2),
        m_b,
        m_o,
        g_a_in.transpose(0, 1, 3, 2),
        g_b_in,
        g_a_down.transpose(0, 1, 3, 2),
        g_b_down,
    )


def solution(mesh):
    in_specs = (
        P(("dp", "expert"), None),
        P(("dp", "expert"), None),
        P(),
        P(),
        P("dp", None),
        P(),
        P(),
        P("dp", None),
        P("dp", None),
        P(),
        P("expert", None, None),
        P("expert", None, None),
        P(None, None, "dp", None),
        P(None, None, "dp"),
        P(None, None, "dp"),
        P("expert", None, None, None),
        P("expert", None, None, None, None),
        P("expert", None, None, None),
        P("expert", None, None, None),
    )
    out_specs = (
        P(("dp", "expert"), None),
        P(("dp", "expert"), None),
        P(None, None, ("dp", "expert"), None),
        P(None, None, ("dp", "expert")),
        P(None, None, ("dp", "expert")),
        P("expert", None, "dp", None),
        P("expert", None, None, None, "dp"),
        P("expert", None, "dp", None),
        P("expert", None, None, "dp"),
    )
    return jax.shard_map(
        on_device, mesh=mesh, in_specs=in_specs, out_specs=out_specs, check_vma=False
    )
```

```python
import numpy as np
import jax
import jax.numpy as jnp
from jax import lax
from jax.experimental import pallas as pl
from jax.experimental.pallas import tpu as pltpu
from jax.sharding import PartitionSpec as P

MODEL_WIDTH = 1024
HQ = 16
KVH = 8
HS = 64
H = 512
TOP = 8
R = 16
NA = 8
QD = HQ * HS
KD = KVH * HS
QKV = QD + 2 * KD

epsilon = 1e-06
f32 = jnp.float32
bf16 = jnp.bfloat16


def nn(left, right):
    return lax.dot_general(left, right, (((1,), (0,)), ((), ())), preferred_element_type=f32)


def nt(left, right):
    return lax.dot_general(left, right, (((1,), (1,)), ((), ())), preferred_element_type=f32)


def tn(left, right):
    return lax.dot_general(left, right, (((0,), (0,)), ((), ())), preferred_element_type=f32)


def lanes_of(shape):
    return lax.broadcasted_iota(jnp.int32, shape, len(shape) - 1)


def row_scale(rows):
    return lax.rsqrt(jnp.mean(rows * rows, -1, keepdims=True) + epsilon)


def norm_back(rows, gain, grad):
    scale = row_scale(rows)
    scaled = grad * gain
    return scale * scaled - rows * (scale * scale * scale) * jnp.mean(
        rows * scaled, -1, keepdims=True
    )


def rope_swap(rows):
    width = rows.shape[-1]
    lane = lanes_of(rows.shape)
    return jnp.where(
        lane % HS < HS // 2,
        pltpu.roll(rows, width - HS // 2, 1),
        pltpu.roll(rows, HS // 2, 1),
    )


def both_halves(pair, half):
    rows = pair.astype(f32)
    lane = lanes_of(rows.shape)
    rolled = pltpu.roll(rows, HS, 1)
    keep = (lane < HS) == (half == 0)
    return jnp.where(keep, rows, rolled).astype(bf16)


def stacked_heads(pair):
    lane = lanes_of(pair.shape)
    zero = jnp.zeros_like(pair)
    return jnp.concatenate(
        [jnp.where(lane < HS, pair, zero), jnp.where(lane < HS, zero, pair)], 0
    )


def params_of(count):
    return pltpu.CompilerParams(
        dimension_semantics=("arbitrary",) * count, vmem_limit_bytes=56 * 1024 * 1024
    )


BLOCK = 128
BLOCKS = MODEL_WIDTH // BLOCK
HALF = MODEL_WIDTH // 2


def column(order, at):
    return pl.ds(pl.multiple_of(order[at] * BLOCK, BLOCK), BLOCK)


def halves(weights, width, index):
    there = 1 if weights[0] is weights[1] else 0
    return [
        pl.BlockSpec((HALF, width), lambda n, s: (0, index(n))),
        pl.BlockSpec((HALF, width), lambda n, s: (there, index(n))),
    ]


def project_kernel(
    order, hid, gain, weight_a, weight_b, low_map, up_map, cos, sin, qkv, low, normed, turned_rows
):
    step = pl.program_id(0)
    blocks = pl.num_programs(0)

    @pl.when(step == 0)
    def _():
        rows = hid[...].astype(f32)
        value = (rows * row_scale(rows) * gain[...].astype(f32)).astype(bf16)
        normed[...] = value
        low[...] = nt(value, low_map[...]).astype(bf16)
        for at in range(BLOCKS):
            turned_rows[:, at * BLOCK : (at + 1) * BLOCK] = normed[:, column(order, at)]

    value = (
        nn(turned_rows[:, :HALF], weight_a[...])
        + nn(turned_rows[:, HALF:], weight_b[...])
        + nn(low[...], up_map[...])
    )

    @pl.when(step < blocks * 3 // 4)
    def _():
        for part in range(value.shape[1] // 128):
            piece = value[:, part * 128 : part * 128 + 128]
            turned = piece * cos[...] + rope_swap(piece) * sin[...]
            qkv[:, part * 128 : part * 128 + 128] = turned.astype(bf16)

    @pl.when(step >= blocks * 3 // 4)
    def _():
        qkv[...] = value.astype(bf16)


def project(order, hidden, gain, weights, low_map, up_map, cos, sin):
    rows = hidden.shape[0]
    block = 512
    ranks = low_map.shape[0]
    full = lambda shape: pl.BlockSpec(shape, lambda n, s: (0, 0))
    return pl.pallas_call(
        project_kernel,
        grid_spec=pltpu.PrefetchScalarGridSpec(
            num_scalar_prefetch=1,
            grid=(QKV // block,),
            in_specs=[
                full((rows, MODEL_WIDTH)),
                full((1, MODEL_WIDTH)),
                *halves(weights, block, lambda n: n),
                full((ranks, MODEL_WIDTH)),
                pl.BlockSpec((ranks, block), lambda n, s: (0, n)),
                full((rows, 128)),
                full((rows, 128)),
            ],
            out_specs=[
                pl.BlockSpec((rows, block), lambda n, s: (0, n)),
                full((rows, ranks)),
                full((rows, MODEL_WIDTH)),
            ],
            scratch_shapes=[pltpu.VMEM((rows, MODEL_WIDTH), bf16)],
        ),
        out_shape=[
            jax.ShapeDtypeStruct((rows, QKV), bf16),
            jax.ShapeDtypeStruct((rows, ranks), bf16),
            jax.ShapeDtypeStruct((rows, MODEL_WIDTH), bf16),
        ],
        compiler_params=params_of(1),
        name="project",
        cost_estimate=pl.CostEstimate(
            flops=2 * rows * QKV * MODEL_WIDTH, transcendentals=0, bytes_accessed=8 << 20
        ),
    )(order, hidden, gain, *weights, low_map, up_map, cos, sin)


ROWB = 128


def length_column(length, count):
    key = lax.broadcasted_iota(jnp.int32, (count, 1), 0)
    return jnp.where(key < length, 0.0, -1e30)


def causal_block():
    key = lax.broadcasted_iota(jnp.int32, (ROWB, 2 * ROWB), 0)
    return jnp.where(key <= lanes_of((ROWB, 2 * ROWB)) % ROWB, 0.0, -1e30)


def masked_scores(queries, keys, start, bias, causal):
    count = start + ROWB
    scores = nt(keys[:count], (queries.astype(f32) * 0.125).astype(bf16))
    near = scores[start:] + (bias[start:count] + causal)
    if start == 0:
        return near
    return jnp.concatenate([scores[:start] + bias[:start], near], 0)


def attend_kernel(scalars, query, key, value, result, lse):
    half = pl.program_id(0) % 2
    keys = both_halves(key[...], half)
    values = both_halves(value[...], half)
    rows = query.shape[0]
    bias = length_column(scalars[0], rows)
    causal = causal_block()
    for start in range(0, rows, ROWB):
        count = start + ROWB
        stacked = stacked_heads(query[start:count, :])
        scores = masked_scores(stacked, keys, start, bias, causal)
        top = jnp.max(scores, 0, keepdims=True)
        shifted = jnp.exp(scores - top)
        total = jnp.sum(shifted, 0, keepdims=True)
        prob = (shifted * (1.0 / total)).astype(bf16)
        mixed = tn(prob, values[:count])
        lane = lanes_of((ROWB, 128))
        result[start:count, :] = jnp.where(lane < HS, mixed[:ROWB], mixed[ROWB:]).astype(bf16)
        logs = top + jnp.log(total)
        lse[0, 0:1, start:count] = logs[:, :ROWB]
        lse[0, 1:2, start:count] = logs[:, ROWB:]


def attend(length, qkv):
    rows = qkv.shape[0]
    pairs = KVH
    return pl.pallas_call(
        attend_kernel,
        grid_spec=pltpu.PrefetchScalarGridSpec(
            num_scalar_prefetch=1,
            grid=(pairs,),
            in_specs=[
                pl.BlockSpec((rows, 128), lambda g, s: (0, g)),
                pl.BlockSpec((rows, 128), lambda g, s: (0, QD // 128 + g // 2)),
                pl.BlockSpec((rows, 128), lambda g, s: (0, (QD + KD) // 128 + g // 2)),
            ],
            out_specs=[
                pl.BlockSpec((rows, 128), lambda g, s: (0, g)),
                pl.BlockSpec((1, 2, rows), lambda g, s: (g, 0, 0)),
            ],
        ),
        out_shape=[
            jax.ShapeDtypeStruct((rows, QD), bf16),
            jax.ShapeDtypeStruct((pairs, 2, rows), f32),
        ],
        compiler_params=params_of(1),
        name="attend",
        cost_estimate=pl.CostEstimate(
            flops=8 * rows * rows * QD, transcendentals=rows * rows * HQ, bytes_accessed=4 << 20
        ),
    )(length, qkv, qkv, qkv)


def attend_back_kernel(
    scalars, query, key, value, grad, lse, cos, sin, grad_query, grad_key, grad_value, key_acc, value_acc
):
    half = pl.program_id(0) % 2
    keys = both_halves(key[...], half)
    values = both_halves(value[...], half)
    rows = query.shape[0]
    bias = length_column(scalars[0], rows)
    causal = causal_block()
    for start in reversed(range(0, rows, ROWB)):
        count = start + ROWB
        stacked = stacked_heads(query[start:count, :])
        grads = stacked_heads(grad[start:count, :])
        scores = masked_scores(stacked, keys, start, bias, causal)
        logs = jnp.concatenate([lse[0, 0:1, start:count], lse[0, 1:2, start:count]], 1)
        prob = jnp.exp(scores - logs)
        grad_prob = nt(values[:count], grads)
        delta = jnp.sum(prob * grad_prob, 0, keepdims=True)
        grad_score = (prob * (grad_prob - delta)).astype(bf16)
        mixed = tn(grad_score, keys[:count])
        lane = lanes_of((ROWB, 128))
        turned = 0.125 * jnp.where(lane < HS, mixed[:ROWB], mixed[ROWB:])
        turned = turned * cos[start:count, :] - rope_swap(turned) * sin[start:count, :]
        grad_query[start:count, :] = turned.astype(bf16)
        key_part = nn(grad_score, stacked)
        value_part = nn(prob.astype(bf16), grads)
        if count == rows:
            key_acc[...] = key_part
            value_acc[...] = value_part
        else:
            key_acc[:count, :] += key_part
            value_acc[:count, :] += value_part
    total = key_acc[...]
    total = 0.125 * (total + pltpu.roll(total, HS, 1))
    total = (total * cos[...] - rope_swap(total) * sin[...]).astype(bf16)
    other = value_acc[...]
    other = (other + pltpu.roll(other, HS, 1)).astype(bf16)

    @pl.when(half == 0)
    def _():
        grad_key[...] = total
        grad_value[...] = other

    @pl.when(half == 1)
    def _():
        low_half = lanes_of(total.shape) < HS
        grad_key[...] = jnp.where(low_half, grad_key[...], total)
        grad_value[...] = jnp.where(low_half, grad_value[...], other)


def attend_back(length, qkv, grad, lse, cos, sin):
    rows = qkv.shape[0]
    pairs = KVH
    return pl.pallas_call(
        attend_back_kernel,
        grid_spec=pltpu.PrefetchScalarGridSpec(
            num_scalar_prefetch=1,
            grid=(pairs,),
            in_specs=[
                pl.BlockSpec((rows, 128), lambda g, s: (0, g)),
                pl.BlockSpec((rows, 128), lambda g, s: (0, QD // 128 + g // 2)),
                pl.BlockSpec((rows, 128), lambda g, s: (0, (QD + KD) // 128 + g // 2)),
                pl.BlockSpec((rows, 128), lambda g, s: (0, g)),
                pl.BlockSpec((1, 2, rows), lambda g, s: (g, 0, 0)),
                pl.BlockSpec((rows, 128), lambda g, s: (0, 0)),
                pl.BlockSpec((rows, 128), lambda g, s: (0, 0)),
            ],
            out_specs=[
                pl.BlockSpec((rows, 128), lambda g, s: (0, g)),
                pl.BlockSpec((rows, 128), lambda g, s: (0, g // 2)),
                pl.BlockSpec((rows, 128), lambda g, s: (0, g // 2)),
            ],
            scratch_shapes=[pltpu.VMEM((rows, 128), f32), pltpu.VMEM((rows, 128), f32)],
        ),
        out_shape=[
            jax.ShapeDtypeStruct((rows, QD), bf16),
            jax.ShapeDtypeStruct((rows, KD), bf16),
            jax.ShapeDtypeStruct((rows, KD), bf16),
        ],
        compiler_params=params_of(1),
        name="attend_back",
        cost_estimate=pl.CostEstimate(
            flops=20 * rows * rows * QD, transcendentals=rows * rows * HQ, bytes_accessed=8 << 20
        ),
    )(length, qkv, qkv, qkv, grad, lse, cos, sin)


def close_kernel(order, att, hid, gain, weight_a, weight_b, low_map, up_map, mid, normed, low):
    low_value = nt(att[...], low_map[...]).astype(bf16)
    low[...] = low_value
    turned = jnp.concatenate([att[:, column(order, at)] for at in range(BLOCKS)], 1)
    stream = hid[...].astype(f32) + (
        nn(turned[:, :HALF], weight_a[...])
        + nn(turned[:, HALF:], weight_b[...])
        + nn(low_value, up_map[...])
    )
    mid[...] = stream
    normed[...] = (stream * row_scale(stream) * gain[...].astype(f32)).astype(bf16)


def close_mixer(order, att, hidden, gain, weights, low_map, up_map):
    rows = hidden.shape[0]
    block = 256
    ranks = low_map.shape[0]
    full = lambda shape: pl.BlockSpec(shape, lambda n, s: (0, 0))
    part = lambda width: pl.BlockSpec((block, width), lambda n, s: (n, 0))
    return pl.pallas_call(
        close_kernel,
        grid_spec=pltpu.PrefetchScalarGridSpec(
            num_scalar_prefetch=1,
            grid=(rows // block,),
            in_specs=[
                part(QD),
                part(MODEL_WIDTH),
                full((1, MODEL_WIDTH)),
                *halves(weights, MODEL_WIDTH, lambda n: QKV // MODEL_WIDTH),
                full((ranks, QD)),
                full((ranks, MODEL_WIDTH)),
            ],
            out_specs=[part(MODEL_WIDTH), part(MODEL_WIDTH), part(ranks)],
        ),
        out_shape=[
            jax.ShapeDtypeStruct((rows, MODEL_WIDTH), f32),
            jax.ShapeDtypeStruct((rows, MODEL_WIDTH), bf16),
            jax.ShapeDtypeStruct((rows, ranks), bf16),
        ],
        compiler_params=params_of(1),
        name="close_mixer",
        cost_estimate=pl.CostEstimate(
            flops=2 * rows * QD * MODEL_WIDTH, transcendentals=0, bytes_accessed=8 << 20
        ),
    )(order, att, hidden, gain, *weights, low_map, up_map)


def side_by_side(left, right):
    values = []
    for at in range(BLOCKS):
        tile = slice(at // 2 * BLOCK, (at // 2 + 1) * BLOCK)
        low_half = lanes_of((R, BLOCK)) < BLOCK // 2
        if at % 2 == 0:
            value = jnp.where(low_half, left[:, tile], pltpu.roll(right[:, tile], BLOCK // 2, 1))
        else:
            value = jnp.where(low_half, pltpu.roll(left[:, tile], BLOCK // 2, 1), right[:, tile])
        values.append(value.astype(bf16))
    return values


def expert_kernel(
    scalars,
    x,
    cot,
    routes,
    router,
    w_in,
    w_down,
    a_in,
    b_in,
    a_down,
    b_down,
    *rest,
):
    (
        sums_out,
        gates_out,
        packed,
        gates,
        gate_sums,
        low_in,
        low_in_turned,
        b_in_all,
        back_low,
        gated_low,
        back_in,
        acts,
        grads,
        low_grads,
        down_acc,
        out_acc,
        grad_acc,
    ) = rest[-17:]
    expert = pl.program_id(0)
    last = pl.num_programs(0) - 1
    rows = x.shape[0]
    block = rows
    local = a_in.shape[0]
    a_in_all = a_in[...].reshape(local * 2 * R, MODEL_WIDTH)
    a_down_all = a_down[...].reshape(local * R, H)
    b_down_all = b_down[...].reshape(local * R, MODEL_WIDTH)

    @pl.when(expert == 0)
    def _():
        logits = nt(x[...], router[...])
        experts = gates_out.shape[0]
        lane = lanes_of(logits.shape)
        name = lane + scalars[4]
        name = jnp.where(name >= experts, name - experts, name)
        name = jnp.where(lane < experts, name, -1)
        chosen = name == routes[:, 0:1]
        for k in range(1, TOP):
            chosen = chosen | (name == routes[:, k : k + 1])
        top = jnp.max(jnp.where(chosen, logits, -1e30), -1, keepdims=True)
        shifted = jnp.where(chosen, jnp.exp(jnp.where(chosen, logits - top, 0.0)), 0.0)
        weights = shifted / jnp.sum(shifted, -1, keepdims=True)
        gates[...] = weights
        gates_out[...] = weights.T[: gates_out.shape[0], :]
        low = nt(x[...], a_in_all)
        low_in[...] = low.astype(bf16)
        low_in_turned[...] = low.T.astype(bf16)
        back_low[...] = nt(cot[...], b_down_all)
        b_in_all[...] = jnp.zeros_like(b_in_all)
        for e in range(local):
            b_in_all[e * 2 * R : e * 2 * R + R, :H] = b_in[e, 0, 0]
            b_in_all[e * 2 * R + R : (e + 1) * 2 * R, H:] = b_in[e, 0, 1]
        gate_sums[...] = jnp.zeros_like(gate_sums)
        gated_low[...] = jnp.zeros_like(gated_low)
        back_in[...] = jnp.zeros_like(back_in)
        out_acc[...] = jnp.zeros_like(out_acc)
        grad_acc[...] = jnp.zeros_like(grad_acc)
        down_acc[...] = jnp.zeros_like(down_acc)

    def row_step(index, carry):
        at = pl.ds(pl.multiple_of(index * block, block), block)
        lane_in = lanes_of((block, local * 2 * R))
        lane_down = lanes_of((block, local * R))
        in_mine = (lane_in >= expert * 2 * R) & (lane_in < (expert + 1) * 2 * R)
        down_mine = (lane_down >= expert * R) & (lane_down < (expert + 1) * R)
        gate_all = gates[at, :]
        gate_lane = lanes_of(gate_all.shape) == expert
        weight = jnp.sum(jnp.where(gate_lane, gate_all, 0.0), -1, keepdims=True)
        mine = low_in[at, :]
        mine = jnp.where(in_mine, mine, jnp.zeros_like(mine))
        both = nn(x[at, :], w_in[0]) + nn(mine, b_in_all[...])
        gate = both[:, :H]
        upper = both[:, H:]
        sigmoid = jax.nn.sigmoid(gate)
        silu = gate * sigmoid
        act = (silu * upper).astype(bf16)
        acts[at, :] = act
        act_wide = act.astype(f32)
        low = jnp.where(down_mine, nt(act, a_down_all), 0.0).astype(bf16).astype(f32)
        plain = nt(cot[at, :], w_down[0])
        low_plain = back_low[at, :]
        dots = jnp.sum(act_wide * plain, -1, keepdims=True) + jnp.sum(
            low * low_plain, -1, keepdims=True
        )
        sum_lane = lanes_of(gate_all.shape) == expert + scalars[2]
        gate_sums[at, :] += jnp.where(sum_lane, dots, 0.0)
        low_grad = jnp.where(down_mine, weight * low_plain, 0.0).astype(bf16)
        low_grads[at, :] = low_grad
        grad_act = weight * plain + nn(low_grad, a_down_all)
        grad_first = grad_act * upper * sigmoid * (1.0 + gate * (1.0 - sigmoid))
        grad_second = grad_act * silu
        grad_both = jnp.concatenate(
            [grad_first.astype(bf16), grad_second.astype(bf16)], 1
        )
        grads[at, :] = grad_both
        gated_low[at, :] += (weight * low).astype(bf16)
        out_acc[at, :] += nn((weight * act_wide).astype(bf16), w_down[0])
        grad_acc[at, :] += nt(grad_both, w_in[0])
        low_back = jnp.where(in_mine, nt(grad_both, b_in_all[...]), 0.0)
        back_in[at, :] += low_back.astype(bf16)
        return carry

    lax.fori_loop(0, rows // block, row_step, 0)

    turned = low_in_turned[pl.ds(pl.multiple_of(expert * 2 * R, 2 * R), 2 * R), :]
    product = nn(turned, grads[...])
    first_b_in = local * 3 * R
    here = pl.ds(pl.multiple_of(first_b_in + expert * R, R), R)
    for at, value in enumerate(side_by_side(product[:R, :H], product[R:, H:])):
        packed[at, 0, here, :] = value
    down_acc[...] += tn(low_grads[...], acts[...])

    @pl.when(expert == last)
    def _():
        sums_out[:rows, :] = (grad_acc[...] + nn(back_in[...], a_in_all)).astype(bf16)
        experts = gates_out.shape[0]
        sums = gate_sums[...].T[:experts, :]
        sums = jnp.concatenate([sums[: experts // 2], sums[experts // 2 :]], 1)
        high = sums.astype(bf16).astype(f32)
        edge = rows + experts
        sums_out[rows:edge, :] = jnp.concatenate([high, sums - high], 0).astype(bf16)
        sums_out[edge:, :] = (out_acc[...] + nn(gated_low[...], b_down_all)).astype(bf16)
        wide = tn(back_in[...], x[...]).astype(bf16)
        tall = tn(gated_low[...], cot[...]).astype(bf16)
        for at in range(BLOCKS):
            columns = slice(at * BLOCK, (at + 1) * BLOCK)
            packed[at, 0, : local * 2 * R, :] = wide[:, columns]
            packed[at, 0, local * 2 * R : first_b_in, :] = tall[:, columns]
        for pair in range(local // 2):
            lower = down_acc[pair * 2 * R : pair * 2 * R + R, :]
            upper = down_acc[pair * 2 * R + R : (pair + 1) * 2 * R, :]
            row = local * 4 * R + pair * R
            for at, value in enumerate(side_by_side(lower, upper)):
                packed[at, 0, row : row + R, :] = value


def run_experts(
    scalars, x, cot, routes, router, w_in, w_down, a_in, b_in, a_down, b_down, experts, slots, packed
):
    rows = x.shape[0]
    local = w_in.shape[0]
    ranks_in = local * 2 * R
    ranks_down = local * R
    height = local * 9 * R // 2
    kept = [] if packed is None else [packed]
    full = lambda shape: pl.BlockSpec(shape, lambda e, s: (0,) * len(shape))
    return pl.pallas_call(
        expert_kernel,
        grid_spec=pltpu.PrefetchScalarGridSpec(
            num_scalar_prefetch=1,
            grid=(local,),
            in_specs=[
                full((rows, MODEL_WIDTH)),
                full((rows, MODEL_WIDTH)),
                pl.BlockSpec((rows, TOP), lambda e, s: (s[0], 0)),
                full((128, MODEL_WIDTH)),
                pl.BlockSpec((1, MODEL_WIDTH, 2 * H), lambda e, s: (e, 0, 0)),
                pl.BlockSpec((1, H, MODEL_WIDTH), lambda e, s: (e, 0, 0)),
                pl.BlockSpec((local, 1, 2 * R, MODEL_WIDTH), lambda e, s: (0, s[1], 0, 0)),
                pl.BlockSpec((local, 1, 2, R, H), lambda e, s: (0, s[1], 0, 0, 0)),
                pl.BlockSpec((local, 1, R, H), lambda e, s: (0, s[1], 0, 0)),
                pl.BlockSpec((local, 1, R, MODEL_WIDTH), lambda e, s: (0, s[1], 0, 0)),
            ]
            + [pl.BlockSpec(memory_space=pl.ANY)] * len(kept),
            out_specs=[
                full((2 * rows + experts, MODEL_WIDTH)),
                full((experts, rows)),
                pl.BlockSpec((BLOCKS, 1, height, BLOCK), lambda e, s: (0, s[3], 0, 0)),
            ],
            scratch_shapes=[
                pltpu.VMEM((rows, 128), f32),
                pltpu.VMEM((rows, 128), f32),
                pltpu.VMEM((rows, ranks_in), bf16),
                pltpu.VMEM((ranks_in, rows), bf16),
                pltpu.VMEM((ranks_in, 2 * H), bf16),
                pltpu.VMEM((rows, ranks_down), f32),
                pltpu.VMEM((rows, ranks_down), bf16),
                pltpu.VMEM((rows, ranks_in), bf16),
                pltpu.VMEM((rows, H), bf16),
                pltpu.VMEM((rows, 2 * H), bf16),
                pltpu.VMEM((rows, ranks_down), bf16),
                pltpu.VMEM((ranks_down, H), f32),
                pltpu.VMEM((rows, MODEL_WIDTH), f32),
                pltpu.VMEM((rows, MODEL_WIDTH), f32),
            ],
        ),
        out_shape=[
            jax.ShapeDtypeStruct((2 * rows + experts, MODEL_WIDTH), bf16),
            jax.ShapeDtypeStruct((experts, rows), f32),
            jax.ShapeDtypeStruct((BLOCKS, slots, height, BLOCK), bf16),
        ],
        input_output_aliases={11: 2} if kept else {},
        compiler_params=params_of(1),
        name="experts",
        cost_estimate=pl.CostEstimate(
            flops=local * rows * 9 * (1 << 20),
            transcendentals=local * rows * H,
            bytes_accessed=20 << 20,
        ),
    )(scalars, x, cot, routes, router, w_in, w_down, a_in, b_in, a_down, b_down, *kept)


def pack_kernel(left, right, both):
    both[:, : left.shape[1]] = left[...]
    both[:, left.shape[1] :] = right[...]


def pack(left, right):
    return pl.pallas_call(
        pack_kernel,
        out_shape=jax.ShapeDtypeStruct((left.shape[0], left.shape[1] + right.shape[1]), left.dtype),
        name="pack",
    )(left, right)


def open_back_kernel(count, order, cot, mid, gain, gates, router, weight_a, weight_b, low_map, up_map, low, att, *rest):
    parts = rest[:count]
    sums = rest[count : 3 * count]
    grad_mid, grad_att, grad_up, grad_low, columns = rest[3 * count :]
    gate_value = gates[...]
    half = gate_value.shape[0] // 2
    sides = []
    for side in range(2):
        value = None
        for at in range(count):
            pair = sums[2 * at + side][...].astype(f32)
            pair = pair[:half] + pair[half:]
            value = pair if value is None else value + pair
        sides.append(value)
    gate_grad = jnp.concatenate(sides, 0)
    logit = gate_value * (gate_grad - jnp.sum(gate_value * gate_grad, 0, keepdims=True))
    first = logit.astype(bf16)
    left = logit - first.astype(f32)
    second = left.astype(bf16)
    third = (left - second.astype(f32)).astype(bf16)
    grad = tn(first, router[...]) + (tn(second, router[...]) + tn(third, router[...]))
    for piece in parts:
        grad = grad + piece[...].astype(f32)
    total = cot[...].astype(f32) + norm_back(mid[...], gain[...].astype(f32), grad)
    grad_mid[...] = total
    branch = total.astype(bf16)
    low_grad = nt(branch, up_map[...]).astype(bf16)
    columns[...] = nn(low_grad, low_map[...])
    for side, weight in enumerate((weight_a, weight_b)):
        value = nt(branch, weight[...])
        for at in range(BLOCKS // 2):
            columns[:, column(order, side * BLOCKS // 2 + at)] += value[:, at * BLOCK : (at + 1) * BLOCK]
    grad_att[...] = columns[...].astype(bf16)
    up_part = tn(low[...], branch)
    low_part = tn(low_grad, att[...])

    @pl.when(pl.program_id(0) == 0)
    def _():
        grad_up[...] = up_part
        grad_low[...] = low_part

    @pl.when(pl.program_id(0) > 0)
    def _():
        grad_up[...] += up_part
        grad_low[...] += low_part


def open_back(order, cot, mid, gain, gates, router, weights, low_map, up_map, low, att, parts):
    rows = cot.shape[0]
    block = 256
    ranks = low_map.shape[0]
    experts = gates.shape[0]
    full = lambda shape: pl.BlockSpec(shape, lambda n, s: (0, 0))
    part = lambda width: pl.BlockSpec((block, width), lambda n, s: (n, 0))
    count = len(parts)
    below = rows // experts
    sums = [
        pl.BlockSpec((experts, block), lambda n, s: (below, n)),
        pl.BlockSpec((experts, block), lambda n, s: (below, rows // block + n)),
    ]

    def body(*refs):
        open_back_kernel(count, *refs)

    return pl.pallas_call(
        body,
        grid_spec=pltpu.PrefetchScalarGridSpec(
            num_scalar_prefetch=1,
            grid=(rows // block,),
            in_specs=[
                part(MODEL_WIDTH),
                part(MODEL_WIDTH),
                full((1, MODEL_WIDTH)),
                pl.BlockSpec((experts, block), lambda n, s: (0, n)),
                full((experts, MODEL_WIDTH)),
                *halves(weights, MODEL_WIDTH, lambda n: QKV // MODEL_WIDTH),
                full((ranks, QD)),
                full((ranks, MODEL_WIDTH)),
                part(ranks),
                part(QD),
            ]
            + [part(MODEL_WIDTH)] * count
            + sums * count,
            out_specs=[
                part(MODEL_WIDTH),
                part(QD),
                full((ranks, MODEL_WIDTH)),
                full((ranks, QD)),
            ],
            scratch_shapes=[pltpu.VMEM((block, QD), f32)],
        ),
        out_shape=[
            jax.ShapeDtypeStruct((rows, MODEL_WIDTH), f32),
            jax.ShapeDtypeStruct((rows, QD), bf16),
            jax.ShapeDtypeStruct((ranks, MODEL_WIDTH), f32),
            jax.ShapeDtypeStruct((ranks, QD), f32),
        ],
        compiler_params=params_of(1),
        name="open_back",
        cost_estimate=pl.CostEstimate(
            flops=2 * rows * QD * MODEL_WIDTH, transcendentals=0, bytes_accessed=14 << 20
        ),
    )(
        order, cot, mid, gain, gates, router, *weights, low_map, up_map, low, att, *parts,
        *[piece for piece in parts for _ in range(2)],
    )


def adapters_back_kernel(
    grad_query, grad_key, grad_value, low, normed, up_map, low_there, up_there, low_out, *results
):
    pieces = (grad_query, grad_key, grad_value)
    bounds = (0, QD, QD + KD, QKV)
    back = None
    ups = []
    for at in range(3):
        block = pieces[at][...]
        ups.append(tn(low[...], block)[at * R : (at + 1) * R])
        part = nt(block, up_map[:, bounds[at] : bounds[at + 1]])
        back = part if back is None else back + part
    value = back.astype(bf16)
    low_out[...] = value
    lows = tn(value, normed[...]) + low_there[...]
    if len(results) == 2:
        grad_up, grad_low = results
        grad_low[...] = lows
        for at in range(3):
            grad_up[:, bounds[at] : bounds[at + 1]] = ups[at]
        return
    (packed,) = results
    grad_up = jnp.concatenate(ups, 1)
    grad_out = up_there[3 * R :, :]
    small = BLOCK // 4
    lane = lanes_of((R, BLOCK))
    for owner in range(packed.shape[0]):
        tile = slice(owner // 4 * BLOCK, (owner // 4 + 1) * BLOCK)
        offset = owner % 4 * small
        first = jnp.zeros((R, BLOCK), f32)
        for at in range(4):
            piece = lows[at * R : (at + 1) * R, tile]
            shift = (at * small - offset) % BLOCK
            piece = pltpu.roll(piece, shift, 1) if shift else piece
            first = jnp.where((lane >= at * small) & (lane < (at + 1) * small), piece, first)
        piece = grad_up[:, owner // 2 * BLOCK : (owner // 2 + 1) * BLOCK]
        piece = pltpu.roll(piece, BLOCK // 2, 1) if owner % 2 else piece
        other = grad_out[:, tile]
        shift = (2 * small - offset) % BLOCK
        other = pltpu.roll(other, shift, 1) if shift else other
        packed[owner, :, :BLOCK] = first.astype(bf16)
        packed[owner, :, BLOCK:] = jnp.where(
            lane < 2 * small, piece, jnp.where(lane < 3 * small, other, 0.0)
        ).astype(bf16)


def adapters_back(grad_query, grad_key, grad_value, low, normed, up_map, low_there, up_there, devices):
    rows = normed.shape[0]
    ranks = up_map.shape[0]
    if devices * BLOCK // 4 == MODEL_WIDTH:
        results = [jax.ShapeDtypeStruct((devices, R, 2 * BLOCK), bf16)]
    else:
        results = [
            jax.ShapeDtypeStruct((R, QKV), f32),
            jax.ShapeDtypeStruct((ranks, MODEL_WIDTH), f32),
        ]
    back_low, *results = pl.pallas_call(
        adapters_back_kernel,
        out_shape=[jax.ShapeDtypeStruct((rows, ranks), bf16)] + results,
        compiler_params=pltpu.CompilerParams(vmem_limit_bytes=56 * 1024 * 1024),
        name="adapters_back",
        cost_estimate=pl.CostEstimate(
            flops=6 * rows * 256 * QKV, transcendentals=0, bytes_accessed=4 << 20
        ),
    )(grad_query, grad_key, grad_value, low, normed, up_map, low_there, up_there)
    if len(results) == 1:
        return results[0], back_low
    grad_up, grad_low = results
    small = MODEL_WIDTH // devices
    packed = jnp.concatenate(
        [
            grad_low.reshape(4, R, devices, small).transpose(2, 1, 0, 3).reshape(devices, R, 4 * small),
            grad_up.reshape(R, devices, 2 * small).transpose(1, 0, 2),
            up_there[3 * R :].reshape(R, devices, small).transpose(1, 0, 2),
            jnp.zeros((devices, R, small), f32),
        ],
        -1,
    )
    return packed.astype(bf16), back_low


def input_back_kernel(
    order, grad_query, grad_key, grad_value, low, weight_a, weight_b, low_map, hid, gain, mid, grad, columns
):
    columns[...] = nn(low[...], low_map[...])
    for side, weight in enumerate((weight_a, weight_b)):
        value = nt(grad_query[...], weight[:, :QD])
        value = value + nt(grad_key[...], weight[:, QD : QD + KD])
        value = value + nt(grad_value[...], weight[:, QD + KD :])
        for at in range(BLOCKS // 2):
            columns[:, column(order, side * BLOCKS // 2 + at)] += value[:, at * BLOCK : (at + 1) * BLOCK]
    rows = hid[...].astype(f32)
    grad[...] = (mid[...] + norm_back(rows, gain[...].astype(f32), columns[...])).astype(bf16)


def input_back(order, grad_query, grad_key, grad_value, low, weights, low_map, hidden, gain, mid):
    rows = hidden.shape[0]
    block = 256
    ranks = low_map.shape[0]
    full = lambda shape: pl.BlockSpec(shape, lambda n, s: (0, 0))
    part = lambda width: pl.BlockSpec((block, width), lambda n, s: (n, 0))
    return pl.pallas_call(
        input_back_kernel,
        grid_spec=pltpu.PrefetchScalarGridSpec(
            num_scalar_prefetch=1,
            grid=(rows // block,),
            in_specs=[
                part(QD),
                part(KD),
                part(KD),
                part(ranks),
                *halves(weights, QKV, lambda n: 0),
                full((ranks, MODEL_WIDTH)),
                part(MODEL_WIDTH),
                full((1, MODEL_WIDTH)),
                part(MODEL_WIDTH),
            ],
            out_specs=part(MODEL_WIDTH),
            scratch_shapes=[pltpu.VMEM((block, MODEL_WIDTH), f32)],
        ),
        out_shape=jax.ShapeDtypeStruct((rows, MODEL_WIDTH), bf16),
        compiler_params=params_of(1),
        name="input_back",
        cost_estimate=pl.CostEstimate(
            flops=2 * rows * QKV * MODEL_WIDTH, transcendentals=0, bytes_accessed=12 << 20
        ),
    )(order, grad_query, grad_key, grad_value, low, *weights, low_map, hidden, gain, mid)


def sum_experts_kernel(ids, pieces, a_in, b_in, a_down, b_down, acc):
    local = a_in.shape[0]
    small = a_down.shape[-1]
    acc[...] = jnp.zeros_like(acc)

    def step(index, carry):
        acc[ids[index]] += pieces[index].astype(f32)
        return carry

    lax.fori_loop(0, pieces.shape[0], step, 0)
    for e in range(local):
        a_in[e] = acc[:, e * 2 * R : (e + 1) * 2 * R, :]
        at = local * 2 * R + e * R
        b_down[e] = acc[:, at : at + R, :]
        at = local * 3 * R + e * R
        both = acc[:, at : at + R, :]
        b_in[e, :, 0] = both[:, :, :small]
        b_in[e, :, 1] = both[:, :, small:]
        at = local * 4 * R + e // 2 * R
        a_down[e] = acc[:, at : at + R, e % 2 * small : (e % 2 + 1) * small]


def sum_experts(ids, pieces, local):
    height = pieces.shape[1]
    lanes = pieces.shape[2]
    small = lanes // 2
    vmem = pl.BlockSpec(memory_space=pltpu.VMEM)
    return pl.pallas_call(
        sum_experts_kernel,
        in_specs=[pl.BlockSpec(memory_space=pltpu.SMEM), vmem],
        out_specs=[vmem, vmem, vmem, vmem],
        out_shape=[
            jax.ShapeDtypeStruct((local, NA, 2 * R, lanes), f32),
            jax.ShapeDtypeStruct((local, NA, 2, R, small), f32),
            jax.ShapeDtypeStruct((local, NA, R, small), f32),
            jax.ShapeDtypeStruct((local, NA, R, lanes), f32),
        ],
        scratch_shapes=[pltpu.VMEM((NA, height, lanes), f32)],
        compiler_params=pltpu.CompilerParams(vmem_limit_bytes=56 * 1024 * 1024),
        name="sum_experts",
    )(ids, pieces)


def sum_mixer_kernel(ids, pieces, grad_low, grad_up, grad_out, acc):
    width = grad_low.shape[-1]
    acc[...] = jnp.zeros_like(acc)

    def step(index, carry):
        acc[ids[index]] += pieces[index].astype(f32)
        return carry

    lax.fori_loop(0, pieces.shape[0], step, 0)
    total = acc[...]
    for at in range(4):
        grad_low[at] = total[:, :, at * width : (at + 1) * width]
    grad_up[...] = total[:, :, 4 * width : 6 * width]
    grad_out[...] = total[:, :, 6 * width : 7 * width]


def sum_mixer(ids, pieces):
    width = pieces.shape[2] // 8
    vmem = pl.BlockSpec(memory_space=pltpu.VMEM)
    return pl.pallas_call(
        sum_mixer_kernel,
        in_specs=[pl.BlockSpec(memory_space=pltpu.SMEM), vmem],
        out_specs=[vmem, vmem, vmem],
        out_shape=[
            jax.ShapeDtypeStruct((4, NA, R, width), f32),
            jax.ShapeDtypeStruct((NA, R, 2 * width), f32),
            jax.ShapeDtypeStruct((NA, R, width), f32),
        ],
        scratch_shapes=[pltpu.VMEM((NA, R, 8 * width), f32)],
        compiler_params=pltpu.CompilerParams(vmem_limit_bytes=56 * 1024 * 1024),
        name="sum_mixer",
    )(ids, pieces)


def rope_tables(rows):
    half = HS // 2
    frequency = (10000.0 ** (-2.0 * np.arange(half, dtype=np.float32) / HS)).astype(np.float32)
    angles = np.arange(rows, dtype=np.float32)[:, None] * frequency[None, :]
    cos = np.cos(angles.astype(np.float64)).astype(np.float32)
    sin = np.sin(angles.astype(np.float64)).astype(np.float32)
    return (
        jnp.asarray(np.concatenate([cos, cos, cos, cos], 1)),
        jnp.asarray(np.concatenate([-sin, sin, -sin, sin], 1)),
    )


def swap(value, bit):
    return lax.ppermute(value, "dp", [(at, at ^ bit) for at in range(BLOCKS)])


def both_neighbours(weight):
    return swap(weight, 2), swap(weight, 4)


def across(pair):
    one, two = pair
    middle = one.shape[0] // 2
    return swap(two[:middle], 2), swap(one[middle:], 4)


def tied(*values):
    return lax.optimization_barrier(values)


def order_of(row):
    if lax.axis_size("dp") != BLOCKS:
        return jnp.arange(BLOCKS, dtype=jnp.int32)
    return row.astype(jnp.int32) ^ jnp.array([0, 2, 4, 6, 1, 3, 5, 7], jnp.int32)


def to_owners(packed, owners, local):
    split = owners // BLOCKS
    if split == 1:
        return packed
    slots = packed.shape[1]
    edge = local * 3 * R
    wide = packed[:, :, :edge].reshape(BLOCKS, slots, edge, split, BLOCK // split)
    wide = wide.transpose(0, 3, 1, 2, 4).reshape(owners, slots, edge, BLOCK // split)
    rest = packed.shape[2] - edge
    narrow = packed[:, :, edge:].reshape(BLOCKS, slots, rest, 2, split, BLOCK // 2 // split)
    narrow = narrow.transpose(0, 4, 1, 2, 3, 5).reshape(owners, slots, rest, BLOCK // split)
    return jnp.concatenate([wide, narrow], 2)


def joined(left, right):
    return (left.astype(f32) + right.astype(f32)).astype(bf16)


def on_device(
    hidden,
    cotangent,
    lengths,
    adapter_ids,
    routes,
    attn_gain,
    ffn_gain,
    query_key_value_weight,
    w_out,
    w_router,
    w_gate_up,
    w_down,
    attention_lowmap,
    attention_query_key_value_upmap,
    attention_output_upmap,
    expert_gate_up_lowmap,
    expert_gate_up_upmap,
    expert_down_lowmap,
    expert_down_upmap,
):
    groups = lax.axis_size("expert")
    owners = lax.axis_size("dp")
    place = lax.axis_index("expert")
    row = lax.axis_index("dp")
    devices = groups * owners
    sequence = row * groups + place
    rows = hidden.shape[0]
    experts = w_router.shape[1]
    local = w_gate_up.shape[0]
    width = MODEL_WIDTH // owners
    attn_gain = attn_gain.reshape(1, MODEL_WIDTH)
    ffn_gain = ffn_gain.reshape(1, MODEL_WIDTH)
    length = lax.dynamic_slice(lengths, (sequence,), (1,))
    forward = [(at, (at + 1) % groups) for at in range(groups)]
    backward = [(at, (at - 1) % groups) for at in range(groups)]

    mine = lax.dynamic_slice(adapter_ids.reshape(owners, groups), (0, place), (owners, 1))[:, 0]
    low_turned = attention_lowmap.transpose(1, 0, 3, 2).reshape(NA, 4 * R, width)
    up_turned = (
        attention_query_key_value_upmap.reshape(NA, R, 2, width)
        .transpose(0, 2, 1, 3)
        .reshape(NA, 2 * R, width)
    )
    adapters = jnp.concatenate([low_turned, up_turned, attention_output_upmap], 1)[mine]
    adapters = lax.all_to_all(adapters, "dp", 0, 0, tiled=True)
    order = order_of(row)
    first = place * local
    router = jnp.roll(w_router.T, -first, axis=0)
    router_wide = jnp.concatenate(
        [router, jnp.zeros((128 - experts, MODEL_WIDTH), router.dtype)], 0
    )

    offsets = [0, 1] + [groups - 1] * (groups > 2) + list(range(2, groups - 1))
    offset = jnp.array(offsets, jnp.int32)
    source = (place - offset + groups) % groups
    tags = adapter_ids.reshape(owners, groups)[:, source]
    slot = jnp.arange(groups, dtype=jnp.int32)
    table = jnp.stack(
        [
            source,
            lax.dynamic_slice(tags, (row, 0), (1, groups))[0],
            offset * local,
            slot,
            jnp.full((groups,), first, jnp.int32),
        ],
        1,
    )

    both = pack(query_key_value_weight, w_out)
    cots = {0: cotangent, 1: lax.ppermute(cotangent, "expert", forward)}
    if owners == BLOCKS:
        pair = both_neighbours(both)
        pair, order, router, router_wide, table, tags, attn_gain, ffn_gain, length = tied(
            pair, order, router, router_wide, table, tags, attn_gain, ffn_gain, length
        )
        near = jnp.concatenate([both, *pair, *across(pair)], 0)
        near, adapters, cots[1], cotangent = tied(near, adapters, cots[1], cotangent)
        weights = near, swap(near, 1)
    else:
        whole = lax.all_gather(both, "dp", axis=0, tiled=True)
        weights = whole, whole
    if groups > 2:
        cots[groups - 1] = lax.ppermute(cotangent, "expert", backward)

    low_map = adapters[:, : 4 * R].transpose(1, 0, 2).reshape(4 * R, MODEL_WIDTH)
    up = (
        adapters[:, 4 * R : 6 * R]
        .reshape(owners, 2, R, width)
        .transpose(2, 0, 1, 3)
        .reshape(R, QKV)
    )
    up_out = adapters[:, 6 * R :].transpose(1, 0, 2).reshape(R, MODEL_WIDTH)
    column = jnp.arange(QKV, dtype=jnp.int32)
    part = jnp.where(column < QD, 0, jnp.where(column < QD + KD, 1, 2))
    up_map = jnp.where(
        part[None, None, :] == jnp.arange(4, dtype=jnp.int32)[:, None, None], up[None], 0
    ).reshape(4 * R, QKV)
    up_out_map = jnp.concatenate([jnp.zeros((3 * R, MODEL_WIDTH), bf16), up_out], 0)

    cos, sin = rope_tables(rows)


    qkv, low, normed_in = project(order, hidden, attn_gain, weights, low_map, up_map, cos, sin)
    if groups > 3:
        cots[1], low = tied(cots[1], low)
    for at in range(2, groups - 1):
        cots[at] = lax.ppermute(cots[at - 1], "expert", forward)
    attended, lse = attend(length, qkv)
    mid, normed_mid, low_out = close_mixer(
        order, attended, hidden, ffn_gain, weights, low_map, up_out_map
    )

    a_in = expert_gate_up_lowmap.transpose(0, 1, 3, 2)
    a_down = expert_down_lowmap.transpose(0, 1, 3, 2)

    xs = {0: normed_mid, 1: lax.ppermute(normed_mid, "expert", forward)}
    packed = None
    ran = {}
    for at, offset in enumerate(offsets):
        ran[offset], gate_part, packed = run_experts(
            table[at],
            xs[offset],
            cots[offset],
            routes,
            router_wide,
            w_gate_up,
            w_down,
            a_in,
            expert_gate_up_upmap,
            a_down,
            expert_down_upmap,
            experts,
            groups,
            packed,
        )
        if at == 0:
            gates = gate_part
            if groups > 2:
                normed_mid, packed = tied(normed_mid, packed)
                xs[groups - 1] = lax.ppermute(normed_mid, "expert", backward)
        elif at < groups - 2:
            value, packed = tied(xs[at], packed)
            xs[at + 1] = lax.ppermute(value, "expert", forward)
        if at == 2:
            first_sums, packed = tied(ran[1], packed)

    pieces = lax.all_to_all(to_owners(packed, owners, local), "dp", 0, 0, tiled=True)
    pieces = pieces.reshape(devices, pieces.shape[2], width)
    g_a_in, g_b_in, g_a_down, g_b_down = sum_experts(tags.reshape(devices), pieces, local)

    edge = rows + experts
    both_far = lax.ppermute(first_sums if groups > 2 else ran[1], "expert", forward)
    grad_far, out_far = both_far, both_far[edge:]
    for offset in range(2, groups):
        grad_part = joined(ran[offset][:edge], grad_far[:edge])
        if offset == groups - 1:
            grad_part, g_a_down = tied(grad_part, g_a_down)
        grad_far = lax.ppermute(grad_part, "expert", forward)
    if groups > 2:
        out_part = joined(ran[2][edge:], out_far)
        out_part, grad_far = tied(out_part, grad_far)
        out_far = lax.ppermute(out_part, "expert", forward)

    grad_mid, grad_attended, grad_up_out, grad_low_out = open_back(
        order,
        cotangent,
        mid,
        ffn_gain,
        gates,
        router,
        weights,
        low_map,
        up_out_map,
        low_out,
        attended,
        [ran[0], grad_far],
    )
    grad_query, grad_key, grad_value = attend_back(length, qkv, grad_attended, lse, cos, sin)
    out_far, grad_query = tied(out_far, grad_query)
    for offset in range(3, groups):
        out_far = lax.ppermute(joined(ran[offset][edge:], out_far), "expert", forward)
    packed, back_low = adapters_back(
        grad_query, grad_key, grad_value, low, normed_in, up_map, grad_low_out, grad_up_out, devices
    )
    packed = lax.all_to_all(packed, ("dp", "expert"), 0, 0, tiled=True)
    m_a, m_b, m_o = sum_mixer(adapter_ids, packed)

    grad_hidden = input_back(
        order, grad_query, grad_key, grad_value, back_low, weights, low_map, hidden, attn_gain, grad_mid
    )
    out = (mid + ran[0][edge:].astype(f32) + out_far.astype(f32)).astype(bf16)
    return (
        out,
        grad_hidden,
        m_a.transpose(0, 1, 3, 2),
        m_b,
        m_o,
        g_a_in.transpose(0, 1, 3, 2),
        g_b_in,
        g_a_down.transpose(0, 1, 3, 2),
        g_b_down,
    )


def solution(mesh):
    in_specs = (
        P(("dp", "expert"), None),
        P(("dp", "expert"), None),
        P(),
        P(),
        P("dp", None),
        P(),
        P(),
        P("dp", None),
        P("dp", None),
        P(),
        P("expert", None, None),
        P("expert", None, None),
        P(None, None, "dp", None),
        P(None, None, "dp"),
        P(None, None, "dp"),
        P("expert", None, None, None),
        P("expert", None, None, None, None),
        P("expert", None, None, None),
        P("expert", None, None, None),
    )
    out_specs = (
        P(("dp", "expert"), None),
        P(("dp", "expert"), None),
        P(None, None, ("dp", "expert"), None),
        P(None, None, ("dp", "expert")),
        P(None, None, ("dp", "expert")),
        P("expert", None, "dp", None),
        P("expert", None, None, None, "dp"),
        P("expert", None, "dp", None),
        P("expert", None, None, "dp"),
    )
    return jax.shard_map(
        on_device, mesh=mesh, in_specs=in_specs, out_specs=out_specs, check_vma=False
    )
```

```python
import numpy as np
import jax
import jax.numpy as jnp
from jax import lax
from jax.experimental import pallas as pl
from jax.experimental.pallas import tpu as pltpu
from jax.sharding import PartitionSpec as P

MODEL_WIDTH = 1024
HQ = 16
KVH = 8
HS = 64
H = 512
TOP = 8
R = 16
NA = 8
QD = HQ * HS
KD = KVH * HS
QKV = QD + 2 * KD

epsilon = 1e-06
f32 = jnp.float32
bf16 = jnp.bfloat16


def nn(left, right):
    return lax.dot_general(left, right, (((1,), (0,)), ((), ())), preferred_element_type=f32)


def nt(left, right):
    return lax.dot_general(left, right, (((1,), (1,)), ((), ())), preferred_element_type=f32)


def tn(left, right):
    return lax.dot_general(left, right, (((0,), (0,)), ((), ())), preferred_element_type=f32)


def lanes_of(shape):
    return lax.broadcasted_iota(jnp.int32, shape, len(shape) - 1)


def row_scale(rows):
    return lax.rsqrt(jnp.mean(rows * rows, -1, keepdims=True) + epsilon)


def norm_back(rows, gain, grad):
    scale = row_scale(rows)
    scaled = grad * gain
    return scale * scaled - rows * (scale * scale * scale) * jnp.mean(
        rows * scaled, -1, keepdims=True
    )


def rope_swap(rows):
    width = rows.shape[-1]
    lane = lanes_of(rows.shape)
    return jnp.where(
        lane % HS < HS // 2,
        pltpu.roll(rows, width - HS // 2, 1),
        pltpu.roll(rows, HS // 2, 1),
    )


def both_halves(pair, half):
    rows = pair.astype(f32)
    lane = lanes_of(rows.shape)
    rolled = pltpu.roll(rows, HS, 1)
    keep = (lane < HS) == (half == 0)
    return jnp.where(keep, rows, rolled).astype(bf16)


def stacked_heads(pair):
    lane = lanes_of(pair.shape)
    zero = jnp.zeros_like(pair)
    return jnp.concatenate(
        [jnp.where(lane < HS, pair, zero), jnp.where(lane < HS, zero, pair)], 0
    )


def params_of(count):
    return pltpu.CompilerParams(
        dimension_semantics=("arbitrary",) * count, vmem_limit_bytes=56 * 1024 * 1024
    )


BLOCK = 128
BLOCKS = MODEL_WIDTH // BLOCK
HALF = MODEL_WIDTH // 2


def column(order, at):
    return pl.ds(pl.multiple_of(order[at] * BLOCK, BLOCK), BLOCK)


def halves(weights, width, index):
    there = 1 if weights[0] is weights[1] else 0
    return [
        pl.BlockSpec((HALF, width), lambda n, s: (0, index(n))),
        pl.BlockSpec((HALF, width), lambda n, s: (there, index(n))),
    ]


def project_kernel(
    order, hid, gain, weight_a, weight_b, low_map, up_map, cos, sin, qkv, low, normed, turned_rows
):
    step = pl.program_id(0)
    blocks = pl.num_programs(0)

    @pl.when(step == 0)
    def _():
        rows = hid[...].astype(f32)
        value = (rows * row_scale(rows) * gain[...].astype(f32)).astype(bf16)
        normed[...] = value
        low[...] = nt(value, low_map[...]).astype(bf16)
        for at in range(BLOCKS):
            turned_rows[:, at * BLOCK : (at + 1) * BLOCK] = normed[:, column(order, at)]

    value = (
        nn(turned_rows[:, :HALF], weight_a[...])
        + nn(turned_rows[:, HALF:], weight_b[...])
        + nn(low[...], up_map[...])
    )

    @pl.when(step < blocks * 3 // 4)
    def _():
        for part in range(value.shape[1] // 128):
            piece = value[:, part * 128 : part * 128 + 128]
            turned = piece * cos[...] + rope_swap(piece) * sin[...]
            qkv[:, part * 128 : part * 128 + 128] = turned.astype(bf16)

    @pl.when(step >= blocks * 3 // 4)
    def _():
        qkv[...] = value.astype(bf16)


def project(order, hidden, gain, weights, low_map, up_map, cos, sin):
    rows = hidden.shape[0]
    block = 512
    ranks = low_map.shape[0]
    full = lambda shape: pl.BlockSpec(shape, lambda n, s: (0, 0))
    return pl.pallas_call(
        project_kernel,
        grid_spec=pltpu.PrefetchScalarGridSpec(
            num_scalar_prefetch=1,
            grid=(QKV // block,),
            in_specs=[
                full((rows, MODEL_WIDTH)),
                full((1, MODEL_WIDTH)),
                *halves(weights, block, lambda n: n),
                full((ranks, MODEL_WIDTH)),
                pl.BlockSpec((ranks, block), lambda n, s: (0, n)),
                full((rows, 128)),
                full((rows, 128)),
            ],
            out_specs=[
                pl.BlockSpec((rows, block), lambda n, s: (0, n)),
                full((rows, ranks)),
                full((rows, MODEL_WIDTH)),
            ],
            scratch_shapes=[pltpu.VMEM((rows, MODEL_WIDTH), bf16)],
        ),
        out_shape=[
            jax.ShapeDtypeStruct((rows, QKV), bf16),
            jax.ShapeDtypeStruct((rows, ranks), bf16),
            jax.ShapeDtypeStruct((rows, MODEL_WIDTH), bf16),
        ],
        compiler_params=params_of(1),
        name="project",
        cost_estimate=pl.CostEstimate(
            flops=2 * rows * QKV * MODEL_WIDTH, transcendentals=0, bytes_accessed=8 << 20
        ),
    )(order, hidden, gain, *weights, low_map, up_map, cos, sin)


ROWB = 128
BACKB = 256


def length_column(length, count):
    key = lax.broadcasted_iota(jnp.int32, (count, 1), 0)
    return jnp.where(key < length, 0.0, -1e30)


def causal_block(block):
    key = lax.broadcasted_iota(jnp.int32, (block, 2 * block), 0)
    return jnp.where(key <= lanes_of((block, 2 * block)) % block, 0.0, -1e30)


def masked_scores(queries, keys, start, bias, causal):
    count = start + causal.shape[0]
    scores = nt(keys[:count], (queries.astype(f32) * 0.125).astype(bf16))
    near = scores[start:] + (bias[start:count] + causal)
    if start == 0:
        return near
    return jnp.concatenate([scores[:start] + bias[:start], near], 0)


def attend_kernel(scalars, query, key, value, result, lse):
    half = pl.program_id(0) % 2
    keys = both_halves(key[...], half)
    values = both_halves(value[...], half)
    rows = query.shape[0]
    bias = length_column(scalars[0], rows)
    causal = causal_block(ROWB)
    for start in range(0, rows, ROWB):
        count = start + ROWB
        stacked = stacked_heads(query[start:count, :])
        scores = masked_scores(stacked, keys, start, bias, causal)
        top = jnp.max(scores, 0, keepdims=True)
        shifted = jnp.exp(scores - top)
        total = jnp.sum(shifted, 0, keepdims=True)
        prob = (shifted * (1.0 / total)).astype(bf16)
        mixed = tn(prob, values[:count])
        lane = lanes_of((ROWB, 128))
        result[start:count, :] = jnp.where(lane < HS, mixed[:ROWB], mixed[ROWB:]).astype(bf16)
        logs = top + jnp.log(total)
        lse[0, 0:1, start:count] = logs[:, :ROWB]
        lse[0, 1:2, start:count] = logs[:, ROWB:]


def attend(length, qkv):
    rows = qkv.shape[0]
    pairs = KVH
    return pl.pallas_call(
        attend_kernel,
        grid_spec=pltpu.PrefetchScalarGridSpec(
            num_scalar_prefetch=1,
            grid=(pairs,),
            in_specs=[
                pl.BlockSpec((rows, 128), lambda g, s: (0, g)),
                pl.BlockSpec((rows, 128), lambda g, s: (0, QD // 128 + g // 2)),
                pl.BlockSpec((rows, 128), lambda g, s: (0, (QD + KD) // 128 + g // 2)),
            ],
            out_specs=[
                pl.BlockSpec((rows, 128), lambda g, s: (0, g)),
                pl.BlockSpec((1, 2, rows), lambda g, s: (g, 0, 0)),
            ],
        ),
        out_shape=[
            jax.ShapeDtypeStruct((rows, QD), bf16),
            jax.ShapeDtypeStruct((pairs, 2, rows), f32),
        ],
        compiler_params=params_of(1),
        name="attend",
        cost_estimate=pl.CostEstimate(
            flops=8 * rows * rows * QD, transcendentals=rows * rows * HQ, bytes_accessed=4 << 20
        ),
    )(length, qkv, qkv, qkv)


def attend_back_kernel(
    scalars, query, key, value, grad, lse, cos, sin, grad_query, grad_key, grad_value, key_acc, value_acc
):
    half = pl.program_id(0) % 2
    keys = both_halves(key[...], half)
    values = both_halves(value[...], half)
    rows = query.shape[0]
    bias = length_column(scalars[0], rows)
    causal = causal_block(BACKB)
    for start in reversed(range(0, rows, BACKB)):
        count = start + BACKB
        stacked = stacked_heads(query[start:count, :])
        grads = stacked_heads(grad[start:count, :])
        scores = masked_scores(stacked, keys, start, bias, causal)
        logs = jnp.concatenate([lse[0, 0:1, start:count], lse[0, 1:2, start:count]], 1)
        prob = jnp.exp(scores - logs)
        grad_prob = nt(values[:count], grads)
        delta = jnp.sum(prob * grad_prob, 0, keepdims=True)
        grad_score = (prob * (grad_prob - delta)).astype(bf16)
        mixed = tn(grad_score, keys[:count])
        lane = lanes_of((BACKB, 128))
        turned = 0.125 * jnp.where(lane < HS, mixed[:BACKB], mixed[BACKB:])
        turned = turned * cos[start:count, :] - rope_swap(turned) * sin[start:count, :]
        grad_query[start:count, :] = turned.astype(bf16)
        key_part = nn(grad_score, stacked)
        value_part = nn(prob.astype(bf16), grads)
        if count == rows:
            key_acc[...] = key_part
            value_acc[...] = value_part
        else:
            key_acc[:count, :] += key_part
            value_acc[:count, :] += value_part
    total = key_acc[...]
    total = 0.125 * (total + pltpu.roll(total, HS, 1))
    total = (total * cos[...] - rope_swap(total) * sin[...]).astype(bf16)
    other = value_acc[...]
    other = (other + pltpu.roll(other, HS, 1)).astype(bf16)

    @pl.when(half == 0)
    def _():
        grad_key[...] = total
        grad_value[...] = other

    @pl.when(half == 1)
    def _():
        low_half = lanes_of(total.shape) < HS
        grad_key[...] = jnp.where(low_half, grad_key[...], total)
        grad_value[...] = jnp.where(low_half, grad_value[...], other)


def attend_back(length, qkv, grad, lse, cos, sin):
    rows = qkv.shape[0]
    pairs = KVH
    return pl.pallas_call(
        attend_back_kernel,
        grid_spec=pltpu.PrefetchScalarGridSpec(
            num_scalar_prefetch=1,
            grid=(pairs,),
            in_specs=[
                pl.BlockSpec((rows, 128), lambda g, s: (0, g)),
                pl.BlockSpec((rows, 128), lambda g, s: (0, QD // 128 + g // 2)),
                pl.BlockSpec((rows, 128), lambda g, s: (0, (QD + KD) // 128 + g // 2)),
                pl.BlockSpec((rows, 128), lambda g, s: (0, g)),
                pl.BlockSpec((1, 2, rows), lambda g, s: (g, 0, 0)),
                pl.BlockSpec((rows, 128), lambda g, s: (0, 0)),
                pl.BlockSpec((rows, 128), lambda g, s: (0, 0)),
            ],
            out_specs=[
                pl.BlockSpec((rows, 128), lambda g, s: (0, g)),
                pl.BlockSpec((rows, 128), lambda g, s: (0, g // 2)),
                pl.BlockSpec((rows, 128), lambda g, s: (0, g // 2)),
            ],
            scratch_shapes=[pltpu.VMEM((rows, 128), f32), pltpu.VMEM((rows, 128), f32)],
        ),
        out_shape=[
            jax.ShapeDtypeStruct((rows, QD), bf16),
            jax.ShapeDtypeStruct((rows, KD), bf16),
            jax.ShapeDtypeStruct((rows, KD), bf16),
        ],
        compiler_params=params_of(1),
        name="attend_back",
        cost_estimate=pl.CostEstimate(
            flops=20 * rows * rows * QD, transcendentals=rows * rows * HQ, bytes_accessed=8 << 20
        ),
    )(length, qkv, qkv, qkv, grad, lse, cos, sin)


def close_kernel(order, att, hid, gain, weight_a, weight_b, low_map, up_map, mid, normed, low):
    low_value = nt(att[...], low_map[...]).astype(bf16)
    low[...] = low_value
    turned = jnp.concatenate([att[:, column(order, at)] for at in range(BLOCKS)], 1)
    stream = hid[...].astype(f32) + (
        nn(turned[:, :HALF], weight_a[...])
        + nn(turned[:, HALF:], weight_b[...])
        + nn(low_value, up_map[...])
    )
    mid[...] = stream
    normed[...] = (stream * row_scale(stream) * gain[...].astype(f32)).astype(bf16)


def close_mixer(order, att, hidden, gain, weights, low_map, up_map):
    rows = hidden.shape[0]
    block = 256
    ranks = low_map.shape[0]
    full = lambda shape: pl.BlockSpec(shape, lambda n, s: (0, 0))
    part = lambda width: pl.BlockSpec((block, width), lambda n, s: (n, 0))
    return pl.pallas_call(
        close_kernel,
        grid_spec=pltpu.PrefetchScalarGridSpec(
            num_scalar_prefetch=1,
            grid=(rows // block,),
            in_specs=[
                part(QD),
                part(MODEL_WIDTH),
                full((1, MODEL_WIDTH)),
                *halves(weights, MODEL_WIDTH, lambda n: QKV // MODEL_WIDTH),
                full((ranks, QD)),
                full((ranks, MODEL_WIDTH)),
            ],
            out_specs=[part(MODEL_WIDTH), part(MODEL_WIDTH), part(ranks)],
        ),
        out_shape=[
            jax.ShapeDtypeStruct((rows, MODEL_WIDTH), f32),
            jax.ShapeDtypeStruct((rows, MODEL_WIDTH), bf16),
            jax.ShapeDtypeStruct((rows, ranks), bf16),
        ],
        compiler_params=params_of(1),
        name="close_mixer",
        cost_estimate=pl.CostEstimate(
            flops=2 * rows * QD * MODEL_WIDTH, transcendentals=0, bytes_accessed=8 << 20
        ),
    )(order, att, hidden, gain, *weights, low_map, up_map)


def side_by_side(left, right):
    values = []
    for at in range(BLOCKS):
        tile = slice(at // 2 * BLOCK, (at // 2 + 1) * BLOCK)
        low_half = lanes_of((R, BLOCK)) < BLOCK // 2
        if at % 2 == 0:
            value = jnp.where(low_half, left[:, tile], pltpu.roll(right[:, tile], BLOCK // 2, 1))
        else:
            value = jnp.where(low_half, pltpu.roll(left[:, tile], BLOCK // 2, 1), right[:, tile])
        values.append(value.astype(bf16))
    return values


def expert_kernel(
    scalars,
    x,
    cot,
    routes,
    router,
    w_in,
    w_down,
    a_in,
    b_in,
    a_down,
    b_down,
    *rest,
):
    (
        sums_out,
        gates_out,
        packed,
        gates,
        gate_sums,
        low_in,
        low_in_turned,
        b_in_all,
        back_low,
        gated_low,
        back_in,
        acts,
        grads,
        low_grads,
        down_acc,
        out_acc,
        grad_acc,
    ) = rest[-17:]
    expert = pl.program_id(0)
    last = pl.num_programs(0) - 1
    rows = x.shape[0]
    block = rows
    local = a_in.shape[0]
    a_in_all = a_in[...].reshape(local * 2 * R, MODEL_WIDTH)
    a_down_all = a_down[...].reshape(local * R, H)
    b_down_all = b_down[...].reshape(local * R, MODEL_WIDTH)

    @pl.when(expert == 0)
    def _():
        logits = nt(x[...], router[...])
        experts = gates_out.shape[0]
        lane = lanes_of(logits.shape)
        name = lane + scalars[4]
        name = jnp.where(name >= experts, name - experts, name)
        name = jnp.where(lane < experts, name, -1)
        chosen = name == routes[:, 0:1]
        for k in range(1, TOP):
            chosen = chosen | (name == routes[:, k : k + 1])
        top = jnp.max(jnp.where(chosen, logits, -1e30), -1, keepdims=True)
        shifted = jnp.where(chosen, jnp.exp(jnp.where(chosen, logits - top, 0.0)), 0.0)
        weights = shifted / jnp.sum(shifted, -1, keepdims=True)
        gates[...] = weights
        gates_out[...] = weights.T[: gates_out.shape[0], :]
        low = nt(x[...], a_in_all)
        low_in[...] = low.astype(bf16)
        low_in_turned[...] = low.T.astype(bf16)
        back_low[...] = nt(cot[...], b_down_all)
        b_in_all[...] = jnp.zeros_like(b_in_all)
        for e in range(local):
            b_in_all[e * 2 * R : e * 2 * R + R, :H] = b_in[e, 0, 0]
            b_in_all[e * 2 * R + R : (e + 1) * 2 * R, H:] = b_in[e, 0, 1]
        gate_sums[...] = jnp.zeros_like(gate_sums)
        gated_low[...] = jnp.zeros_like(gated_low)
        back_in[...] = jnp.zeros_like(back_in)
        out_acc[...] = jnp.zeros_like(out_acc)
        grad_acc[...] = jnp.zeros_like(grad_acc)
        down_acc[...] = jnp.zeros_like(down_acc)

    def row_step(index, carry):
        at = pl.ds(pl.multiple_of(index * block, block), block)
        lane_in = lanes_of((block, local * 2 * R))
        lane_down = lanes_of((block, local * R))
        in_mine = (lane_in >= expert * 2 * R) & (lane_in < (expert + 1) * 2 * R)
        down_mine = (lane_down >= expert * R) & (lane_down < (expert + 1) * R)
        gate_all = gates[at, :]
        gate_lane = lanes_of(gate_all.shape) == expert
        weight = jnp.sum(jnp.where(gate_lane, gate_all, 0.0), -1, keepdims=True)
        mine = low_in[at, :]
        mine = jnp.where(in_mine, mine, jnp.zeros_like(mine))
        both = nn(x[at, :], w_in[0]) + nn(mine, b_in_all[...])
        gate = both[:, :H]
        upper = both[:, H:]
        sigmoid = jax.nn.sigmoid(gate)
        silu = gate * sigmoid
        act = (silu * upper).astype(bf16)
        acts[at, :] = act
        act_wide = act.astype(f32)
        low = jnp.where(down_mine, nt(act, a_down_all), 0.0).astype(bf16).astype(f32)
        plain = nt(cot[at, :], w_down[0])
        low_plain = back_low[at, :]
        dots = jnp.sum(act_wide * plain, -1, keepdims=True) + jnp.sum(
            low * low_plain, -1, keepdims=True
        )
        sum_lane = lanes_of(gate_all.shape) == expert + scalars[2]
        gate_sums[at, :] += jnp.where(sum_lane, dots, 0.0)
        low_grad = jnp.where(down_mine, weight * low_plain, 0.0).astype(bf16)
        low_grads[at, :] = low_grad
        grad_act = weight * plain + nn(low_grad, a_down_all)
        grad_first = grad_act * upper * sigmoid * (1.0 + gate * (1.0 - sigmoid))
        grad_second = grad_act * silu
        grad_both = jnp.concatenate(
            [grad_first.astype(bf16), grad_second.astype(bf16)], 1
        )
        grads[at, :] = grad_both
        gated_low[at, :] += (weight * low).astype(bf16)
        out_acc[at, :] += nn((weight * act_wide).astype(bf16), w_down[0])
        grad_acc[at, :] += nt(grad_both, w_in[0])
        low_back = jnp.where(in_mine, nt(grad_both, b_in_all[...]), 0.0)
        back_in[at, :] += low_back.astype(bf16)
        return carry

    lax.fori_loop(0, rows // block, row_step, 0)

    turned = low_in_turned[pl.ds(pl.multiple_of(expert * 2 * R, 2 * R), 2 * R), :]
    product = nn(turned, grads[...])
    first_b_in = local * 3 * R
    here = pl.ds(pl.multiple_of(first_b_in + expert * R, R), R)
    for at, value in enumerate(side_by_side(product[:R, :H], product[R:, H:])):
        packed[at, 0, here, :] = value
    down_acc[...] += tn(low_grads[...], acts[...])

    @pl.when(expert == last)
    def _():
        sums_out[:rows, :] = (grad_acc[...] + nn(back_in[...], a_in_all)).astype(bf16)
        experts = gates_out.shape[0]
        sums = gate_sums[...].T[:experts, :]
        sums = jnp.concatenate([sums[: experts // 2], sums[experts // 2 :]], 1)
        high = sums.astype(bf16).astype(f32)
        edge = rows + experts
        sums_out[rows:edge, :] = jnp.concatenate([high, sums - high], 0).astype(bf16)
        sums_out[edge:, :] = (out_acc[...] + nn(gated_low[...], b_down_all)).astype(bf16)
        wide = tn(back_in[...], x[...]).astype(bf16)
        tall = tn(gated_low[...], cot[...]).astype(bf16)
        for at in range(BLOCKS):
            columns = slice(at * BLOCK, (at + 1) * BLOCK)
            packed[at, 0, : local * 2 * R, :] = wide[:, columns]
            packed[at, 0, local * 2 * R : first_b_in, :] = tall[:, columns]
        for pair in range(local // 2):
            lower = down_acc[pair * 2 * R : pair * 2 * R + R, :]
            upper = down_acc[pair * 2 * R + R : (pair + 1) * 2 * R, :]
            row = local * 4 * R + pair * R
            for at, value in enumerate(side_by_side(lower, upper)):
                packed[at, 0, row : row + R, :] = value


def run_experts(
    scalars, x, cot, routes, router, w_in, w_down, a_in, b_in, a_down, b_down, experts, slots, packed
):
    rows = x.shape[0]
    local = w_in.shape[0]
    ranks_in = local * 2 * R
    ranks_down = local * R
    height = local * 9 * R // 2
    kept = [] if packed is None else [packed]
    full = lambda shape: pl.BlockSpec(shape, lambda e, s: (0,) * len(shape))
    return pl.pallas_call(
        expert_kernel,
        grid_spec=pltpu.PrefetchScalarGridSpec(
            num_scalar_prefetch=1,
            grid=(local,),
            in_specs=[
                full((rows, MODEL_WIDTH)),
                full((rows, MODEL_WIDTH)),
                pl.BlockSpec((rows, TOP), lambda e, s: (s[0], 0)),
                full((128, MODEL_WIDTH)),
                pl.BlockSpec((1, MODEL_WIDTH, 2 * H), lambda e, s: (e, 0, 0)),
                pl.BlockSpec((1, H, MODEL_WIDTH), lambda e, s: (e, 0, 0)),
                pl.BlockSpec((local, 1, 2 * R, MODEL_WIDTH), lambda e, s: (0, s[1], 0, 0)),
                pl.BlockSpec((local, 1, 2, R, H), lambda e, s: (0, s[1], 0, 0, 0)),
                pl.BlockSpec((local, 1, R, H), lambda e, s: (0, s[1], 0, 0)),
                pl.BlockSpec((local, 1, R, MODEL_WIDTH), lambda e, s: (0, s[1], 0, 0)),
            ]
            + [pl.BlockSpec(memory_space=pl.ANY)] * len(kept),
            out_specs=[
                full((2 * rows + experts, MODEL_WIDTH)),
                full((experts, rows)),
                pl.BlockSpec((BLOCKS, 1, height, BLOCK), lambda e, s: (0, s[3], 0, 0)),
            ],
            scratch_shapes=[
                pltpu.VMEM((rows, 128), f32),
                pltpu.VMEM((rows, 128), f32),
                pltpu.VMEM((rows, ranks_in), bf16),
                pltpu.VMEM((ranks_in, rows), bf16),
                pltpu.VMEM((ranks_in, 2 * H), bf16),
                pltpu.VMEM((rows, ranks_down), f32),
                pltpu.VMEM((rows, ranks_down), bf16),
                pltpu.VMEM((rows, ranks_in), bf16),
                pltpu.VMEM((rows, H), bf16),
                pltpu.VMEM((rows, 2 * H), bf16),
                pltpu.VMEM((rows, ranks_down), bf16),
                pltpu.VMEM((ranks_down, H), f32),
                pltpu.VMEM((rows, MODEL_WIDTH), f32),
                pltpu.VMEM((rows, MODEL_WIDTH), f32),
            ],
        ),
        out_shape=[
            jax.ShapeDtypeStruct((2 * rows + experts, MODEL_WIDTH), bf16),
            jax.ShapeDtypeStruct((experts, rows), f32),
            jax.ShapeDtypeStruct((BLOCKS, slots, height, BLOCK), bf16),
        ],
        input_output_aliases={11: 2} if kept else {},
        compiler_params=params_of(1),
        name="experts",
        cost_estimate=pl.CostEstimate(
            flops=local * rows * 9 * (1 << 20),
            transcendentals=local * rows * H,
            bytes_accessed=20 << 20,
        ),
    )(scalars, x, cot, routes, router, w_in, w_down, a_in, b_in, a_down, b_down, *kept)


def pack_kernel(left, right, both):
    both[:, : left.shape[1]] = left[...]
    both[:, left.shape[1] :] = right[...]


def pack(left, right):
    return pl.pallas_call(
        pack_kernel,
        out_shape=jax.ShapeDtypeStruct((left.shape[0], left.shape[1] + right.shape[1]), left.dtype),
        name="pack",
    )(left, right)


def open_back_kernel(count, order, cot, mid, gain, gates, router, weight_a, weight_b, low_map, up_map, low, att, *rest):
    parts = rest[:count]
    sums = rest[count : 3 * count]
    grad_mid, grad_att, grad_up, grad_low, columns = rest[3 * count :]
    gate_value = gates[...]
    half = gate_value.shape[0] // 2
    sides = []
    for side in range(2):
        value = None
        for at in range(count):
            pair = sums[2 * at + side][...].astype(f32)
            pair = pair[:half] + pair[half:]
            value = pair if value is None else value + pair
        sides.append(value)
    gate_grad = jnp.concatenate(sides, 0)
    logit = gate_value * (gate_grad - jnp.sum(gate_value * gate_grad, 0, keepdims=True))
    first = logit.astype(bf16)
    left = logit - first.astype(f32)
    second = left.astype(bf16)
    third = (left - second.astype(f32)).astype(bf16)
    grad = tn(first, router[...]) + (tn(second, router[...]) + tn(third, router[...]))
    for piece in parts:
        grad = grad + piece[...].astype(f32)
    total = cot[...].astype(f32) + norm_back(mid[...], gain[...].astype(f32), grad)
    grad_mid[...] = total
    branch = total.astype(bf16)
    low_grad = nt(branch, up_map[...]).astype(bf16)
    columns[...] = nn(low_grad, low_map[...])
    for side, weight in enumerate((weight_a, weight_b)):
        value = nt(branch, weight[...])
        for at in range(BLOCKS // 2):
            columns[:, column(order, side * BLOCKS // 2 + at)] += value[:, at * BLOCK : (at + 1) * BLOCK]
    grad_att[...] = columns[...].astype(bf16)
    up_part = tn(low[...], branch)
    low_part = tn(low_grad, att[...])

    @pl.when(pl.program_id(0) == 0)
    def _():
        grad_up[...] = up_part
        grad_low[...] = low_part

    @pl.when(pl.program_id(0) > 0)
    def _():
        grad_up[...] += up_part
        grad_low[...] += low_part


def open_back(order, cot, mid, gain, gates, router, weights, low_map, up_map, low, att, parts):
    rows = cot.shape[0]
    block = 256
    ranks = low_map.shape[0]
    experts = gates.shape[0]
    full = lambda shape: pl.BlockSpec(shape, lambda n, s: (0, 0))
    part = lambda width: pl.BlockSpec((block, width), lambda n, s: (n, 0))
    count = len(parts)
    below = rows // experts
    sums = [
        pl.BlockSpec((experts, block), lambda n, s: (below, n)),
        pl.BlockSpec((experts, block), lambda n, s: (below, rows // block + n)),
    ]

    def body(*refs):
        open_back_kernel(count, *refs)

    return pl.pallas_call(
        body,
        grid_spec=pltpu.PrefetchScalarGridSpec(
            num_scalar_prefetch=1,
            grid=(rows // block,),
            in_specs=[
                part(MODEL_WIDTH),
                part(MODEL_WIDTH),
                full((1, MODEL_WIDTH)),
                pl.BlockSpec((experts, block), lambda n, s: (0, n)),
                full((experts, MODEL_WIDTH)),
                *halves(weights, MODEL_WIDTH, lambda n: QKV // MODEL_WIDTH),
                full((ranks, QD)),
                full((ranks, MODEL_WIDTH)),
                part(ranks),
                part(QD),
            ]
            + [part(MODEL_WIDTH)] * count
            + sums * count,
            out_specs=[
                part(MODEL_WIDTH),
                part(QD),
                full((ranks, MODEL_WIDTH)),
                full((ranks, QD)),
            ],
            scratch_shapes=[pltpu.VMEM((block, QD), f32)],
        ),
        out_shape=[
            jax.ShapeDtypeStruct((rows, MODEL_WIDTH), f32),
            jax.ShapeDtypeStruct((rows, QD), bf16),
            jax.ShapeDtypeStruct((ranks, MODEL_WIDTH), f32),
            jax.ShapeDtypeStruct((ranks, QD), f32),
        ],
        compiler_params=params_of(1),
        name="open_back",
        cost_estimate=pl.CostEstimate(
            flops=2 * rows * QD * MODEL_WIDTH, transcendentals=0, bytes_accessed=14 << 20
        ),
    )(
        order, cot, mid, gain, gates, router, *weights, low_map, up_map, low, att, *parts,
        *[piece for piece in parts for _ in range(2)],
    )


def adapters_back_kernel(
    grad_query, grad_key, grad_value, low, normed, up_map, low_there, up_there, low_out, *results
):
    pieces = (grad_query, grad_key, grad_value)
    bounds = (0, QD, QD + KD, QKV)
    back = None
    ups = []
    for at in range(3):
        block = pieces[at][...]
        ups.append(tn(low[...], block)[at * R : (at + 1) * R])
        part = nt(block, up_map[:, bounds[at] : bounds[at + 1]])
        back = part if back is None else back + part
    value = back.astype(bf16)
    low_out[...] = value
    lows = tn(value, normed[...]) + low_there[...]
    if len(results) == 2:
        grad_up, grad_low = results
        grad_low[...] = lows
        for at in range(3):
            grad_up[:, bounds[at] : bounds[at + 1]] = ups[at]
        return
    (packed,) = results
    grad_up = jnp.concatenate(ups, 1)
    grad_out = up_there[3 * R :, :]
    small = BLOCK // 4
    lane = lanes_of((R, BLOCK))
    for owner in range(packed.shape[0]):
        tile = slice(owner // 4 * BLOCK, (owner // 4 + 1) * BLOCK)
        offset = owner % 4 * small
        first = jnp.zeros((R, BLOCK), f32)
        for at in range(4):
            piece = lows[at * R : (at + 1) * R, tile]
            shift = (at * small - offset) % BLOCK
            piece = pltpu.roll(piece, shift, 1) if shift else piece
            first = jnp.where((lane >= at * small) & (lane < (at + 1) * small), piece, first)
        piece = grad_up[:, owner // 2 * BLOCK : (owner // 2 + 1) * BLOCK]
        piece = pltpu.roll(piece, BLOCK // 2, 1) if owner % 2 else piece
        other = grad_out[:, tile]
        shift = (2 * small - offset) % BLOCK
        other = pltpu.roll(other, shift, 1) if shift else other
        packed[owner, :, :BLOCK] = first.astype(bf16)
        packed[owner, :, BLOCK:] = jnp.where(
            lane < 2 * small, piece, jnp.where(lane < 3 * small, other, 0.0)
        ).astype(bf16)


def adapters_back(grad_query, grad_key, grad_value, low, normed, up_map, low_there, up_there, devices):
    rows = normed.shape[0]
    ranks = up_map.shape[0]
    if devices * BLOCK // 4 == MODEL_WIDTH:
        results = [jax.ShapeDtypeStruct((devices, R, 2 * BLOCK), bf16)]
    else:
        results = [
            jax.ShapeDtypeStruct((R, QKV), f32),
            jax.ShapeDtypeStruct((ranks, MODEL_WIDTH), f32),
        ]
    back_low, *results = pl.pallas_call(
        adapters_back_kernel,
        out_shape=[jax.ShapeDtypeStruct((rows, ranks), bf16)] + results,
        compiler_params=pltpu.CompilerParams(vmem_limit_bytes=56 * 1024 * 1024),
        name="adapters_back",
        cost_estimate=pl.CostEstimate(
            flops=6 * rows * 256 * QKV, transcendentals=0, bytes_accessed=4 << 20
        ),
    )(grad_query, grad_key, grad_value, low, normed, up_map, low_there, up_there)
    if len(results) == 1:
        return results[0], back_low
    grad_up, grad_low = results
    small = MODEL_WIDTH // devices
    packed = jnp.concatenate(
        [
            grad_low.reshape(4, R, devices, small).transpose(2, 1, 0, 3).reshape(devices, R, 4 * small),
            grad_up.reshape(R, devices, 2 * small).transpose(1, 0, 2),
            up_there[3 * R :].reshape(R, devices, small).transpose(1, 0, 2),
            jnp.zeros((devices, R, small), f32),
        ],
        -1,
    )
    return packed.astype(bf16), back_low


def input_back_kernel(
    order, grad_query, grad_key, grad_value, low, weight_a, weight_b, low_map, hid, gain, mid, grad, columns
):
    columns[...] = nn(low[...], low_map[...])
    for side, weight in enumerate((weight_a, weight_b)):
        value = nt(grad_query[...], weight[:, :QD])
        value = value + nt(grad_key[...], weight[:, QD : QD + KD])
        value = value + nt(grad_value[...], weight[:, QD + KD :])
        for at in range(BLOCKS // 2):
            columns[:, column(order, side * BLOCKS // 2 + at)] += value[:, at * BLOCK : (at + 1) * BLOCK]
    rows = hid[...].astype(f32)
    grad[...] = (mid[...] + norm_back(rows, gain[...].astype(f32), columns[...])).astype(bf16)


def input_back(order, grad_query, grad_key, grad_value, low, weights, low_map, hidden, gain, mid):
    rows = hidden.shape[0]
    block = 256
    ranks = low_map.shape[0]
    full = lambda shape: pl.BlockSpec(shape, lambda n, s: (0, 0))
    part = lambda width: pl.BlockSpec((block, width), lambda n, s: (n, 0))
    return pl.pallas_call(
        input_back_kernel,
        grid_spec=pltpu.PrefetchScalarGridSpec(
            num_scalar_prefetch=1,
            grid=(rows // block,),
            in_specs=[
                part(QD),
                part(KD),
                part(KD),
                part(ranks),
                *halves(weights, QKV, lambda n: 0),
                full((ranks, MODEL_WIDTH)),
                part(MODEL_WIDTH),
                full((1, MODEL_WIDTH)),
                part(MODEL_WIDTH),
            ],
            out_specs=part(MODEL_WIDTH),
            scratch_shapes=[pltpu.VMEM((block, MODEL_WIDTH), f32)],
        ),
        out_shape=jax.ShapeDtypeStruct((rows, MODEL_WIDTH), bf16),
        compiler_params=params_of(1),
        name="input_back",
        cost_estimate=pl.CostEstimate(
            flops=2 * rows * QKV * MODEL_WIDTH, transcendentals=0, bytes_accessed=12 << 20
        ),
    )(order, grad_query, grad_key, grad_value, low, *weights, low_map, hidden, gain, mid)


def sum_experts_kernel(ids, pieces, a_in, b_in, a_down, b_down, acc):
    local = a_in.shape[0]
    small = a_down.shape[-1]
    acc[...] = jnp.zeros_like(acc)

    def step(index, carry):
        acc[ids[index]] += pieces[index].astype(f32)
        return carry

    lax.fori_loop(0, pieces.shape[0], step, 0)
    for e in range(local):
        a_in[e] = acc[:, e * 2 * R : (e + 1) * 2 * R, :]
        at = local * 2 * R + e * R
        b_down[e] = acc[:, at : at + R, :]
        at = local * 3 * R + e * R
        both = acc[:, at : at + R, :]
        b_in[e, :, 0] = both[:, :, :small]
        b_in[e, :, 1] = both[:, :, small:]
        at = local * 4 * R + e // 2 * R
        a_down[e] = acc[:, at : at + R, e % 2 * small : (e % 2 + 1) * small]


def sum_experts(ids, pieces, local):
    height = pieces.shape[1]
    lanes = pieces.shape[2]
    small = lanes // 2
    vmem = pl.BlockSpec(memory_space=pltpu.VMEM)
    return pl.pallas_call(
        sum_experts_kernel,
        in_specs=[pl.BlockSpec(memory_space=pltpu.SMEM), vmem],
        out_specs=[vmem, vmem, vmem, vmem],
        out_shape=[
            jax.ShapeDtypeStruct((local, NA, 2 * R, lanes), f32),
            jax.ShapeDtypeStruct((local, NA, 2, R, small), f32),
            jax.ShapeDtypeStruct((local, NA, R, small), f32),
            jax.ShapeDtypeStruct((local, NA, R, lanes), f32),
        ],
        scratch_shapes=[pltpu.VMEM((NA, height, lanes), f32)],
        compiler_params=pltpu.CompilerParams(vmem_limit_bytes=56 * 1024 * 1024),
        name="sum_experts",
    )(ids, pieces)


def sum_mixer_kernel(ids, pieces, grad_low, grad_up, grad_out, acc):
    width = grad_low.shape[-1]
    acc[...] = jnp.zeros_like(acc)

    def step(index, carry):
        acc[ids[index]] += pieces[index].astype(f32)
        return carry

    lax.fori_loop(0, pieces.shape[0], step, 0)
    total = acc[...]
    for at in range(4):
        grad_low[at] = total[:, :, at * width : (at + 1) * width]
    grad_up[...] = total[:, :, 4 * width : 6 * width]
    grad_out[...] = total[:, :, 6 * width : 7 * width]


def sum_mixer(ids, pieces):
    width = pieces.shape[2] // 8
    vmem = pl.BlockSpec(memory_space=pltpu.VMEM)
    return pl.pallas_call(
        sum_mixer_kernel,
        in_specs=[pl.BlockSpec(memory_space=pltpu.SMEM), vmem],
        out_specs=[vmem, vmem, vmem],
        out_shape=[
            jax.ShapeDtypeStruct((4, NA, R, width), f32),
            jax.ShapeDtypeStruct((NA, R, 2 * width), f32),
            jax.ShapeDtypeStruct((NA, R, width), f32),
        ],
        scratch_shapes=[pltpu.VMEM((NA, R, 8 * width), f32)],
        compiler_params=pltpu.CompilerParams(vmem_limit_bytes=56 * 1024 * 1024),
        name="sum_mixer",
    )(ids, pieces)


def rope_tables(rows):
    half = HS // 2
    frequency = (10000.0 ** (-2.0 * np.arange(half, dtype=np.float32) / HS)).astype(np.float32)
    angles = np.arange(rows, dtype=np.float32)[:, None] * frequency[None, :]
    cos = np.cos(angles.astype(np.float64)).astype(np.float32)
    sin = np.sin(angles.astype(np.float64)).astype(np.float32)
    return (
        jnp.asarray(np.concatenate([cos, cos, cos, cos], 1)),
        jnp.asarray(np.concatenate([-sin, sin, -sin, sin], 1)),
    )


def swap(value, bit):
    return lax.ppermute(value, "dp", [(at, at ^ bit) for at in range(BLOCKS)])


def both_neighbours(weight):
    return swap(weight, 2), swap(weight, 4)


def across(pair):
    one, two = pair
    middle = one.shape[0] // 2
    return swap(two[:middle], 2), swap(one[middle:], 4)


def tied(*values):
    return lax.optimization_barrier(values)


def order_of(row):
    if lax.axis_size("dp") != BLOCKS:
        return jnp.arange(BLOCKS, dtype=jnp.int32)
    return row.astype(jnp.int32) ^ jnp.array([0, 2, 4, 6, 1, 3, 5, 7], jnp.int32)


def to_owners(packed, owners, local):
    split = owners // BLOCKS
    if split == 1:
        return packed
    slots = packed.shape[1]
    edge = local * 3 * R
    wide = packed[:, :, :edge].reshape(BLOCKS, slots, edge, split, BLOCK // split)
    wide = wide.transpose(0, 3, 1, 2, 4).reshape(owners, slots, edge, BLOCK // split)
    rest = packed.shape[2] - edge
    narrow = packed[:, :, edge:].reshape(BLOCKS, slots, rest, 2, split, BLOCK // 2 // split)
    narrow = narrow.transpose(0, 4, 1, 2, 3, 5).reshape(owners, slots, rest, BLOCK // split)
    return jnp.concatenate([wide, narrow], 2)


def joined(left, right):
    return (left.astype(f32) + right.astype(f32)).astype(bf16)


def on_device(
    hidden,
    cotangent,
    lengths,
    adapter_ids,
    routes,
    attn_gain,
    ffn_gain,
    query_key_value_weight,
    w_out,
    w_router,
    w_gate_up,
    w_down,
    attention_lowmap,
    attention_query_key_value_upmap,
    attention_output_upmap,
    expert_gate_up_lowmap,
    expert_gate_up_upmap,
    expert_down_lowmap,
    expert_down_upmap,
):
    groups = lax.axis_size("expert")
    owners = lax.axis_size("dp")
    place = lax.axis_index("expert")
    row = lax.axis_index("dp")
    devices = groups * owners
    sequence = row * groups + place
    rows = hidden.shape[0]
    experts = w_router.shape[1]
    local = w_gate_up.shape[0]
    width = MODEL_WIDTH // owners
    attn_gain = attn_gain.reshape(1, MODEL_WIDTH)
    ffn_gain = ffn_gain.reshape(1, MODEL_WIDTH)
    length = lax.dynamic_slice(lengths, (sequence,), (1,))
    forward = [(at, (at + 1) % groups) for at in range(groups)]
    backward = [(at, (at - 1) % groups) for at in range(groups)]

    mine = lax.dynamic_slice(adapter_ids.reshape(owners, groups), (0, place), (owners, 1))[:, 0]
    low_turned = attention_lowmap.transpose(1, 0, 3, 2).reshape(NA, 4 * R, width)
    up_turned = (
        attention_query_key_value_upmap.reshape(NA, R, 2, width)
        .transpose(0, 2, 1, 3)
        .reshape(NA, 2 * R, width)
    )
    adapters = jnp.concatenate([low_turned, up_turned, attention_output_upmap], 1)[mine]
    adapters = lax.all_to_all(adapters, "dp", 0, 0, tiled=True)
    order = order_of(row)
    first = place * local
    router = jnp.roll(w_router.T, -first, axis=0)
    router_wide = jnp.concatenate(
        [router, jnp.zeros((128 - experts, MODEL_WIDTH), router.dtype)], 0
    )

    offsets = [0, 1] + [groups - 1] * (groups > 2) + list(range(2, groups - 1))
    offset = jnp.array(offsets, jnp.int32)
    source = (place - offset + groups) % groups
    tags = adapter_ids.reshape(owners, groups)[:, source]
    slot = jnp.arange(groups, dtype=jnp.int32)
    table = jnp.stack(
        [
            source,
            lax.dynamic_slice(tags, (row, 0), (1, groups))[0],
            offset * local,
            slot,
            jnp.full((groups,), first, jnp.int32),
        ],
        1,
    )

    both = pack(query_key_value_weight, w_out)
    cots = {0: cotangent, 1: lax.ppermute(cotangent, "expert", forward)}
    if owners == BLOCKS:
        pair = both_neighbours(both)
        pair, order, router, router_wide, table, tags, attn_gain, ffn_gain, length = tied(
            pair, order, router, router_wide, table, tags, attn_gain, ffn_gain, length
        )
        near = jnp.concatenate([both, *pair, *across(pair)], 0)
        near, adapters, cots[1], cotangent = tied(near, adapters, cots[1], cotangent)
        weights = near, swap(near, 1)
    else:
        whole = lax.all_gather(both, "dp", axis=0, tiled=True)
        weights = whole, whole
    if groups > 2:
        cots[groups - 1] = lax.ppermute(cotangent, "expert", backward)

    low_map = adapters[:, : 4 * R].transpose(1, 0, 2).reshape(4 * R, MODEL_WIDTH)
    up = (
        adapters[:, 4 * R : 6 * R]
        .reshape(owners, 2, R, width)
        .transpose(2, 0, 1, 3)
        .reshape(R, QKV)
    )
    up_out = adapters[:, 6 * R :].transpose(1, 0, 2).reshape(R, MODEL_WIDTH)
    column = jnp.arange(QKV, dtype=jnp.int32)
    part = jnp.where(column < QD, 0, jnp.where(column < QD + KD, 1, 2))
    up_map = jnp.where(
        part[None, None, :] == jnp.arange(4, dtype=jnp.int32)[:, None, None], up[None], 0
    ).reshape(4 * R, QKV)
    up_out_map = jnp.concatenate([jnp.zeros((3 * R, MODEL_WIDTH), bf16), up_out], 0)

    cos, sin = rope_tables(rows)


    qkv, low, normed_in = project(order, hidden, attn_gain, weights, low_map, up_map, cos, sin)
    if groups > 3:
        cots[1], low = tied(cots[1], low)
    for at in range(2, groups - 1):
        cots[at] = lax.ppermute(cots[at - 1], "expert", forward)
    attended, lse = attend(length, qkv)
    mid, normed_mid, low_out = close_mixer(
        order, attended, hidden, ffn_gain, weights, low_map, up_out_map
    )

    a_in = expert_gate_up_lowmap.transpose(0, 1, 3, 2)
    a_down = expert_down_lowmap.transpose(0, 1, 3, 2)

    xs = {0: normed_mid, 1: lax.ppermute(normed_mid, "expert", forward)}
    packed = None
    ran = {}
    for at, offset in enumerate(offsets):
        ran[offset], gate_part, packed = run_experts(
            table[at],
            xs[offset],
            cots[offset],
            routes,
            router_wide,
            w_gate_up,
            w_down,
            a_in,
            expert_gate_up_upmap,
            a_down,
            expert_down_upmap,
            experts,
            groups,
            packed,
        )
        if at == 0:
            gates = gate_part
            if groups > 2:
                normed_mid, packed = tied(normed_mid, packed)
                xs[groups - 1] = lax.ppermute(normed_mid, "expert", backward)
        elif at < groups - 2:
            value, packed = tied(xs[at], packed)
            xs[at + 1] = lax.ppermute(value, "expert", forward)
        if at == 2:
            first_sums, packed = tied(ran[1], packed)

    pieces = lax.all_to_all(to_owners(packed, owners, local), "dp", 0, 0, tiled=True)
    pieces = pieces.reshape(devices, pieces.shape[2], width)
    g_a_in, g_b_in, g_a_down, g_b_down = sum_experts(tags.reshape(devices), pieces, local)

    edge = rows + experts
    both_far = lax.ppermute(first_sums if groups > 2 else ran[1], "expert", forward)
    grad_far, out_far = both_far, both_far[edge:]
    for offset in range(2, groups):
        grad_part = joined(ran[offset][:edge], grad_far[:edge])
        if offset == groups - 1:
            grad_part, g_a_down = tied(grad_part, g_a_down)
        grad_far = lax.ppermute(grad_part, "expert", forward)
    if groups > 2:
        out_part = joined(ran[2][edge:], out_far)
        out_part, grad_far = tied(out_part, grad_far)
        out_far = lax.ppermute(out_part, "expert", forward)

    grad_mid, grad_attended, grad_up_out, grad_low_out = open_back(
        order,
        cotangent,
        mid,
        ffn_gain,
        gates,
        router,
        weights,
        low_map,
        up_out_map,
        low_out,
        attended,
        [ran[0], grad_far],
    )
    grad_query, grad_key, grad_value = attend_back(length, qkv, grad_attended, lse, cos, sin)
    out_far, grad_query = tied(out_far, grad_query)
    for offset in range(3, groups):
        out_far = lax.ppermute(joined(ran[offset][edge:], out_far), "expert", forward)
    packed, back_low = adapters_back(
        grad_query, grad_key, grad_value, low, normed_in, up_map, grad_low_out, grad_up_out, devices
    )
    packed = lax.all_to_all(packed, ("dp", "expert"), 0, 0, tiled=True)

    grad_hidden = input_back(
        order, grad_query, grad_key, grad_value, back_low, weights, low_map, hidden, attn_gain, grad_mid
    )
    out = (mid + ran[0][edge:].astype(f32) + out_far.astype(f32)).astype(bf16)
    out, packed = tied(out, packed)
    m_a, m_b, m_o = sum_mixer(adapter_ids, packed)
    return (
        out,
        grad_hidden,
        m_a.transpose(0, 1, 3, 2),
        m_b,
        m_o,
        g_a_in.transpose(0, 1, 3, 2),
        g_b_in,
        g_a_down.transpose(0, 1, 3, 2),
        g_b_down,
    )


def solution(mesh):
    in_specs = (
        P(("dp", "expert"), None),
        P(("dp", "expert"), None),
        P(),
        P(),
        P("dp", None),
        P(),
        P(),
        P("dp", None),
        P("dp", None),
        P(),
        P("expert", None, None),
        P("expert", None, None),
        P(None, None, "dp", None),
        P(None, None, "dp"),
        P(None, None, "dp"),
        P("expert", None, None, None),
        P("expert", None, None, None, None),
        P("expert", None, None, None),
        P("expert", None, None, None),
    )
    out_specs = (
        P(("dp", "expert"), None),
        P(("dp", "expert"), None),
        P(None, None, ("dp", "expert"), None),
        P(None, None, ("dp", "expert")),
        P(None, None, ("dp", "expert")),
        P("expert", None, "dp", None),
        P("expert", None, None, None, "dp"),
        P("expert", None, "dp", None),
        P("expert", None, None, "dp"),
    )
    return jax.shard_map(
        on_device, mesh=mesh, in_specs=in_specs, out_specs=out_specs, check_vma=False
    )
```

```python
import numpy as np
import jax
import jax.numpy as jnp
from jax import lax
from jax.experimental import pallas as pl
from jax.experimental.pallas import tpu as pltpu
from jax.sharding import PartitionSpec as P

MODEL_WIDTH = 1024
HQ = 16
KVH = 8
HS = 64
H = 512
TOP = 8
R = 16
NA = 8
QD = HQ * HS
KD = KVH * HS
QKV = QD + 2 * KD

epsilon = 1e-06
f32 = jnp.float32
bf16 = jnp.bfloat16


def nn(left, right):
    return lax.dot_general(left, right, (((1,), (0,)), ((), ())), preferred_element_type=f32)


def nt(left, right):
    return lax.dot_general(left, right, (((1,), (1,)), ((), ())), preferred_element_type=f32)


def tn(left, right):
    return lax.dot_general(left, right, (((0,), (0,)), ((), ())), preferred_element_type=f32)


def lanes_of(shape):
    return lax.broadcasted_iota(jnp.int32, shape, len(shape) - 1)


def row_scale(rows):
    return lax.rsqrt(jnp.mean(rows * rows, -1, keepdims=True) + epsilon)


def norm_back(rows, gain, grad):
    scale = row_scale(rows)
    scaled = grad * gain
    return scale * scaled - rows * (scale * scale * scale) * jnp.mean(
        rows * scaled, -1, keepdims=True
    )


def rope_swap(rows):
    width = rows.shape[-1]
    lane = lanes_of(rows.shape)
    return jnp.where(
        lane % HS < HS // 2,
        pltpu.roll(rows, width - HS // 2, 1),
        pltpu.roll(rows, HS // 2, 1),
    )


def both_halves(pair, half):
    rows = pair.astype(f32)
    lane = lanes_of(rows.shape)
    rolled = pltpu.roll(rows, HS, 1)
    keep = (lane < HS) == (half == 0)
    return jnp.where(keep, rows, rolled).astype(bf16)


def stacked_heads(pair):
    lane = lanes_of(pair.shape)
    zero = jnp.zeros_like(pair)
    return jnp.concatenate(
        [jnp.where(lane < HS, pair, zero), jnp.where(lane < HS, zero, pair)], 0
    )


def params_of(count):
    return pltpu.CompilerParams(
        dimension_semantics=("arbitrary",) * count, vmem_limit_bytes=56 * 1024 * 1024
    )


BLOCK = 128
BLOCKS = MODEL_WIDTH // BLOCK
HALF = MODEL_WIDTH // 2


def column(order, at):
    return pl.ds(pl.multiple_of(order[at] * BLOCK, BLOCK), BLOCK)


def halves(weights, width, index):
    there = 1 if weights[0] is weights[1] else 0
    return [
        pl.BlockSpec((HALF, width), lambda n, s: (0, index(n))),
        pl.BlockSpec((HALF, width), lambda n, s: (there, index(n))),
    ]


def project_kernel(
    order, hid, gain, weight_a, weight_b, low_map, up_map, cos, sin, qkv, low, normed, turned_rows
):
    step = pl.program_id(0)
    blocks = pl.num_programs(0)

    @pl.when(step == 0)
    def _():
        rows = hid[...].astype(f32)
        value = (rows * row_scale(rows) * gain[...].astype(f32)).astype(bf16)
        normed[...] = value
        low[...] = nt(value, low_map[...]).astype(bf16)
        for at in range(BLOCKS):
            turned_rows[:, at * BLOCK : (at + 1) * BLOCK] = normed[:, column(order, at)]

    value = (
        nn(turned_rows[:, :HALF], weight_a[...])
        + nn(turned_rows[:, HALF:], weight_b[...])
        + nn(low[...], up_map[...])
    )

    @pl.when(step < blocks * 3 // 4)
    def _():
        for part in range(value.shape[1] // 128):
            piece = value[:, part * 128 : part * 128 + 128]
            turned = piece * cos[...] + rope_swap(piece) * sin[...]
            qkv[:, part * 128 : part * 128 + 128] = turned.astype(bf16)

    @pl.when(step >= blocks * 3 // 4)
    def _():
        qkv[...] = value.astype(bf16)


def project(order, hidden, gain, weights, low_map, up_map, cos, sin):
    rows = hidden.shape[0]
    block = 512
    ranks = low_map.shape[0]
    full = lambda shape: pl.BlockSpec(shape, lambda n, s: (0, 0))
    return pl.pallas_call(
        project_kernel,
        grid_spec=pltpu.PrefetchScalarGridSpec(
            num_scalar_prefetch=1,
            grid=(QKV // block,),
            in_specs=[
                full((rows, MODEL_WIDTH)),
                full((1, MODEL_WIDTH)),
                *halves(weights, block, lambda n: n),
                full((ranks, MODEL_WIDTH)),
                pl.BlockSpec((ranks, block), lambda n, s: (0, n)),
                full((rows, 128)),
                full((rows, 128)),
            ],
            out_specs=[
                pl.BlockSpec((rows, block), lambda n, s: (0, n)),
                full((rows, ranks)),
                full((rows, MODEL_WIDTH)),
            ],
            scratch_shapes=[pltpu.VMEM((rows, MODEL_WIDTH), bf16)],
        ),
        out_shape=[
            jax.ShapeDtypeStruct((rows, QKV), bf16),
            jax.ShapeDtypeStruct((rows, ranks), bf16),
            jax.ShapeDtypeStruct((rows, MODEL_WIDTH), bf16),
        ],
        compiler_params=params_of(1),
        name="project",
        cost_estimate=pl.CostEstimate(
            flops=2 * rows * QKV * MODEL_WIDTH, transcendentals=0, bytes_accessed=8 << 20
        ),
    )(order, hidden, gain, *weights, low_map, up_map, cos, sin)


ROWB = 128
BACKB = 256


def length_column(length, count):
    key = lax.broadcasted_iota(jnp.int32, (count, 1), 0)
    return jnp.where(key < length, 0.0, -1e30)


def causal_block(block):
    key = lax.broadcasted_iota(jnp.int32, (block, 2 * block), 0)
    return jnp.where(key <= lanes_of((block, 2 * block)) % block, 0.0, -1e30)


def masked_scores(queries, keys, start, bias, causal):
    count = start + causal.shape[0]
    scores = nt(keys[:count], (queries.astype(f32) * 0.125).astype(bf16))
    near = scores[start:] + (bias[start:count] + causal)
    if start == 0:
        return near
    return jnp.concatenate([scores[:start] + bias[:start], near], 0)


def attend_kernel(scalars, query, key, value, result, lse):
    half = pl.program_id(0) % 2
    keys = both_halves(key[...], half)
    values = both_halves(value[...], half)
    rows = query.shape[0]
    bias = length_column(scalars[0], rows)
    causal = causal_block(ROWB)
    for start in range(0, rows, ROWB):
        count = start + ROWB
        stacked = stacked_heads(query[start:count, :])
        scores = masked_scores(stacked, keys, start, bias, causal)
        top = jnp.max(scores, 0, keepdims=True)
        shifted = jnp.exp(scores - top)
        total = jnp.sum(shifted, 0, keepdims=True)
        prob = (shifted * (1.0 / total)).astype(bf16)
        mixed = tn(prob, values[:count])
        lane = lanes_of((ROWB, 128))
        result[start:count, :] = jnp.where(lane < HS, mixed[:ROWB], mixed[ROWB:]).astype(bf16)
        logs = top + jnp.log(total)
        lse[0, 0:1, start:count] = logs[:, :ROWB]
        lse[0, 1:2, start:count] = logs[:, ROWB:]


def attend(length, qkv):
    rows = qkv.shape[0]
    pairs = KVH
    return pl.pallas_call(
        attend_kernel,
        grid_spec=pltpu.PrefetchScalarGridSpec(
            num_scalar_prefetch=1,
            grid=(pairs,),
            in_specs=[
                pl.BlockSpec((rows, 128), lambda g, s: (0, g)),
                pl.BlockSpec((rows, 128), lambda g, s: (0, QD // 128 + g // 2)),
                pl.BlockSpec((rows, 128), lambda g, s: (0, (QD + KD) // 128 + g // 2)),
            ],
            out_specs=[
                pl.BlockSpec((rows, 128), lambda g, s: (0, g)),
                pl.BlockSpec((1, 2, rows), lambda g, s: (g, 0, 0)),
            ],
        ),
        out_shape=[
            jax.ShapeDtypeStruct((rows, QD), bf16),
            jax.ShapeDtypeStruct((pairs, 2, rows), f32),
        ],
        compiler_params=params_of(1),
        name="attend",
        cost_estimate=pl.CostEstimate(
            flops=8 * rows * rows * QD, transcendentals=rows * rows * HQ, bytes_accessed=4 << 20
        ),
    )(length, qkv, qkv, qkv)


def attend_back_kernel(
    scalars, query, key, value, grad, lse, cos, sin, grad_query, grad_key, grad_value, key_acc, value_acc
):
    half = pl.program_id(0) % 2
    keys = both_halves(key[...], half)
    values = both_halves(value[...], half)
    rows = query.shape[0]
    bias = length_column(scalars[0], rows)
    causal = causal_block(BACKB)
    for start in reversed(range(0, rows, BACKB)):
        count = start + BACKB
        stacked = stacked_heads(query[start:count, :])
        grads = stacked_heads(grad[start:count, :])
        scores = masked_scores(stacked, keys, start, bias, causal)
        logs = jnp.concatenate([lse[0, 0:1, start:count], lse[0, 1:2, start:count]], 1)
        prob = jnp.exp(scores - logs)
        grad_prob = nt(values[:count], grads)
        delta = jnp.sum(prob * grad_prob, 0, keepdims=True)
        grad_score = (prob * (grad_prob - delta)).astype(bf16)
        mixed = tn(grad_score, keys[:count])
        lane = lanes_of((BACKB, 128))
        turned = 0.125 * jnp.where(lane < HS, mixed[:BACKB], mixed[BACKB:])
        turned = turned * cos[start:count, :] - rope_swap(turned) * sin[start:count, :]
        grad_query[start:count, :] = turned.astype(bf16)
        key_part = nn(grad_score, stacked)
        value_part = nn(prob.astype(bf16), grads)
        if count == rows:
            key_acc[...] = key_part
            value_acc[...] = value_part
        else:
            key_acc[:count, :] += key_part
            value_acc[:count, :] += value_part
    total = key_acc[...]
    total = 0.125 * (total + pltpu.roll(total, HS, 1))
    total = (total * cos[...] - rope_swap(total) * sin[...]).astype(bf16)
    other = value_acc[...]
    other = (other + pltpu.roll(other, HS, 1)).astype(bf16)

    @pl.when(half == 0)
    def _():
        grad_key[...] = total
        grad_value[...] = other

    @pl.when(half == 1)
    def _():
        low_half = lanes_of(total.shape) < HS
        grad_key[...] = jnp.where(low_half, grad_key[...], total)
        grad_value[...] = jnp.where(low_half, grad_value[...], other)


def attend_back(length, qkv, grad, lse, cos, sin):
    rows = qkv.shape[0]
    pairs = KVH
    return pl.pallas_call(
        attend_back_kernel,
        grid_spec=pltpu.PrefetchScalarGridSpec(
            num_scalar_prefetch=1,
            grid=(pairs,),
            in_specs=[
                pl.BlockSpec((rows, 128), lambda g, s: (0, g)),
                pl.BlockSpec((rows, 128), lambda g, s: (0, QD // 128 + g // 2)),
                pl.BlockSpec((rows, 128), lambda g, s: (0, (QD + KD) // 128 + g // 2)),
                pl.BlockSpec((rows, 128), lambda g, s: (0, g)),
                pl.BlockSpec((1, 2, rows), lambda g, s: (g, 0, 0)),
                pl.BlockSpec((rows, 128), lambda g, s: (0, 0)),
                pl.BlockSpec((rows, 128), lambda g, s: (0, 0)),
            ],
            out_specs=[
                pl.BlockSpec((rows, 128), lambda g, s: (0, g)),
                pl.BlockSpec((rows, 128), lambda g, s: (0, g // 2)),
                pl.BlockSpec((rows, 128), lambda g, s: (0, g // 2)),
            ],
            scratch_shapes=[pltpu.VMEM((rows, 128), f32), pltpu.VMEM((rows, 128), f32)],
        ),
        out_shape=[
            jax.ShapeDtypeStruct((rows, QD), bf16),
            jax.ShapeDtypeStruct((rows, KD), bf16),
            jax.ShapeDtypeStruct((rows, KD), bf16),
        ],
        compiler_params=params_of(1),
        name="attend_back",
        cost_estimate=pl.CostEstimate(
            flops=20 * rows * rows * QD, transcendentals=rows * rows * HQ, bytes_accessed=8 << 20
        ),
    )(length, qkv, qkv, qkv, grad, lse, cos, sin)


def close_kernel(order, att, hid, gain, weight_a, weight_b, low_map, up_map, mid, normed, low):
    low_value = nt(att[...], low_map[...]).astype(bf16)
    low[...] = low_value
    turned = jnp.concatenate([att[:, column(order, at)] for at in range(BLOCKS)], 1)
    stream = hid[...].astype(f32) + (
        nn(turned[:, :HALF], weight_a[...])
        + nn(turned[:, HALF:], weight_b[...])
        + nn(low_value, up_map[...])
    )
    mid[...] = stream
    normed[...] = (stream * row_scale(stream) * gain[...].astype(f32)).astype(bf16)


def close_mixer(order, att, hidden, gain, weights, low_map, up_map):
    rows = hidden.shape[0]
    block = 256
    ranks = low_map.shape[0]
    full = lambda shape: pl.BlockSpec(shape, lambda n, s: (0, 0))
    part = lambda width: pl.BlockSpec((block, width), lambda n, s: (n, 0))
    return pl.pallas_call(
        close_kernel,
        grid_spec=pltpu.PrefetchScalarGridSpec(
            num_scalar_prefetch=1,
            grid=(rows // block,),
            in_specs=[
                part(QD),
                part(MODEL_WIDTH),
                full((1, MODEL_WIDTH)),
                *halves(weights, MODEL_WIDTH, lambda n: QKV // MODEL_WIDTH),
                full((ranks, QD)),
                full((ranks, MODEL_WIDTH)),
            ],
            out_specs=[part(MODEL_WIDTH), part(MODEL_WIDTH), part(ranks)],
        ),
        out_shape=[
            jax.ShapeDtypeStruct((rows, MODEL_WIDTH), f32),
            jax.ShapeDtypeStruct((rows, MODEL_WIDTH), bf16),
            jax.ShapeDtypeStruct((rows, ranks), bf16),
        ],
        compiler_params=params_of(1),
        name="close_mixer",
        cost_estimate=pl.CostEstimate(
            flops=2 * rows * QD * MODEL_WIDTH, transcendentals=0, bytes_accessed=8 << 20
        ),
    )(order, att, hidden, gain, *weights, low_map, up_map)


def side_by_side(left, right):
    values = []
    for at in range(BLOCKS):
        tile = slice(at // 2 * BLOCK, (at // 2 + 1) * BLOCK)
        low_half = lanes_of((R, BLOCK)) < BLOCK // 2
        if at % 2 == 0:
            value = jnp.where(low_half, left[:, tile], pltpu.roll(right[:, tile], BLOCK // 2, 1))
        else:
            value = jnp.where(low_half, pltpu.roll(left[:, tile], BLOCK // 2, 1), right[:, tile])
        values.append(value.astype(bf16))
    return values


def expert_kernel(
    scalars,
    x,
    cot,
    routes,
    router,
    w_in,
    w_down,
    a_in,
    b_in,
    a_down,
    b_down,
    *rest,
):
    (
        sums_out,
        gates_out,
        packed,
        gates,
        gate_sums,
        low_in,
        low_in_turned,
        b_in_all,
        back_low,
        gated_low,
        back_in,
        acts,
        grads,
        low_grads,
        down_acc,
        out_acc,
        grad_acc,
    ) = rest[-17:]
    expert = pl.program_id(0)
    last = pl.num_programs(0) - 1
    rows = x.shape[0]
    block = rows
    local = a_in.shape[0]
    a_in_all = a_in[...].reshape(local * 2 * R, MODEL_WIDTH)
    a_down_all = a_down[...].reshape(local * R, H)
    b_down_all = b_down[...].reshape(local * R, MODEL_WIDTH)

    @pl.when(expert == 0)
    def _():
        logits = nt(x[...], router[...])
        experts = gates_out.shape[0]
        lane = lanes_of(logits.shape)
        name = lane + scalars[4]
        name = jnp.where(name >= experts, name - experts, name)
        name = jnp.where(lane < experts, name, -1)
        chosen = name == routes[:, 0:1]
        for k in range(1, TOP):
            chosen = chosen | (name == routes[:, k : k + 1])
        top = jnp.max(jnp.where(chosen, logits, -1e30), -1, keepdims=True)
        shifted = jnp.where(chosen, jnp.exp(jnp.where(chosen, logits - top, 0.0)), 0.0)
        weights = shifted / jnp.sum(shifted, -1, keepdims=True)
        gates[...] = weights
        gates_out[...] = weights.T[: gates_out.shape[0], :]
        low = nt(x[...], a_in_all)
        low_in[...] = low.astype(bf16)
        low_in_turned[...] = low.T.astype(bf16)
        back_low[...] = nt(cot[...], b_down_all)
        b_in_all[...] = jnp.zeros_like(b_in_all)
        for e in range(local):
            b_in_all[e * 2 * R : e * 2 * R + R, :H] = b_in[e, 0, 0]
            b_in_all[e * 2 * R + R : (e + 1) * 2 * R, H:] = b_in[e, 0, 1]
        gate_sums[...] = jnp.zeros_like(gate_sums)
        gated_low[...] = jnp.zeros_like(gated_low)
        back_in[...] = jnp.zeros_like(back_in)
        out_acc[...] = jnp.zeros_like(out_acc)
        grad_acc[...] = jnp.zeros_like(grad_acc)
        down_acc[...] = jnp.zeros_like(down_acc)

    def row_step(index, carry):
        at = pl.ds(pl.multiple_of(index * block, block), block)
        lane_in = lanes_of((block, local * 2 * R))
        lane_down = lanes_of((block, local * R))
        in_mine = (lane_in >= expert * 2 * R) & (lane_in < (expert + 1) * 2 * R)
        down_mine = (lane_down >= expert * R) & (lane_down < (expert + 1) * R)
        gate_all = gates[at, :]
        gate_lane = lanes_of(gate_all.shape) == expert
        weight = jnp.sum(jnp.where(gate_lane, gate_all, 0.0), -1, keepdims=True)
        mine = low_in[at, :]
        mine = jnp.where(in_mine, mine, jnp.zeros_like(mine))
        both = nn(x[at, :], w_in[0]) + nn(mine, b_in_all[...])
        gate = both[:, :H]
        upper = both[:, H:]
        sigmoid = jax.nn.sigmoid(gate)
        silu = gate * sigmoid
        act = (silu * upper).astype(bf16)
        acts[at, :] = act
        act_wide = act.astype(f32)
        low = jnp.where(down_mine, nt(act, a_down_all), 0.0).astype(bf16).astype(f32)
        plain = nt(cot[at, :], w_down[0])
        low_plain = back_low[at, :]
        dots = jnp.sum(act_wide * plain, -1, keepdims=True) + jnp.sum(
            low * low_plain, -1, keepdims=True
        )
        sum_lane = lanes_of(gate_all.shape) == expert + scalars[2]
        gate_sums[at, :] += jnp.where(sum_lane, dots, 0.0)
        low_grad = jnp.where(down_mine, weight * low_plain, 0.0).astype(bf16)
        low_grads[at, :] = low_grad
        grad_act = weight * plain + nn(low_grad, a_down_all)
        grad_first = grad_act * upper * sigmoid * (1.0 + gate * (1.0 - sigmoid))
        grad_second = grad_act * silu
        grad_both = jnp.concatenate(
            [grad_first.astype(bf16), grad_second.astype(bf16)], 1
        )
        grads[at, :] = grad_both
        gated_low[at, :] += (weight * low).astype(bf16)
        out_acc[at, :] += nn((weight * act_wide).astype(bf16), w_down[0])
        grad_acc[at, :] += nt(grad_both, w_in[0])
        low_back = jnp.where(in_mine, nt(grad_both, b_in_all[...]), 0.0)
        back_in[at, :] += low_back.astype(bf16)
        return carry

    lax.fori_loop(0, rows // block, row_step, 0)

    turned = low_in_turned[pl.ds(pl.multiple_of(expert * 2 * R, 2 * R), 2 * R), :]
    product = nn(turned, grads[...])
    first_b_in = local * 3 * R
    here = pl.ds(pl.multiple_of(first_b_in + expert * R, R), R)
    for at, value in enumerate(side_by_side(product[:R, :H], product[R:, H:])):
        packed[at, 0, here, :] = value
    down_acc[...] += tn(low_grads[...], acts[...])

    @pl.when(expert == last)
    def _():
        sums_out[:rows, :] = (grad_acc[...] + nn(back_in[...], a_in_all)).astype(bf16)
        experts = gates_out.shape[0]
        sums = gate_sums[...].T[:experts, :]
        sums = jnp.concatenate([sums[: experts // 2], sums[experts // 2 :]], 1)
        high = sums.astype(bf16).astype(f32)
        edge = rows + experts
        sums_out[rows:edge, :] = jnp.concatenate([high, sums - high], 0).astype(bf16)
        sums_out[edge:, :] = (out_acc[...] + nn(gated_low[...], b_down_all)).astype(bf16)
        wide = tn(back_in[...], x[...]).astype(bf16)
        tall = tn(gated_low[...], cot[...]).astype(bf16)
        for at in range(BLOCKS):
            columns = slice(at * BLOCK, (at + 1) * BLOCK)
            packed[at, 0, : local * 2 * R, :] = wide[:, columns]
            packed[at, 0, local * 2 * R : first_b_in, :] = tall[:, columns]
        for pair in range(local // 2):
            lower = down_acc[pair * 2 * R : pair * 2 * R + R, :]
            upper = down_acc[pair * 2 * R + R : (pair + 1) * 2 * R, :]
            row = local * 4 * R + pair * R
            for at, value in enumerate(side_by_side(lower, upper)):
                packed[at, 0, row : row + R, :] = value


def run_experts(
    scalars, x, cot, routes, router, w_in, w_down, a_in, b_in, a_down, b_down, experts, slots, packed
):
    rows = x.shape[0]
    local = w_in.shape[0]
    ranks_in = local * 2 * R
    ranks_down = local * R
    height = local * 9 * R // 2
    kept = [] if packed is None else [packed]
    full = lambda shape: pl.BlockSpec(shape, lambda e, s: (0,) * len(shape))
    return pl.pallas_call(
        expert_kernel,
        grid_spec=pltpu.PrefetchScalarGridSpec(
            num_scalar_prefetch=1,
            grid=(local,),
            in_specs=[
                full((rows, MODEL_WIDTH)),
                full((rows, MODEL_WIDTH)),
                pl.BlockSpec((rows, TOP), lambda e, s: (s[0], 0)),
                full((128, MODEL_WIDTH)),
                pl.BlockSpec((1, MODEL_WIDTH, 2 * H), lambda e, s: (e, 0, 0)),
                pl.BlockSpec((1, H, MODEL_WIDTH), lambda e, s: (e, 0, 0)),
                pl.BlockSpec((local, 1, 2 * R, MODEL_WIDTH), lambda e, s: (0, s[1], 0, 0)),
                pl.BlockSpec((local, 1, 2, R, H), lambda e, s: (0, s[1], 0, 0, 0)),
                pl.BlockSpec((local, 1, R, H), lambda e, s: (0, s[1], 0, 0)),
                pl.BlockSpec((local, 1, R, MODEL_WIDTH), lambda e, s: (0, s[1], 0, 0)),
            ]
            + [pl.BlockSpec(memory_space=pl.ANY)] * len(kept),
            out_specs=[
                full((2 * rows + experts, MODEL_WIDTH)),
                full((experts, rows)),
                pl.BlockSpec((BLOCKS, 1, height, BLOCK), lambda e, s: (0, s[3], 0, 0)),
            ],
            scratch_shapes=[
                pltpu.VMEM((rows, 128), f32),
                pltpu.VMEM((rows, 128), f32),
                pltpu.VMEM((rows, ranks_in), bf16),
                pltpu.VMEM((ranks_in, rows), bf16),
                pltpu.VMEM((ranks_in, 2 * H), bf16),
                pltpu.VMEM((rows, ranks_down), f32),
                pltpu.VMEM((rows, ranks_down), bf16),
                pltpu.VMEM((rows, ranks_in), bf16),
                pltpu.VMEM((rows, H), bf16),
                pltpu.VMEM((rows, 2 * H), bf16),
                pltpu.VMEM((rows, ranks_down), bf16),
                pltpu.VMEM((ranks_down, H), f32),
                pltpu.VMEM((rows, MODEL_WIDTH), f32),
                pltpu.VMEM((rows, MODEL_WIDTH), f32),
            ],
        ),
        out_shape=[
            jax.ShapeDtypeStruct((2 * rows + experts, MODEL_WIDTH), bf16),
            jax.ShapeDtypeStruct((experts, rows), f32),
            jax.ShapeDtypeStruct((BLOCKS, slots, height, BLOCK), bf16),
        ],
        input_output_aliases={11: 2} if kept else {},
        compiler_params=params_of(1),
        name="experts",
        cost_estimate=pl.CostEstimate(
            flops=local * rows * 9 * (1 << 20),
            transcendentals=local * rows * H,
            bytes_accessed=20 << 20,
        ),
    )(scalars, x, cot, routes, router, w_in, w_down, a_in, b_in, a_down, b_down, *kept)


def pack_kernel(left, right, both):
    both[:, : left.shape[1]] = left[...]
    both[:, left.shape[1] :] = right[...]


def pack(left, right):
    return pl.pallas_call(
        pack_kernel,
        out_shape=jax.ShapeDtypeStruct((left.shape[0], left.shape[1] + right.shape[1]), left.dtype),
        name="pack",
    )(left, right)


def open_back_kernel(count, order, cot, mid, gain, gates, router, weight_a, weight_b, low_map, up_map, low, att, *rest):
    parts = rest[:count]
    sums = rest[count : 3 * count]
    grad_mid, grad_att, grad_up, grad_low, columns = rest[3 * count :]
    gate_value = gates[...]
    half = gate_value.shape[0] // 2
    sides = []
    for side in range(2):
        value = None
        for at in range(count):
            pair = sums[2 * at + side][...].astype(f32)
            pair = pair[:half] + pair[half:]
            value = pair if value is None else value + pair
        sides.append(value)
    gate_grad = jnp.concatenate(sides, 0)
    logit = gate_value * (gate_grad - jnp.sum(gate_value * gate_grad, 0, keepdims=True))
    first = logit.astype(bf16)
    left = logit - first.astype(f32)
    second = left.astype(bf16)
    third = (left - second.astype(f32)).astype(bf16)
    grad = tn(first, router[...]) + (tn(second, router[...]) + tn(third, router[...]))
    for piece in parts:
        grad = grad + piece[...].astype(f32)
    total = cot[...].astype(f32) + norm_back(mid[...], gain[...].astype(f32), grad)
    grad_mid[...] = total
    branch = total.astype(bf16)
    low_grad = nt(branch, up_map[...]).astype(bf16)
    columns[...] = nn(low_grad, low_map[...])
    for side, weight in enumerate((weight_a, weight_b)):
        value = nt(branch, weight[...])
        for at in range(BLOCKS // 2):
            columns[:, column(order, side * BLOCKS // 2 + at)] += value[:, at * BLOCK : (at + 1) * BLOCK]
    grad_att[...] = columns[...].astype(bf16)
    up_part = tn(low[...], branch)
    low_part = tn(low_grad, att[...])

    @pl.when(pl.program_id(0) == 0)
    def _():
        grad_up[...] = up_part
        grad_low[...] = low_part

    @pl.when(pl.program_id(0) > 0)
    def _():
        grad_up[...] += up_part
        grad_low[...] += low_part


def open_back(order, cot, mid, gain, gates, router, weights, low_map, up_map, low, att, parts):
    rows = cot.shape[0]
    block = 256
    ranks = low_map.shape[0]
    experts = gates.shape[0]
    full = lambda shape: pl.BlockSpec(shape, lambda n, s: (0, 0))
    part = lambda width: pl.BlockSpec((block, width), lambda n, s: (n, 0))
    count = len(parts)
    below = rows // experts
    sums = [
        pl.BlockSpec((experts, block), lambda n, s: (below, n)),
        pl.BlockSpec((experts, block), lambda n, s: (below, rows // block + n)),
    ]

    def body(*refs):
        open_back_kernel(count, *refs)

    return pl.pallas_call(
        body,
        grid_spec=pltpu.PrefetchScalarGridSpec(
            num_scalar_prefetch=1,
            grid=(rows // block,),
            in_specs=[
                part(MODEL_WIDTH),
                part(MODEL_WIDTH),
                full((1, MODEL_WIDTH)),
                pl.BlockSpec((experts, block), lambda n, s: (0, n)),
                full((experts, MODEL_WIDTH)),
                *halves(weights, MODEL_WIDTH, lambda n: QKV // MODEL_WIDTH),
                full((ranks, QD)),
                full((ranks, MODEL_WIDTH)),
                part(ranks),
                part(QD),
            ]
            + [part(MODEL_WIDTH)] * count
            + sums * count,
            out_specs=[
                part(MODEL_WIDTH),
                part(QD),
                full((ranks, MODEL_WIDTH)),
                full((ranks, QD)),
            ],
            scratch_shapes=[pltpu.VMEM((block, QD), f32)],
        ),
        out_shape=[
            jax.ShapeDtypeStruct((rows, MODEL_WIDTH), f32),
            jax.ShapeDtypeStruct((rows, QD), bf16),
            jax.ShapeDtypeStruct((ranks, MODEL_WIDTH), f32),
            jax.ShapeDtypeStruct((ranks, QD), f32),
        ],
        compiler_params=params_of(1),
        name="open_back",
        cost_estimate=pl.CostEstimate(
            flops=2 * rows * QD * MODEL_WIDTH, transcendentals=0, bytes_accessed=14 << 20
        ),
    )(
        order, cot, mid, gain, gates, router, *weights, low_map, up_map, low, att, *parts,
        *[piece for piece in parts for _ in range(2)],
    )


def adapters_back_kernel(
    grad_query, grad_key, grad_value, low, normed, up_map, low_there, up_there, low_out, *results
):
    pieces = (grad_query, grad_key, grad_value)
    bounds = (0, QD, QD + KD, QKV)
    back = None
    ups = []
    for at in range(3):
        block = pieces[at][...]
        ups.append(tn(low[...], block)[at * R : (at + 1) * R])
        part = nt(block, up_map[:, bounds[at] : bounds[at + 1]])
        back = part if back is None else back + part
    value = back.astype(bf16)
    low_out[...] = value
    lows = tn(value, normed[...]) + low_there[...]
    if len(results) == 2:
        grad_up, grad_low = results
        grad_low[...] = lows
        for at in range(3):
            grad_up[:, bounds[at] : bounds[at + 1]] = ups[at]
        return
    (packed,) = results
    grad_up = jnp.concatenate(ups, 1)
    grad_out = up_there[3 * R :, :]
    small = BLOCK // 4
    lane = lanes_of((R, BLOCK))
    for owner in range(packed.shape[0]):
        tile = slice(owner // 4 * BLOCK, (owner // 4 + 1) * BLOCK)
        offset = owner % 4 * small
        first = jnp.zeros((R, BLOCK), f32)
        for at in range(4):
            piece = lows[at * R : (at + 1) * R, tile]
            shift = (at * small - offset) % BLOCK
            piece = pltpu.roll(piece, shift, 1) if shift else piece
            first = jnp.where((lane >= at * small) & (lane < (at + 1) * small), piece, first)
        piece = grad_up[:, owner // 2 * BLOCK : (owner // 2 + 1) * BLOCK]
        piece = pltpu.roll(piece, BLOCK // 2, 1) if owner % 2 else piece
        other = grad_out[:, tile]
        shift = (2 * small - offset) % BLOCK
        other = pltpu.roll(other, shift, 1) if shift else other
        packed[owner, :, :BLOCK] = first.astype(bf16)
        packed[owner, :, BLOCK:] = jnp.where(
            lane < 2 * small, piece, jnp.where(lane < 3 * small, other, 0.0)
        ).astype(bf16)


def adapters_back(grad_query, grad_key, grad_value, low, normed, up_map, low_there, up_there, devices):
    rows = normed.shape[0]
    ranks = up_map.shape[0]
    if devices * BLOCK // 4 == MODEL_WIDTH:
        results = [jax.ShapeDtypeStruct((devices, R, 2 * BLOCK), bf16)]
    else:
        results = [
            jax.ShapeDtypeStruct((R, QKV), f32),
            jax.ShapeDtypeStruct((ranks, MODEL_WIDTH), f32),
        ]
    back_low, *results = pl.pallas_call(
        adapters_back_kernel,
        out_shape=[jax.ShapeDtypeStruct((rows, ranks), bf16)] + results,
        compiler_params=pltpu.CompilerParams(vmem_limit_bytes=56 * 1024 * 1024),
        name="adapters_back",
        cost_estimate=pl.CostEstimate(
            flops=6 * rows * 256 * QKV, transcendentals=0, bytes_accessed=4 << 20
        ),
    )(grad_query, grad_key, grad_value, low, normed, up_map, low_there, up_there)
    if len(results) == 1:
        return results[0], back_low
    grad_up, grad_low = results
    small = MODEL_WIDTH // devices
    packed = jnp.concatenate(
        [
            grad_low.reshape(4, R, devices, small).transpose(2, 1, 0, 3).reshape(devices, R, 4 * small),
            grad_up.reshape(R, devices, 2 * small).transpose(1, 0, 2),
            up_there[3 * R :].reshape(R, devices, small).transpose(1, 0, 2),
            jnp.zeros((devices, R, small), f32),
        ],
        -1,
    )
    return packed.astype(bf16), back_low


def input_back_kernel(
    order, grad_query, grad_key, grad_value, low, weight_a, weight_b, low_map, hid, gain, mid, grad, columns
):
    columns[...] = nn(low[...], low_map[...])
    for side, weight in enumerate((weight_a, weight_b)):
        value = nt(grad_query[...], weight[:, :QD])
        value = value + nt(grad_key[...], weight[:, QD : QD + KD])
        value = value + nt(grad_value[...], weight[:, QD + KD :])
        for at in range(BLOCKS // 2):
            columns[:, column(order, side * BLOCKS // 2 + at)] += value[:, at * BLOCK : (at + 1) * BLOCK]
    rows = hid[...].astype(f32)
    grad[...] = (mid[...] + norm_back(rows, gain[...].astype(f32), columns[...])).astype(bf16)


def input_back(order, grad_query, grad_key, grad_value, low, weights, low_map, hidden, gain, mid):
    rows = hidden.shape[0]
    block = 256
    ranks = low_map.shape[0]
    full = lambda shape: pl.BlockSpec(shape, lambda n, s: (0, 0))
    part = lambda width: pl.BlockSpec((block, width), lambda n, s: (n, 0))
    return pl.pallas_call(
        input_back_kernel,
        grid_spec=pltpu.PrefetchScalarGridSpec(
            num_scalar_prefetch=1,
            grid=(rows // block,),
            in_specs=[
                part(QD),
                part(KD),
                part(KD),
                part(ranks),
                *halves(weights, QKV, lambda n: 0),
                full((ranks, MODEL_WIDTH)),
                part(MODEL_WIDTH),
                full((1, MODEL_WIDTH)),
                part(MODEL_WIDTH),
            ],
            out_specs=part(MODEL_WIDTH),
            scratch_shapes=[pltpu.VMEM((block, MODEL_WIDTH), f32)],
        ),
        out_shape=jax.ShapeDtypeStruct((rows, MODEL_WIDTH), bf16),
        compiler_params=params_of(1),
        name="input_back",
        cost_estimate=pl.CostEstimate(
            flops=2 * rows * QKV * MODEL_WIDTH, transcendentals=0, bytes_accessed=12 << 20
        ),
    )(order, grad_query, grad_key, grad_value, low, *weights, low_map, hidden, gain, mid)


def sum_experts_kernel(ids, pieces, a_in, b_in, a_down, b_down, acc):
    local = a_in.shape[0]
    small = a_down.shape[-1]
    acc[...] = jnp.zeros_like(acc)

    def step(index, carry):
        acc[ids[index]] += pieces[index].astype(f32)
        return carry

    lax.fori_loop(0, pieces.shape[0], step, 0)
    for e in range(local):
        a_in[e] = acc[:, e * 2 * R : (e + 1) * 2 * R, :]
        at = local * 2 * R + e * R
        b_down[e] = acc[:, at : at + R, :]
        at = local * 3 * R + e * R
        both = acc[:, at : at + R, :]
        b_in[e, :, 0] = both[:, :, :small]
        b_in[e, :, 1] = both[:, :, small:]
        at = local * 4 * R + e // 2 * R
        a_down[e] = acc[:, at : at + R, e % 2 * small : (e % 2 + 1) * small]


def sum_experts(ids, pieces, local):
    height = pieces.shape[1]
    lanes = pieces.shape[2]
    small = lanes // 2
    vmem = pl.BlockSpec(memory_space=pltpu.VMEM)
    return pl.pallas_call(
        sum_experts_kernel,
        in_specs=[pl.BlockSpec(memory_space=pltpu.SMEM), vmem],
        out_specs=[vmem, vmem, vmem, vmem],
        out_shape=[
            jax.ShapeDtypeStruct((local, NA, 2 * R, lanes), f32),
            jax.ShapeDtypeStruct((local, NA, 2, R, small), f32),
            jax.ShapeDtypeStruct((local, NA, R, small), f32),
            jax.ShapeDtypeStruct((local, NA, R, lanes), f32),
        ],
        scratch_shapes=[pltpu.VMEM((NA, height, lanes), f32)],
        compiler_params=pltpu.CompilerParams(vmem_limit_bytes=56 * 1024 * 1024),
        name="sum_experts",
    )(ids, pieces)


def sum_mixer_kernel(ids, pieces, grad_low, grad_up, grad_out, acc):
    width = grad_low.shape[-1]
    acc[...] = jnp.zeros_like(acc)

    def step(index, carry):
        acc[ids[index]] += pieces[index].astype(f32)
        return carry

    lax.fori_loop(0, pieces.shape[0], step, 0)
    total = acc[...]
    for at in range(4):
        grad_low[at] = total[:, :, at * width : (at + 1) * width]
    grad_up[...] = total[:, :, 4 * width : 6 * width]
    grad_out[...] = total[:, :, 6 * width : 7 * width]


def sum_mixer(ids, pieces):
    width = pieces.shape[2] // 8
    vmem = pl.BlockSpec(memory_space=pltpu.VMEM)
    return pl.pallas_call(
        sum_mixer_kernel,
        in_specs=[pl.BlockSpec(memory_space=pltpu.SMEM), vmem],
        out_specs=[vmem, vmem, vmem],
        out_shape=[
            jax.ShapeDtypeStruct((4, NA, R, width), f32),
            jax.ShapeDtypeStruct((NA, R, 2 * width), f32),
            jax.ShapeDtypeStruct((NA, R, width), f32),
        ],
        scratch_shapes=[pltpu.VMEM((NA, R, 8 * width), f32)],
        compiler_params=pltpu.CompilerParams(vmem_limit_bytes=56 * 1024 * 1024),
        name="sum_mixer",
    )(ids, pieces)


def rope_tables(rows):
    half = HS // 2
    frequency = (10000.0 ** (-2.0 * np.arange(half, dtype=np.float32) / HS)).astype(np.float32)
    angles = np.arange(rows, dtype=np.float32)[:, None] * frequency[None, :]
    cos = np.cos(angles.astype(np.float64)).astype(np.float32)
    sin = np.sin(angles.astype(np.float64)).astype(np.float32)
    return (
        jnp.asarray(np.concatenate([cos, cos, cos, cos], 1)),
        jnp.asarray(np.concatenate([-sin, sin, -sin, sin], 1)),
    )


def swap(value, bit):
    return lax.ppermute(value, "dp", [(at, at ^ bit) for at in range(BLOCKS)])


def both_neighbours(weight):
    return swap(weight, 2), swap(weight, 4)


def across(pair):
    one, two = pair
    middle = one.shape[0] // 2
    return swap(two[:middle], 2), swap(one[middle:], 4)


def tied(*values):
    return lax.optimization_barrier(values)


def order_of(row):
    if lax.axis_size("dp") != BLOCKS:
        return jnp.arange(BLOCKS, dtype=jnp.int32)
    return row.astype(jnp.int32) ^ jnp.array([0, 2, 4, 6, 1, 3, 5, 7], jnp.int32)


def to_owners(packed, owners, local):
    split = owners // BLOCKS
    if split == 1:
        return packed
    slots = packed.shape[1]
    edge = local * 3 * R
    wide = packed[:, :, :edge].reshape(BLOCKS, slots, edge, split, BLOCK // split)
    wide = wide.transpose(0, 3, 1, 2, 4).reshape(owners, slots, edge, BLOCK // split)
    rest = packed.shape[2] - edge
    narrow = packed[:, :, edge:].reshape(BLOCKS, slots, rest, 2, split, BLOCK // 2 // split)
    narrow = narrow.transpose(0, 4, 1, 2, 3, 5).reshape(owners, slots, rest, BLOCK // split)
    return jnp.concatenate([wide, narrow], 2)


def joined(left, right):
    return (left.astype(f32) + right.astype(f32)).astype(bf16)


def maps_of(adapters, owners, width):
    low_map = adapters[:, : 4 * R].transpose(1, 0, 2).reshape(4 * R, MODEL_WIDTH)
    up = (
        adapters[:, 4 * R : 6 * R]
        .reshape(owners, 2, R, width)
        .transpose(2, 0, 1, 3)
        .reshape(R, QKV)
    )
    up_out = adapters[:, 6 * R :].transpose(1, 0, 2).reshape(R, MODEL_WIDTH)
    column = jnp.arange(QKV, dtype=jnp.int32)
    part = jnp.where(column < QD, 0, jnp.where(column < QD + KD, 1, 2))
    up_map = jnp.where(
        part[None, None, :] == jnp.arange(4, dtype=jnp.int32)[:, None, None], up[None], 0
    ).reshape(4 * R, QKV)
    up_out_map = jnp.concatenate([jnp.zeros((3 * R, MODEL_WIDTH), bf16), up_out], 0)
    return low_map, up_map, up_out_map


def on_device(
    hidden,
    cotangent,
    lengths,
    adapter_ids,
    routes,
    attn_gain,
    ffn_gain,
    query_key_value_weight,
    w_out,
    w_router,
    w_gate_up,
    w_down,
    attention_lowmap,
    attention_query_key_value_upmap,
    attention_output_upmap,
    expert_gate_up_lowmap,
    expert_gate_up_upmap,
    expert_down_lowmap,
    expert_down_upmap,
):
    groups = lax.axis_size("expert")
    owners = lax.axis_size("dp")
    place = lax.axis_index("expert")
    row = lax.axis_index("dp")
    devices = groups * owners
    sequence = row * groups + place
    rows = hidden.shape[0]
    experts = w_router.shape[1]
    local = w_gate_up.shape[0]
    width = MODEL_WIDTH // owners
    attn_gain = attn_gain.reshape(1, MODEL_WIDTH)
    ffn_gain = ffn_gain.reshape(1, MODEL_WIDTH)
    length = lax.dynamic_slice(lengths, (sequence,), (1,))
    forward = [(at, (at + 1) % groups) for at in range(groups)]
    backward = [(at, (at - 1) % groups) for at in range(groups)]

    mine = lax.dynamic_slice(adapter_ids.reshape(owners, groups), (0, place), (owners, 1))[:, 0]
    low_turned = attention_lowmap.transpose(1, 0, 3, 2).reshape(NA, 4 * R, width)
    up_turned = (
        attention_query_key_value_upmap.reshape(NA, R, 2, width)
        .transpose(0, 2, 1, 3)
        .reshape(NA, 2 * R, width)
    )
    adapters = jnp.concatenate([low_turned, up_turned, attention_output_upmap], 1)[mine]
    adapters = lax.all_to_all(adapters, "dp", 0, 0, tiled=True)
    order = order_of(row)
    first = place * local
    router = jnp.roll(w_router.T, -first, axis=0)
    router_wide = jnp.concatenate(
        [router, jnp.zeros((128 - experts, MODEL_WIDTH), router.dtype)], 0
    )

    offsets = [0, 1] + [groups - 1] * (groups > 2) + list(range(2, groups - 1))
    offset = jnp.array(offsets, jnp.int32)
    source = (place - offset + groups) % groups
    tags = adapter_ids.reshape(owners, groups)[:, source]
    slot = jnp.arange(groups, dtype=jnp.int32)
    table = jnp.stack(
        [
            source,
            lax.dynamic_slice(tags, (row, 0), (1, groups))[0],
            offset * local,
            slot,
            jnp.full((groups,), first, jnp.int32),
        ],
        1,
    )

    steps = [table[at] for at in range(groups)]
    both = pack(query_key_value_weight, w_out)
    cots = {0: cotangent, 1: lax.ppermute(cotangent, "expert", forward)}
    if owners == BLOCKS:
        pair = both_neighbours(both)
        pair, order, router, router_wide, steps, tags, attn_gain, ffn_gain, length = tied(
            pair, order, router, router_wide, steps, tags, attn_gain, ffn_gain, length
        )
        sides, adapters = tied(across(pair), adapters)
        low_map, up_map, up_out_map = maps_of(adapters, owners, width)
        near = jnp.concatenate([both, *pair, *sides], 0)
        near, low_map, up_map, up_out_map, cots[1], cotangent = tied(
            near, low_map, up_map, up_out_map, cots[1], cotangent
        )
        weights = near, swap(near, 1)
    else:
        low_map, up_map, up_out_map = maps_of(adapters, owners, width)
        whole = lax.all_gather(both, "dp", axis=0, tiled=True)
        weights = whole, whole
    if groups > 2:
        cots[groups - 1] = lax.ppermute(cotangent, "expert", backward)

    cos, sin = rope_tables(rows)


    qkv, low, normed_in = project(order, hidden, attn_gain, weights, low_map, up_map, cos, sin)
    if groups > 3:
        cots[1], low = tied(cots[1], low)
    for at in range(2, groups - 1):
        cots[at] = lax.ppermute(cots[at - 1], "expert", forward)
    attended, lse = attend(length, qkv)
    mid, normed_mid, low_out = close_mixer(
        order, attended, hidden, ffn_gain, weights, low_map, up_out_map
    )

    a_in = expert_gate_up_lowmap.transpose(0, 1, 3, 2)
    a_down = expert_down_lowmap.transpose(0, 1, 3, 2)

    xs = {0: normed_mid, 1: lax.ppermute(normed_mid, "expert", forward)}
    packed = None
    ran = {}
    for at, offset in enumerate(offsets):
        ran[offset], gate_part, packed = run_experts(
            steps[at],
            xs[offset],
            cots[offset],
            routes,
            router_wide,
            w_gate_up,
            w_down,
            a_in,
            expert_gate_up_upmap,
            a_down,
            expert_down_upmap,
            experts,
            groups,
            packed,
        )
        if at == 0:
            gates = gate_part
            if groups > 2:
                normed_mid, packed = tied(normed_mid, packed)
                xs[groups - 1] = lax.ppermute(normed_mid, "expert", backward)
        elif at < groups - 2:
            value, packed = tied(xs[at], packed)
            xs[at + 1] = lax.ppermute(value, "expert", forward)
        if at == 2:
            first_sums, packed = tied(ran[1], packed)

    pieces = lax.all_to_all(to_owners(packed, owners, local), "dp", 0, 0, tiled=True)
    pieces = pieces.reshape(devices, pieces.shape[2], width)
    g_a_in, g_b_in, g_a_down, g_b_down = sum_experts(tags.reshape(devices), pieces, local)

    edge = rows + experts
    both_far = lax.ppermute(first_sums if groups > 2 else ran[1], "expert", forward)
    grad_far, out_far = both_far, both_far[edge:]
    for offset in range(2, groups):
        grad_part = joined(ran[offset][:edge], grad_far[:edge])
        if offset == groups - 1:
            grad_part, g_a_down = tied(grad_part, g_a_down)
        grad_far = lax.ppermute(grad_part, "expert", forward)
    if groups > 2:
        out_part = joined(ran[2][edge:], out_far)
        out_part, grad_far = tied(out_part, grad_far)
        out_far = lax.ppermute(out_part, "expert", forward)

    grad_mid, grad_attended, grad_up_out, grad_low_out = open_back(
        order,
        cotangent,
        mid,
        ffn_gain,
        gates,
        router,
        weights,
        low_map,
        up_out_map,
        low_out,
        attended,
        [ran[0], grad_far],
    )
    grad_query, grad_key, grad_value = attend_back(length, qkv, grad_attended, lse, cos, sin)
    out_far, grad_query = tied(out_far, grad_query)
    for offset in range(3, groups):
        out_far = lax.ppermute(joined(ran[offset][edge:], out_far), "expert", forward)
    packed, back_low = adapters_back(
        grad_query, grad_key, grad_value, low, normed_in, up_map, grad_low_out, grad_up_out, devices
    )
    packed = lax.all_to_all(packed, ("dp", "expert"), 0, 0, tiled=True)

    grad_hidden = input_back(
        order, grad_query, grad_key, grad_value, back_low, weights, low_map, hidden, attn_gain, grad_mid
    )
    out = (mid + ran[0][edge:].astype(f32) + out_far.astype(f32)).astype(bf16)
    out, packed = tied(out, packed)
    m_a, m_b, m_o = sum_mixer(adapter_ids, packed)
    return (
        out,
        grad_hidden,
        m_a.transpose(0, 1, 3, 2),
        m_b,
        m_o,
        g_a_in.transpose(0, 1, 3, 2),
        g_b_in,
        g_a_down.transpose(0, 1, 3, 2),
        g_b_down,
    )


def solution(mesh):
    in_specs = (
        P(("dp", "expert"), None),
        P(("dp", "expert"), None),
        P(),
        P(),
        P("dp", None),
        P(),
        P(),
        P("dp", None),
        P("dp", None),
        P(),
        P("expert", None, None),
        P("expert", None, None),
        P(None, None, "dp", None),
        P(None, None, "dp"),
        P(None, None, "dp"),
        P("expert", None, None, None),
        P("expert", None, None, None, None),
        P("expert", None, None, None),
        P("expert", None, None, None),
    )
    out_specs = (
        P(("dp", "expert"), None),
        P(("dp", "expert"), None),
        P(None, None, ("dp", "expert"), None),
        P(None, None, ("dp", "expert")),
        P(None, None, ("dp", "expert")),
        P("expert", None, "dp", None),
        P("expert", None, None, None, "dp"),
        P("expert", None, "dp", None),
        P("expert", None, None, "dp"),
    )
    return jax.shard_map(
        on_device, mesh=mesh, in_specs=in_specs, out_specs=out_specs, check_vma=False
    )
```

```python
import numpy as np
import jax
import jax.numpy as jnp
from jax import lax
from jax.experimental import pallas as pl
from jax.experimental.pallas import tpu as pltpu
from jax.sharding import PartitionSpec as P

MODEL_WIDTH = 1024
HQ = 16
KVH = 8
HS = 64
H = 512
TOP = 8
R = 16
NA = 8
QD = HQ * HS
KD = KVH * HS
QKV = QD + 2 * KD

epsilon = 1e-06
f32 = jnp.float32
bf16 = jnp.bfloat16


def nn(left, right):
    return lax.dot_general(left, right, (((1,), (0,)), ((), ())), preferred_element_type=f32)


def nt(left, right):
    return lax.dot_general(left, right, (((1,), (1,)), ((), ())), preferred_element_type=f32)


def tn(left, right):
    return lax.dot_general(left, right, (((0,), (0,)), ((), ())), preferred_element_type=f32)


def lanes_of(shape):
    return lax.broadcasted_iota(jnp.int32, shape, len(shape) - 1)


def row_scale(rows):
    return lax.rsqrt(jnp.mean(rows * rows, -1, keepdims=True) + epsilon)


def norm_back(rows, gain, grad):
    scale = row_scale(rows)
    scaled = grad * gain
    return scale * scaled - rows * (scale * scale * scale) * jnp.mean(
        rows * scaled, -1, keepdims=True
    )


def rope_swap(rows):
    width = rows.shape[-1]
    lane = lanes_of(rows.shape)
    return jnp.where(
        lane % HS < HS // 2,
        pltpu.roll(rows, width - HS // 2, 1),
        pltpu.roll(rows, HS // 2, 1),
    )


def both_halves(pair, half):
    rows = pair.astype(f32)
    lane = lanes_of(rows.shape)
    rolled = pltpu.roll(rows, HS, 1)
    keep = (lane < HS) == (half == 0)
    return jnp.where(keep, rows, rolled).astype(bf16)


def stacked_heads(pair):
    lane = lanes_of(pair.shape)
    zero = jnp.zeros_like(pair)
    return jnp.concatenate(
        [jnp.where(lane < HS, pair, zero), jnp.where(lane < HS, zero, pair)], 0
    )


def params_of(count):
    return pltpu.CompilerParams(
        dimension_semantics=("arbitrary",) * count, vmem_limit_bytes=56 * 1024 * 1024
    )


BLOCK = 128
BLOCKS = MODEL_WIDTH // BLOCK
HALF = MODEL_WIDTH // 2


def column(order, at):
    return pl.ds(pl.multiple_of(order[at] * BLOCK, BLOCK), BLOCK)


def halves(weights, width, index):
    there = 1 if weights[0] is weights[1] else 0
    return [
        pl.BlockSpec((HALF, width), lambda n, s: (0, index(n))),
        pl.BlockSpec((HALF, width), lambda n, s: (there, index(n))),
    ]


def project_kernel(
    order, hid, gain, weight_a, weight_b, low_map, up_map, cos, sin, qkv, low, normed, turned_rows
):
    step = pl.program_id(0)
    blocks = pl.num_programs(0)

    @pl.when(step == 0)
    def _():
        rows = hid[...].astype(f32)
        value = (rows * row_scale(rows) * gain[...].astype(f32)).astype(bf16)
        normed[...] = value
        low[...] = nt(value, low_map[...]).astype(bf16)
        for at in range(BLOCKS):
            turned_rows[:, at * BLOCK : (at + 1) * BLOCK] = normed[:, column(order, at)]

    value = (
        nn(turned_rows[:, :HALF], weight_a[...])
        + nn(turned_rows[:, HALF:], weight_b[...])
        + nn(low[...], up_map[...])
    )

    @pl.when(step < blocks * 3 // 4)
    def _():
        for part in range(value.shape[1] // 128):
            piece = value[:, part * 128 : part * 128 + 128]
            turned = piece * cos[...] + rope_swap(piece) * sin[...]
            qkv[:, part * 128 : part * 128 + 128] = turned.astype(bf16)

    @pl.when(step >= blocks * 3 // 4)
    def _():
        qkv[...] = value.astype(bf16)


def project(order, hidden, gain, weights, low_map, up_map, cos, sin):
    rows = hidden.shape[0]
    block = 512
    ranks = low_map.shape[0]
    full = lambda shape: pl.BlockSpec(shape, lambda n, s: (0, 0))
    return pl.pallas_call(
        project_kernel,
        grid_spec=pltpu.PrefetchScalarGridSpec(
            num_scalar_prefetch=1,
            grid=(QKV // block,),
            in_specs=[
                full((rows, MODEL_WIDTH)),
                full((1, MODEL_WIDTH)),
                *halves(weights, block, lambda n: n),
                full((ranks, MODEL_WIDTH)),
                pl.BlockSpec((ranks, block), lambda n, s: (0, n)),
                full((rows, 128)),
                full((rows, 128)),
            ],
            out_specs=[
                pl.BlockSpec((rows, block), lambda n, s: (0, n)),
                full((rows, ranks)),
                full((rows, MODEL_WIDTH)),
            ],
            scratch_shapes=[pltpu.VMEM((rows, MODEL_WIDTH), bf16)],
        ),
        out_shape=[
            jax.ShapeDtypeStruct((rows, QKV), bf16),
            jax.ShapeDtypeStruct((rows, ranks), bf16),
            jax.ShapeDtypeStruct((rows, MODEL_WIDTH), bf16),
        ],
        compiler_params=params_of(1),
        name="project",
        cost_estimate=pl.CostEstimate(
            flops=2 * rows * QKV * MODEL_WIDTH, transcendentals=0, bytes_accessed=8 << 20
        ),
    )(order, hidden, gain, *weights, low_map, up_map, cos, sin)


ROWB = 128
BACKB = 256


def length_column(length, count):
    key = lax.broadcasted_iota(jnp.int32, (count, 1), 0)
    return jnp.where(key < length, 0.0, -1e30)


def causal_block(block):
    key = lax.broadcasted_iota(jnp.int32, (block, 2 * block), 0)
    return jnp.where(key <= lanes_of((block, 2 * block)) % block, 0.0, -1e30)


def masked_scores(queries, keys, start, bias, causal):
    count = start + causal.shape[0]
    scores = nt(keys[:count], (queries.astype(f32) * 0.125).astype(bf16))
    near = scores[start:] + (bias[start:count] + causal)
    if start == 0:
        return near
    return jnp.concatenate([scores[:start] + bias[:start], near], 0)


def attend_kernel(scalars, query, key, value, result, lse):
    half = pl.program_id(0) % 2
    keys = both_halves(key[...], half)
    values = both_halves(value[...], half)
    rows = query.shape[0]
    bias = length_column(scalars[0], rows)
    causal = causal_block(ROWB)
    for start in range(0, rows, ROWB):
        count = start + ROWB
        stacked = stacked_heads(query[start:count, :])
        scores = masked_scores(stacked, keys, start, bias, causal)
        top = jnp.max(scores, 0, keepdims=True)
        shifted = jnp.exp(scores - top)
        total = jnp.sum(shifted, 0, keepdims=True)
        prob = (shifted * (1.0 / total)).astype(bf16)
        mixed = tn(prob, values[:count])
        lane = lanes_of((ROWB, 128))
        result[start:count, :] = jnp.where(lane < HS, mixed[:ROWB], mixed[ROWB:]).astype(bf16)
        logs = top + jnp.log(total)
        lse[0, 0:1, start:count] = logs[:, :ROWB]
        lse[0, 1:2, start:count] = logs[:, ROWB:]


def attend(length, qkv):
    rows = qkv.shape[0]
    pairs = KVH
    return pl.pallas_call(
        attend_kernel,
        grid_spec=pltpu.PrefetchScalarGridSpec(
            num_scalar_prefetch=1,
            grid=(pairs,),
            in_specs=[
                pl.BlockSpec((rows, 128), lambda g, s: (0, g)),
                pl.BlockSpec((rows, 128), lambda g, s: (0, QD // 128 + g // 2)),
                pl.BlockSpec((rows, 128), lambda g, s: (0, (QD + KD) // 128 + g // 2)),
            ],
            out_specs=[
                pl.BlockSpec((rows, 128), lambda g, s: (0, g)),
                pl.BlockSpec((1, 2, rows), lambda g, s: (g, 0, 0)),
            ],
        ),
        out_shape=[
            jax.ShapeDtypeStruct((rows, QD), bf16),
            jax.ShapeDtypeStruct((pairs, 2, rows), f32),
        ],
        compiler_params=params_of(1),
        name="attend",
        cost_estimate=pl.CostEstimate(
            flops=8 * rows * rows * QD, transcendentals=rows * rows * HQ, bytes_accessed=4 << 20
        ),
    )(length, qkv, qkv, qkv)


def attend_back_kernel(
    scalars, query, key, value, grad, lse, cos, sin, grad_query, grad_key, grad_value, key_acc, value_acc
):
    half = pl.program_id(0) % 2
    keys = both_halves(key[...], half)
    values = both_halves(value[...], half)
    rows = query.shape[0]
    bias = length_column(scalars[0], rows)
    causal = causal_block(BACKB)
    for start in reversed(range(0, rows, BACKB)):
        count = start + BACKB
        stacked = stacked_heads(query[start:count, :])
        grads = stacked_heads(grad[start:count, :])
        scores = masked_scores(stacked, keys, start, bias, causal)
        logs = jnp.concatenate([lse[0, 0:1, start:count], lse[0, 1:2, start:count]], 1)
        prob = jnp.exp(scores - logs)
        grad_prob = nt(values[:count], grads)
        delta = jnp.sum(prob * grad_prob, 0, keepdims=True)
        grad_score = (prob * (grad_prob - delta)).astype(bf16)
        mixed = tn(grad_score, keys[:count])
        lane = lanes_of((BACKB, 128))
        turned = 0.125 * jnp.where(lane < HS, mixed[:BACKB], mixed[BACKB:])
        turned = turned * cos[start:count, :] - rope_swap(turned) * sin[start:count, :]
        grad_query[start:count, :] = turned.astype(bf16)
        key_part = nn(grad_score, stacked)
        value_part = nn(prob.astype(bf16), grads)
        if count == rows:
            key_acc[...] = key_part
            value_acc[...] = value_part
        else:
            key_acc[:count, :] += key_part
            value_acc[:count, :] += value_part
    total = key_acc[...]
    total = 0.125 * (total + pltpu.roll(total, HS, 1))
    total = (total * cos[...] - rope_swap(total) * sin[...]).astype(bf16)
    other = value_acc[...]
    other = (other + pltpu.roll(other, HS, 1)).astype(bf16)

    @pl.when(half == 0)
    def _():
        grad_key[...] = total
        grad_value[...] = other

    @pl.when(half == 1)
    def _():
        low_half = lanes_of(total.shape) < HS
        grad_key[...] = jnp.where(low_half, grad_key[...], total)
        grad_value[...] = jnp.where(low_half, grad_value[...], other)


def attend_back(length, qkv, grad, lse, cos, sin):
    rows = qkv.shape[0]
    pairs = KVH
    return pl.pallas_call(
        attend_back_kernel,
        grid_spec=pltpu.PrefetchScalarGridSpec(
            num_scalar_prefetch=1,
            grid=(pairs,),
            in_specs=[
                pl.BlockSpec((rows, 128), lambda g, s: (0, g)),
                pl.BlockSpec((rows, 128), lambda g, s: (0, QD // 128 + g // 2)),
                pl.BlockSpec((rows, 128), lambda g, s: (0, (QD + KD) // 128 + g // 2)),
                pl.BlockSpec((rows, 128), lambda g, s: (0, g)),
                pl.BlockSpec((1, 2, rows), lambda g, s: (g, 0, 0)),
                pl.BlockSpec((rows, 128), lambda g, s: (0, 0)),
                pl.BlockSpec((rows, 128), lambda g, s: (0, 0)),
            ],
            out_specs=[
                pl.BlockSpec((rows, 128), lambda g, s: (0, g)),
                pl.BlockSpec((rows, 128), lambda g, s: (0, g // 2)),
                pl.BlockSpec((rows, 128), lambda g, s: (0, g // 2)),
            ],
            scratch_shapes=[pltpu.VMEM((rows, 128), f32), pltpu.VMEM((rows, 128), f32)],
        ),
        out_shape=[
            jax.ShapeDtypeStruct((rows, QD), bf16),
            jax.ShapeDtypeStruct((rows, KD), bf16),
            jax.ShapeDtypeStruct((rows, KD), bf16),
        ],
        compiler_params=params_of(1),
        name="attend_back",
        cost_estimate=pl.CostEstimate(
            flops=20 * rows * rows * QD, transcendentals=rows * rows * HQ, bytes_accessed=8 << 20
        ),
    )(length, qkv, qkv, qkv, grad, lse, cos, sin)


def close_kernel(order, att, hid, gain, weight_a, weight_b, low_map, up_map, mid, normed, low):
    low_value = nt(att[...], low_map[...]).astype(bf16)
    low[...] = low_value
    turned = jnp.concatenate([att[:, column(order, at)] for at in range(BLOCKS)], 1)
    stream = hid[...].astype(f32) + (
        nn(turned[:, :HALF], weight_a[...])
        + nn(turned[:, HALF:], weight_b[...])
        + nn(low_value, up_map[...])
    )
    mid[...] = stream
    normed[...] = (stream * row_scale(stream) * gain[...].astype(f32)).astype(bf16)


def close_mixer(order, att, hidden, gain, weights, low_map, up_map):
    rows = hidden.shape[0]
    block = 256
    ranks = low_map.shape[0]
    full = lambda shape: pl.BlockSpec(shape, lambda n, s: (0, 0))
    part = lambda width: pl.BlockSpec((block, width), lambda n, s: (n, 0))
    return pl.pallas_call(
        close_kernel,
        grid_spec=pltpu.PrefetchScalarGridSpec(
            num_scalar_prefetch=1,
            grid=(rows // block,),
            in_specs=[
                part(QD),
                part(MODEL_WIDTH),
                full((1, MODEL_WIDTH)),
                *halves(weights, MODEL_WIDTH, lambda n: QKV // MODEL_WIDTH),
                full((ranks, QD)),
                full((ranks, MODEL_WIDTH)),
            ],
            out_specs=[part(MODEL_WIDTH), part(MODEL_WIDTH), part(ranks)],
        ),
        out_shape=[
            jax.ShapeDtypeStruct((rows, MODEL_WIDTH), f32),
            jax.ShapeDtypeStruct((rows, MODEL_WIDTH), bf16),
            jax.ShapeDtypeStruct((rows, ranks), bf16),
        ],
        compiler_params=params_of(1),
        name="close_mixer",
        cost_estimate=pl.CostEstimate(
            flops=2 * rows * QD * MODEL_WIDTH, transcendentals=0, bytes_accessed=8 << 20
        ),
    )(order, att, hidden, gain, *weights, low_map, up_map)


def side_by_side(left, right):
    values = []
    for at in range(BLOCKS):
        tile = slice(at // 2 * BLOCK, (at // 2 + 1) * BLOCK)
        low_half = lanes_of((R, BLOCK)) < BLOCK // 2
        if at % 2 == 0:
            value = jnp.where(low_half, left[:, tile], pltpu.roll(right[:, tile], BLOCK // 2, 1))
        else:
            value = jnp.where(low_half, pltpu.roll(left[:, tile], BLOCK // 2, 1), right[:, tile])
        values.append(value.astype(bf16))
    return values


def expert_kernel(
    scalars,
    x,
    cot,
    routes,
    router,
    w_in,
    w_down,
    a_in,
    b_in,
    a_down,
    b_down,
    *rest,
):
    (
        sums_out,
        gates_out,
        packed,
        gates,
        gate_sums,
        low_in,
        low_in_turned,
        b_in_all,
        back_low,
        gated_low,
        back_in,
        acts,
        grads,
        low_grads,
        down_acc,
        out_acc,
        grad_acc,
    ) = rest[-17:]
    expert = pl.program_id(0)
    last = pl.num_programs(0) - 1
    rows = x.shape[0]
    block = rows
    local = a_in.shape[0]
    a_in_all = a_in[...].reshape(local * 2 * R, MODEL_WIDTH)
    a_down_all = a_down[...].reshape(local * R, H)
    b_down_all = b_down[...].reshape(local * R, MODEL_WIDTH)

    @pl.when(expert == 0)
    def _():
        logits = nt(x[...], router[...])
        experts = gates_out.shape[0]
        lane = lanes_of(logits.shape)
        name = lane + scalars[4]
        name = jnp.where(name >= experts, name - experts, name)
        name = jnp.where(lane < experts, name, -1)
        chosen = name == routes[:, 0:1]
        for k in range(1, TOP):
            chosen = chosen | (name == routes[:, k : k + 1])
        top = jnp.max(jnp.where(chosen, logits, -1e30), -1, keepdims=True)
        shifted = jnp.where(chosen, jnp.exp(jnp.where(chosen, logits - top, 0.0)), 0.0)
        weights = shifted / jnp.sum(shifted, -1, keepdims=True)
        gates[...] = weights
        gates_out[...] = weights.T[: gates_out.shape[0], :]
        low = nt(x[...], a_in_all)
        low_in[...] = low.astype(bf16)
        low_in_turned[...] = low.T.astype(bf16)
        back_low[...] = nt(cot[...], b_down_all)
        b_in_all[...] = jnp.zeros_like(b_in_all)
        for e in range(local):
            b_in_all[e * 2 * R : e * 2 * R + R, :H] = b_in[e, 0, 0]
            b_in_all[e * 2 * R + R : (e + 1) * 2 * R, H:] = b_in[e, 0, 1]
        gate_sums[...] = jnp.zeros_like(gate_sums)
        gated_low[...] = jnp.zeros_like(gated_low)
        back_in[...] = jnp.zeros_like(back_in)
        out_acc[...] = jnp.zeros_like(out_acc)
        grad_acc[...] = jnp.zeros_like(grad_acc)
        down_acc[...] = jnp.zeros_like(down_acc)

    def row_step(index, carry):
        at = pl.ds(pl.multiple_of(index * block, block), block)
        lane_in = lanes_of((block, local * 2 * R))
        lane_down = lanes_of((block, local * R))
        in_mine = (lane_in >= expert * 2 * R) & (lane_in < (expert + 1) * 2 * R)
        down_mine = (lane_down >= expert * R) & (lane_down < (expert + 1) * R)
        gate_all = gates[at, :]
        gate_lane = lanes_of(gate_all.shape) == expert
        weight = jnp.sum(jnp.where(gate_lane, gate_all, 0.0), -1, keepdims=True)
        mine = low_in[at, :]
        mine = jnp.where(in_mine, mine, jnp.zeros_like(mine))
        both = nn(x[at, :], w_in[0]) + nn(mine, b_in_all[...])
        gate = both[:, :H]
        upper = both[:, H:]
        sigmoid = jax.nn.sigmoid(gate)
        silu = gate * sigmoid
        act = (silu * upper).astype(bf16)
        acts[at, :] = act
        act_wide = act.astype(f32)
        low = jnp.where(down_mine, nt(act, a_down_all), 0.0).astype(bf16).astype(f32)
        plain = nt(cot[at, :], w_down[0])
        low_plain = back_low[at, :]
        dots = jnp.sum(act_wide * plain, -1, keepdims=True) + jnp.sum(
            low * low_plain, -1, keepdims=True
        )
        sum_lane = lanes_of(gate_all.shape) == expert + scalars[2]
        gate_sums[at, :] += jnp.where(sum_lane, dots, 0.0)
        low_grad = jnp.where(down_mine, weight * low_plain, 0.0).astype(bf16)
        low_grads[at, :] = low_grad
        grad_act = weight * plain + nn(low_grad, a_down_all)
        grad_first = grad_act * upper * sigmoid * (1.0 + gate * (1.0 - sigmoid))
        grad_second = grad_act * silu
        grad_both = jnp.concatenate(
            [grad_first.astype(bf16), grad_second.astype(bf16)], 1
        )
        grads[at, :] = grad_both
        gated_low[at, :] += (weight * low).astype(bf16)
        out_acc[at, :] += nn((weight * act_wide).astype(bf16), w_down[0])
        grad_acc[at, :] += nt(grad_both, w_in[0])
        low_back = jnp.where(in_mine, nt(grad_both, b_in_all[...]), 0.0)
        back_in[at, :] += low_back.astype(bf16)
        return carry

    lax.fori_loop(0, rows // block, row_step, 0)

    turned = low_in_turned[pl.ds(pl.multiple_of(expert * 2 * R, 2 * R), 2 * R), :]
    product = nn(turned, grads[...])
    first_b_in = local * 3 * R
    here = pl.ds(pl.multiple_of(first_b_in + expert * R, R), R)
    for at, value in enumerate(side_by_side(product[:R, :H], product[R:, H:])):
        packed[at, 0, here, :] = value
    down_acc[...] += tn(low_grads[...], acts[...])

    @pl.when(expert == last)
    def _():
        sums_out[:rows, :] = (grad_acc[...] + nn(back_in[...], a_in_all)).astype(bf16)
        experts = gates_out.shape[0]
        sums = gate_sums[...].T[:experts, :]
        sums = jnp.concatenate([sums[: experts // 2], sums[experts // 2 :]], 1)
        high = sums.astype(bf16).astype(f32)
        edge = rows + experts
        sums_out[rows:edge, :] = jnp.concatenate([high, sums - high], 0).astype(bf16)
        sums_out[edge:, :] = (out_acc[...] + nn(gated_low[...], b_down_all)).astype(bf16)
        wide = tn(back_in[...], x[...]).astype(bf16)
        tall = tn(gated_low[...], cot[...]).astype(bf16)
        for at in range(BLOCKS):
            columns = slice(at * BLOCK, (at + 1) * BLOCK)
            packed[at, 0, : local * 2 * R, :] = wide[:, columns]
            packed[at, 0, local * 2 * R : first_b_in, :] = tall[:, columns]
        for pair in range(local // 2):
            lower = down_acc[pair * 2 * R : pair * 2 * R + R, :]
            upper = down_acc[pair * 2 * R + R : (pair + 1) * 2 * R, :]
            row = local * 4 * R + pair * R
            for at, value in enumerate(side_by_side(lower, upper)):
                packed[at, 0, row : row + R, :] = value


def run_experts(
    scalars, x, cot, routes, router, w_in, w_down, a_in, b_in, a_down, b_down, experts, slots, packed
):
    rows = x.shape[0]
    local = w_in.shape[0]
    ranks_in = local * 2 * R
    ranks_down = local * R
    height = local * 9 * R // 2
    kept = [] if packed is None else [packed]
    full = lambda shape: pl.BlockSpec(shape, lambda e, s: (0,) * len(shape))
    return pl.pallas_call(
        expert_kernel,
        grid_spec=pltpu.PrefetchScalarGridSpec(
            num_scalar_prefetch=1,
            grid=(local,),
            in_specs=[
                full((rows, MODEL_WIDTH)),
                full((rows, MODEL_WIDTH)),
                pl.BlockSpec((rows, TOP), lambda e, s: (s[0], 0)),
                full((128, MODEL_WIDTH)),
                pl.BlockSpec((1, MODEL_WIDTH, 2 * H), lambda e, s: (e, 0, 0)),
                pl.BlockSpec((1, H, MODEL_WIDTH), lambda e, s: (e, 0, 0)),
                pl.BlockSpec((local, 1, 2 * R, MODEL_WIDTH), lambda e, s: (0, s[1], 0, 0)),
                pl.BlockSpec((local, 1, 2, R, H), lambda e, s: (0, s[1], 0, 0, 0)),
                pl.BlockSpec((local, 1, R, H), lambda e, s: (0, s[1], 0, 0)),
                pl.BlockSpec((local, 1, R, MODEL_WIDTH), lambda e, s: (0, s[1], 0, 0)),
            ]
            + [pl.BlockSpec(memory_space=pl.ANY)] * len(kept),
            out_specs=[
                full((2 * rows + experts, MODEL_WIDTH)),
                full((experts, rows)),
                pl.BlockSpec((BLOCKS, 1, height, BLOCK), lambda e, s: (0, s[3], 0, 0)),
            ],
            scratch_shapes=[
                pltpu.VMEM((rows, 128), f32),
                pltpu.VMEM((rows, 128), f32),
                pltpu.VMEM((rows, ranks_in), bf16),
                pltpu.VMEM((ranks_in, rows), bf16),
                pltpu.VMEM((ranks_in, 2 * H), bf16),
                pltpu.VMEM((rows, ranks_down), f32),
                pltpu.VMEM((rows, ranks_down), bf16),
                pltpu.VMEM((rows, ranks_in), bf16),
                pltpu.VMEM((rows, H), bf16),
                pltpu.VMEM((rows, 2 * H), bf16),
                pltpu.VMEM((rows, ranks_down), bf16),
                pltpu.VMEM((ranks_down, H), f32),
                pltpu.VMEM((rows, MODEL_WIDTH), f32),
                pltpu.VMEM((rows, MODEL_WIDTH), f32),
            ],
        ),
        out_shape=[
            jax.ShapeDtypeStruct((2 * rows + experts, MODEL_WIDTH), bf16),
            jax.ShapeDtypeStruct((experts, rows), f32),
            jax.ShapeDtypeStruct((BLOCKS, slots, height, BLOCK), bf16),
        ],
        input_output_aliases={11: 2} if kept else {},
        compiler_params=params_of(1),
        name="experts",
        cost_estimate=pl.CostEstimate(
            flops=local * rows * 9 * (1 << 20),
            transcendentals=local * rows * H,
            bytes_accessed=20 << 20,
        ),
    )(scalars, x, cot, routes, router, w_in, w_down, a_in, b_in, a_down, b_down, *kept)


def pack_kernel(left, right, both):
    both[:, : left.shape[1]] = left[...]
    both[:, left.shape[1] :] = right[...]


def pack(left, right):
    return pl.pallas_call(
        pack_kernel,
        out_shape=jax.ShapeDtypeStruct((left.shape[0], left.shape[1] + right.shape[1]), left.dtype),
        name="pack",
    )(left, right)


def open_back_kernel(count, order, cot, mid, gain, gates, router, weight_a, weight_b, low_map, up_map, low, att, *rest):
    parts = rest[:count]
    sums = rest[count : 3 * count]
    grad_mid, grad_att, grad_up, grad_low, columns = rest[3 * count :]
    gate_value = gates[...]
    half = gate_value.shape[0] // 2
    sides = []
    for side in range(2):
        value = None
        for at in range(count):
            pair = sums[2 * at + side][...].astype(f32)
            pair = pair[:half] + pair[half:]
            value = pair if value is None else value + pair
        sides.append(value)
    gate_grad = jnp.concatenate(sides, 0)
    logit = gate_value * (gate_grad - jnp.sum(gate_value * gate_grad, 0, keepdims=True))
    first = logit.astype(bf16)
    left = logit - first.astype(f32)
    second = left.astype(bf16)
    third = (left - second.astype(f32)).astype(bf16)
    grad = tn(first, router[...]) + (tn(second, router[...]) + tn(third, router[...]))
    for piece in parts:
        grad = grad + piece[...].astype(f32)
    total = cot[...].astype(f32) + norm_back(mid[...], gain[...].astype(f32), grad)
    grad_mid[...] = total
    branch = total.astype(bf16)
    low_grad = nt(branch, up_map[...]).astype(bf16)
    columns[...] = nn(low_grad, low_map[...])
    for side, weight in enumerate((weight_a, weight_b)):
        value = nt(branch, weight[...])
        for at in range(BLOCKS // 2):
            columns[:, column(order, side * BLOCKS // 2 + at)] += value[:, at * BLOCK : (at + 1) * BLOCK]
    grad_att[...] = columns[...].astype(bf16)
    up_part = tn(low[...], branch)
    low_part = tn(low_grad, att[...])

    @pl.when(pl.program_id(0) == 0)
    def _():
        grad_up[...] = up_part
        grad_low[...] = low_part

    @pl.when(pl.program_id(0) > 0)
    def _():
        grad_up[...] += up_part
        grad_low[...] += low_part


def open_back(order, cot, mid, gain, gates, router, weights, low_map, up_map, low, att, parts):
    rows = cot.shape[0]
    block = 256
    ranks = low_map.shape[0]
    experts = gates.shape[0]
    full = lambda shape: pl.BlockSpec(shape, lambda n, s: (0, 0))
    part = lambda width: pl.BlockSpec((block, width), lambda n, s: (n, 0))
    count = len(parts)
    below = rows // experts
    sums = [
        pl.BlockSpec((experts, block), lambda n, s: (below, n)),
        pl.BlockSpec((experts, block), lambda n, s: (below, rows // block + n)),
    ]

    def body(*refs):
        open_back_kernel(count, *refs)

    return pl.pallas_call(
        body,
        grid_spec=pltpu.PrefetchScalarGridSpec(
            num_scalar_prefetch=1,
            grid=(rows // block,),
            in_specs=[
                part(MODEL_WIDTH),
                part(MODEL_WIDTH),
                full((1, MODEL_WIDTH)),
                pl.BlockSpec((experts, block), lambda n, s: (0, n)),
                full((experts, MODEL_WIDTH)),
                *halves(weights, MODEL_WIDTH, lambda n: QKV // MODEL_WIDTH),
                full((ranks, QD)),
                full((ranks, MODEL_WIDTH)),
                part(ranks),
                part(QD),
            ]
            + [part(MODEL_WIDTH)] * count
            + sums * count,
            out_specs=[
                part(MODEL_WIDTH),
                part(QD),
                full((ranks, MODEL_WIDTH)),
                full((ranks, QD)),
            ],
            scratch_shapes=[pltpu.VMEM((block, QD), f32)],
        ),
        out_shape=[
            jax.ShapeDtypeStruct((rows, MODEL_WIDTH), f32),
            jax.ShapeDtypeStruct((rows, QD), bf16),
            jax.ShapeDtypeStruct((ranks, MODEL_WIDTH), f32),
            jax.ShapeDtypeStruct((ranks, QD), f32),
        ],
        compiler_params=params_of(1),
        name="open_back",
        cost_estimate=pl.CostEstimate(
            flops=2 * rows * QD * MODEL_WIDTH, transcendentals=0, bytes_accessed=14 << 20
        ),
    )(
        order, cot, mid, gain, gates, router, *weights, low_map, up_map, low, att, *parts,
        *[piece for piece in parts for _ in range(2)],
    )


def adapters_back_kernel(
    grad_query, grad_key, grad_value, low, normed, up_map, low_there, up_there, low_out, *results
):
    pieces = (grad_query, grad_key, grad_value)
    bounds = (0, QD, QD + KD, QKV)
    back = None
    ups = []
    for at in range(3):
        block = pieces[at][...]
        ups.append(tn(low[...], block)[at * R : (at + 1) * R])
        part = nt(block, up_map[:, bounds[at] : bounds[at + 1]])
        back = part if back is None else back + part
    value = back.astype(bf16)
    low_out[...] = value
    lows = tn(value, normed[...]) + low_there[...]
    if len(results) == 2:
        grad_up, grad_low = results
        grad_low[...] = lows
        for at in range(3):
            grad_up[:, bounds[at] : bounds[at + 1]] = ups[at]
        return
    (packed,) = results
    grad_up = jnp.concatenate(ups, 1)
    grad_out = up_there[3 * R :, :]
    small = BLOCK // 4
    lane = lanes_of((R, BLOCK))
    for owner in range(packed.shape[0]):
        tile = slice(owner // 4 * BLOCK, (owner // 4 + 1) * BLOCK)
        offset = owner % 4 * small
        first = jnp.zeros((R, BLOCK), f32)
        for at in range(4):
            piece = lows[at * R : (at + 1) * R, tile]
            shift = (at * small - offset) % BLOCK
            piece = pltpu.roll(piece, shift, 1) if shift else piece
            first = jnp.where((lane >= at * small) & (lane < (at + 1) * small), piece, first)
        piece = grad_up[:, owner // 2 * BLOCK : (owner // 2 + 1) * BLOCK]
        piece = pltpu.roll(piece, BLOCK // 2, 1) if owner % 2 else piece
        other = grad_out[:, tile]
        shift = (2 * small - offset) % BLOCK
        other = pltpu.roll(other, shift, 1) if shift else other
        packed[owner, :, :BLOCK] = first.astype(bf16)
        packed[owner, :, BLOCK:] = jnp.where(
            lane < 2 * small, piece, jnp.where(lane < 3 * small, other, 0.0)
        ).astype(bf16)


def adapters_back(grad_query, grad_key, grad_value, low, normed, up_map, low_there, up_there, devices):
    rows = normed.shape[0]
    ranks = up_map.shape[0]
    if devices * BLOCK // 4 == MODEL_WIDTH:
        results = [jax.ShapeDtypeStruct((devices, R, 2 * BLOCK), bf16)]
    else:
        results = [
            jax.ShapeDtypeStruct((R, QKV), f32),
            jax.ShapeDtypeStruct((ranks, MODEL_WIDTH), f32),
        ]
    back_low, *results = pl.pallas_call(
        adapters_back_kernel,
        out_shape=[jax.ShapeDtypeStruct((rows, ranks), bf16)] + results,
        compiler_params=pltpu.CompilerParams(vmem_limit_bytes=56 * 1024 * 1024),
        name="adapters_back",
        cost_estimate=pl.CostEstimate(
            flops=6 * rows * 256 * QKV, transcendentals=0, bytes_accessed=4 << 20
        ),
    )(grad_query, grad_key, grad_value, low, normed, up_map, low_there, up_there)
    if len(results) == 1:
        return results[0], back_low
    grad_up, grad_low = results
    small = MODEL_WIDTH // devices
    packed = jnp.concatenate(
        [
            grad_low.reshape(4, R, devices, small).transpose(2, 1, 0, 3).reshape(devices, R, 4 * small),
            grad_up.reshape(R, devices, 2 * small).transpose(1, 0, 2),
            up_there[3 * R :].reshape(R, devices, small).transpose(1, 0, 2),
            jnp.zeros((devices, R, small), f32),
        ],
        -1,
    )
    return packed.astype(bf16), back_low


def input_back_kernel(
    order, grad_query, grad_key, grad_value, low, weight_a, weight_b, low_map, hid, gain, mid, grad, columns
):
    columns[...] = nn(low[...], low_map[...])
    for side, weight in enumerate((weight_a, weight_b)):
        value = nt(grad_query[...], weight[:, :QD])
        value = value + nt(grad_key[...], weight[:, QD : QD + KD])
        value = value + nt(grad_value[...], weight[:, QD + KD :])
        for at in range(BLOCKS // 2):
            columns[:, column(order, side * BLOCKS // 2 + at)] += value[:, at * BLOCK : (at + 1) * BLOCK]
    rows = hid[...].astype(f32)
    grad[...] = (mid[...] + norm_back(rows, gain[...].astype(f32), columns[...])).astype(bf16)


def input_back(order, grad_query, grad_key, grad_value, low, weights, low_map, hidden, gain, mid):
    rows = hidden.shape[0]
    block = 256
    ranks = low_map.shape[0]
    full = lambda shape: pl.BlockSpec(shape, lambda n, s: (0, 0))
    part = lambda width: pl.BlockSpec((block, width), lambda n, s: (n, 0))
    return pl.pallas_call(
        input_back_kernel,
        grid_spec=pltpu.PrefetchScalarGridSpec(
            num_scalar_prefetch=1,
            grid=(rows // block,),
            in_specs=[
                part(QD),
                part(KD),
                part(KD),
                part(ranks),
                *halves(weights, QKV, lambda n: 0),
                full((ranks, MODEL_WIDTH)),
                part(MODEL_WIDTH),
                full((1, MODEL_WIDTH)),
                part(MODEL_WIDTH),
            ],
            out_specs=part(MODEL_WIDTH),
            scratch_shapes=[pltpu.VMEM((block, MODEL_WIDTH), f32)],
        ),
        out_shape=jax.ShapeDtypeStruct((rows, MODEL_WIDTH), bf16),
        compiler_params=params_of(1),
        name="input_back",
        cost_estimate=pl.CostEstimate(
            flops=2 * rows * QKV * MODEL_WIDTH, transcendentals=0, bytes_accessed=12 << 20
        ),
    )(order, grad_query, grad_key, grad_value, low, *weights, low_map, hidden, gain, mid)


def sum_experts_kernel(ids, pieces, a_in, b_in, a_down, b_down, acc):
    local = a_in.shape[0]
    small = a_down.shape[-1]
    acc[...] = jnp.zeros_like(acc)

    def step(index, carry):
        acc[ids[index]] += pieces[index].astype(f32)
        return carry

    lax.fori_loop(0, pieces.shape[0], step, 0)
    for e in range(local):
        a_in[e] = acc[:, e * 2 * R : (e + 1) * 2 * R, :]
        at = local * 2 * R + e * R
        b_down[e] = acc[:, at : at + R, :]
        at = local * 3 * R + e * R
        both = acc[:, at : at + R, :]
        b_in[e, :, 0] = both[:, :, :small]
        b_in[e, :, 1] = both[:, :, small:]
        at = local * 4 * R + e // 2 * R
        a_down[e] = acc[:, at : at + R, e % 2 * small : (e % 2 + 1) * small]


def sum_experts(ids, pieces, local):
    height = pieces.shape[1]
    lanes = pieces.shape[2]
    small = lanes // 2
    vmem = pl.BlockSpec(memory_space=pltpu.VMEM)
    return pl.pallas_call(
        sum_experts_kernel,
        in_specs=[pl.BlockSpec(memory_space=pltpu.SMEM), vmem],
        out_specs=[vmem, vmem, vmem, vmem],
        out_shape=[
            jax.ShapeDtypeStruct((local, NA, 2 * R, lanes), f32),
            jax.ShapeDtypeStruct((local, NA, 2, R, small), f32),
            jax.ShapeDtypeStruct((local, NA, R, small), f32),
            jax.ShapeDtypeStruct((local, NA, R, lanes), f32),
        ],
        scratch_shapes=[pltpu.VMEM((NA, height, lanes), f32)],
        compiler_params=pltpu.CompilerParams(vmem_limit_bytes=56 * 1024 * 1024),
        name="sum_experts",
    )(ids, pieces)


def sum_mixer_kernel(ids, pieces, grad_low, grad_up, grad_out, acc):
    width = grad_low.shape[-1]
    acc[...] = jnp.zeros_like(acc)

    def step(index, carry):
        acc[ids[index]] += pieces[index].astype(f32)
        return carry

    lax.fori_loop(0, pieces.shape[0], step, 0)
    total = acc[...]
    for at in range(4):
        grad_low[at] = total[:, :, at * width : (at + 1) * width]
    grad_up[...] = total[:, :, 4 * width : 6 * width]
    grad_out[...] = total[:, :, 6 * width : 7 * width]


def sum_mixer(ids, pieces):
    width = pieces.shape[2] // 8
    vmem = pl.BlockSpec(memory_space=pltpu.VMEM)
    return pl.pallas_call(
        sum_mixer_kernel,
        in_specs=[pl.BlockSpec(memory_space=pltpu.SMEM), vmem],
        out_specs=[vmem, vmem, vmem],
        out_shape=[
            jax.ShapeDtypeStruct((4, NA, R, width), f32),
            jax.ShapeDtypeStruct((NA, R, 2 * width), f32),
            jax.ShapeDtypeStruct((NA, R, width), f32),
        ],
        scratch_shapes=[pltpu.VMEM((NA, R, 8 * width), f32)],
        compiler_params=pltpu.CompilerParams(vmem_limit_bytes=56 * 1024 * 1024),
        name="sum_mixer",
    )(ids, pieces)


def rope_tables(rows):
    half = HS // 2
    frequency = (10000.0 ** (-2.0 * np.arange(half, dtype=np.float32) / HS)).astype(np.float32)
    angles = np.arange(rows, dtype=np.float32)[:, None] * frequency[None, :]
    cos = np.cos(angles.astype(np.float64)).astype(np.float32)
    sin = np.sin(angles.astype(np.float64)).astype(np.float32)
    return (
        jnp.asarray(np.concatenate([cos, cos, cos, cos], 1)),
        jnp.asarray(np.concatenate([-sin, sin, -sin, sin], 1)),
    )


def swap(value, bit):
    return lax.ppermute(value, "dp", [(at, at ^ bit) for at in range(BLOCKS)])


def both_neighbours(weight):
    return swap(weight, 2), swap(weight, 4)


def across(pair):
    one, two = pair
    middle = one.shape[0] // 2
    return swap(two[:middle], 2), swap(one[middle:], 4)


def tied(*values):
    return lax.optimization_barrier(values)


def order_of(row):
    if lax.axis_size("dp") != BLOCKS:
        return jnp.arange(BLOCKS, dtype=jnp.int32)
    return row.astype(jnp.int32) ^ jnp.array([0, 2, 4, 6, 1, 3, 5, 7], jnp.int32)


def to_owners(packed, owners, local):
    split = owners // BLOCKS
    if split == 1:
        return packed
    slots = packed.shape[1]
    edge = local * 3 * R
    wide = packed[:, :, :edge].reshape(BLOCKS, slots, edge, split, BLOCK // split)
    wide = wide.transpose(0, 3, 1, 2, 4).reshape(owners, slots, edge, BLOCK // split)
    rest = packed.shape[2] - edge
    narrow = packed[:, :, edge:].reshape(BLOCKS, slots, rest, 2, split, BLOCK // 2 // split)
    narrow = narrow.transpose(0, 4, 1, 2, 3, 5).reshape(owners, slots, rest, BLOCK // split)
    return jnp.concatenate([wide, narrow], 2)


def joined(left, right):
    return (left.astype(f32) + right.astype(f32)).astype(bf16)


def on_device(
    hidden,
    cotangent,
    lengths,
    adapter_ids,
    routes,
    attn_gain,
    ffn_gain,
    query_key_value_weight,
    w_out,
    w_router,
    w_gate_up,
    w_down,
    attention_lowmap,
    attention_query_key_value_upmap,
    attention_output_upmap,
    expert_gate_up_lowmap,
    expert_gate_up_upmap,
    expert_down_lowmap,
    expert_down_upmap,
):
    groups = lax.axis_size("expert")
    owners = lax.axis_size("dp")
    place = lax.axis_index("expert")
    row = lax.axis_index("dp")
    devices = groups * owners
    sequence = row * groups + place
    rows = hidden.shape[0]
    experts = w_router.shape[1]
    local = w_gate_up.shape[0]
    width = MODEL_WIDTH // owners
    attn_gain = attn_gain.reshape(1, MODEL_WIDTH)
    ffn_gain = ffn_gain.reshape(1, MODEL_WIDTH)
    length = lax.dynamic_slice(lengths, (sequence,), (1,))
    forward = [(at, (at + 1) % groups) for at in range(groups)]
    backward = [(at, (at - 1) % groups) for at in range(groups)]

    mine = lax.dynamic_slice(adapter_ids.reshape(owners, groups), (0, place), (owners, 1))[:, 0]
    low_turned = attention_lowmap.transpose(1, 0, 3, 2).reshape(NA, 4 * R, width)
    up_turned = (
        attention_query_key_value_upmap.reshape(NA, R, 2, width)
        .transpose(0, 2, 1, 3)
        .reshape(NA, 2 * R, width)
    )
    adapters = jnp.concatenate([low_turned, up_turned, attention_output_upmap], 1)[mine]
    adapters = lax.all_to_all(adapters, "dp", 0, 0, tiled=True)
    order = order_of(row)
    first = place * local
    router = jnp.roll(w_router.T, -first, axis=0)
    router_wide = jnp.concatenate(
        [router, jnp.zeros((128 - experts, MODEL_WIDTH), router.dtype)], 0
    )

    offsets = [0, 1] + [groups - 1] * (groups > 2) + list(range(2, groups - 1))
    offset = jnp.array(offsets, jnp.int32)
    source = (place - offset + groups) % groups
    tags = adapter_ids.reshape(owners, groups)[:, source]
    slot = jnp.arange(groups, dtype=jnp.int32)
    table = jnp.stack(
        [
            source,
            lax.dynamic_slice(tags, (row, 0), (1, groups))[0],
            offset * local,
            slot,
            jnp.full((groups,), first, jnp.int32),
        ],
        1,
    )

    steps = [table[at] for at in range(groups)]
    both = pack(query_key_value_weight, w_out)
    cots = {0: cotangent, 1: lax.ppermute(cotangent, "expert", forward)}
    if owners == BLOCKS:
        pair = both_neighbours(both)
        pair, order, router, router_wide, steps, tags, attn_gain, ffn_gain, length = tied(
            pair, order, router, router_wide, steps, tags, attn_gain, ffn_gain, length
        )
        near = jnp.concatenate([both, *pair, *across(pair)], 0)
        near, adapters, cots[1], cotangent = tied(near, adapters, cots[1], cotangent)
        weights = near, swap(near, 1)
    else:
        whole = lax.all_gather(both, "dp", axis=0, tiled=True)
        weights = whole, whole
    if groups > 2:
        cots[groups - 1] = lax.ppermute(cotangent, "expert", backward)

    low_map = adapters[:, : 4 * R].transpose(1, 0, 2).reshape(4 * R, MODEL_WIDTH)
    up = (
        adapters[:, 4 * R : 6 * R]
        .reshape(owners, 2, R, width)
        .transpose(2, 0, 1, 3)
        .reshape(R, QKV)
    )
    up_out = adapters[:, 6 * R :].transpose(1, 0, 2).reshape(R, MODEL_WIDTH)
    column = jnp.arange(QKV, dtype=jnp.int32)
    part = jnp.where(column < QD, 0, jnp.where(column < QD + KD, 1, 2))
    up_map = jnp.where(
        part[None, None, :] == jnp.arange(4, dtype=jnp.int32)[:, None, None], up[None], 0
    ).reshape(4 * R, QKV)
    up_out_map = jnp.concatenate([jnp.zeros((3 * R, MODEL_WIDTH), bf16), up_out], 0)

    cos, sin = rope_tables(rows)


    qkv, low, normed_in = project(order, hidden, attn_gain, weights, low_map, up_map, cos, sin)
    if groups > 3:
        cots[1], low = tied(cots[1], low)
    for at in range(2, groups - 1):
        cots[at] = lax.ppermute(cots[at - 1], "expert", forward)
    attended, lse = attend(length, qkv)
    mid, normed_mid, low_out = close_mixer(
        order, attended, hidden, ffn_gain, weights, low_map, up_out_map
    )

    a_in = expert_gate_up_lowmap.transpose(0, 1, 3, 2)
    a_down = expert_down_lowmap.transpose(0, 1, 3, 2)

    xs = {0: normed_mid, 1: lax.ppermute(normed_mid, "expert", forward)}
    packed = None
    ran = {}
    for at, offset in enumerate(offsets):
        ran[offset], gate_part, packed = run_experts(
            steps[at],
            xs[offset],
            cots[offset],
            routes,
            router_wide,
            w_gate_up,
            w_down,
            a_in,
            expert_gate_up_upmap,
            a_down,
            expert_down_upmap,
            experts,
            groups,
            packed,
        )
        if at == 0:
            gates = gate_part
            if groups > 2:
                normed_mid, packed = tied(normed_mid, packed)
                xs[groups - 1] = lax.ppermute(normed_mid, "expert", backward)
        elif at < groups - 2:
            value, packed = tied(xs[at], packed)
            xs[at + 1] = lax.ppermute(value, "expert", forward)
        if at == 2:
            first_sums, packed = tied(ran[1], packed)

    pieces = lax.all_to_all(to_owners(packed, owners, local), "dp", 0, 0, tiled=True)
    pieces = pieces.reshape(devices, pieces.shape[2], width)
    g_a_in, g_b_in, g_a_down, g_b_down = sum_experts(tags.reshape(devices), pieces, local)

    edge = rows + experts
    both_far = lax.ppermute(first_sums if groups > 2 else ran[1], "expert", forward)
    grad_far, out_far = both_far, both_far[edge:]
    for offset in range(2, groups):
        grad_part = joined(ran[offset][:edge], grad_far[:edge])
        if offset == groups - 1:
            grad_part, g_a_down = tied(grad_part, g_a_down)
        grad_far = lax.ppermute(grad_part, "expert", forward)
    if groups > 2:
        out_part = joined(ran[2][edge:], out_far)
        out_part, grad_far = tied(out_part, grad_far)
        out_far = lax.ppermute(out_part, "expert", forward)

    grad_mid, grad_attended, grad_up_out, grad_low_out = open_back(
        order,
        cotangent,
        mid,
        ffn_gain,
        gates,
        router,
        weights,
        low_map,
        up_out_map,
        low_out,
        attended,
        [ran[0], grad_far],
    )
    grad_query, grad_key, grad_value = attend_back(length, qkv, grad_attended, lse, cos, sin)
    out_far, grad_query = tied(out_far, grad_query)
    for offset in range(3, groups):
        out_far = lax.ppermute(joined(ran[offset][edge:], out_far), "expert", forward)
    packed, back_low = adapters_back(
        grad_query, grad_key, grad_value, low, normed_in, up_map, grad_low_out, grad_up_out, devices
    )
    packed = lax.all_to_all(packed, ("dp", "expert"), 0, 0, tiled=True)

    grad_hidden = input_back(
        order, grad_query, grad_key, grad_value, back_low, weights, low_map, hidden, attn_gain, grad_mid
    )
    out = (mid + ran[0][edge:].astype(f32) + out_far.astype(f32)).astype(bf16)
    out, packed = tied(out, packed)
    m_a, m_b, m_o = sum_mixer(adapter_ids, packed)
    return (
        out,
        grad_hidden,
        m_a.transpose(0, 1, 3, 2),
        m_b,
        m_o,
        g_a_in.transpose(0, 1, 3, 2),
        g_b_in,
        g_a_down.transpose(0, 1, 3, 2),
        g_b_down,
    )


def solution(mesh):
    in_specs = (
        P(("dp", "expert"), None),
        P(("dp", "expert"), None),
        P(),
        P(),
        P("dp", None),
        P(),
        P(),
        P("dp", None),
        P("dp", None),
        P(),
        P("expert", None, None),
        P("expert", None, None),
        P(None, None, "dp", None),
        P(None, None, "dp"),
        P(None, None, "dp"),
        P("expert", None, None, None),
        P("expert", None, None, None, None),
        P("expert", None, None, None),
        P("expert", None, None, None),
    )
    out_specs = (
        P(("dp", "expert"), None),
        P(("dp", "expert"), None),
        P(None, None, ("dp", "expert"), None),
        P(None, None, ("dp", "expert")),
        P(None, None, ("dp", "expert")),
        P("expert", None, "dp", None),
        P("expert", None, None, None, "dp"),
        P("expert", None, "dp", None),
        P("expert", None, None, "dp"),
    )
    return jax.shard_map(
        on_device, mesh=mesh, in_specs=in_specs, out_specs=out_specs, check_vma=False
    )
```
